32 devices in a mesh: rep: 4 (over x, core), shard: 8 (over z, y).
Axes of the slice: x: 2, y: 2, z: 4, core: 2. Of those that a mesh axis runs over, the one named last changes fastest.
Arguments:
- tokens: bfloat16 [4096, 768], P(('rep', 'shard')), may hold values from -6 to 6
- segment_ids: int32 [4096], P(('rep', 'shard')), may hold values from 0 to 3, as said below
- cotangent: bfloat16 [4096, 768], P(('rep', 'shard')), may hold values from -6 to 6
- ln1_gain: bfloat16 [1, 768], P(None, 'shard'), may hold values from 0.25 to 1.75
- ln1_bias: bfloat16 [1, 768], P(None, 'shard'), may hold values from -3 to 3
- qkv_weight: bfloat16 [1, 768, 2304], P(None, 'shard'), may hold values from -0.21875 to 0.21875
- qv_bias: bfloat16 [1, 1536], P(None, 'shard'), may hold values from -3 to 3
- out_weight: bfloat16 [1, 768, 768], P(None, 'shard'), may hold values from -0.875 to 0.875
- out_bias: bfloat16 [1, 768], P(None, 'shard'), may hold values from -3 to 3
- ln2_gain: bfloat16 [1, 768], P(None, 'shard'), may hold values from 0.25 to 1.75
- ln2_bias: bfloat16 [1, 768], P(None, 'shard'), may hold values from -3 to 3
- fc_weight: bfloat16 [1, 768, 3072], P(None, 'shard'), may hold values from -0.21875 to 0.21875
- fc_bias: bfloat16 [1, 3072], P(None, 'shard'), may hold values from -3 to 3
- proj_weight: bfloat16 [1, 3072, 768], P(None, 'shard'), may hold values from -0.109375 to 0.109375
- proj_bias: bfloat16 [1, 768], P(None, 'shard'), may hold values from -3 to 3
Outputs:
- out_tokens: bfloat16 [4096, 768], P(('rep', 'shard'))
- input_grad: float32 [4096, 768], P(('rep', 'shard'))
- grad_ln1_gain: float32 [1, 768], P(None, 'shard')
- grad_ln1_bias: float32 [1, 768], P(None, 'shard')
- grad_qkv_weight: float32 [1, 768, 2304], P(None, 'shard')
- grad_qv_bias: float32 [1, 1536], P(None, 'shard')
- grad_out_weight: float32 [1, 768, 768], P(None, 'shard')
- grad_out_bias: float32 [1, 768], P(None, 'shard')
- grad_ln2_gain: float32 [1, 768], P(None, 'shard')
- grad_ln2_bias: float32 [1, 768], P(None, 'shard')
- grad_fc_weight: float32 [1, 768, 3072], P(None, 'shard')
- grad_fc_bias: float32 [1, 3072], P(None, 'shard')
- grad_proj_weight: float32 [1, 3072, 768], P(None, 'shard')
- grad_proj_bias: float32 [1, 768], P(None, 'shard')
The draws below stay inside these ranges and needn't reach their ends.
Inputs may be any that keep to these rules, and one draw needn't show every extreme that they name: `segment_ids`: each aligned block of 128 rows (one device's rows) holds three documents with ids 0, 1, 2 in this order, each of one row or more, followed by padding rows of id 3, which attend among themselves; the first block has no padding and the last block is half padding.
All inputs are finite; a program needn't handle non-finite values.
Results may differ from the reference program's by a relative error of at most 0.0098.
Values may be sent and summed in bfloat16 or wider, within the bound.
A program may use at most 128 MiB of HBM per device.

```python
import jax
import jax.numpy as jnp
from jax import lax

D = 768
HEADS = 12
HEAD = 64
FF = 3072
LAYERS = 1
CAP = 128
TOKENS = 4096


def draw_segment_ids(key, part):
    blocks = TOKENS // CAP
    key_live, key_first, key_second = jax.random.split(key, 3)
    block_index = jnp.arange(blocks, dtype=jnp.int32).reshape(blocks, 1)
    spare_rows = jax.random.randint(key_live, (blocks, 1), 0, CAP // 2 + 1)
    spare_rows = jnp.where(block_index == blocks - 1, CAP // 2, spare_rows)
    spare_rows = jnp.where(block_index == 0, 0, spare_rows)
    live_rows = CAP - spare_rows
    first_cut = jax.random.randint(key_first, (blocks, 1), live_rows // 4, live_rows // 2 + 1)
    second = jax.random.randint(key_second, (blocks, 1), live_rows // 2 + 1, live_rows * 3 // 4 + 2)
    position = jnp.arange(CAP, dtype=jnp.int32).reshape(1, CAP)
    segment = (position >= first_cut).astype(jnp.int32) + (position >= second).astype(jnp.int32)
    segment = segment + (position >= live_rows).astype(jnp.int32)
    return segment.reshape(TOKENS).astype(jnp.int32)


def levels(key, dims, cuts, smallest, top_value):
    def one(axis_at, blocks):
        steps = jax.random.uniform(jax.random.fold_in(jax.random.fold_in(key, 6), axis_at), (blocks,), jnp.float32, smallest / len(cuts), top_value / len(cuts))
        return jnp.repeat(jnp.exp(steps), dims[axis_at] // blocks).reshape((-1,) + (1,) * (len(dims) - axis_at - 1))

    factor_of = one(*cuts[0])
    for cut in cuts[1:]:
        factor_of = factor_of * one(*cut)
    return factor_of


def centred(stream_key, dims, scale, bound, cuts=(), kind=jnp.bfloat16):
    values = jax.random.normal(stream_key, dims, jnp.float32) * scale
    if len(cuts) > 0:
        values = levels(stream_key, dims, cuts, -0.22, 0.18) * values
    return jnp.clip(values, min=-bound, max=bound).astype(kind)


def setup_inputs(seed: int = 0) -> dict:
    arg_keys = jax.random.split(jax.random.key(seed), 16)
    return {
        "tokens": centred(arg_keys[0], (TOKENS, D), 1.0, 6.0, ((0, 32),)),
        "segment_ids": draw_segment_ids(jax.random.fold_in(arg_keys[15], 71), 0),
        "cotangent": centred(arg_keys[2], (TOKENS, D), 1.0, 6.0, ((0, 32),)),
        "ln1_gain": jnp.clip(1.0 + 0.15 * jax.random.normal(arg_keys[3], (LAYERS, D), jnp.float32), 0.25, 1.75).astype(jnp.bfloat16),
        "ln1_bias": centred(arg_keys[4], (LAYERS, D), 0.5, 3.0, ((1, 8),)),
        "qkv_weight": centred(arg_keys[5], (LAYERS, D, 3 * D), D ** -0.5, 0.21875, ((1, 8),)),
        "qv_bias": centred(arg_keys[6], (LAYERS, 2 * D), 0.5, 3.0, ((1, 8),)),
        "out_weight": centred(arg_keys[7], (LAYERS, D, D), (D // 16) ** -0.5, 0.875, ((1, 8),)),
        "out_bias": centred(arg_keys[8], (LAYERS, D), 0.5, 3.0, ((1, 8),)),
        "ln2_gain": jnp.clip(1.0 + 0.15 * jax.random.normal(arg_keys[9], (LAYERS, D), jnp.float32), 0.25, 1.75).astype(jnp.bfloat16),
        "ln2_bias": centred(arg_keys[10], (LAYERS, D), 0.5, 3.0, ((1, 8),)),
        "fc_weight": centred(arg_keys[11], (LAYERS, D, FF), D ** -0.5, 0.21875, ((1, 8),)),
        "fc_bias": centred(arg_keys[12], (LAYERS, FF), 0.5, 3.0, ((1, 8),)),
        "proj_weight": centred(arg_keys[13], (LAYERS, FF, D), FF ** -0.5, 0.109375, ((1, 8),)),
        "proj_bias": centred(arg_keys[14], (LAYERS, D), 0.5, 3.0, ((1, 8),)),
    }


@jax.custom_vjp
def low(v):
    return lax.optimization_barrier(v.astype(jnp.bfloat16)).astype(jnp.float32)

@jax.custom_vjp
def low_back(v):
    return v

def low_keep(v):
    return (low(v), None)

def low_pass(kept, grad):
    return (grad,)

def back_keep(v):
    return (v, None)

def back_low(kept, grad):
    return (low(grad),)
low.defvjp(low_keep, low_pass)
low_back.defvjp(back_keep, back_low)
epsilon = 1e-05
highest = lax.Precision.HIGHEST

def layer_norm(inputs, norm_gain, norm_shift):
    center = inputs - lax.optimization_barrier(jnp.mean(inputs, axis=-1, keepdims=True))
    inverse_std = lax.rsqrt(lax.optimization_barrier(jnp.mean(center * center, axis=-1, keepdims=True)) + epsilon)
    return center * inverse_std * norm_gain + norm_shift

def one_layer(inputs, allowed, weights):
    ln1_gain, ln1_bias, qkv_weight, qv_bias, out_weight, out_bias, ln2_gain, ln2_bias, fc_weight, fc_bias, proj_weight, proj_bias = weights
    row_count = inputs.shape[0]
    width_all = inputs.shape[1]
    first_low = low(layer_norm(inputs, ln1_gain, ln1_bias))
    offset = jnp.concatenate([qv_bias[:width_all], jnp.zeros((width_all,), jnp.float32), qv_bias[width_all:]])
    projected = low(low_back(jnp.dot(first_low, qkv_weight, precision=highest) + offset))
    queries = projected[:, :width_all].reshape(row_count, HEADS, HEAD)
    keys_all = projected[:, width_all:2 * width_all].reshape(row_count, HEADS, HEAD)
    values_all = projected[:, 2 * width_all:].reshape(row_count, HEADS, HEAD)
    scores = low_back(jnp.einsum('qhd,khd->hqk', queries, keys_all, precision=highest) * HEAD ** (-0.5))
    attn_probs = jax.nn.softmax(jnp.where(allowed[None], scores, -1e+30), axis=-1)
    attn_mixed = jnp.einsum('hqk,khd->qhd', low(attn_probs), values_all, precision=highest)
    attn_mixed = low(low_back(attn_mixed.reshape(row_count, width_all)))
    after_attn = inputs + low_back(jnp.dot(attn_mixed, out_weight, precision=highest) + out_bias)
    second_low = low(layer_norm(after_attn, ln2_gain, ln2_bias))
    hidden_pre = low_back(jnp.dot(second_low, fc_weight, precision=highest) + fc_bias)
    hidden_low = low(jax.nn.gelu(hidden_pre, approximate=True))
    return after_attn + low_back(jnp.dot(hidden_low, proj_weight, precision=highest) + proj_bias)

def reference(tokens, segment_ids, cotangent, ln1_gain, ln1_bias, qkv_weight, qv_bias, out_weight, out_bias, ln2_gain, ln2_bias, fc_weight, fc_bias, proj_weight, proj_bias):
    weights = tuple((stacked.astype(jnp.float32) for stacked in (ln1_gain, ln1_bias, qkv_weight, qv_bias, out_weight, out_bias, ln2_gain, ln2_bias, fc_weight, fc_bias, proj_weight, proj_bias)))
    block_rows = tokens.astype(jnp.float32).reshape(-1, CAP, D)
    block_ids = segment_ids.reshape(-1, CAP)
    block_cots = cotangent.astype(jnp.float32).reshape(-1, CAP, D)
    positions = jnp.arange(CAP)

    def block_step(totals, block_data):
        rows_in, ids_in, cot_in = block_data
        allowed = (ids_in[:, None] == ids_in[None, :]) & (positions[None, :] <= positions[:, None])

        def forward(params, inputs):
            for layer_index in range(LAYERS):
                inputs = one_layer(inputs, allowed, tuple((stacked[layer_index] for stacked in params)))
            return inputs
        result, pullback = jax.vjp(forward, weights, rows_in)
        grad_params, grad_rows = pullback(cot_in)
        summed = tuple((total + extra for total, extra in zip(totals, grad_params)))
        return (summed, (result.astype(jnp.bfloat16), grad_rows))
    initial = tuple((jnp.zeros(stacked.shape, jnp.float32) for stacked in weights))
    totals, (outputs, input_grads) = lax.scan(block_step, initial, (block_rows, block_ids, block_cots))
    return (outputs.reshape(-1, D), input_grads.reshape(-1, D), totals[0], totals[1], totals[2], totals[3], totals[4], totals[5], totals[6], totals[7], totals[8], totals[9], totals[10], totals[11])
```

```python
import jax
import jax.numpy as jnp
from jax import lax
from jax.sharding import PartitionSpec as P

HEADS = 12
HEAD = 64
LAYERS = 1

epsilon = 1e-05

def to_float(value):
    return value.astype(jnp.float32)


def layer_norm(inputs, norm_gain, norm_shift):
    center = inputs - jnp.mean(inputs, axis=-1, keepdims=True)
    inverse_std = lax.rsqrt(jnp.mean(center * center, axis=-1, keepdims=True) + epsilon)
    normed = center * inverse_std
    return (normed * norm_gain + norm_shift, normed, inverse_std)


def norm_back(upstream, normed, inverse_std, norm_gain):
    scaled = upstream * norm_gain
    inner_term = scaled - jnp.mean(scaled, axis=-1, keepdims=True)
    inner_term = inner_term - normed * jnp.mean(scaled * normed, axis=-1, keepdims=True)
    return (inverse_std * inner_term, jnp.sum(upstream * normed, axis=0), jnp.sum(upstream, axis=0))


def layer_forward(inputs, allowed, small, weights):
    ln1_gain, ln1_bias, qv_bias, out_bias, ln2_gain, ln2_bias, fc_bias, proj_bias = small
    qkv_weight, out_weight, fc_weight, proj_weight = weights
    row_count = inputs.shape[0]
    width_all = inputs.shape[1]
    first_norm, normed_one, inverse_one = layer_norm(inputs, ln1_gain, ln1_bias)
    first_low = first_norm.astype(jnp.bfloat16)
    offset = jnp.concatenate(
        [qv_bias[:width_all], jnp.zeros((width_all,), jnp.float32), qv_bias[width_all:]]
    )
    projected = (
        jnp.dot(first_low, qkv_weight, preferred_element_type=jnp.float32) + offset
    ).astype(jnp.bfloat16)
    queries = projected[:, :width_all].reshape(row_count, HEADS, HEAD)
    keys_all = projected[:, width_all : 2 * width_all].reshape(row_count, HEADS, HEAD)
    values_all = projected[:, 2 * width_all :].reshape(row_count, HEADS, HEAD)
    scores = jnp.einsum(
        "qhd,khd->hqk", queries, keys_all, preferred_element_type=jnp.float32
    ) * HEAD ** (-0.5)
    scores = jnp.where(allowed[None], scores, -1e30)
    row_max = jnp.max(scores, axis=-1, keepdims=True)
    log_total = row_max + jnp.log(jnp.sum(jnp.exp(scores - row_max), axis=-1, keepdims=True))
    attn_probs = jnp.exp(scores - log_total)
    probs_low = attn_probs.astype(jnp.bfloat16)
    attn_mixed = jnp.einsum(
        "hqk,khd->qhd", probs_low, values_all, preferred_element_type=jnp.float32
    )
    attn_mixed = attn_mixed.reshape(row_count, width_all).astype(jnp.bfloat16)
    after_attn = (
        inputs + jnp.dot(attn_mixed, out_weight, preferred_element_type=jnp.float32) + out_bias
    )
    second_norm, normed_two, inverse_two = layer_norm(after_attn, ln2_gain, ln2_bias)
    second_low = second_norm.astype(jnp.bfloat16)
    hidden_pre = jnp.dot(second_low, fc_weight, preferred_element_type=jnp.float32) + fc_bias
    hidden_low = jax.nn.gelu(hidden_pre, approximate=True).astype(jnp.bfloat16)
    result = (
        after_attn + jnp.dot(hidden_low, proj_weight, preferred_element_type=jnp.float32) + proj_bias
    )
    return dict(
        normed_one=normed_one,
        inverse_one=inverse_one,
        first_low=first_low,
        queries=queries,
        keys_all=keys_all,
        values_all=values_all,
        attn_probs=attn_probs,
        probs_low=probs_low,
        attn_mixed=attn_mixed,
        normed_two=normed_two,
        inverse_two=inverse_two,
        second_low=second_low,
        hidden_pre=hidden_pre,
        hidden_low=hidden_low,
        result=result,
    )


def layer_backward(upstream, saved, small, weights):
    ln1_gain, ln1_bias, qv_bias, out_bias, ln2_gain, ln2_bias, fc_bias, proj_bias = small
    qkv_weight, out_weight, fc_weight, proj_weight = weights
    row_count = upstream.shape[0]
    width_all = upstream.shape[1]
    proj_in = upstream.astype(jnp.bfloat16)
    grad_proj_b = jnp.sum(to_float(proj_in), axis=0)
    hidden_grad = jnp.einsum("td,fd->tf", proj_in, proj_weight, preferred_element_type=jnp.float32)
    _, gelu_pull = jax.vjp(lambda value: jax.nn.gelu(value, approximate=True), saved["hidden_pre"])
    pre_grad = gelu_pull(hidden_grad)[0].astype(jnp.bfloat16)
    grad_fc_b = jnp.sum(to_float(pre_grad), axis=0)
    second_grad = jnp.einsum("tf,df->td", pre_grad, fc_weight, preferred_element_type=jnp.float32)
    norm_part, grad_ln2_g, grad_ln2_b = norm_back(
        second_grad, saved["normed_two"], saved["inverse_two"], ln2_gain
    )
    residual_grad = upstream + norm_part
    branch_in = residual_grad.astype(jnp.bfloat16)
    grad_out_b = jnp.sum(to_float(branch_in), axis=0)
    mixed_grad = jnp.einsum("td,cd->tc", branch_in, out_weight, preferred_element_type=jnp.float32)
    mixed_grad = mixed_grad.astype(jnp.bfloat16).reshape(row_count, HEADS, HEAD)
    prob_grad = jnp.einsum(
        "qhd,khd->hqk", mixed_grad, saved["values_all"], preferred_element_type=jnp.float32
    )
    value_grad = jnp.einsum(
        "hqk,qhd->khd", saved["probs_low"], mixed_grad, preferred_element_type=jnp.float32
    )
    attn_probs = saved["attn_probs"]
    row_delta = jnp.sum(attn_probs * prob_grad, axis=-1, keepdims=True)
    score_grad = (attn_probs * (prob_grad - row_delta)).astype(jnp.bfloat16)
    query_grad = jnp.einsum(
        "hqk,khd->qhd", score_grad, saved["keys_all"], preferred_element_type=jnp.float32
    ) * HEAD ** (-0.5)
    key_grad = jnp.einsum(
        "hqk,qhd->khd", score_grad, saved["queries"], preferred_element_type=jnp.float32
    ) * HEAD ** (-0.5)
    joined_grad = jnp.concatenate(
        [
            query_grad.reshape(row_count, width_all),
            key_grad.reshape(row_count, width_all),
            value_grad.reshape(row_count, width_all),
        ],
        axis=1,
    ).astype(jnp.bfloat16)
    column_sums = jnp.sum(to_float(joined_grad), axis=0)
    grad_qv_b = jnp.concatenate([column_sums[:width_all], column_sums[2 * width_all :]])
    first_grad = jnp.einsum(
        "te,ce->tc", joined_grad, qkv_weight, preferred_element_type=jnp.float32
    )
    norm_first, grad_ln1_g, grad_ln1_b = norm_back(
        first_grad, saved["normed_one"], saved["inverse_one"], ln1_gain
    )
    small_grads = (
        grad_ln1_g,
        grad_ln1_b,
        grad_qv_b,
        grad_out_b,
        grad_ln2_g,
        grad_ln2_b,
        grad_fc_b,
        grad_proj_b,
    )
    pairs = (
        (saved["first_low"], joined_grad),
        (saved["attn_mixed"], branch_in),
        (saved["second_low"], pre_grad),
        (saved["hidden_low"], proj_in),
    )
    return (residual_grad + norm_first, small_grads, pairs)


def swap_core(value):
    rep = lax.axis_size("rep")
    return lax.ppermute(value, "rep", perm=[(i, i ^ 1) for i in range(rep)])


def swap_x(value):
    rep = lax.axis_size("rep")
    return lax.ppermute(value, "rep", perm=[(i, i ^ 2) for i in range(rep)])


def join_halves(mine, theirs, core, axis):
    first = jnp.where(core == 0, mine, theirs)
    second = jnp.where(core == 0, theirs, mine)
    return jnp.concatenate([first, second], axis=axis)


def take_half(value, core, axis):
    half = value.shape[axis] // 2
    return lax.dynamic_slice_in_dim(value, core * half, half, axis=axis)


def per_device(
    tokens,
    segment_ids,
    cotangent,
    ln1_gain,
    ln1_bias,
    qkv_weight,
    qv_bias,
    out_weight,
    out_bias,
    ln2_gain,
    ln2_bias,
    fc_weight,
    fc_bias,
    proj_weight,
    proj_bias,
):
    rep = lax.axis_size("rep")
    assert rep == 4
    core = lax.axis_index("rep") % 2
    row_count = tokens.shape[0]
    positions = jnp.arange(row_count)
    allowed = (segment_ids[:, None] == segment_ids[None, :]) & (
        positions[None, :] <= positions[:, None]
    )
    layer_index = 0
    small_local = (ln1_gain, ln1_bias, qv_bias, out_bias, ln2_gain, ln2_bias, fc_bias, proj_bias)
    small_local = [v[layer_index] for v in small_local]
    widths = [v.shape[0] for v in small_local]
    packed = jnp.concatenate(small_local)
    packed_all = lax.all_gather(packed, "shard", axis=0, tiled=False)
    small = []
    start = 0
    for width in widths:
        small.append(to_float(packed_all[:, start : start + width].reshape(-1)))
        start += width
    small = tuple(small)

    local_weights = (
        qkv_weight[layer_index],
        out_weight[layer_index],
        fc_weight[layer_index],
        proj_weight[layer_index],
    )
    weights = []
    for local in local_weights:
        mine = lax.all_gather(take_half(local, core, 1), "shard", axis=0, tiled=True)
        theirs = swap_core(mine)
        weights.append(join_halves(mine, theirs, core, 1))
    weights = tuple(weights)

    residual = to_float(tokens)
    saved = layer_forward(residual, allowed, small, weights)
    out_tokens = saved["result"].astype(jnp.bfloat16)
    upstream = to_float(cotangent)
    input_grad, small_grads, pairs = layer_backward(upstream, saved, small, weights)

    outgoing = jnp.concatenate(
        [x for x, _ in pairs] + [take_half(dy, 1 - core, 1) for _, dy in pairs], axis=1
    )
    incoming = swap_core(outgoing)
    start = 0
    partner_x = []
    for x, _ in pairs:
        partner_x.append(incoming[:, start : start + x.shape[1]])
        start += x.shape[1]
    partner_dy = []
    for _, dy in pairs:
        partner_dy.append(incoming[:, start : start + dy.shape[1] // 2])
        start += dy.shape[1] // 2

    owned = []
    for (x, dy), px, pdy in zip(pairs, partner_x, partner_dy):
        rows = jnp.concatenate([x, px], axis=0)
        grads = jnp.concatenate([take_half(dy, core, 1), pdy], axis=0)
        half_grad = jnp.einsum("tc,te->ce", rows, grads, preferred_element_type=jnp.float32)
        share = lax.psum_scatter(half_grad, "shard", scatter_dimension=0, tiled=True)
        share = share + swap_x(share)
        owned.append(join_halves(share, swap_core(share), core, 1)[None])

    shard = lax.axis_size("shard")
    small_split = jnp.concatenate(
        [g.reshape(shard, -1) for g in small_grads], axis=1
    )
    small_share = lax.psum_scatter(small_split, "shard", scatter_dimension=0, tiled=True)
    small_share = lax.psum(small_share, "rep")
    small_owned = []
    start = 0
    for g in small_grads:
        width = g.shape[0] // shard
        small_owned.append(small_share[:, start : start + width])
        start += width

    (g_ln1_g, g_ln1_b, g_qv_b, g_out_b, g_ln2_g, g_ln2_b, g_fc_b, g_proj_b) = small_owned
    g_qkv, g_out, g_fc, g_proj = owned
    return (
        out_tokens,
        input_grad,
        g_ln1_g,
        g_ln1_b,
        g_qkv,
        g_qv_b,
        g_out,
        g_out_b,
        g_ln2_g,
        g_ln2_b,
        g_fc,
        g_fc_b,
        g_proj,
        g_proj_b,
    )


def solution(mesh):
    placed = (
        P(("rep", "shard"), None),
        P(("rep", "shard")),
        P(("rep", "shard"), None),
        P(None, "shard"),
        P(None, "shard"),
        P(None, "shard", None),
        P(None, "shard"),
        P(None, "shard", None),
        P(None, "shard"),
        P(None, "shard"),
        P(None, "shard"),
        P(None, "shard", None),
        P(None, "shard"),
        P(None, "shard", None),
        P(None, "shard"),
    )
    return jax.shard_map(
        per_device,
        mesh=mesh,
        in_specs=placed,
        out_specs=(
            P(("rep", "shard"), None),
            P(("rep", "shard"), None),
            P(None, "shard"),
            P(None, "shard"),
            P(None, "shard", None),
            P(None, "shard"),
            P(None, "shard", None),
            P(None, "shard"),
            P(None, "shard"),
            P(None, "shard"),
            P(None, "shard", None),
            P(None, "shard"),
            P(None, "shard", None),
            P(None, "shard"),
        ),
        check_vma=False,
    )
```

```python
import jax
import jax.numpy as jnp
from jax import lax
from jax.sharding import PartitionSpec as P

HEADS = 12
HEAD = 64
LAYERS = 1

epsilon = 1e-05

def to_float(value):
    return value.astype(jnp.float32)


def layer_norm(inputs, norm_gain, norm_shift):
    center = inputs - jnp.mean(inputs, axis=-1, keepdims=True)
    inverse_std = lax.rsqrt(jnp.mean(center * center, axis=-1, keepdims=True) + epsilon)
    normed = center * inverse_std
    return (normed * norm_gain + norm_shift, normed, inverse_std)


def norm_back(upstream, normed, inverse_std, norm_gain):
    scaled = upstream * norm_gain
    inner_term = scaled - jnp.mean(scaled, axis=-1, keepdims=True)
    inner_term = inner_term - normed * jnp.mean(scaled * normed, axis=-1, keepdims=True)
    return (inverse_std * inner_term, jnp.sum(upstream * normed, axis=0), jnp.sum(upstream, axis=0))


def layer_forward(inputs, allowed, small, weights):
    ln1_gain, ln1_bias, qv_bias, out_bias, ln2_gain, ln2_bias, fc_bias, proj_bias = small
    qkv_weight, out_weight, fc_weight, proj_weight = weights
    row_count = inputs.shape[0]
    width_all = inputs.shape[1]
    first_norm, normed_one, inverse_one = layer_norm(inputs, ln1_gain, ln1_bias)
    first_low = first_norm.astype(jnp.bfloat16)
    offset = jnp.concatenate(
        [qv_bias[:width_all], jnp.zeros((width_all,), jnp.float32), qv_bias[width_all:]]
    )
    projected = (
        jnp.dot(first_low, qkv_weight, preferred_element_type=jnp.float32) + offset
    ).astype(jnp.bfloat16)
    queries = projected[:, :width_all].reshape(row_count, HEADS, HEAD)
    keys_all = projected[:, width_all : 2 * width_all].reshape(row_count, HEADS, HEAD)
    values_all = projected[:, 2 * width_all :].reshape(row_count, HEADS, HEAD)
    scores = jnp.einsum(
        "qhd,khd->hqk", queries, keys_all, preferred_element_type=jnp.float32
    ) * HEAD ** (-0.5)
    scores = jnp.where(allowed[None], scores, -1e30)
    row_max = jnp.max(scores, axis=-1, keepdims=True)
    log_total = row_max + jnp.log(jnp.sum(jnp.exp(scores - row_max), axis=-1, keepdims=True))
    attn_probs = jnp.exp(scores - log_total)
    probs_low = attn_probs.astype(jnp.bfloat16)
    attn_mixed = jnp.einsum(
        "hqk,khd->qhd", probs_low, values_all, preferred_element_type=jnp.float32
    )
    attn_mixed = attn_mixed.reshape(row_count, width_all).astype(jnp.bfloat16)
    after_attn = (
        inputs + jnp.dot(attn_mixed, out_weight, preferred_element_type=jnp.float32) + out_bias
    )
    second_norm, normed_two, inverse_two = layer_norm(after_attn, ln2_gain, ln2_bias)
    second_low = second_norm.astype(jnp.bfloat16)
    hidden_pre = jnp.dot(second_low, fc_weight, preferred_element_type=jnp.float32) + fc_bias
    hidden_low = jax.nn.gelu(hidden_pre, approximate=True).astype(jnp.bfloat16)
    result = (
        after_attn + jnp.dot(hidden_low, proj_weight, preferred_element_type=jnp.float32) + proj_bias
    )
    return dict(
        normed_one=normed_one,
        inverse_one=inverse_one,
        first_low=first_low,
        queries=queries,
        keys_all=keys_all,
        values_all=values_all,
        attn_probs=attn_probs,
        probs_low=probs_low,
        attn_mixed=attn_mixed,
        normed_two=normed_two,
        inverse_two=inverse_two,
        second_low=second_low,
        hidden_pre=hidden_pre,
        hidden_low=hidden_low,
        result=result,
    )


def layer_backward(upstream, saved, small, weights):
    ln1_gain, ln1_bias, qv_bias, out_bias, ln2_gain, ln2_bias, fc_bias, proj_bias = small
    qkv_weight, out_weight, fc_weight, proj_weight = weights
    row_count = upstream.shape[0]
    width_all = upstream.shape[1]
    proj_in = upstream.astype(jnp.bfloat16)
    grad_proj_b = jnp.sum(to_float(proj_in), axis=0)
    hidden_grad = jnp.einsum("td,fd->tf", proj_in, proj_weight, preferred_element_type=jnp.float32)
    _, gelu_pull = jax.vjp(lambda value: jax.nn.gelu(value, approximate=True), saved["hidden_pre"])
    pre_grad = gelu_pull(hidden_grad)[0].astype(jnp.bfloat16)
    grad_fc_b = jnp.sum(to_float(pre_grad), axis=0)
    second_grad = jnp.einsum("tf,df->td", pre_grad, fc_weight, preferred_element_type=jnp.float32)
    norm_part, grad_ln2_g, grad_ln2_b = norm_back(
        second_grad, saved["normed_two"], saved["inverse_two"], ln2_gain
    )
    residual_grad = upstream + norm_part
    branch_in = residual_grad.astype(jnp.bfloat16)
    grad_out_b = jnp.sum(to_float(branch_in), axis=0)
    mixed_grad = jnp.einsum("td,cd->tc", branch_in, out_weight, preferred_element_type=jnp.float32)
    mixed_grad = mixed_grad.astype(jnp.bfloat16).reshape(row_count, HEADS, HEAD)
    prob_grad = jnp.einsum(
        "qhd,khd->hqk", mixed_grad, saved["values_all"], preferred_element_type=jnp.float32
    )
    value_grad = jnp.einsum(
        "hqk,qhd->khd", saved["probs_low"], mixed_grad, preferred_element_type=jnp.float32
    )
    attn_probs = saved["attn_probs"]
    row_delta = jnp.sum(attn_probs * prob_grad, axis=-1, keepdims=True)
    score_grad = (attn_probs * (prob_grad - row_delta)).astype(jnp.bfloat16)
    query_grad = jnp.einsum(
        "hqk,khd->qhd", score_grad, saved["keys_all"], preferred_element_type=jnp.float32
    ) * HEAD ** (-0.5)
    key_grad = jnp.einsum(
        "hqk,qhd->khd", score_grad, saved["queries"], preferred_element_type=jnp.float32
    ) * HEAD ** (-0.5)
    joined_grad = jnp.concatenate(
        [
            query_grad.reshape(row_count, width_all),
            key_grad.reshape(row_count, width_all),
            value_grad.reshape(row_count, width_all),
        ],
        axis=1,
    ).astype(jnp.bfloat16)
    column_sums = jnp.sum(to_float(joined_grad), axis=0)
    grad_qv_b = jnp.concatenate([column_sums[:width_all], column_sums[2 * width_all :]])
    first_grad = jnp.einsum(
        "te,ce->tc", joined_grad, qkv_weight, preferred_element_type=jnp.float32
    )
    norm_first, grad_ln1_g, grad_ln1_b = norm_back(
        first_grad, saved["normed_one"], saved["inverse_one"], ln1_gain
    )
    small_grads = (
        grad_ln1_g,
        grad_ln1_b,
        grad_qv_b,
        grad_out_b,
        grad_ln2_g,
        grad_ln2_b,
        grad_fc_b,
        grad_proj_b,
    )
    pairs = (
        (saved["first_low"], joined_grad),
        (saved["attn_mixed"], branch_in),
        (saved["second_low"], pre_grad),
        (saved["hidden_low"], proj_in),
    )
    return (residual_grad + norm_first, small_grads, pairs)


def swap_core(value):
    rep = lax.axis_size("rep")
    return lax.ppermute(value, "rep", perm=[(i, i ^ 1) for i in range(rep)])


def swap_x(value):
    rep = lax.axis_size("rep")
    return lax.ppermute(value, "rep", perm=[(i, i ^ 2) for i in range(rep)])


def join_halves(mine, theirs, core, axis):
    first = jnp.where(core == 0, mine, theirs)
    second = jnp.where(core == 0, theirs, mine)
    return jnp.concatenate([first, second], axis=axis)


def take_half(value, core, axis):
    half = value.shape[axis] // 2
    return lax.dynamic_slice_in_dim(value, core * half, half, axis=axis)


def per_device(
    tokens,
    segment_ids,
    cotangent,
    ln1_gain,
    ln1_bias,
    qkv_weight,
    qv_bias,
    out_weight,
    out_bias,
    ln2_gain,
    ln2_bias,
    fc_weight,
    fc_bias,
    proj_weight,
    proj_bias,
):
    rep = lax.axis_size("rep")
    assert rep == 4
    core = lax.axis_index("rep") % 2
    row_count = tokens.shape[0]
    positions = jnp.arange(row_count)
    allowed = (segment_ids[:, None] == segment_ids[None, :]) & (
        positions[None, :] <= positions[:, None]
    )
    layer_index = 0
    shard = lax.axis_size("shard")
    small_local = (ln1_gain, ln1_bias, qv_bias, out_bias, ln2_gain, ln2_bias, fc_bias, proj_bias)
    small_local = [v[layer_index] for v in small_local]
    widths = [v.shape[0] for v in small_local]
    local_weights = (
        qkv_weight[layer_index],
        out_weight[layer_index],
        fc_weight[layer_index],
        proj_weight[layer_index],
    )
    rows_local = local_weights[0].shape[0]
    halves = [take_half(w, core, 1) for w in local_weights]
    half_widths = [h.size // rows_local for h in halves]
    slab = jnp.concatenate(
        [h.reshape(rows_local, -1) for h in halves]
        + [jnp.concatenate(small_local).reshape(rows_local, -1)],
        axis=1,
    )
    gathered = lax.all_gather(slab, "shard", axis=0, tiled=True)
    weight_cols = sum(half_widths)
    theirs_all = swap_core(gathered[:, :weight_cols])
    weights = []
    start = 0
    for local, h, width in zip(local_weights, halves, half_widths):
        def unslab(block):
            return block.reshape(shard, rows_local, width).reshape(shard * h.shape[0], h.shape[1])
        mine = unslab(gathered[:, start : start + width])
        theirs = unslab(theirs_all[:, start : start + width])
        weights.append(join_halves(mine, theirs, core, 1))
        start += width
    weights = tuple(weights)
    packed_all = gathered[:, weight_cols:].reshape(shard, -1)
    small = []
    start = 0
    for width in widths:
        small.append(to_float(packed_all[:, start : start + width].reshape(-1)))
        start += width
    small = tuple(small)

    residual = to_float(tokens)
    saved = layer_forward(residual, allowed, small, weights)
    out_tokens = saved["result"].astype(jnp.bfloat16)
    upstream = to_float(cotangent)
    input_grad, small_grads, pairs = layer_backward(upstream, saved, small, weights)

    outgoing = jnp.concatenate(
        [x for x, _ in pairs] + [take_half(dy, 1 - core, 1) for _, dy in pairs], axis=1
    )
    incoming = swap_core(outgoing)
    start = 0
    partner_x = []
    for x, _ in pairs:
        partner_x.append(incoming[:, start : start + x.shape[1]])
        start += x.shape[1]
    partner_dy = []
    for _, dy in pairs:
        partner_dy.append(incoming[:, start : start + dy.shape[1] // 2])
        start += dy.shape[1] // 2

    grad_slabs = []
    for (x, dy), px, pdy in zip(pairs, partner_x, partner_dy):
        rows = jnp.concatenate([x, px], axis=0)
        grads = jnp.concatenate([take_half(dy, core, 1), pdy], axis=0)
        half_grad = jnp.einsum("tc,te->ce", rows, grads, preferred_element_type=jnp.float32)
        grad_slabs.append(half_grad.reshape(shard, -1, half_grad.shape[1]).reshape(shard * rows_local, -1))
    small_split = jnp.concatenate([g.reshape(shard, -1) for g in small_grads], axis=1)
    grad_slabs.append(small_split.reshape(shard * rows_local, -1))
    share = lax.psum_scatter(jnp.concatenate(grad_slabs, axis=1), "shard", scatter_dimension=0, tiled=True)
    share = share + swap_x(share)
    partner_share = swap_core(share)
    owned = []
    start = 0
    for h, width in zip(halves, half_widths):
        def unslab(block):
            return block.reshape(h.shape[0], h.shape[1])
        mine = unslab(share[:, start : start + width])
        theirs = unslab(partner_share[:, start : start + width])
        owned.append(join_halves(mine, theirs, core, 1)[None])
        start += width
    small_share = (share[:, start:] + partner_share[:, start:]).reshape(1, -1)
    small_owned = []
    start = 0
    for g in small_grads:
        width = g.shape[0] // shard
        small_owned.append(small_share[:, start : start + width])
        start += width

    (g_ln1_g, g_ln1_b, g_qv_b, g_out_b, g_ln2_g, g_ln2_b, g_fc_b, g_proj_b) = small_owned
    g_qkv, g_out, g_fc, g_proj = owned
    return (
        out_tokens,
        input_grad,
        g_ln1_g,
        g_ln1_b,
        g_qkv,
        g_qv_b,
        g_out,
        g_out_b,
        g_ln2_g,
        g_ln2_b,
        g_fc,
        g_fc_b,
        g_proj,
        g_proj_b,
    )


def solution(mesh):
    placed = (
        P(("rep", "shard"), None),
        P(("rep", "shard")),
        P(("rep", "shard"), None),
        P(None, "shard"),
        P(None, "shard"),
        P(None, "shard", None),
        P(None, "shard"),
        P(None, "shard", None),
        P(None, "shard"),
        P(None, "shard"),
        P(None, "shard"),
        P(None, "shard", None),
        P(None, "shard"),
        P(None, "shard", None),
        P(None, "shard"),
    )
    return jax.shard_map(
        per_device,
        mesh=mesh,
        in_specs=placed,
        out_specs=(
            P(("rep", "shard"), None),
            P(("rep", "shard"), None),
            P(None, "shard"),
            P(None, "shard"),
            P(None, "shard", None),
            P(None, "shard"),
            P(None, "shard", None),
            P(None, "shard"),
            P(None, "shard"),
            P(None, "shard"),
            P(None, "shard", None),
            P(None, "shard"),
            P(None, "shard", None),
            P(None, "shard"),
        ),
        check_vma=False,
    )
```

```python
import functools

import jax
import jax.numpy as jnp
from jax import lax
from jax.experimental import pallas as pl
from jax.experimental.pallas import tpu as pltpu
from jax.sharding import PartitionSpec as P

MESH = pl.DeviceIdType.MESH

HEADS = 12
HEAD = 64
LAYERS = 1

epsilon = 1e-05

def to_float(value):
    return value.astype(jnp.float32)


def layer_norm(inputs, norm_gain, norm_shift):
    center = inputs - jnp.mean(inputs, axis=-1, keepdims=True)
    inverse_std = lax.rsqrt(jnp.mean(center * center, axis=-1, keepdims=True) + epsilon)
    normed = center * inverse_std
    return (normed * norm_gain + norm_shift, normed, inverse_std)


def norm_back(upstream, normed, inverse_std, norm_gain):
    scaled = upstream * norm_gain
    inner_term = scaled - jnp.mean(scaled, axis=-1, keepdims=True)
    inner_term = inner_term - normed * jnp.mean(scaled * normed, axis=-1, keepdims=True)
    return (inverse_std * inner_term, jnp.sum(upstream * normed, axis=0), jnp.sum(upstream, axis=0))


def layer_forward(inputs, allowed, small, weights):
    ln1_gain, ln1_bias, qv_bias, out_bias, ln2_gain, ln2_bias, fc_bias, proj_bias = small
    qkv_weight, out_weight, fc_weight, proj_weight = weights
    row_count = inputs.shape[0]
    width_all = inputs.shape[1]
    first_norm, normed_one, inverse_one = layer_norm(inputs, ln1_gain, ln1_bias)
    first_low = first_norm.astype(jnp.bfloat16)
    offset = jnp.concatenate(
        [qv_bias[:width_all], jnp.zeros((width_all,), jnp.float32), qv_bias[width_all:]]
    )
    projected = (
        jnp.dot(first_low, qkv_weight, preferred_element_type=jnp.float32) + offset
    ).astype(jnp.bfloat16)
    queries = projected[:, :width_all].reshape(row_count, HEADS, HEAD)
    keys_all = projected[:, width_all : 2 * width_all].reshape(row_count, HEADS, HEAD)
    values_all = projected[:, 2 * width_all :].reshape(row_count, HEADS, HEAD)
    scores = jnp.einsum(
        "qhd,khd->hqk", queries, keys_all, preferred_element_type=jnp.float32
    ) * HEAD ** (-0.5)
    scores = jnp.where(allowed[None], scores, -1e30)
    row_max = jnp.max(scores, axis=-1, keepdims=True)
    log_total = row_max + jnp.log(jnp.sum(jnp.exp(scores - row_max), axis=-1, keepdims=True))
    attn_probs = jnp.exp(scores - log_total)
    probs_low = attn_probs.astype(jnp.bfloat16)
    attn_mixed = jnp.einsum(
        "hqk,khd->qhd", probs_low, values_all, preferred_element_type=jnp.float32
    )
    attn_mixed = attn_mixed.reshape(row_count, width_all).astype(jnp.bfloat16)
    after_attn = (
        inputs + jnp.dot(attn_mixed, out_weight, preferred_element_type=jnp.float32) + out_bias
    )
    second_norm, normed_two, inverse_two = layer_norm(after_attn, ln2_gain, ln2_bias)
    second_low = second_norm.astype(jnp.bfloat16)
    hidden_pre = jnp.dot(second_low, fc_weight, preferred_element_type=jnp.float32) + fc_bias
    hidden_low = jax.nn.gelu(hidden_pre, approximate=True).astype(jnp.bfloat16)
    result = (
        after_attn + jnp.dot(hidden_low, proj_weight, preferred_element_type=jnp.float32) + proj_bias
    )
    return dict(
        normed_one=normed_one,
        inverse_one=inverse_one,
        first_low=first_low,
        queries=queries,
        keys_all=keys_all,
        values_all=values_all,
        attn_probs=attn_probs,
        probs_low=probs_low,
        attn_mixed=attn_mixed,
        normed_two=normed_two,
        inverse_two=inverse_two,
        second_low=second_low,
        hidden_pre=hidden_pre,
        hidden_low=hidden_low,
        result=result,
    )


def layer_backward(upstream, saved, small, weights):
    ln1_gain, ln1_bias, qv_bias, out_bias, ln2_gain, ln2_bias, fc_bias, proj_bias = small
    qkv_weight, out_weight, fc_weight, proj_weight = weights
    row_count = upstream.shape[0]
    width_all = upstream.shape[1]
    proj_in = upstream.astype(jnp.bfloat16)
    grad_proj_b = jnp.sum(to_float(proj_in), axis=0)
    hidden_grad = jnp.einsum("td,fd->tf", proj_in, proj_weight, preferred_element_type=jnp.float32)
    _, gelu_pull = jax.vjp(lambda value: jax.nn.gelu(value, approximate=True), saved["hidden_pre"])
    pre_grad = gelu_pull(hidden_grad)[0].astype(jnp.bfloat16)
    grad_fc_b = jnp.sum(to_float(pre_grad), axis=0)
    second_grad = jnp.einsum("tf,df->td", pre_grad, fc_weight, preferred_element_type=jnp.float32)
    norm_part, grad_ln2_g, grad_ln2_b = norm_back(
        second_grad, saved["normed_two"], saved["inverse_two"], ln2_gain
    )
    residual_grad = upstream + norm_part
    branch_in = residual_grad.astype(jnp.bfloat16)
    grad_out_b = jnp.sum(to_float(branch_in), axis=0)
    mixed_grad = jnp.einsum("td,cd->tc", branch_in, out_weight, preferred_element_type=jnp.float32)
    mixed_grad = mixed_grad.astype(jnp.bfloat16).reshape(row_count, HEADS, HEAD)
    prob_grad = jnp.einsum(
        "qhd,khd->hqk", mixed_grad, saved["values_all"], preferred_element_type=jnp.float32
    )
    value_grad = jnp.einsum(
        "hqk,qhd->khd", saved["probs_low"], mixed_grad, preferred_element_type=jnp.float32
    )
    attn_probs = saved["attn_probs"]
    row_delta = jnp.sum(attn_probs * prob_grad, axis=-1, keepdims=True)
    score_grad = (attn_probs * (prob_grad - row_delta)).astype(jnp.bfloat16)
    query_grad = jnp.einsum(
        "hqk,khd->qhd", score_grad, saved["keys_all"], preferred_element_type=jnp.float32
    ) * HEAD ** (-0.5)
    key_grad = jnp.einsum(
        "hqk,qhd->khd", score_grad, saved["queries"], preferred_element_type=jnp.float32
    ) * HEAD ** (-0.5)
    joined_grad = jnp.concatenate(
        [
            query_grad.reshape(row_count, width_all),
            key_grad.reshape(row_count, width_all),
            value_grad.reshape(row_count, width_all),
        ],
        axis=1,
    ).astype(jnp.bfloat16)
    column_sums = jnp.sum(to_float(joined_grad), axis=0)
    grad_qv_b = jnp.concatenate([column_sums[:width_all], column_sums[2 * width_all :]])
    first_grad = jnp.einsum(
        "te,ce->tc", joined_grad, qkv_weight, preferred_element_type=jnp.float32
    )
    norm_first, grad_ln1_g, grad_ln1_b = norm_back(
        first_grad, saved["normed_one"], saved["inverse_one"], ln1_gain
    )
    small_grads = (
        grad_ln1_g,
        grad_ln1_b,
        grad_qv_b,
        grad_out_b,
        grad_ln2_g,
        grad_ln2_b,
        grad_fc_b,
        grad_proj_b,
    )
    pairs = (
        (saved["first_low"], joined_grad),
        (saved["attn_mixed"], branch_in),
        (saved["second_low"], pre_grad),
        (saved["hidden_low"], proj_in),
    )
    return (residual_grad + norm_first, small_grads, pairs)


def ring_position(shard_index, n):
    if n != 8:
        return shard_index
    y = shard_index % 2
    z = shard_index // 2
    return z * (1 - 2 * y) + 7 * y


def ring_shard(position, n):
    position = position % n
    if n != 8:
        return position
    y = position // 4
    z = (position % 4) * (1 - 2 * y) + 3 * y
    return z * 2 + y


FIRST_CORE_HALF = (0, 3)


def gather_kernel(n, count, *refs):
    local = refs[:count]
    full = refs[count : 2 * count]
    ring_send, ring_recv, pair_send, pair_recv = refs[2 * count :]
    rep = lax.axis_index("rep")
    shard = lax.axis_index("shard")
    core = rep % 2
    step_dir = 1 - 2 * core
    partner = (rep + step_dir, shard)
    here = ring_position(shard, n)
    target = (rep, ring_shard(here + step_dir, n))
    source = (rep, ring_shard(here - step_dir, n))
    steps = n // 2
    split_last = n % 2 == 0

    barrier = pltpu.get_barrier_semaphore()
    for peer in (target, source, partner):
        pl.semaphore_signal(barrier, inc=1, device_id=peer, device_id_type=MESH)
    pl.semaphore_wait(barrier, 3)

    def mine_at(k, w):
        if split_last and k == steps:
            return (core == 0) == (w in FIRST_CORE_HALF)
        return True

    def guarded(cond, fn):
        if cond is True:
            fn()
        else:
            pl.when(cond)(fn)

    def slot(position):
        return ring_shard(position, n)

    def ring_copy(k, w):
        src_pos = here - step_dir * (k - 1)
        src = local[w] if k == 1 else full[w].at[slot(src_pos)]
        return pltpu.make_async_remote_copy(
            src_ref=src,
            dst_ref=full[w].at[slot(src_pos)],
            send_sem=ring_send.at[k - 1, w],
            recv_sem=ring_recv.at[k - 1, w],
            device_id=target,
            device_id_type=MESH,
        )

    def incoming_ring(k, w):
        pos = here - step_dir * k
        return pltpu.make_async_remote_copy(
            src_ref=full[w].at[slot(pos)],
            dst_ref=full[w].at[slot(pos)],
            send_sem=ring_send.at[k - 1, w],
            recv_sem=ring_recv.at[k - 1, w],
            device_id=source,
            device_id_type=MESH,
        )

    def pair_copy(k, w, pos):
        src = local[w] if k == 0 else full[w].at[slot(pos)]
        return pltpu.make_async_remote_copy(
            src_ref=src,
            dst_ref=full[w].at[slot(pos)],
            send_sem=pair_send.at[k, w],
            recv_sem=pair_recv.at[k, w],
            device_id=partner,
            device_id_type=MESH,
        )

    for w in range(count):
        pair_copy(0, w, here).start()
    for w in range(count):
        guarded(mine_at(1, w), lambda w=w: ring_copy(1, w).start())
    for k in range(1, steps + 1):
        for w in range(count):
            def arrived(k=k, w=w):
                incoming_ring(k, w).wait_recv()
                if k < steps:
                    guarded(mine_at(k + 1, w), lambda: ring_copy(k + 1, w).start())
                pair_copy(k, w, here - step_dir * k).start()
            guarded(mine_at(k, w), arrived)
    for w in range(count):
        pair_copy(0, w, here).wait_recv()
    for k in range(1, steps + 1):
        for w in range(count):
            theirs = mine_at(k, w)
            theirs = True if theirs is True else jnp.logical_not(theirs)
            guarded(theirs, lambda k=k, w=w: pair_copy(k, w, here + step_dir * k).wait_recv())
    for w in range(count):
        pair_copy(0, w, here).wait_send()
    for k in range(1, steps + 1):
        for w in range(count):
            def sent(k=k, w=w):
                ring_copy(k, w).wait_send()
                pair_copy(k, w, here - step_dir * k).wait_send()
            guarded(mine_at(k, w), sent)


def gather_weights(locals_, n):
    count = len(locals_)
    steps = n // 2
    return pl.pallas_call(
        functools.partial(gather_kernel, n, count),
        out_shape=[jax.ShapeDtypeStruct((n,) + a.shape, a.dtype) for a in locals_],
        in_specs=[pl.BlockSpec(memory_space=pl.ANY)] * count,
        out_specs=[pl.BlockSpec(memory_space=pl.ANY)] * count,
        scratch_shapes=[
            pltpu.SemaphoreType.DMA((steps, count)),
            pltpu.SemaphoreType.DMA((steps, count)),
            pltpu.SemaphoreType.DMA((steps + 1, count)),
            pltpu.SemaphoreType.DMA((steps + 1, count)),
        ],
        compiler_params=pltpu.CompilerParams(collective_id=0, has_side_effects=True),
    )(*locals_)


def swap_core(value):
    rep = lax.axis_size("rep")
    return lax.ppermute(value, "rep", perm=[(i, i ^ 1) for i in range(rep)])


def swap_x(value):
    rep = lax.axis_size("rep")
    return lax.ppermute(value, "rep", perm=[(i, i ^ 2) for i in range(rep)])


def join_halves(mine, theirs, core, axis):
    first = jnp.where(core == 0, mine, theirs)
    second = jnp.where(core == 0, theirs, mine)
    return jnp.concatenate([first, second], axis=axis)


def take_half(value, core, axis):
    half = value.shape[axis] // 2
    return lax.dynamic_slice_in_dim(value, core * half, half, axis=axis)


def per_device(
    tokens,
    segment_ids,
    cotangent,
    ln1_gain,
    ln1_bias,
    qkv_weight,
    qv_bias,
    out_weight,
    out_bias,
    ln2_gain,
    ln2_bias,
    fc_weight,
    fc_bias,
    proj_weight,
    proj_bias,
):
    rep = lax.axis_size("rep")
    assert rep == 4
    core = lax.axis_index("rep") % 2
    row_count = tokens.shape[0]
    positions = jnp.arange(row_count)
    allowed = (segment_ids[:, None] == segment_ids[None, :]) & (
        positions[None, :] <= positions[:, None]
    )
    layer_index = 0
    shard = lax.axis_size("shard")
    small_local = (ln1_gain, ln1_bias, qv_bias, out_bias, ln2_gain, ln2_bias, fc_bias, proj_bias)
    small_local = [v[layer_index] for v in small_local]
    widths = [v.shape[0] for v in small_local]
    local_weights = (
        qkv_weight[layer_index],
        out_weight[layer_index],
        fc_weight[layer_index],
        proj_weight[layer_index],
    )
    rows_local = local_weights[0].shape[0]
    small_row = jnp.concatenate(small_local).reshape(1, -1)
    fulls = gather_weights(list(local_weights) + [small_row], shard)
    weights = tuple(f.reshape(-1, f.shape[-1]) for f in fulls[:4])
    halves = [take_half(w, core, 1) for w in local_weights]
    half_widths = [h.size // rows_local for h in halves]
    packed_all = fulls[4].reshape(shard, -1)
    small = []
    start = 0
    for width in widths:
        small.append(to_float(packed_all[:, start : start + width].reshape(-1)))
        start += width
    small = tuple(small)

    residual = to_float(tokens)
    saved = layer_forward(residual, allowed, small, weights)
    out_tokens = saved["result"].astype(jnp.bfloat16)
    upstream = to_float(cotangent)
    input_grad, small_grads, pairs = layer_backward(upstream, saved, small, weights)

    outgoing = jnp.concatenate(
        [x for x, _ in pairs] + [take_half(dy, 1 - core, 1) for _, dy in pairs], axis=1
    )
    incoming = swap_core(outgoing)
    start = 0
    partner_x = []
    for x, _ in pairs:
        partner_x.append(incoming[:, start : start + x.shape[1]])
        start += x.shape[1]
    partner_dy = []
    for _, dy in pairs:
        partner_dy.append(incoming[:, start : start + dy.shape[1] // 2])
        start += dy.shape[1] // 2

    grad_slabs = []
    for (x, dy), px, pdy in zip(pairs, partner_x, partner_dy):
        rows = jnp.concatenate([x, px], axis=0)
        grads = jnp.concatenate([take_half(dy, core, 1), pdy], axis=0)
        half_grad = jnp.einsum("tc,te->ce", rows, grads, preferred_element_type=jnp.float32)
        grad_slabs.append(half_grad.reshape(shard, -1, half_grad.shape[1]).reshape(shard * rows_local, -1))
    small_split = jnp.concatenate([g.reshape(shard, -1) for g in small_grads], axis=1)
    grad_slabs.append(small_split.reshape(shard * rows_local, -1))
    share = lax.psum_scatter(jnp.concatenate(grad_slabs, axis=1), "shard", scatter_dimension=0, tiled=True)
    share = share + swap_x(share)
    partner_share = swap_core(share)
    owned = []
    start = 0
    for h, width in zip(halves, half_widths):
        def unslab(block):
            return block.reshape(h.shape[0], h.shape[1])
        mine = unslab(share[:, start : start + width])
        theirs = unslab(partner_share[:, start : start + width])
        owned.append(join_halves(mine, theirs, core, 1)[None])
        start += width
    small_share = (share[:, start:] + partner_share[:, start:]).reshape(1, -1)
    small_owned = []
    start = 0
    for g in small_grads:
        width = g.shape[0] // shard
        small_owned.append(small_share[:, start : start + width])
        start += width

    (g_ln1_g, g_ln1_b, g_qv_b, g_out_b, g_ln2_g, g_ln2_b, g_fc_b, g_proj_b) = small_owned
    g_qkv, g_out, g_fc, g_proj = owned
    return (
        out_tokens,
        input_grad,
        g_ln1_g,
        g_ln1_b,
        g_qkv,
        g_qv_b,
        g_out,
        g_out_b,
        g_ln2_g,
        g_ln2_b,
        g_fc,
        g_fc_b,
        g_proj,
        g_proj_b,
    )


def solution(mesh):
    placed = (
        P(("rep", "shard"), None),
        P(("rep", "shard")),
        P(("rep", "shard"), None),
        P(None, "shard"),
        P(None, "shard"),
        P(None, "shard", None),
        P(None, "shard"),
        P(None, "shard", None),
        P(None, "shard"),
        P(None, "shard"),
        P(None, "shard"),
        P(None, "shard", None),
        P(None, "shard"),
        P(None, "shard", None),
        P(None, "shard"),
    )
    return jax.shard_map(
        per_device,
        mesh=mesh,
        in_specs=placed,
        out_specs=(
            P(("rep", "shard"), None),
            P(("rep", "shard"), None),
            P(None, "shard"),
            P(None, "shard"),
            P(None, "shard", None),
            P(None, "shard"),
            P(None, "shard", None),
            P(None, "shard"),
            P(None, "shard"),
            P(None, "shard"),
            P(None, "shard", None),
            P(None, "shard"),
            P(None, "shard", None),
            P(None, "shard"),
        ),
        check_vma=False,
    )
```

```python
import functools

import jax
import jax.numpy as jnp
from jax import lax
from jax.experimental import pallas as pl
from jax.experimental.pallas import tpu as pltpu
from jax.sharding import PartitionSpec as P

MESH = pl.DeviceIdType.MESH

HEADS = 12
HEAD = 64
LAYERS = 1

epsilon = 1e-05

def to_float(value):
    return value.astype(jnp.float32)


def layer_norm(inputs, norm_gain, norm_shift):
    center = inputs - jnp.mean(inputs, axis=-1, keepdims=True)
    inverse_std = lax.rsqrt(jnp.mean(center * center, axis=-1, keepdims=True) + epsilon)
    normed = center * inverse_std
    return (normed * norm_gain + norm_shift, normed, inverse_std)


def norm_back(upstream, normed, inverse_std, norm_gain):
    scaled = upstream * norm_gain
    inner_term = scaled - jnp.mean(scaled, axis=-1, keepdims=True)
    inner_term = inner_term - normed * jnp.mean(scaled * normed, axis=-1, keepdims=True)
    return (inverse_std * inner_term, jnp.sum(upstream * normed, axis=0), jnp.sum(upstream, axis=0))


def layer_forward(inputs, allowed, small, weights):
    ln1_gain, ln1_bias, qv_bias, out_bias, ln2_gain, ln2_bias, fc_bias, proj_bias = small
    qkv_weight, out_weight, fc_weight, proj_weight = weights
    row_count = inputs.shape[0]
    width_all = inputs.shape[1]
    first_norm, normed_one, inverse_one = layer_norm(inputs, ln1_gain, ln1_bias)
    first_low = first_norm.astype(jnp.bfloat16)
    offset = jnp.concatenate(
        [qv_bias[:width_all], jnp.zeros((width_all,), jnp.float32), qv_bias[width_all:]]
    )
    projected = (
        jnp.dot(first_low, qkv_weight, preferred_element_type=jnp.float32) + offset
    ).astype(jnp.bfloat16)
    queries = projected[:, :width_all].reshape(row_count, HEADS, HEAD)
    keys_all = projected[:, width_all : 2 * width_all].reshape(row_count, HEADS, HEAD)
    values_all = projected[:, 2 * width_all :].reshape(row_count, HEADS, HEAD)
    scores = jnp.einsum(
        "qhd,khd->hqk", queries, keys_all, preferred_element_type=jnp.float32
    ) * HEAD ** (-0.5)
    scores = jnp.where(allowed[None], scores, -1e30)
    row_max = jnp.max(scores, axis=-1, keepdims=True)
    log_total = row_max + jnp.log(jnp.sum(jnp.exp(scores - row_max), axis=-1, keepdims=True))
    attn_probs = jnp.exp(scores - log_total)
    probs_low = attn_probs.astype(jnp.bfloat16)
    attn_mixed = jnp.einsum(
        "hqk,khd->qhd", probs_low, values_all, preferred_element_type=jnp.float32
    )
    attn_mixed = attn_mixed.reshape(row_count, width_all).astype(jnp.bfloat16)
    after_attn = (
        inputs + jnp.dot(attn_mixed, out_weight, preferred_element_type=jnp.float32) + out_bias
    )
    second_norm, normed_two, inverse_two = layer_norm(after_attn, ln2_gain, ln2_bias)
    second_low = second_norm.astype(jnp.bfloat16)
    hidden_pre = jnp.dot(second_low, fc_weight, preferred_element_type=jnp.float32) + fc_bias
    hidden_low = jax.nn.gelu(hidden_pre, approximate=True).astype(jnp.bfloat16)
    result = (
        after_attn + jnp.dot(hidden_low, proj_weight, preferred_element_type=jnp.float32) + proj_bias
    )
    return dict(
        normed_one=normed_one,
        inverse_one=inverse_one,
        first_low=first_low,
        queries=queries,
        keys_all=keys_all,
        values_all=values_all,
        attn_probs=attn_probs,
        probs_low=probs_low,
        attn_mixed=attn_mixed,
        normed_two=normed_two,
        inverse_two=inverse_two,
        second_low=second_low,
        hidden_pre=hidden_pre,
        hidden_low=hidden_low,
        result=result,
    )


def layer_backward(upstream, saved, small, weights):
    ln1_gain, ln1_bias, qv_bias, out_bias, ln2_gain, ln2_bias, fc_bias, proj_bias = small
    qkv_weight, out_weight, fc_weight, proj_weight = weights
    row_count = upstream.shape[0]
    width_all = upstream.shape[1]
    proj_in = upstream.astype(jnp.bfloat16)
    grad_proj_b = jnp.sum(to_float(proj_in), axis=0)
    hidden_grad = jnp.einsum("td,fd->tf", proj_in, proj_weight, preferred_element_type=jnp.float32)
    _, gelu_pull = jax.vjp(lambda value: jax.nn.gelu(value, approximate=True), saved["hidden_pre"])
    pre_grad = gelu_pull(hidden_grad)[0].astype(jnp.bfloat16)
    grad_fc_b = jnp.sum(to_float(pre_grad), axis=0)
    second_grad = jnp.einsum("tf,df->td", pre_grad, fc_weight, preferred_element_type=jnp.float32)
    norm_part, grad_ln2_g, grad_ln2_b = norm_back(
        second_grad, saved["normed_two"], saved["inverse_two"], ln2_gain
    )
    residual_grad = upstream + norm_part
    branch_in = residual_grad.astype(jnp.bfloat16)
    grad_out_b = jnp.sum(to_float(branch_in), axis=0)
    mixed_grad = jnp.einsum("td,cd->tc", branch_in, out_weight, preferred_element_type=jnp.float32)
    mixed_grad = mixed_grad.astype(jnp.bfloat16).reshape(row_count, HEADS, HEAD)
    prob_grad = jnp.einsum(
        "qhd,khd->hqk", mixed_grad, saved["values_all"], preferred_element_type=jnp.float32
    )
    value_grad = jnp.einsum(
        "hqk,qhd->khd", saved["probs_low"], mixed_grad, preferred_element_type=jnp.float32
    )
    attn_probs = saved["attn_probs"]
    row_delta = jnp.sum(attn_probs * prob_grad, axis=-1, keepdims=True)
    score_grad = (attn_probs * (prob_grad - row_delta)).astype(jnp.bfloat16)
    query_grad = jnp.einsum(
        "hqk,khd->qhd", score_grad, saved["keys_all"], preferred_element_type=jnp.float32
    ) * HEAD ** (-0.5)
    key_grad = jnp.einsum(
        "hqk,qhd->khd", score_grad, saved["queries"], preferred_element_type=jnp.float32
    ) * HEAD ** (-0.5)
    joined_grad = jnp.concatenate(
        [
            query_grad.reshape(row_count, width_all),
            key_grad.reshape(row_count, width_all),
            value_grad.reshape(row_count, width_all),
        ],
        axis=1,
    ).astype(jnp.bfloat16)
    column_sums = jnp.sum(to_float(joined_grad), axis=0)
    grad_qv_b = jnp.concatenate([column_sums[:width_all], column_sums[2 * width_all :]])
    first_grad = jnp.einsum(
        "te,ce->tc", joined_grad, qkv_weight, preferred_element_type=jnp.float32
    )
    norm_first, grad_ln1_g, grad_ln1_b = norm_back(
        first_grad, saved["normed_one"], saved["inverse_one"], ln1_gain
    )
    small_grads = (
        grad_ln1_g,
        grad_ln1_b,
        grad_qv_b,
        grad_out_b,
        grad_ln2_g,
        grad_ln2_b,
        grad_fc_b,
        grad_proj_b,
    )
    pairs = (
        (saved["first_low"], joined_grad),
        (saved["attn_mixed"], branch_in),
        (saved["second_low"], pre_grad),
        (saved["hidden_low"], proj_in),
    )
    return (residual_grad + norm_first, small_grads, pairs)


def ring_position(shard_index, n):
    if n != 8:
        return shard_index
    y = shard_index % 2
    z = shard_index // 2
    return z * (1 - 2 * y) + 7 * y


def ring_shard(position, n):
    position = position % n
    if n != 8:
        return position
    y = position // 4
    z = (position % 4) * (1 - 2 * y) + 3 * y
    return z * 2 + y


FIRST_CORE_HALF = (0, 3)


def gather_kernel(n, count, *refs):
    local = refs[:count]
    full = refs[count : 2 * count]
    ring_send, ring_recv, pair_send, pair_recv = refs[2 * count :]
    rep = lax.axis_index("rep")
    shard = lax.axis_index("shard")
    core = rep % 2
    step_dir = 1 - 2 * core
    partner = (rep + step_dir, shard)
    here = ring_position(shard, n)
    target = (rep, ring_shard(here + step_dir, n))
    source = (rep, ring_shard(here - step_dir, n))
    steps = n // 2
    split_last = n % 2 == 0

    barrier = pltpu.get_barrier_semaphore()
    for peer in (target, source, partner):
        pl.semaphore_signal(barrier, inc=1, device_id=peer, device_id_type=MESH)
    pl.semaphore_wait(barrier, 3)

    def mine_at(k, w):
        if split_last and k == steps:
            return (core == 0) == (w in FIRST_CORE_HALF)
        return True

    def guarded(cond, fn):
        if cond is True:
            fn()
        else:
            pl.when(cond)(fn)

    def slot(position):
        return ring_shard(position, n)

    def ring_copy(k, w):
        src_pos = here - step_dir * (k - 1)
        src = local[w] if k == 1 else full[w].at[slot(src_pos)]
        return pltpu.make_async_remote_copy(
            src_ref=src,
            dst_ref=full[w].at[slot(src_pos)],
            send_sem=ring_send.at[k - 1, w],
            recv_sem=ring_recv.at[k - 1, w],
            device_id=target,
            device_id_type=MESH,
        )

    def incoming_ring(k, w):
        pos = here - step_dir * k
        return pltpu.make_async_remote_copy(
            src_ref=full[w].at[slot(pos)],
            dst_ref=full[w].at[slot(pos)],
            send_sem=ring_send.at[k - 1, w],
            recv_sem=ring_recv.at[k - 1, w],
            device_id=source,
            device_id_type=MESH,
        )

    def pair_copy(k, w, pos):
        src = local[w] if k == 0 else full[w].at[slot(pos)]
        return pltpu.make_async_remote_copy(
            src_ref=src,
            dst_ref=full[w].at[slot(pos)],
            send_sem=pair_send.at[k, w],
            recv_sem=pair_recv.at[k, w],
            device_id=partner,
            device_id_type=MESH,
        )

    for w in range(count):
        pair_copy(0, w, here).start()
    for w in range(count):
        guarded(mine_at(1, w), lambda w=w: ring_copy(1, w).start())
    for k in range(1, steps + 1):
        for w in range(count):
            def arrived(k=k, w=w):
                incoming_ring(k, w).wait_recv()
                if k < steps:
                    guarded(mine_at(k + 1, w), lambda: ring_copy(k + 1, w).start())
                pair_copy(k, w, here - step_dir * k).start()
            guarded(mine_at(k, w), arrived)
    for w in range(count):
        pair_copy(0, w, here).wait_recv()
    for k in range(1, steps + 1):
        for w in range(count):
            theirs = mine_at(k, w)
            theirs = True if theirs is True else jnp.logical_not(theirs)
            guarded(theirs, lambda k=k, w=w: pair_copy(k, w, here + step_dir * k).wait_recv())
    for w in range(count):
        pair_copy(0, w, here).wait_send()
    for k in range(1, steps + 1):
        for w in range(count):
            def sent(k=k, w=w):
                ring_copy(k, w).wait_send()
                pair_copy(k, w, here - step_dir * k).wait_send()
            guarded(mine_at(k, w), sent)


def gather_weights(locals_, n):
    count = len(locals_)
    steps = n // 2
    return pl.pallas_call(
        functools.partial(gather_kernel, n, count),
        out_shape=[jax.ShapeDtypeStruct((n,) + a.shape, a.dtype) for a in locals_],
        in_specs=[pl.BlockSpec(memory_space=pl.ANY)] * count,
        out_specs=[pl.BlockSpec(memory_space=pl.ANY)] * count,
        scratch_shapes=[
            pltpu.SemaphoreType.DMA((steps, count)),
            pltpu.SemaphoreType.DMA((steps, count)),
            pltpu.SemaphoreType.DMA((steps + 1, count)),
            pltpu.SemaphoreType.DMA((steps + 1, count)),
        ],
        compiler_params=pltpu.CompilerParams(collective_id=0, has_side_effects=True),
    )(*locals_)


def add_rows(dst, parts, rows, chunk):
    def body(i, carry):
        window = pl.ds(pl.multiple_of(i * chunk, chunk), chunk)
        total = parts[0][window, :]
        for part in parts[1:]:
            total = total + part[window, :]
        dst[window, :] = total
        return carry

    lax.fori_loop(0, rows // chunk, body, 0)


def reduce_kernel(n, count, *refs):
    contrib = refs[:count]
    out = refs[count : 2 * count]
    land, send, other, own = (refs[2 * count + i * count : 2 * count + (i + 1) * count] for i in range(4))
    load_sem, own_sem, ring_send, ring_recv, pair_send, pair_recv = refs[6 * count :]
    rep = lax.axis_index("rep")
    shard = lax.axis_index("shard")
    core = rep % 2
    step_dir = 1 - 2 * core
    partner = (rep + step_dir, shard)
    here = ring_position(shard, n)
    target = (rep, ring_shard(here + step_dir, n))
    source = (rep, ring_shard(here - step_dir, n))
    steps = n // 2
    split_first = n % 2 == 0

    def carried(k, w):
        if split_first and k == 1:
            return (core == 0) == (w in FIRST_CORE_HALF)
        return True

    def guarded(cond, fn):
        if cond is True:
            fn()
        else:
            pl.when(cond)(fn)

    def block_at(k):
        return here + step_dir * (steps - k + 1)

    def load(k, w):
        return pltpu.make_async_copy(contrib[w].at[ring_shard(block_at(k), n)], send[w].at[k - 1], load_sem.at[k - 1, w])

    def load_own(w):
        return pltpu.make_async_copy(contrib[w].at[shard], own[w], own_sem.at[w])

    def ring_copy(k, w, device):
        return pltpu.make_async_remote_copy(
            src_ref=send[w].at[k - 1],
            dst_ref=land[w].at[k - 1],
            send_sem=ring_send.at[k - 1, w],
            recv_sem=ring_recv.at[k - 1, w],
            device_id=device,
            device_id_type=MESH,
        )

    def pair_copy(w):
        return pltpu.make_async_remote_copy(
            src_ref=land[w].at[steps - 1],
            dst_ref=other[w],
            send_sem=pair_send.at[w],
            recv_sem=pair_recv.at[w],
            device_id=partner,
            device_id_type=MESH,
        )

    for w in range(count):
        load_own(w).start()
    for k in range(1, steps + 1):
        for w in range(count):
            guarded(carried(k, w), lambda k=k, w=w: load(k, w).start())

    barrier = pltpu.get_barrier_semaphore()
    for peer in (target, source, partner):
        pl.semaphore_signal(barrier, inc=1, device_id=peer, device_id_type=MESH)
    pl.semaphore_wait(barrier, 3)

    for k in range(1, steps + 1):
        for w in range(count):
            def step(k=k, w=w):
                load(k, w).wait()
                if k > 1:
                    def accumulate():
                        ring_copy(k - 1, w, source).wait_recv()
                        rows = send[w].shape[1]
                        chunk = 8 if rows % 8 == 0 else rows
                        add_rows(send[w].at[k - 1], [send[w].at[k - 1], land[w].at[k - 2]], rows, chunk)
                    guarded(carried(k - 1, w), accumulate)
                ring_copy(k, w, target).start()
            guarded(carried(k, w), step)
    for w in range(count):
        ring_copy(steps, w, source).wait_recv()
        pair_copy(w).start()
    for w in range(count):
        pair_copy(w).wait_recv()
        load_own(w).wait()
        rows = own[w].shape[0]
        chunk = 8 if rows % 8 == 0 else rows
        mine = land[w].at[steps - 1]

        @pl.when(core == 0)
        def _():
            add_rows(out[w], [own[w], mine, other[w]], rows, chunk)

        @pl.when(core == 1)
        def _():
            add_rows(out[w], [own[w], other[w], mine], rows, chunk)

    for w in range(count):
        pair_copy(w).wait_send()
    for k in range(1, steps + 1):
        for w in range(count):
            guarded(carried(k, w), lambda k=k, w=w: ring_copy(k, w, target).wait_send())


def reduce_gradients(contribs, n):
    count = len(contribs)
    steps = n // 2
    blocks = [c.shape[1:] for c in contribs]
    vmem = lambda shape: pltpu.VMEM(shape, jnp.float32)
    return pl.pallas_call(
        functools.partial(reduce_kernel, n, count),
        out_shape=[jax.ShapeDtypeStruct(b, jnp.float32) for b in blocks],
        in_specs=[pl.BlockSpec(memory_space=pl.ANY)] * count,
        out_specs=[pl.BlockSpec(memory_space=pltpu.VMEM)] * count,
        scratch_shapes=[vmem((steps,) + b) for b in blocks]
        + [vmem((steps,) + b) for b in blocks]
        + [vmem(b) for b in blocks]
        + [vmem(b) for b in blocks]
        + [
            pltpu.SemaphoreType.DMA((steps, count)),
            pltpu.SemaphoreType.DMA((count,)),
            pltpu.SemaphoreType.DMA((steps, count)),
            pltpu.SemaphoreType.DMA((steps, count)),
            pltpu.SemaphoreType.DMA((count,)),
            pltpu.SemaphoreType.DMA((count,)),
        ],
        compiler_params=pltpu.CompilerParams(
            collective_id=1, has_side_effects=True, vmem_limit_bytes=60 * 1024 * 1024
        ),
    )(*contribs)


def swap_core(value):
    rep = lax.axis_size("rep")
    return lax.ppermute(value, "rep", perm=[(i, i ^ 1) for i in range(rep)])


def swap_x(value):
    rep = lax.axis_size("rep")
    return lax.ppermute(value, "rep", perm=[(i, i ^ 2) for i in range(rep)])


def join_halves(mine, theirs, core, axis):
    first = jnp.where(core == 0, mine, theirs)
    second = jnp.where(core == 0, theirs, mine)
    return jnp.concatenate([first, second], axis=axis)


def take_half(value, core, axis):
    half = value.shape[axis] // 2
    return lax.dynamic_slice_in_dim(value, core * half, half, axis=axis)


def per_device(
    tokens,
    segment_ids,
    cotangent,
    ln1_gain,
    ln1_bias,
    qkv_weight,
    qv_bias,
    out_weight,
    out_bias,
    ln2_gain,
    ln2_bias,
    fc_weight,
    fc_bias,
    proj_weight,
    proj_bias,
):
    rep = lax.axis_size("rep")
    assert rep == 4
    core = lax.axis_index("rep") % 2
    row_count = tokens.shape[0]
    positions = jnp.arange(row_count)
    allowed = (segment_ids[:, None] == segment_ids[None, :]) & (
        positions[None, :] <= positions[:, None]
    )
    layer_index = 0
    shard = lax.axis_size("shard")
    small_local = (ln1_gain, ln1_bias, qv_bias, out_bias, ln2_gain, ln2_bias, fc_bias, proj_bias)
    small_local = [v[layer_index] for v in small_local]
    widths = [v.shape[0] for v in small_local]
    local_weights = (
        qkv_weight[layer_index],
        out_weight[layer_index],
        fc_weight[layer_index],
        proj_weight[layer_index],
    )
    rows_local = local_weights[0].shape[0]
    small_row = jnp.concatenate(small_local).reshape(1, -1)
    fulls = gather_weights(list(local_weights) + [small_row], shard)
    weights = tuple(f.reshape(-1, f.shape[-1]) for f in fulls[:4])
    halves = [take_half(w, core, 1) for w in local_weights]
    half_widths = [h.size // rows_local for h in halves]
    packed_all = fulls[4].reshape(shard, -1)
    small = []
    start = 0
    for width in widths:
        small.append(to_float(packed_all[:, start : start + width].reshape(-1)))
        start += width
    small = tuple(small)

    residual = to_float(tokens)
    saved = layer_forward(residual, allowed, small, weights)
    out_tokens = saved["result"].astype(jnp.bfloat16)
    upstream = to_float(cotangent)
    input_grad, small_grads, pairs = layer_backward(upstream, saved, small, weights)

    outgoing = jnp.concatenate([x for x, _ in pairs] + [dy for _, dy in pairs], axis=1)
    incoming = swap_core(outgoing)
    small_mine = jnp.concatenate([g.reshape(shard, -1) for g in small_grads], axis=1)
    small_theirs = swap_core(small_mine)
    small_chip = jnp.where(core == 0, small_mine + small_theirs, small_theirs + small_mine)
    contribs = []
    start = 0
    partner_x = []
    for x, _ in pairs:
        partner_x.append(incoming[:, start : start + x.shape[1]])
        start += x.shape[1]
    for (x, dy), px in zip(pairs, partner_x):
        pdy = incoming[:, start : start + dy.shape[1]]
        start += dy.shape[1]
        rows = join_halves(x, px, core, 0)
        grads = join_halves(dy, pdy, core, 0)
        grad = jnp.einsum("tc,te->ce", rows, grads, preferred_element_type=jnp.float32)
        contribs.append(grad.reshape(shard, -1, grad.shape[1]))
    contribs.append(small_chip.reshape(shard, 1, -1))
    plane = reduce_gradients(contribs, shard)
    owned = []
    for total in plane:
        half = take_half(total, core, 1)
        half = half + swap_x(half)
        owned.append(join_halves(half, swap_core(half), core, 1))
    small_share = owned[4]
    owned = [o[None] for o in owned[:4]]
    small_owned = []
    start = 0
    for g in small_grads:
        width = g.shape[0] // shard
        small_owned.append(small_share[:, start : start + width])
        start += width

    (g_ln1_g, g_ln1_b, g_qv_b, g_out_b, g_ln2_g, g_ln2_b, g_fc_b, g_proj_b) = small_owned
    g_qkv, g_out, g_fc, g_proj = owned
    return (
        out_tokens,
        input_grad,
        g_ln1_g,
        g_ln1_b,
        g_qkv,
        g_qv_b,
        g_out,
        g_out_b,
        g_ln2_g,
        g_ln2_b,
        g_fc,
        g_fc_b,
        g_proj,
        g_proj_b,
    )


def solution(mesh):
    placed = (
        P(("rep", "shard"), None),
        P(("rep", "shard")),
        P(("rep", "shard"), None),
        P(None, "shard"),
        P(None, "shard"),
        P(None, "shard", None),
        P(None, "shard"),
        P(None, "shard", None),
        P(None, "shard"),
        P(None, "shard"),
        P(None, "shard"),
        P(None, "shard", None),
        P(None, "shard"),
        P(None, "shard", None),
        P(None, "shard"),
    )
    return jax.shard_map(
        per_device,
        mesh=mesh,
        in_specs=placed,
        out_specs=(
            P(("rep", "shard"), None),
            P(("rep", "shard"), None),
            P(None, "shard"),
            P(None, "shard"),
            P(None, "shard", None),
            P(None, "shard"),
            P(None, "shard", None),
            P(None, "shard"),
            P(None, "shard"),
            P(None, "shard"),
            P(None, "shard", None),
            P(None, "shard"),
            P(None, "shard", None),
            P(None, "shard"),
        ),
        check_vma=False,
    )
```

```python
import functools

import jax
import jax.numpy as jnp
from jax import lax
from jax.experimental import pallas as pl
from jax.experimental.pallas import tpu as pltpu
from jax.sharding import PartitionSpec as P

MESH = pl.DeviceIdType.MESH

HEADS = 12
HEAD = 64
LAYERS = 1

epsilon = 1e-05

def to_float(value):
    return value.astype(jnp.float32)


def layer_norm(inputs, norm_gain, norm_shift):
    center = inputs - jnp.mean(inputs, axis=-1, keepdims=True)
    inverse_std = lax.rsqrt(jnp.mean(center * center, axis=-1, keepdims=True) + epsilon)
    normed = center * inverse_std
    return (normed * norm_gain + norm_shift, normed, inverse_std)


def norm_back(upstream, normed, inverse_std, norm_gain):
    scaled = upstream * norm_gain
    inner_term = scaled - jnp.mean(scaled, axis=-1, keepdims=True)
    inner_term = inner_term - normed * jnp.mean(scaled * normed, axis=-1, keepdims=True)
    return (inverse_std * inner_term, jnp.sum(upstream * normed, axis=0), jnp.sum(upstream, axis=0))


def layer_forward(inputs, allowed, small, weights):
    ln1_gain, ln1_bias, qv_bias, out_bias, ln2_gain, ln2_bias, fc_bias, proj_bias = small
    qkv_weight, out_weight, fc_weight, proj_weight = weights
    row_count = inputs.shape[0]
    width_all = inputs.shape[1]
    first_norm, normed_one, inverse_one = layer_norm(inputs, ln1_gain, ln1_bias)
    first_low = first_norm.astype(jnp.bfloat16)
    offset = jnp.concatenate(
        [qv_bias[:width_all], jnp.zeros((width_all,), jnp.float32), qv_bias[width_all:]]
    )
    projected = (
        jnp.dot(first_low, qkv_weight, preferred_element_type=jnp.float32) + offset
    ).astype(jnp.bfloat16)
    queries = projected[:, :width_all].reshape(row_count, HEADS, HEAD)
    keys_all = projected[:, width_all : 2 * width_all].reshape(row_count, HEADS, HEAD)
    values_all = projected[:, 2 * width_all :].reshape(row_count, HEADS, HEAD)
    scores = jnp.einsum(
        "qhd,khd->hqk", queries, keys_all, preferred_element_type=jnp.float32
    ) * HEAD ** (-0.5)
    scores = jnp.where(allowed[None], scores, -1e30)
    row_max = jnp.max(scores, axis=-1, keepdims=True)
    log_total = row_max + jnp.log(jnp.sum(jnp.exp(scores - row_max), axis=-1, keepdims=True))
    attn_probs = jnp.exp(scores - log_total)
    probs_low = attn_probs.astype(jnp.bfloat16)
    attn_mixed = jnp.einsum(
        "hqk,khd->qhd", probs_low, values_all, preferred_element_type=jnp.float32
    )
    attn_mixed = attn_mixed.reshape(row_count, width_all).astype(jnp.bfloat16)
    after_attn = (
        inputs + jnp.dot(attn_mixed, out_weight, preferred_element_type=jnp.float32) + out_bias
    )
    second_norm, normed_two, inverse_two = layer_norm(after_attn, ln2_gain, ln2_bias)
    second_low = second_norm.astype(jnp.bfloat16)
    hidden_pre = jnp.dot(second_low, fc_weight, preferred_element_type=jnp.float32) + fc_bias
    hidden_low = jax.nn.gelu(hidden_pre, approximate=True).astype(jnp.bfloat16)
    result = (
        after_attn + jnp.dot(hidden_low, proj_weight, preferred_element_type=jnp.float32) + proj_bias
    )
    return dict(
        normed_one=normed_one,
        inverse_one=inverse_one,
        first_low=first_low,
        queries=queries,
        keys_all=keys_all,
        values_all=values_all,
        attn_probs=attn_probs,
        probs_low=probs_low,
        attn_mixed=attn_mixed,
        normed_two=normed_two,
        inverse_two=inverse_two,
        second_low=second_low,
        hidden_pre=hidden_pre,
        hidden_low=hidden_low,
        result=result,
    )


def layer_backward(upstream, saved, small, weights):
    ln1_gain, ln1_bias, qv_bias, out_bias, ln2_gain, ln2_bias, fc_bias, proj_bias = small
    qkv_weight, out_weight, fc_weight, proj_weight = weights
    row_count = upstream.shape[0]
    width_all = upstream.shape[1]
    proj_in = upstream.astype(jnp.bfloat16)
    grad_proj_b = jnp.sum(to_float(proj_in), axis=0)
    hidden_grad = jnp.einsum("td,fd->tf", proj_in, proj_weight, preferred_element_type=jnp.float32)
    _, gelu_pull = jax.vjp(lambda value: jax.nn.gelu(value, approximate=True), saved["hidden_pre"])
    pre_grad = gelu_pull(hidden_grad)[0].astype(jnp.bfloat16)
    grad_fc_b = jnp.sum(to_float(pre_grad), axis=0)
    second_grad = jnp.einsum("tf,df->td", pre_grad, fc_weight, preferred_element_type=jnp.float32)
    norm_part, grad_ln2_g, grad_ln2_b = norm_back(
        second_grad, saved["normed_two"], saved["inverse_two"], ln2_gain
    )
    residual_grad = upstream + norm_part
    branch_in = residual_grad.astype(jnp.bfloat16)
    grad_out_b = jnp.sum(to_float(branch_in), axis=0)
    mixed_grad = jnp.einsum("td,cd->tc", branch_in, out_weight, preferred_element_type=jnp.float32)
    mixed_grad = mixed_grad.astype(jnp.bfloat16).reshape(row_count, HEADS, HEAD)
    prob_grad = jnp.einsum(
        "qhd,khd->hqk", mixed_grad, saved["values_all"], preferred_element_type=jnp.float32
    )
    value_grad = jnp.einsum(
        "hqk,qhd->khd", saved["probs_low"], mixed_grad, preferred_element_type=jnp.float32
    )
    attn_probs = saved["attn_probs"]
    row_delta = jnp.sum(attn_probs * prob_grad, axis=-1, keepdims=True)
    score_grad = (attn_probs * (prob_grad - row_delta)).astype(jnp.bfloat16)
    query_grad = jnp.einsum(
        "hqk,khd->qhd", score_grad, saved["keys_all"], preferred_element_type=jnp.float32
    ) * HEAD ** (-0.5)
    key_grad = jnp.einsum(
        "hqk,qhd->khd", score_grad, saved["queries"], preferred_element_type=jnp.float32
    ) * HEAD ** (-0.5)
    joined_grad = jnp.concatenate(
        [
            query_grad.reshape(row_count, width_all),
            key_grad.reshape(row_count, width_all),
            value_grad.reshape(row_count, width_all),
        ],
        axis=1,
    ).astype(jnp.bfloat16)
    column_sums = jnp.sum(to_float(joined_grad), axis=0)
    grad_qv_b = jnp.concatenate([column_sums[:width_all], column_sums[2 * width_all :]])
    first_grad = jnp.einsum(
        "te,ce->tc", joined_grad, qkv_weight, preferred_element_type=jnp.float32
    )
    norm_first, grad_ln1_g, grad_ln1_b = norm_back(
        first_grad, saved["normed_one"], saved["inverse_one"], ln1_gain
    )
    small_grads = (
        grad_ln1_g,
        grad_ln1_b,
        grad_qv_b,
        grad_out_b,
        grad_ln2_g,
        grad_ln2_b,
        grad_fc_b,
        grad_proj_b,
    )
    pairs = (
        (saved["first_low"], joined_grad),
        (saved["attn_mixed"], branch_in),
        (saved["second_low"], pre_grad),
        (saved["hidden_low"], proj_in),
    )
    return (residual_grad + norm_first, small_grads, pairs)


def ring_position(shard_index, n):
    if n != 8:
        return shard_index
    y = shard_index % 2
    z = shard_index // 2
    return z * (1 - 2 * y) + 7 * y


def ring_shard(position, n):
    position = position % n
    if n != 8:
        return position
    y = position // 4
    z = (position % 4) * (1 - 2 * y) + 3 * y
    return z * 2 + y


FIRST_CORE_HALF = (0, 3)


def gather_kernel(n, count, *refs):
    local = refs[:count]
    full = refs[count : 2 * count]
    ring_send, ring_recv, pair_send, pair_recv = refs[2 * count :]
    rep = lax.axis_index("rep")
    shard = lax.axis_index("shard")
    core = rep % 2
    step_dir = 1 - 2 * core
    partner = (rep + step_dir, shard)
    here = ring_position(shard, n)
    target = (rep, ring_shard(here + step_dir, n))
    source = (rep, ring_shard(here - step_dir, n))
    steps = n // 2
    split_last = n % 2 == 0

    barrier = pltpu.get_barrier_semaphore()
    for peer in (target, source, partner):
        pl.semaphore_signal(barrier, inc=1, device_id=peer, device_id_type=MESH)
    pl.semaphore_wait(barrier, 3)

    def mine_at(k, w):
        if split_last and k == steps:
            return (core == 0) == (w in FIRST_CORE_HALF)
        return True

    def guarded(cond, fn):
        if cond is True:
            fn()
        else:
            pl.when(cond)(fn)

    def slot(position):
        return ring_shard(position, n)

    def ring_copy(k, w):
        src_pos = here - step_dir * (k - 1)
        src = local[w] if k == 1 else full[w].at[slot(src_pos)]
        return pltpu.make_async_remote_copy(
            src_ref=src,
            dst_ref=full[w].at[slot(src_pos)],
            send_sem=ring_send.at[k - 1, w],
            recv_sem=ring_recv.at[k - 1, w],
            device_id=target,
            device_id_type=MESH,
        )

    def incoming_ring(k, w):
        pos = here - step_dir * k
        return pltpu.make_async_remote_copy(
            src_ref=full[w].at[slot(pos)],
            dst_ref=full[w].at[slot(pos)],
            send_sem=ring_send.at[k - 1, w],
            recv_sem=ring_recv.at[k - 1, w],
            device_id=source,
            device_id_type=MESH,
        )

    def pair_copy(k, w, pos):
        src = local[w] if k == 0 else full[w].at[slot(pos)]
        return pltpu.make_async_remote_copy(
            src_ref=src,
            dst_ref=full[w].at[slot(pos)],
            send_sem=pair_send.at[k, w],
            recv_sem=pair_recv.at[k, w],
            device_id=partner,
            device_id_type=MESH,
        )

    for w in range(count):
        pair_copy(0, w, here).start()
    for w in range(count):
        guarded(mine_at(1, w), lambda w=w: ring_copy(1, w).start())
    for k in range(1, steps + 1):
        for w in range(count):
            def arrived(k=k, w=w):
                incoming_ring(k, w).wait_recv()
                if k < steps:
                    guarded(mine_at(k + 1, w), lambda: ring_copy(k + 1, w).start())
                pair_copy(k, w, here - step_dir * k).start()
            guarded(mine_at(k, w), arrived)
    for w in range(count):
        pair_copy(0, w, here).wait_recv()
    for k in range(1, steps + 1):
        for w in range(count):
            theirs = mine_at(k, w)
            theirs = True if theirs is True else jnp.logical_not(theirs)
            guarded(theirs, lambda k=k, w=w: pair_copy(k, w, here + step_dir * k).wait_recv())
    for w in range(count):
        pair_copy(0, w, here).wait_send()
    for k in range(1, steps + 1):
        for w in range(count):
            def sent(k=k, w=w):
                ring_copy(k, w).wait_send()
                pair_copy(k, w, here - step_dir * k).wait_send()
            guarded(mine_at(k, w), sent)


def gather_weights(locals_, n):
    count = len(locals_)
    steps = n // 2
    return pl.pallas_call(
        functools.partial(gather_kernel, n, count),
        out_shape=[jax.ShapeDtypeStruct((n,) + a.shape, a.dtype) for a in locals_],
        in_specs=[pl.BlockSpec(memory_space=pl.ANY)] * count,
        out_specs=[pl.BlockSpec(memory_space=pl.ANY)] * count,
        scratch_shapes=[
            pltpu.SemaphoreType.DMA((steps, count)),
            pltpu.SemaphoreType.DMA((steps, count)),
            pltpu.SemaphoreType.DMA((steps + 1, count)),
            pltpu.SemaphoreType.DMA((steps + 1, count)),
        ],
        compiler_params=pltpu.CompilerParams(collective_id=0, has_side_effects=True),
    )(*locals_)


def add_rows(dst, parts, rows, chunk):
    def body(i, carry):
        window = pl.ds(pl.multiple_of(i * chunk, chunk), chunk)
        total = parts[0][window, :]
        for part in parts[1:]:
            total = total + part[window, :]
        dst[window, :] = total
        return carry

    lax.fori_loop(0, rows // chunk, body, 0)


def reduce_kernel(n, count, *refs):
    contrib = refs[:count]
    out = refs[count : 2 * count]
    land, send, other, own, xland = (
        refs[2 * count + i * count : 2 * count + (i + 1) * count] for i in range(5)
    )
    (load_sem, own_sem, ring_send, ring_recv, pair_send, pair_recv, x_send, x_recv, back_send, back_recv) = refs[
        7 * count :
    ]
    rep = lax.axis_index("rep")
    shard = lax.axis_index("shard")
    core = rep % 2
    step_dir = 1 - 2 * core
    partner = (rep + step_dir, shard)
    x_partner = ((rep + 2) % 4, shard)
    here = ring_position(shard, n)
    target = (rep, ring_shard(here + step_dir, n))
    source = (rep, ring_shard(here - step_dir, n))
    steps = n // 2
    split_first = n % 2 == 0

    def carried(k, w):
        if split_first and k == 1:
            return (core == 0) == (w in FIRST_CORE_HALF)
        return True

    def guarded(cond, fn):
        if cond is True:
            fn()
        else:
            pl.when(cond)(fn)

    def block_at(k):
        return here + step_dir * (steps - k + 1)

    def load(k, w):
        return pltpu.make_async_copy(contrib[w].at[ring_shard(block_at(k), n)], send[w].at[k - 1], load_sem.at[k - 1, w])

    def load_own(w):
        return pltpu.make_async_copy(contrib[w].at[shard], own[w], own_sem.at[w])

    def remote(src, dst, ssem, rsem, device):
        return pltpu.make_async_remote_copy(
            src_ref=src, dst_ref=dst, send_sem=ssem, recv_sem=rsem, device_id=device, device_id_type=MESH
        )

    def ring_copy(k, w, device):
        return remote(send[w].at[k - 1], land[w].at[k - 1], ring_send.at[k - 1, w], ring_recv.at[k - 1, w], device)

    def pair_copy(w):
        return remote(land[w].at[steps - 1], other[w], pair_send.at[w], pair_recv.at[w], partner)

    def x_copy(w):
        return remote(own[w], xland[w], x_send.at[w], x_recv.at[w], x_partner)

    def back_copy(w):
        return remote(out[w], out[w], back_send.at[w], back_recv.at[w], partner)

    def owner(w):
        return core == w % 2

    for w in range(count):
        load_own(w).start()
    for k in range(1, steps + 1):
        for w in range(count):
            guarded(carried(k, w), lambda k=k, w=w: load(k, w).start())

    barrier = pltpu.get_barrier_semaphore()
    for peer in (target, source, partner, x_partner):
        pl.semaphore_signal(barrier, inc=1, device_id=peer, device_id_type=MESH)
    pl.semaphore_wait(barrier, 4)

    def add_into(dst, parts):
        rows = dst.shape[0]
        chunk = 8 if rows % 8 == 0 else rows
        add_rows(dst, parts, rows, chunk)

    for k in range(1, steps + 1):
        for w in range(count):
            def step(k=k, w=w):
                load(k, w).wait()
                if k > 1:
                    def accumulate():
                        ring_copy(k - 1, w, source).wait_recv()
                        add_into(send[w].at[k - 1], [send[w].at[k - 1], land[w].at[k - 2]])
                    guarded(carried(k - 1, w), accumulate)
                ring_copy(k, w, target).start()
            guarded(carried(k, w), step)

    for w in range(count):
        ring_copy(steps, w, source).wait_recv()
        pl.when(jnp.logical_not(owner(w)))(lambda w=w: pair_copy(w).start())
        mine = land[w].at[steps - 1]

        def finish(w=w, mine=mine):
            pair_copy(w).wait_recv()
            load_own(w).wait()

            @pl.when(core == 0)
            def _():
                add_into(own[w], [own[w], mine, other[w]])

            @pl.when(core == 1)
            def _():
                add_into(own[w], [own[w], other[w], mine])

            x_copy(w).start()
            x_copy(w).wait_recv()
            add_into(out[w], [own[w], xland[w]])
            back_copy(w).start()

        pl.when(owner(w))(finish)

    for w in range(count):
        def not_owner(w=w):
            load_own(w).wait()
            back_copy(w).wait_recv()
            pair_copy(w).wait_send()

        def was_owner(w=w):
            x_copy(w).wait_send()
            back_copy(w).wait_send()

        pl.when(owner(w))(was_owner)
        pl.when(jnp.logical_not(owner(w)))(not_owner)
    for k in range(1, steps + 1):
        for w in range(count):
            guarded(carried(k, w), lambda k=k, w=w: ring_copy(k, w, target).wait_send())


def reduce_gradients(contribs, n):
    count = len(contribs)
    steps = n // 2
    blocks = [c.shape[1:] for c in contribs]
    vmem = lambda shape: pltpu.VMEM(shape, jnp.float32)
    dma = pltpu.SemaphoreType.DMA
    return pl.pallas_call(
        functools.partial(reduce_kernel, n, count),
        out_shape=[jax.ShapeDtypeStruct(b, jnp.float32) for b in blocks],
        in_specs=[pl.BlockSpec(memory_space=pl.ANY)] * count,
        out_specs=[pl.BlockSpec(memory_space=pltpu.VMEM)] * count,
        scratch_shapes=[vmem((steps,) + b) for b in blocks]
        + [vmem((steps,) + b) for b in blocks]
        + [vmem(b) for b in blocks]
        + [vmem(b) for b in blocks]
        + [vmem(b) for b in blocks]
        + [
            dma((steps, count)),
            dma((count,)),
            dma((steps, count)),
            dma((steps, count)),
            dma((count,)),
            dma((count,)),
            dma((count,)),
            dma((count,)),
            dma((count,)),
            dma((count,)),
        ],
        compiler_params=pltpu.CompilerParams(
            collective_id=1, has_side_effects=True, vmem_limit_bytes=60 * 1024 * 1024
        ),
    )(*contribs)


def swap_core(value):
    rep = lax.axis_size("rep")
    return lax.ppermute(value, "rep", perm=[(i, i ^ 1) for i in range(rep)])


def swap_x(value):
    rep = lax.axis_size("rep")
    return lax.ppermute(value, "rep", perm=[(i, i ^ 2) for i in range(rep)])


def join_halves(mine, theirs, core, axis):
    first = jnp.where(core == 0, mine, theirs)
    second = jnp.where(core == 0, theirs, mine)
    return jnp.concatenate([first, second], axis=axis)


def take_half(value, core, axis):
    half = value.shape[axis] // 2
    return lax.dynamic_slice_in_dim(value, core * half, half, axis=axis)


def per_device(
    tokens,
    segment_ids,
    cotangent,
    ln1_gain,
    ln1_bias,
    qkv_weight,
    qv_bias,
    out_weight,
    out_bias,
    ln2_gain,
    ln2_bias,
    fc_weight,
    fc_bias,
    proj_weight,
    proj_bias,
):
    rep = lax.axis_size("rep")
    assert rep == 4
    core = lax.axis_index("rep") % 2
    row_count = tokens.shape[0]
    positions = jnp.arange(row_count)
    allowed = (segment_ids[:, None] == segment_ids[None, :]) & (
        positions[None, :] <= positions[:, None]
    )
    layer_index = 0
    shard = lax.axis_size("shard")
    small_local = (ln1_gain, ln1_bias, qv_bias, out_bias, ln2_gain, ln2_bias, fc_bias, proj_bias)
    small_local = [v[layer_index] for v in small_local]
    widths = [v.shape[0] for v in small_local]
    local_weights = (
        qkv_weight[layer_index],
        out_weight[layer_index],
        fc_weight[layer_index],
        proj_weight[layer_index],
    )
    rows_local = local_weights[0].shape[0]
    small_row = jnp.concatenate(small_local).reshape(1, -1)
    fulls = gather_weights(list(local_weights) + [small_row], shard)
    weights = tuple(f.reshape(-1, f.shape[-1]) for f in fulls[:4])
    halves = [take_half(w, core, 1) for w in local_weights]
    half_widths = [h.size // rows_local for h in halves]
    packed_all = fulls[4].reshape(shard, -1)
    small = []
    start = 0
    for width in widths:
        small.append(to_float(packed_all[:, start : start + width].reshape(-1)))
        start += width
    small = tuple(small)

    residual = to_float(tokens)
    saved = layer_forward(residual, allowed, small, weights)
    out_tokens = saved["result"].astype(jnp.bfloat16)
    upstream = to_float(cotangent)
    input_grad, small_grads, pairs = layer_backward(upstream, saved, small, weights)

    outgoing = jnp.concatenate([x for x, _ in pairs] + [dy for _, dy in pairs], axis=1)
    incoming = swap_core(outgoing)
    small_mine = jnp.concatenate([g.reshape(shard, -1) for g in small_grads], axis=1)
    small_theirs = swap_core(small_mine)
    small_chip = jnp.where(core == 0, small_mine + small_theirs, small_theirs + small_mine)
    contribs = []
    start = 0
    partner_x = []
    for x, _ in pairs:
        partner_x.append(incoming[:, start : start + x.shape[1]])
        start += x.shape[1]
    for (x, dy), px in zip(pairs, partner_x):
        pdy = incoming[:, start : start + dy.shape[1]]
        start += dy.shape[1]
        rows = join_halves(x, px, core, 0)
        grads = join_halves(dy, pdy, core, 0)
        grad = jnp.einsum("tc,te->ce", rows, grads, preferred_element_type=jnp.float32)
        contribs.append(grad.reshape(shard, -1, grad.shape[1]))
    contribs.append(small_chip.reshape(shard, 1, -1))
    totals = reduce_gradients(contribs, shard)
    small_share = totals[4]
    owned = [t[None] for t in totals[:4]]
    small_owned = []
    start = 0
    for g in small_grads:
        width = g.shape[0] // shard
        small_owned.append(small_share[:, start : start + width])
        start += width

    (g_ln1_g, g_ln1_b, g_qv_b, g_out_b, g_ln2_g, g_ln2_b, g_fc_b, g_proj_b) = small_owned
    g_qkv, g_out, g_fc, g_proj = owned
    return (
        out_tokens,
        input_grad,
        g_ln1_g,
        g_ln1_b,
        g_qkv,
        g_qv_b,
        g_out,
        g_out_b,
        g_ln2_g,
        g_ln2_b,
        g_fc,
        g_fc_b,
        g_proj,
        g_proj_b,
    )


def solution(mesh):
    placed = (
        P(("rep", "shard"), None),
        P(("rep", "shard")),
        P(("rep", "shard"), None),
        P(None, "shard"),
        P(None, "shard"),
        P(None, "shard", None),
        P(None, "shard"),
        P(None, "shard", None),
        P(None, "shard"),
        P(None, "shard"),
        P(None, "shard"),
        P(None, "shard", None),
        P(None, "shard"),
        P(None, "shard", None),
        P(None, "shard"),
    )
    return jax.shard_map(
        per_device,
        mesh=mesh,
        in_specs=placed,
        out_specs=(
            P(("rep", "shard"), None),
            P(("rep", "shard"), None),
            P(None, "shard"),
            P(None, "shard"),
            P(None, "shard", None),
            P(None, "shard"),
            P(None, "shard", None),
            P(None, "shard"),
            P(None, "shard"),
            P(None, "shard"),
            P(None, "shard", None),
            P(None, "shard"),
            P(None, "shard", None),
            P(None, "shard"),
        ),
        check_vma=False,
    )
```

```python
import functools

import jax
import jax.numpy as jnp
from jax import lax
from jax.experimental import pallas as pl
from jax.experimental.pallas import tpu as pltpu
from jax.sharding import PartitionSpec as P

MESH = pl.DeviceIdType.MESH

HEADS = 12
HEAD = 64
LAYERS = 1

epsilon = 1e-05

def to_float(value):
    return value.astype(jnp.float32)


def layer_norm(inputs, norm_gain, norm_shift):
    center = inputs - jnp.mean(inputs, axis=-1, keepdims=True)
    inverse_std = lax.rsqrt(jnp.mean(center * center, axis=-1, keepdims=True) + epsilon)
    normed = center * inverse_std
    return (normed * norm_gain + norm_shift, normed, inverse_std)


def norm_back(upstream, normed, inverse_std, norm_gain):
    scaled = upstream * norm_gain
    inner_term = scaled - jnp.mean(scaled, axis=-1, keepdims=True)
    inner_term = inner_term - normed * jnp.mean(scaled * normed, axis=-1, keepdims=True)
    return (inverse_std * inner_term, jnp.sum(upstream * normed, axis=0), jnp.sum(upstream, axis=0))


def layer_forward(inputs, allowed, small, weights):
    ln1_gain, ln1_bias, qv_bias, out_bias, ln2_gain, ln2_bias, fc_bias, proj_bias = small
    qkv_weight, out_weight, fc_weight, proj_weight = weights
    row_count = inputs.shape[0]
    width_all = inputs.shape[1]
    first_norm, normed_one, inverse_one = layer_norm(inputs, ln1_gain, ln1_bias)
    first_low = first_norm.astype(jnp.bfloat16)
    offset = jnp.concatenate(
        [qv_bias[:width_all], jnp.zeros((width_all,), jnp.float32), qv_bias[width_all:]]
    )
    projected = (
        jnp.dot(first_low, qkv_weight, preferred_element_type=jnp.float32) + offset
    ).astype(jnp.bfloat16)
    queries = projected[:, :width_all].reshape(row_count, HEADS, HEAD)
    keys_all = projected[:, width_all : 2 * width_all].reshape(row_count, HEADS, HEAD)
    values_all = projected[:, 2 * width_all :].reshape(row_count, HEADS, HEAD)
    scores = jnp.einsum(
        "qhd,khd->hqk", queries, keys_all, preferred_element_type=jnp.float32
    ) * HEAD ** (-0.5)
    scores = jnp.where(allowed[None], scores, -1e30)
    row_max = jnp.max(scores, axis=-1, keepdims=True)
    log_total = row_max + jnp.log(jnp.sum(jnp.exp(scores - row_max), axis=-1, keepdims=True))
    attn_probs = jnp.exp(scores - log_total)
    probs_low = attn_probs.astype(jnp.bfloat16)
    attn_mixed = jnp.einsum(
        "hqk,khd->qhd", probs_low, values_all, preferred_element_type=jnp.float32
    )
    attn_mixed = attn_mixed.reshape(row_count, width_all).astype(jnp.bfloat16)
    after_attn = (
        inputs + jnp.dot(attn_mixed, out_weight, preferred_element_type=jnp.float32) + out_bias
    )
    second_norm, normed_two, inverse_two = layer_norm(after_attn, ln2_gain, ln2_bias)
    second_low = second_norm.astype(jnp.bfloat16)
    hidden_pre = jnp.dot(second_low, fc_weight, preferred_element_type=jnp.float32) + fc_bias
    hidden_low = jax.nn.gelu(hidden_pre, approximate=True).astype(jnp.bfloat16)
    result = (
        after_attn + jnp.dot(hidden_low, proj_weight, preferred_element_type=jnp.float32) + proj_bias
    )
    return dict(
        normed_one=normed_one,
        inverse_one=inverse_one,
        first_low=first_low,
        queries=queries,
        keys_all=keys_all,
        values_all=values_all,
        attn_probs=attn_probs,
        probs_low=probs_low,
        attn_mixed=attn_mixed,
        normed_two=normed_two,
        inverse_two=inverse_two,
        second_low=second_low,
        hidden_pre=hidden_pre,
        hidden_low=hidden_low,
        result=result,
    )


def layer_backward(upstream, saved, small, weights):
    ln1_gain, ln1_bias, qv_bias, out_bias, ln2_gain, ln2_bias, fc_bias, proj_bias = small
    qkv_weight, out_weight, fc_weight, proj_weight = weights
    row_count = upstream.shape[0]
    width_all = upstream.shape[1]
    proj_in = upstream.astype(jnp.bfloat16)
    grad_proj_b = jnp.sum(to_float(proj_in), axis=0)
    hidden_grad = jnp.einsum("td,fd->tf", proj_in, proj_weight, preferred_element_type=jnp.float32)
    _, gelu_pull = jax.vjp(lambda value: jax.nn.gelu(value, approximate=True), saved["hidden_pre"])
    pre_grad = gelu_pull(hidden_grad)[0].astype(jnp.bfloat16)
    grad_fc_b = jnp.sum(to_float(pre_grad), axis=0)
    second_grad = jnp.einsum("tf,df->td", pre_grad, fc_weight, preferred_element_type=jnp.float32)
    norm_part, grad_ln2_g, grad_ln2_b = norm_back(
        second_grad, saved["normed_two"], saved["inverse_two"], ln2_gain
    )
    residual_grad = upstream + norm_part
    branch_in = residual_grad.astype(jnp.bfloat16)
    grad_out_b = jnp.sum(to_float(branch_in), axis=0)
    mixed_grad = jnp.einsum("td,cd->tc", branch_in, out_weight, preferred_element_type=jnp.float32)
    mixed_grad = mixed_grad.astype(jnp.bfloat16).reshape(row_count, HEADS, HEAD)
    prob_grad = jnp.einsum(
        "qhd,khd->hqk", mixed_grad, saved["values_all"], preferred_element_type=jnp.float32
    )
    value_grad = jnp.einsum(
        "hqk,qhd->khd", saved["probs_low"], mixed_grad, preferred_element_type=jnp.float32
    )
    attn_probs = saved["attn_probs"]
    row_delta = jnp.sum(attn_probs * prob_grad, axis=-1, keepdims=True)
    score_grad = (attn_probs * (prob_grad - row_delta)).astype(jnp.bfloat16)
    query_grad = jnp.einsum(
        "hqk,khd->qhd", score_grad, saved["keys_all"], preferred_element_type=jnp.float32
    ) * HEAD ** (-0.5)
    key_grad = jnp.einsum(
        "hqk,qhd->khd", score_grad, saved["queries"], preferred_element_type=jnp.float32
    ) * HEAD ** (-0.5)
    joined_grad = jnp.concatenate(
        [
            query_grad.reshape(row_count, width_all),
            key_grad.reshape(row_count, width_all),
            value_grad.reshape(row_count, width_all),
        ],
        axis=1,
    ).astype(jnp.bfloat16)
    column_sums = jnp.sum(to_float(joined_grad), axis=0)
    grad_qv_b = jnp.concatenate([column_sums[:width_all], column_sums[2 * width_all :]])
    first_grad = jnp.einsum(
        "te,ce->tc", joined_grad, qkv_weight, preferred_element_type=jnp.float32
    )
    norm_first, grad_ln1_g, grad_ln1_b = norm_back(
        first_grad, saved["normed_one"], saved["inverse_one"], ln1_gain
    )
    small_grads = (
        grad_ln1_g,
        grad_ln1_b,
        grad_qv_b,
        grad_out_b,
        grad_ln2_g,
        grad_ln2_b,
        grad_fc_b,
        grad_proj_b,
    )
    pairs = (
        (saved["first_low"], joined_grad),
        (saved["attn_mixed"], branch_in),
        (saved["second_low"], pre_grad),
        (saved["hidden_low"], proj_in),
    )
    return (residual_grad + norm_first, small_grads, pairs)


def ring_position(shard_index, n):
    if n != 8:
        return shard_index
    y = shard_index % 2
    z = shard_index // 2
    return z * (1 - 2 * y) + 7 * y


def ring_shard(position, n):
    position = position % n
    if n != 8:
        return position
    y = position // 4
    z = (position % 4) * (1 - 2 * y) + 3 * y
    return z * 2 + y


FIRST_CORE_HALF = (0, 3)


def gather_kernel(n, count, *refs):
    local = refs[:count]
    full = refs[count : 2 * count]
    ring_send, ring_recv, pair_send, pair_recv = refs[2 * count :]
    rep = lax.axis_index("rep")
    shard = lax.axis_index("shard")
    core = rep % 2
    step_dir = 1 - 2 * core
    partner = (rep + step_dir, shard)
    here = ring_position(shard, n)
    target = (rep, ring_shard(here + step_dir, n))
    source = (rep, ring_shard(here - step_dir, n))
    steps = n // 2
    split_last = n % 2 == 0

    barrier = pltpu.get_barrier_semaphore()
    for peer in (target, source, partner):
        pl.semaphore_signal(barrier, inc=1, device_id=peer, device_id_type=MESH)
    pl.semaphore_wait(barrier, 3)

    def mine_at(k, w):
        if split_last and k == steps:
            return (core == 0) == (w in FIRST_CORE_HALF)
        return True

    def guarded(cond, fn):
        if cond is True:
            fn()
        else:
            pl.when(cond)(fn)

    def slot(position):
        return ring_shard(position, n)

    def ring_copy(k, w):
        src_pos = here - step_dir * (k - 1)
        src = local[w] if k == 1 else full[w].at[slot(src_pos)]
        return pltpu.make_async_remote_copy(
            src_ref=src,
            dst_ref=full[w].at[slot(src_pos)],
            send_sem=ring_send.at[k - 1, w],
            recv_sem=ring_recv.at[k - 1, w],
            device_id=target,
            device_id_type=MESH,
        )

    def incoming_ring(k, w):
        pos = here - step_dir * k
        return pltpu.make_async_remote_copy(
            src_ref=full[w].at[slot(pos)],
            dst_ref=full[w].at[slot(pos)],
            send_sem=ring_send.at[k - 1, w],
            recv_sem=ring_recv.at[k - 1, w],
            device_id=source,
            device_id_type=MESH,
        )

    def pair_copy(k, w, pos):
        src = local[w] if k == 0 else full[w].at[slot(pos)]
        return pltpu.make_async_remote_copy(
            src_ref=src,
            dst_ref=full[w].at[slot(pos)],
            send_sem=pair_send.at[k, w],
            recv_sem=pair_recv.at[k, w],
            device_id=partner,
            device_id_type=MESH,
        )

    for w in range(count):
        pair_copy(0, w, here).start()
    for w in range(count):
        guarded(mine_at(1, w), lambda w=w: ring_copy(1, w).start())
    for k in range(1, steps + 1):
        for w in range(count):
            def arrived(k=k, w=w):
                incoming_ring(k, w).wait_recv()
                if k < steps:
                    guarded(mine_at(k + 1, w), lambda: ring_copy(k + 1, w).start())
                pair_copy(k, w, here - step_dir * k).start()
            guarded(mine_at(k, w), arrived)
    for w in range(count):
        pair_copy(0, w, here).wait_recv()
    for k in range(1, steps + 1):
        for w in range(count):
            theirs = mine_at(k, w)
            theirs = True if theirs is True else jnp.logical_not(theirs)
            guarded(theirs, lambda k=k, w=w: pair_copy(k, w, here + step_dir * k).wait_recv())
    for w in range(count):
        pair_copy(0, w, here).wait_send()
    for k in range(1, steps + 1):
        for w in range(count):
            def sent(k=k, w=w):
                ring_copy(k, w).wait_send()
                pair_copy(k, w, here - step_dir * k).wait_send()
            guarded(mine_at(k, w), sent)


def gather_weights(locals_, n):
    count = len(locals_)
    steps = n // 2
    return pl.pallas_call(
        functools.partial(gather_kernel, n, count),
        out_shape=[jax.ShapeDtypeStruct((n,) + a.shape, a.dtype) for a in locals_],
        in_specs=[pl.BlockSpec(memory_space=pl.ANY)] * count,
        out_specs=[pl.BlockSpec(memory_space=pl.ANY)] * count,
        scratch_shapes=[
            pltpu.SemaphoreType.DMA((steps, count)),
            pltpu.SemaphoreType.DMA((steps, count)),
            pltpu.SemaphoreType.DMA((steps + 1, count)),
            pltpu.SemaphoreType.DMA((steps + 1, count)),
        ],
        compiler_params=pltpu.CompilerParams(collective_id=0, has_side_effects=True),
    )(*locals_)


def add_rows(dst, parts, rows, chunk):
    def body(i, carry):
        window = pl.ds(pl.multiple_of(i * chunk, chunk), chunk)
        total = parts[0][window, :]
        for part in parts[1:]:
            total = total + part[window, :]
        dst[window, :] = total
        return carry

    lax.fori_loop(0, rows // chunk, body, 0)


def reduce_kernel(n, count, *refs):
    contrib = refs[:count]
    out = refs[count : 2 * count]
    land, send, other, own, xland = (
        refs[2 * count + i * count : 2 * count + (i + 1) * count] for i in range(5)
    )
    (load_sem, own_sem, ring_send, ring_recv, pair_send, pair_recv, x_send, x_recv, back_send, back_recv) = refs[
        7 * count :
    ]
    rep = lax.axis_index("rep")
    shard = lax.axis_index("shard")
    core = rep % 2
    step_dir = 1 - 2 * core
    partner = (rep + step_dir, shard)
    x_partner = ((rep + 2) % 4, shard)
    here = ring_position(shard, n)
    target = (rep, ring_shard(here + step_dir, n))
    source = (rep, ring_shard(here - step_dir, n))
    steps = n // 2
    split_first = n % 2 == 0

    def carried(k, w):
        if split_first and k == 1:
            return (core == 0) == (w in FIRST_CORE_HALF)
        return True

    def guarded(cond, fn):
        if cond is True:
            fn()
        else:
            pl.when(cond)(fn)

    def block_at(k):
        return here + step_dir * (steps - k + 1)

    def load(k, w):
        return pltpu.make_async_copy(contrib[w].at[ring_shard(block_at(k), n)], send[w].at[k - 1], load_sem.at[k - 1, w])

    def load_own(w):
        return pltpu.make_async_copy(contrib[w].at[shard], own[w], own_sem.at[w])

    def remote(src, dst, ssem, rsem, device):
        return pltpu.make_async_remote_copy(
            src_ref=src, dst_ref=dst, send_sem=ssem, recv_sem=rsem, device_id=device, device_id_type=MESH
        )

    def ring_copy(k, w, device):
        return remote(send[w].at[k - 1], land[w].at[k - 1], ring_send.at[k - 1, w], ring_recv.at[k - 1, w], device)

    def pair_copy(w):
        return remote(land[w].at[steps - 1], other[w], pair_send.at[w], pair_recv.at[w], partner)

    def x_copy(w):
        return remote(own[w], xland[w], x_send.at[w], x_recv.at[w], x_partner)

    def back_copy(w):
        return remote(out[w], out[w], back_send.at[w], back_recv.at[w], partner)

    def owner(w):
        return core == w % 2

    for w in range(count):
        load_own(w).start()
    for k in range(1, steps + 1):
        for w in range(count):
            guarded(carried(k, w), lambda k=k, w=w: load(k, w).start())

    barrier = pltpu.get_barrier_semaphore()
    for peer in (target, source, partner, x_partner):
        pl.semaphore_signal(barrier, inc=1, device_id=peer, device_id_type=MESH)
    pl.semaphore_wait(barrier, 4)

    def add_into(dst, parts):
        rows = dst.shape[0]
        chunk = 8 if rows % 8 == 0 else rows
        add_rows(dst, parts, rows, chunk)

    def step(k, w):
        load(k, w).wait()
        if k > 1:
            def accumulate():
                ring_copy(k - 1, w, source).wait_recv()
                add_into(send[w].at[k - 1], [send[w].at[k - 1], land[w].at[k - 2]])
            guarded(carried(k - 1, w), accumulate)
        ring_copy(k, w, target).start()

    def arrive(w):
        ring_copy(steps, w, source).wait_recv()
        pl.when(jnp.logical_not(owner(w)))(lambda: pair_copy(w).start())
        mine = land[w].at[steps - 1]

        def plane():
            pair_copy(w).wait_recv()
            load_own(w).wait()

            @pl.when(core == 0)
            def _():
                add_into(own[w], [own[w], mine, other[w]])

            @pl.when(core == 1)
            def _():
                add_into(own[w], [own[w], other[w], mine])

            x_copy(w).start()

        pl.when(owner(w))(plane)

    def total(w):
        x_copy(w).wait_recv()
        add_into(out[w], [own[w], xland[w]])
        back_copy(w).start()

    slots = steps + count - 1
    for t in range(slots + 1):
        for w in range(count):
            k = t - w + 1
            if 1 <= k <= steps:
                guarded(carried(k, w), lambda k=k, w=w: step(k, w))
        for w in range(count):
            if steps + w == t:
                arrive(w)
    for w in range(count):
        pl.when(owner(w))(lambda w=w: total(w))

    for w in range(count):
        def not_owner(w=w):
            load_own(w).wait()
            back_copy(w).wait_recv()
            pair_copy(w).wait_send()

        def was_owner(w=w):
            x_copy(w).wait_send()
            back_copy(w).wait_send()

        pl.when(owner(w))(was_owner)
        pl.when(jnp.logical_not(owner(w)))(not_owner)
    for k in range(1, steps + 1):
        for w in range(count):
            guarded(carried(k, w), lambda k=k, w=w: ring_copy(k, w, target).wait_send())


def reduce_gradients(contribs, n):
    count = len(contribs)
    steps = n // 2
    blocks = [c.shape[1:] for c in contribs]
    vmem = lambda shape: pltpu.VMEM(shape, jnp.float32)
    dma = pltpu.SemaphoreType.DMA
    return pl.pallas_call(
        functools.partial(reduce_kernel, n, count),
        out_shape=[jax.ShapeDtypeStruct(b, jnp.float32) for b in blocks],
        in_specs=[pl.BlockSpec(memory_space=pl.ANY)] * count,
        out_specs=[pl.BlockSpec(memory_space=pltpu.VMEM)] * count,
        scratch_shapes=[vmem((steps,) + b) for b in blocks]
        + [vmem((steps,) + b) for b in blocks]
        + [vmem(b) for b in blocks]
        + [vmem(b) for b in blocks]
        + [vmem(b) for b in blocks]
        + [
            dma((steps, count)),
            dma((count,)),
            dma((steps, count)),
            dma((steps, count)),
            dma((count,)),
            dma((count,)),
            dma((count,)),
            dma((count,)),
            dma((count,)),
            dma((count,)),
        ],
        compiler_params=pltpu.CompilerParams(
            collective_id=1, has_side_effects=True, vmem_limit_bytes=60 * 1024 * 1024
        ),
    )(*contribs)


def swap_core(value):
    rep = lax.axis_size("rep")
    return lax.ppermute(value, "rep", perm=[(i, i ^ 1) for i in range(rep)])


def swap_x(value):
    rep = lax.axis_size("rep")
    return lax.ppermute(value, "rep", perm=[(i, i ^ 2) for i in range(rep)])


def join_halves(mine, theirs, core, axis):
    first = jnp.where(core == 0, mine, theirs)
    second = jnp.where(core == 0, theirs, mine)
    return jnp.concatenate([first, second], axis=axis)


def take_half(value, core, axis):
    half = value.shape[axis] // 2
    return lax.dynamic_slice_in_dim(value, core * half, half, axis=axis)


def per_device(
    tokens,
    segment_ids,
    cotangent,
    ln1_gain,
    ln1_bias,
    qkv_weight,
    qv_bias,
    out_weight,
    out_bias,
    ln2_gain,
    ln2_bias,
    fc_weight,
    fc_bias,
    proj_weight,
    proj_bias,
):
    rep = lax.axis_size("rep")
    assert rep == 4
    core = lax.axis_index("rep") % 2
    row_count = tokens.shape[0]
    positions = jnp.arange(row_count)
    allowed = (segment_ids[:, None] == segment_ids[None, :]) & (
        positions[None, :] <= positions[:, None]
    )
    layer_index = 0
    shard = lax.axis_size("shard")
    small_local = (ln1_gain, ln1_bias, qv_bias, out_bias, ln2_gain, ln2_bias, fc_bias, proj_bias)
    small_local = [v[layer_index] for v in small_local]
    widths = [v.shape[0] for v in small_local]
    local_weights = (
        qkv_weight[layer_index],
        out_weight[layer_index],
        fc_weight[layer_index],
        proj_weight[layer_index],
    )
    rows_local = local_weights[0].shape[0]
    small_row = jnp.concatenate(small_local).reshape(1, -1)
    fulls = gather_weights(list(local_weights) + [small_row], shard)
    weights = tuple(f.reshape(-1, f.shape[-1]) for f in fulls[:4])
    halves = [take_half(w, core, 1) for w in local_weights]
    half_widths = [h.size // rows_local for h in halves]
    packed_all = fulls[4].reshape(shard, -1)
    small = []
    start = 0
    for width in widths:
        small.append(to_float(packed_all[:, start : start + width].reshape(-1)))
        start += width
    small = tuple(small)

    residual = to_float(tokens)
    saved = layer_forward(residual, allowed, small, weights)
    out_tokens = saved["result"].astype(jnp.bfloat16)
    upstream = to_float(cotangent)
    input_grad, small_grads, pairs = layer_backward(upstream, saved, small, weights)

    outgoing = jnp.concatenate([x for x, _ in pairs] + [dy for _, dy in pairs], axis=1)
    incoming = swap_core(outgoing)
    small_mine = jnp.concatenate([g.reshape(shard, -1) for g in small_grads], axis=1)
    small_theirs = swap_core(small_mine)
    small_chip = jnp.where(core == 0, small_mine + small_theirs, small_theirs + small_mine)
    contribs = []
    start = 0
    partner_x = []
    for x, _ in pairs:
        partner_x.append(incoming[:, start : start + x.shape[1]])
        start += x.shape[1]
    for (x, dy), px in zip(pairs, partner_x):
        pdy = incoming[:, start : start + dy.shape[1]]
        start += dy.shape[1]
        rows = join_halves(x, px, core, 0)
        grads = join_halves(dy, pdy, core, 0)
        grad = jnp.einsum("tc,te->ce", rows, grads, preferred_element_type=jnp.float32)
        contribs.append(grad.reshape(shard, -1, grad.shape[1]))
    contribs.append(small_chip.reshape(shard, 1, -1))
    totals = reduce_gradients(contribs, shard)
    small_share = totals[4]
    owned = [t[None] for t in totals[:4]]
    small_owned = []
    start = 0
    for g in small_grads:
        width = g.shape[0] // shard
        small_owned.append(small_share[:, start : start + width])
        start += width

    (g_ln1_g, g_ln1_b, g_qv_b, g_out_b, g_ln2_g, g_ln2_b, g_fc_b, g_proj_b) = small_owned
    g_qkv, g_out, g_fc, g_proj = owned
    return (
        out_tokens,
        input_grad,
        g_ln1_g,
        g_ln1_b,
        g_qkv,
        g_qv_b,
        g_out,
        g_out_b,
        g_ln2_g,
        g_ln2_b,
        g_fc,
        g_fc_b,
        g_proj,
        g_proj_b,
    )


def solution(mesh):
    placed = (
        P(("rep", "shard"), None),
        P(("rep", "shard")),
        P(("rep", "shard"), None),
        P(None, "shard"),
        P(None, "shard"),
        P(None, "shard", None),
        P(None, "shard"),
        P(None, "shard", None),
        P(None, "shard"),
        P(None, "shard"),
        P(None, "shard"),
        P(None, "shard", None),
        P(None, "shard"),
        P(None, "shard", None),
        P(None, "shard"),
    )
    return jax.shard_map(
        per_device,
        mesh=mesh,
        in_specs=placed,
        out_specs=(
            P(("rep", "shard"), None),
            P(("rep", "shard"), None),
            P(None, "shard"),
            P(None, "shard"),
            P(None, "shard", None),
            P(None, "shard"),
            P(None, "shard", None),
            P(None, "shard"),
            P(None, "shard"),
            P(None, "shard"),
            P(None, "shard", None),
            P(None, "shard"),
            P(None, "shard", None),
            P(None, "shard"),
        ),
        check_vma=False,
    )
```

```python
import functools

import jax
import jax.numpy as jnp
from jax import lax
from jax.experimental import pallas as pl
from jax.experimental.pallas import tpu as pltpu
from jax.sharding import PartitionSpec as P

MESH = pl.DeviceIdType.MESH

HEADS = 12
HEAD = 64
LAYERS = 1

epsilon = 1e-05

def to_float(value):
    return value.astype(jnp.float32)


def layer_norm(inputs, norm_gain, norm_shift):
    center = inputs - jnp.mean(inputs, axis=-1, keepdims=True)
    inverse_std = lax.rsqrt(jnp.mean(center * center, axis=-1, keepdims=True) + epsilon)
    normed = center * inverse_std
    return (normed * norm_gain + norm_shift, normed, inverse_std)


def norm_back(upstream, normed, inverse_std, norm_gain):
    scaled = upstream * norm_gain
    inner_term = scaled - jnp.mean(scaled, axis=-1, keepdims=True)
    inner_term = inner_term - normed * jnp.mean(scaled * normed, axis=-1, keepdims=True)
    return (inverse_std * inner_term, jnp.sum(upstream * normed, axis=0), jnp.sum(upstream, axis=0))


def layer_forward(inputs, allowed, small, weights):
    ln1_gain, ln1_bias, qv_bias, out_bias, ln2_gain, ln2_bias, fc_bias, proj_bias = small
    qkv_weight, out_weight, fc_weight, proj_weight = weights
    row_count = inputs.shape[0]
    width_all = inputs.shape[1]
    first_norm, normed_one, inverse_one = layer_norm(inputs, ln1_gain, ln1_bias)
    first_low = first_norm.astype(jnp.bfloat16)
    offset = jnp.concatenate(
        [qv_bias[:width_all], jnp.zeros((width_all,), jnp.float32), qv_bias[width_all:]]
    )
    projected = (
        jnp.dot(first_low, qkv_weight, preferred_element_type=jnp.float32) + offset
    ).astype(jnp.bfloat16)
    queries = projected[:, :width_all].reshape(row_count, HEADS, HEAD)
    keys_all = projected[:, width_all : 2 * width_all].reshape(row_count, HEADS, HEAD)
    values_all = projected[:, 2 * width_all :].reshape(row_count, HEADS, HEAD)
    scores = jnp.einsum(
        "qhd,khd->hqk", queries, keys_all, preferred_element_type=jnp.float32
    ) * HEAD ** (-0.5)
    scores = jnp.where(allowed[None], scores, -1e30)
    row_max = jnp.max(scores, axis=-1, keepdims=True)
    log_total = row_max + jnp.log(jnp.sum(jnp.exp(scores - row_max), axis=-1, keepdims=True))
    attn_probs = jnp.exp(scores - log_total)
    probs_low = attn_probs.astype(jnp.bfloat16)
    attn_mixed = jnp.einsum(
        "hqk,khd->qhd", probs_low, values_all, preferred_element_type=jnp.float32
    )
    attn_mixed = attn_mixed.reshape(row_count, width_all).astype(jnp.bfloat16)
    after_attn = (
        inputs + jnp.dot(attn_mixed, out_weight, preferred_element_type=jnp.float32) + out_bias
    )
    second_norm, normed_two, inverse_two = layer_norm(after_attn, ln2_gain, ln2_bias)
    second_low = second_norm.astype(jnp.bfloat16)
    hidden_pre = jnp.dot(second_low, fc_weight, preferred_element_type=jnp.float32) + fc_bias
    hidden_low = jax.nn.gelu(hidden_pre, approximate=True).astype(jnp.bfloat16)
    result = (
        after_attn + jnp.dot(hidden_low, proj_weight, preferred_element_type=jnp.float32) + proj_bias
    )
    return dict(
        normed_one=normed_one,
        inverse_one=inverse_one,
        first_low=first_low,
        queries=queries,
        keys_all=keys_all,
        values_all=values_all,
        attn_probs=attn_probs,
        probs_low=probs_low,
        attn_mixed=attn_mixed,
        normed_two=normed_two,
        inverse_two=inverse_two,
        second_low=second_low,
        hidden_pre=hidden_pre,
        hidden_low=hidden_low,
        result=result,
    )


def layer_backward(upstream, saved, small, weights):
    ln1_gain, ln1_bias, qv_bias, out_bias, ln2_gain, ln2_bias, fc_bias, proj_bias = small
    qkv_weight, out_weight, fc_weight, proj_weight = weights
    row_count = upstream.shape[0]
    width_all = upstream.shape[1]
    proj_in = upstream.astype(jnp.bfloat16)
    grad_proj_b = jnp.sum(to_float(proj_in), axis=0)
    hidden_grad = jnp.einsum("td,fd->tf", proj_in, proj_weight, preferred_element_type=jnp.float32)
    _, gelu_pull = jax.vjp(lambda value: jax.nn.gelu(value, approximate=True), saved["hidden_pre"])
    pre_grad = gelu_pull(hidden_grad)[0].astype(jnp.bfloat16)
    grad_fc_b = jnp.sum(to_float(pre_grad), axis=0)
    second_grad = jnp.einsum("tf,df->td", pre_grad, fc_weight, preferred_element_type=jnp.float32)
    norm_part, grad_ln2_g, grad_ln2_b = norm_back(
        second_grad, saved["normed_two"], saved["inverse_two"], ln2_gain
    )
    residual_grad = upstream + norm_part
    branch_in = residual_grad.astype(jnp.bfloat16)
    grad_out_b = jnp.sum(to_float(branch_in), axis=0)
    mixed_grad = jnp.einsum("td,cd->tc", branch_in, out_weight, preferred_element_type=jnp.float32)
    mixed_grad = mixed_grad.astype(jnp.bfloat16).reshape(row_count, HEADS, HEAD)
    prob_grad = jnp.einsum(
        "qhd,khd->hqk", mixed_grad, saved["values_all"], preferred_element_type=jnp.float32
    )
    value_grad = jnp.einsum(
        "hqk,qhd->khd", saved["probs_low"], mixed_grad, preferred_element_type=jnp.float32
    )
    attn_probs = saved["attn_probs"]
    row_delta = jnp.sum(attn_probs * prob_grad, axis=-1, keepdims=True)
    score_grad = (attn_probs * (prob_grad - row_delta)).astype(jnp.bfloat16)
    query_grad = jnp.einsum(
        "hqk,khd->qhd", score_grad, saved["keys_all"], preferred_element_type=jnp.float32
    ) * HEAD ** (-0.5)
    key_grad = jnp.einsum(
        "hqk,qhd->khd", score_grad, saved["queries"], preferred_element_type=jnp.float32
    ) * HEAD ** (-0.5)
    joined_grad = jnp.concatenate(
        [
            query_grad.reshape(row_count, width_all),
            key_grad.reshape(row_count, width_all),
            value_grad.reshape(row_count, width_all),
        ],
        axis=1,
    ).astype(jnp.bfloat16)
    column_sums = jnp.sum(to_float(joined_grad), axis=0)
    grad_qv_b = jnp.concatenate([column_sums[:width_all], column_sums[2 * width_all :]])
    first_grad = jnp.einsum(
        "te,ce->tc", joined_grad, qkv_weight, preferred_element_type=jnp.float32
    )
    norm_first, grad_ln1_g, grad_ln1_b = norm_back(
        first_grad, saved["normed_one"], saved["inverse_one"], ln1_gain
    )
    small_grads = (
        grad_ln1_g,
        grad_ln1_b,
        grad_qv_b,
        grad_out_b,
        grad_ln2_g,
        grad_ln2_b,
        grad_fc_b,
        grad_proj_b,
    )
    pairs = (
        (saved["first_low"], joined_grad),
        (saved["attn_mixed"], branch_in),
        (saved["second_low"], pre_grad),
        (saved["hidden_low"], proj_in),
    )
    return (residual_grad + norm_first, small_grads, pairs)


def ring_position(shard_index, n):
    if n != 8:
        return shard_index
    y = shard_index % 2
    z = shard_index // 2
    return z * (1 - 2 * y) + 7 * y


def ring_shard(position, n):
    position = position % n
    if n != 8:
        return position
    y = position // 4
    z = (position % 4) * (1 - 2 * y) + 3 * y
    return z * 2 + y


FIRST_CORE_HALF = (0, 3)


X_ONLY = (2, 3)


def gather_kernel(n, count, *refs):
    local = refs[:count]
    full = refs[count : 2 * count]
    ring_send, ring_recv, pair_send, pair_recv, x_send, x_recv, relay_send, relay_recv = refs[2 * count :]
    rep = lax.axis_index("rep")
    shard = lax.axis_index("shard")
    core = rep % 2
    plane = rep // 2
    step_dir = 1 - 2 * core
    partner = (rep + step_dir, shard)
    x_partner = ((rep + 2) % 4, shard)
    here = ring_position(shard, n)
    target = (rep, ring_shard(here + step_dir, n))
    source = (rep, ring_shard(here - step_dir, n))
    steps = n // 2
    split_last = n % 2 == 0

    barrier = pltpu.get_barrier_semaphore()
    for peer in (target, source, partner, x_partner):
        pl.semaphore_signal(barrier, inc=1, device_id=peer, device_id_type=MESH)
    pl.semaphore_wait(barrier, 4)

    def both(a, b):
        if a is True:
            return b
        if b is True:
            return a
        return jnp.logical_and(a, b)

    def core_carries(k, w, which_core):
        if split_last and k == steps:
            return (which_core == 0) == (w in FIRST_CORE_HALF)
        return True

    def plane_carries(w, which_plane):
        if w == X_ONLY[0]:
            return which_plane == 0
        if w == X_ONLY[1]:
            return which_plane == 1
        return True

    def ring_in(k, w):
        return both(plane_carries(w, plane), core_carries(k, w, core))

    def x_out(k, w):
        if w not in X_ONLY:
            return False
        return both(plane_carries(w, plane), core_carries(k, w, core))

    def x_in(k, w):
        if w not in X_ONLY:
            return False
        return both(plane_carries(w, 1 - plane), core_carries(k, w, core))

    def partner_ring_in(k, w):
        return both(plane_carries(w, plane), core_carries(k, w, 1 - core))

    def partner_x_in(k, w):
        if w not in X_ONLY:
            return False
        return both(plane_carries(w, 1 - plane), core_carries(k, w, 1 - core))

    def guarded(cond, fn):
        if cond is False:
            return
        if cond is True:
            fn()
        else:
            pl.when(cond)(fn)

    def slot(position):
        return ring_shard(position, n)

    def remote(src, dst, ssem, rsem, device):
        return pltpu.make_async_remote_copy(
            src_ref=src, dst_ref=dst, send_sem=ssem, recv_sem=rsem, device_id=device, device_id_type=MESH
        )

    def ring_copy(k, w):
        src_pos = here - step_dir * (k - 1)
        src = local[w] if k == 1 else full[w].at[slot(src_pos)]
        return remote(src, full[w].at[slot(src_pos)], ring_send.at[k - 1, w], ring_recv.at[k - 1, w], target)

    def incoming_ring(k, w):
        pos = slot(here - step_dir * k)
        return remote(full[w].at[pos], full[w].at[pos], ring_send.at[k - 1, w], ring_recv.at[k - 1, w], source)

    def pair_copy(k, w, pos):
        src = local[w] if k == 0 else full[w].at[slot(pos)]
        return remote(src, full[w].at[slot(pos)], pair_send.at[k, w], pair_recv.at[k, w], partner)

    def x_copy(k, w):
        pos = slot(here - step_dir * k)
        return remote(full[w].at[pos], full[w].at[pos], x_send.at[k - 1, w], x_recv.at[k - 1, w], x_partner)

    def relay_copy(k, w, pos):
        pos = slot(pos)
        return remote(full[w].at[pos], full[w].at[pos], relay_send.at[k - 1, w], relay_recv.at[k - 1, w], partner)

    for w in range(count):
        pair_copy(0, w, here).start()
    for w in range(count):
        guarded(ring_in(1, w), lambda w=w: ring_copy(1, w).start())
    for k in range(1, steps + 1):
        for w in range(count):
            def arrived(k=k, w=w):
                incoming_ring(k, w).wait_recv()
                if k < steps:
                    guarded(ring_in(k + 1, w), lambda: ring_copy(k + 1, w).start())
                guarded(x_out(k, w), lambda: x_copy(k, w).start())
                pair_copy(k, w, here - step_dir * k).start()
            guarded(ring_in(k, w), arrived)
        for w in range(count):
            def crossed(k=k, w=w):
                x_copy(k, w).wait_recv()
                relay_copy(k, w, here - step_dir * k).start()
            guarded(x_in(k, w), crossed)
    for w in range(count):
        pair_copy(0, w, here).wait_recv()
    for k in range(1, steps + 1):
        for w in range(count):
            guarded(partner_ring_in(k, w), lambda k=k, w=w: pair_copy(k, w, here + step_dir * k).wait_recv())
            guarded(partner_x_in(k, w), lambda k=k, w=w: relay_copy(k, w, here + step_dir * k).wait_recv())
    for w in range(count):
        pair_copy(0, w, here).wait_send()
    for k in range(1, steps + 1):
        for w in range(count):
            def sent(k=k, w=w):
                ring_copy(k, w).wait_send()
                pair_copy(k, w, here - step_dir * k).wait_send()
            guarded(ring_in(k, w), sent)
            guarded(x_out(k, w), lambda k=k, w=w: x_copy(k, w).wait_send())
            guarded(x_in(k, w), lambda k=k, w=w: relay_copy(k, w, here - step_dir * k).wait_send())


def gather_weights(locals_, n):
    count = len(locals_)
    steps = n // 2
    dma = pltpu.SemaphoreType.DMA
    return pl.pallas_call(
        functools.partial(gather_kernel, n, count),
        out_shape=[jax.ShapeDtypeStruct((n,) + a.shape, a.dtype) for a in locals_],
        in_specs=[pl.BlockSpec(memory_space=pl.ANY)] * count,
        out_specs=[pl.BlockSpec(memory_space=pl.ANY)] * count,
        scratch_shapes=[
            dma((steps, count)),
            dma((steps, count)),
            dma((steps + 1, count)),
            dma((steps + 1, count)),
            dma((steps, count)),
            dma((steps, count)),
            dma((steps, count)),
            dma((steps, count)),
        ],
        compiler_params=pltpu.CompilerParams(collective_id=0, has_side_effects=True),
    )(*locals_)


def add_rows(dst, parts, rows, chunk):
    def body(i, carry):
        window = pl.ds(pl.multiple_of(i * chunk, chunk), chunk)
        total = parts[0][window, :]
        for part in parts[1:]:
            total = total + part[window, :]
        dst[window, :] = total
        return carry

    lax.fori_loop(0, rows // chunk, body, 0)


def reduce_kernel(n, count, *refs):
    contrib = refs[:count]
    out = refs[count : 2 * count]
    land, send, other, own, xland = (
        refs[2 * count + i * count : 2 * count + (i + 1) * count] for i in range(5)
    )
    (load_sem, own_sem, ring_send, ring_recv, pair_send, pair_recv, x_send, x_recv, back_send, back_recv) = refs[
        7 * count :
    ]
    rep = lax.axis_index("rep")
    shard = lax.axis_index("shard")
    core = rep % 2
    step_dir = 1 - 2 * core
    partner = (rep + step_dir, shard)
    x_partner = ((rep + 2) % 4, shard)
    here = ring_position(shard, n)
    target = (rep, ring_shard(here + step_dir, n))
    source = (rep, ring_shard(here - step_dir, n))
    steps = n // 2
    split_first = n % 2 == 0

    def carried(k, w):
        if split_first and k == 1:
            return (core == 0) == (w in FIRST_CORE_HALF)
        return True

    def guarded(cond, fn):
        if cond is True:
            fn()
        else:
            pl.when(cond)(fn)

    def block_at(k):
        return here + step_dir * (steps - k + 1)

    def load(k, w):
        return pltpu.make_async_copy(contrib[w].at[ring_shard(block_at(k), n)], send[w].at[k - 1], load_sem.at[k - 1, w])

    def load_own(w):
        return pltpu.make_async_copy(contrib[w].at[shard], own[w], own_sem.at[w])

    def remote(src, dst, ssem, rsem, device):
        return pltpu.make_async_remote_copy(
            src_ref=src, dst_ref=dst, send_sem=ssem, recv_sem=rsem, device_id=device, device_id_type=MESH
        )

    def ring_copy(k, w, device):
        return remote(send[w].at[k - 1], land[w].at[k - 1], ring_send.at[k - 1, w], ring_recv.at[k - 1, w], device)

    def pair_copy(w):
        return remote(land[w].at[steps - 1], other[w], pair_send.at[w], pair_recv.at[w], partner)

    def x_copy(w):
        return remote(own[w], xland[w], x_send.at[w], x_recv.at[w], x_partner)

    def back_copy(w):
        return remote(out[w], out[w], back_send.at[w], back_recv.at[w], partner)

    def owner(w):
        return core == w % 2

    for w in range(count):
        load_own(w).start()
    for k in range(1, steps + 1):
        for w in range(count):
            guarded(carried(k, w), lambda k=k, w=w: load(k, w).start())

    barrier = pltpu.get_barrier_semaphore()
    for peer in (target, source, partner, x_partner):
        pl.semaphore_signal(barrier, inc=1, device_id=peer, device_id_type=MESH)
    pl.semaphore_wait(barrier, 4)

    def add_into(dst, parts):
        rows = dst.shape[0]
        chunk = 8 if rows % 8 == 0 else rows
        add_rows(dst, parts, rows, chunk)

    def step(k, w):
        load(k, w).wait()
        if k > 1:
            def accumulate():
                ring_copy(k - 1, w, source).wait_recv()
                add_into(send[w].at[k - 1], [send[w].at[k - 1], land[w].at[k - 2]])
            guarded(carried(k - 1, w), accumulate)
        ring_copy(k, w, target).start()

    def arrive(w):
        ring_copy(steps, w, source).wait_recv()
        pl.when(jnp.logical_not(owner(w)))(lambda: pair_copy(w).start())
        mine = land[w].at[steps - 1]

        def plane():
            pair_copy(w).wait_recv()
            load_own(w).wait()

            @pl.when(core == 0)
            def _():
                add_into(own[w], [own[w], mine, other[w]])

            @pl.when(core == 1)
            def _():
                add_into(own[w], [own[w], other[w], mine])

            x_copy(w).start()

        pl.when(owner(w))(plane)

    def total(w):
        x_copy(w).wait_recv()
        add_into(out[w], [own[w], xland[w]])
        back_copy(w).start()

    slots = steps + count - 1
    for t in range(slots + 1):
        for w in range(count):
            k = t - w + 1
            if 1 <= k <= steps:
                guarded(carried(k, w), lambda k=k, w=w: step(k, w))
        for w in range(count):
            if steps + w == t:
                arrive(w)
    for w in range(count):
        pl.when(owner(w))(lambda w=w: total(w))

    for w in range(count):
        def not_owner(w=w):
            load_own(w).wait()
            back_copy(w).wait_recv()
            pair_copy(w).wait_send()

        def was_owner(w=w):
            x_copy(w).wait_send()
            back_copy(w).wait_send()

        pl.when(owner(w))(was_owner)
        pl.when(jnp.logical_not(owner(w)))(not_owner)
    for k in range(1, steps + 1):
        for w in range(count):
            guarded(carried(k, w), lambda k=k, w=w: ring_copy(k, w, target).wait_send())


def reduce_gradients(contribs, n):
    count = len(contribs)
    steps = n // 2
    blocks = [c.shape[1:] for c in contribs]
    vmem = lambda shape: pltpu.VMEM(shape, jnp.float32)
    dma = pltpu.SemaphoreType.DMA
    return pl.pallas_call(
        functools.partial(reduce_kernel, n, count),
        out_shape=[jax.ShapeDtypeStruct(b, jnp.float32) for b in blocks],
        in_specs=[pl.BlockSpec(memory_space=pl.ANY)] * count,
        out_specs=[pl.BlockSpec(memory_space=pltpu.VMEM)] * count,
        scratch_shapes=[vmem((steps,) + b) for b in blocks]
        + [vmem((steps,) + b) for b in blocks]
        + [vmem(b) for b in blocks]
        + [vmem(b) for b in blocks]
        + [vmem(b) for b in blocks]
        + [
            dma((steps, count)),
            dma((count,)),
            dma((steps, count)),
            dma((steps, count)),
            dma((count,)),
            dma((count,)),
            dma((count,)),
            dma((count,)),
            dma((count,)),
            dma((count,)),
        ],
        compiler_params=pltpu.CompilerParams(
            collective_id=1, has_side_effects=True, vmem_limit_bytes=60 * 1024 * 1024
        ),
    )(*contribs)


def swap_core(value):
    rep = lax.axis_size("rep")
    return lax.ppermute(value, "rep", perm=[(i, i ^ 1) for i in range(rep)])


def swap_x(value):
    rep = lax.axis_size("rep")
    return lax.ppermute(value, "rep", perm=[(i, i ^ 2) for i in range(rep)])


def join_halves(mine, theirs, core, axis):
    first = jnp.where(core == 0, mine, theirs)
    second = jnp.where(core == 0, theirs, mine)
    return jnp.concatenate([first, second], axis=axis)


def take_half(value, core, axis):
    half = value.shape[axis] // 2
    return lax.dynamic_slice_in_dim(value, core * half, half, axis=axis)


def per_device(
    tokens,
    segment_ids,
    cotangent,
    ln1_gain,
    ln1_bias,
    qkv_weight,
    qv_bias,
    out_weight,
    out_bias,
    ln2_gain,
    ln2_bias,
    fc_weight,
    fc_bias,
    proj_weight,
    proj_bias,
):
    rep = lax.axis_size("rep")
    assert rep == 4
    core = lax.axis_index("rep") % 2
    row_count = tokens.shape[0]
    positions = jnp.arange(row_count)
    allowed = (segment_ids[:, None] == segment_ids[None, :]) & (
        positions[None, :] <= positions[:, None]
    )
    layer_index = 0
    shard = lax.axis_size("shard")
    small_local = (ln1_gain, ln1_bias, qv_bias, out_bias, ln2_gain, ln2_bias, fc_bias, proj_bias)
    small_local = [v[layer_index] for v in small_local]
    widths = [v.shape[0] for v in small_local]
    local_weights = (
        qkv_weight[layer_index],
        out_weight[layer_index],
        fc_weight[layer_index],
        proj_weight[layer_index],
    )
    rows_local = local_weights[0].shape[0]
    small_row = jnp.concatenate(small_local).reshape(1, -1)
    fulls = gather_weights(list(local_weights) + [small_row], shard)
    weights = tuple(f.reshape(-1, f.shape[-1]) for f in fulls[:4])
    halves = [take_half(w, core, 1) for w in local_weights]
    half_widths = [h.size // rows_local for h in halves]
    packed_all = fulls[4].reshape(shard, -1)
    small = []
    start = 0
    for width in widths:
        small.append(to_float(packed_all[:, start : start + width].reshape(-1)))
        start += width
    small = tuple(small)

    residual = to_float(tokens)
    saved = layer_forward(residual, allowed, small, weights)
    out_tokens = saved["result"].astype(jnp.bfloat16)
    upstream = to_float(cotangent)
    input_grad, small_grads, pairs = layer_backward(upstream, saved, small, weights)

    outgoing = jnp.concatenate([x for x, _ in pairs] + [dy for _, dy in pairs], axis=1)
    incoming = swap_core(outgoing)
    small_mine = jnp.concatenate([g.reshape(shard, -1) for g in small_grads], axis=1)
    small_theirs = swap_core(small_mine)
    small_chip = jnp.where(core == 0, small_mine + small_theirs, small_theirs + small_mine)
    contribs = []
    start = 0
    partner_x = []
    for x, _ in pairs:
        partner_x.append(incoming[:, start : start + x.shape[1]])
        start += x.shape[1]
    for (x, dy), px in zip(pairs, partner_x):
        pdy = incoming[:, start : start + dy.shape[1]]
        start += dy.shape[1]
        rows = join_halves(x, px, core, 0)
        grads = join_halves(dy, pdy, core, 0)
        grad = jnp.einsum("tc,te->ce", rows, grads, preferred_element_type=jnp.float32)
        contribs.append(grad.reshape(shard, -1, grad.shape[1]))
    contribs.append(small_chip.reshape(shard, 1, -1))
    totals = reduce_gradients(contribs, shard)
    small_share = totals[4]
    owned = [t[None] for t in totals[:4]]
    small_owned = []
    start = 0
    for g in small_grads:
        width = g.shape[0] // shard
        small_owned.append(small_share[:, start : start + width])
        start += width

    (g_ln1_g, g_ln1_b, g_qv_b, g_out_b, g_ln2_g, g_ln2_b, g_fc_b, g_proj_b) = small_owned
    g_qkv, g_out, g_fc, g_proj = owned
    return (
        out_tokens,
        input_grad,
        g_ln1_g,
        g_ln1_b,
        g_qkv,
        g_qv_b,
        g_out,
        g_out_b,
        g_ln2_g,
        g_ln2_b,
        g_fc,
        g_fc_b,
        g_proj,
        g_proj_b,
    )


def solution(mesh):
    placed = (
        P(("rep", "shard"), None),
        P(("rep", "shard")),
        P(("rep", "shard"), None),
        P(None, "shard"),
        P(None, "shard"),
        P(None, "shard", None),
        P(None, "shard"),
        P(None, "shard", None),
        P(None, "shard"),
        P(None, "shard"),
        P(None, "shard"),
        P(None, "shard", None),
        P(None, "shard"),
        P(None, "shard", None),
        P(None, "shard"),
    )
    return jax.shard_map(
        per_device,
        mesh=mesh,
        in_specs=placed,
        out_specs=(
            P(("rep", "shard"), None),
            P(("rep", "shard"), None),
            P(None, "shard"),
            P(None, "shard"),
            P(None, "shard", None),
            P(None, "shard"),
            P(None, "shard", None),
            P(None, "shard"),
            P(None, "shard"),
            P(None, "shard"),
            P(None, "shard", None),
            P(None, "shard"),
            P(None, "shard", None),
            P(None, "shard"),
        ),
        check_vma=False,
    )
```

```python
import functools

import jax
import jax.numpy as jnp
from jax import lax
from jax.experimental import pallas as pl
from jax.experimental.pallas import tpu as pltpu
from jax.sharding import PartitionSpec as P

MESH = pl.DeviceIdType.MESH

HEADS = 12
HEAD = 64
LAYERS = 1

epsilon = 1e-05

def to_float(value):
    return value.astype(jnp.float32)


def layer_norm(inputs, norm_gain, norm_shift):
    center = inputs - jnp.mean(inputs, axis=-1, keepdims=True)
    inverse_std = lax.rsqrt(jnp.mean(center * center, axis=-1, keepdims=True) + epsilon)
    normed = center * inverse_std
    return (normed * norm_gain + norm_shift, normed, inverse_std)


def norm_back(upstream, normed, inverse_std, norm_gain):
    scaled = upstream * norm_gain
    inner_term = scaled - jnp.mean(scaled, axis=-1, keepdims=True)
    inner_term = inner_term - normed * jnp.mean(scaled * normed, axis=-1, keepdims=True)
    return (inverse_std * inner_term, jnp.sum(upstream * normed, axis=0), jnp.sum(upstream, axis=0))


def layer_forward(inputs, allowed, small, weights):
    ln1_gain, ln1_bias, qv_bias, out_bias, ln2_gain, ln2_bias, fc_bias, proj_bias = small
    qkv_weight, out_weight, fc_weight, proj_weight = weights
    row_count = inputs.shape[0]
    width_all = inputs.shape[1]
    first_norm, normed_one, inverse_one = layer_norm(inputs, ln1_gain, ln1_bias)
    first_low = first_norm.astype(jnp.bfloat16)
    offset = jnp.concatenate(
        [qv_bias[:width_all], jnp.zeros((width_all,), jnp.float32), qv_bias[width_all:]]
    )
    projected = (
        jnp.dot(first_low, qkv_weight, preferred_element_type=jnp.float32) + offset
    ).astype(jnp.bfloat16)
    queries = projected[:, :width_all].reshape(row_count, HEADS, HEAD)
    keys_all = projected[:, width_all : 2 * width_all].reshape(row_count, HEADS, HEAD)
    values_all = projected[:, 2 * width_all :].reshape(row_count, HEADS, HEAD)
    scores = jnp.einsum(
        "qhd,khd->hqk", queries, keys_all, preferred_element_type=jnp.float32
    ) * HEAD ** (-0.5)
    scores = jnp.where(allowed[None], scores, -1e30)
    row_max = jnp.max(scores, axis=-1, keepdims=True)
    log_total = row_max + jnp.log(jnp.sum(jnp.exp(scores - row_max), axis=-1, keepdims=True))
    attn_probs = jnp.exp(scores - log_total)
    probs_low = attn_probs.astype(jnp.bfloat16)
    attn_mixed = jnp.einsum(
        "hqk,khd->qhd", probs_low, values_all, preferred_element_type=jnp.float32
    )
    attn_mixed = attn_mixed.reshape(row_count, width_all).astype(jnp.bfloat16)
    after_attn = (
        inputs + jnp.dot(attn_mixed, out_weight, preferred_element_type=jnp.float32) + out_bias
    )
    second_norm, normed_two, inverse_two = layer_norm(after_attn, ln2_gain, ln2_bias)
    second_low = second_norm.astype(jnp.bfloat16)
    hidden_pre = jnp.dot(second_low, fc_weight, preferred_element_type=jnp.float32) + fc_bias
    hidden_low = jax.nn.gelu(hidden_pre, approximate=True).astype(jnp.bfloat16)
    result = (
        after_attn + jnp.dot(hidden_low, proj_weight, preferred_element_type=jnp.float32) + proj_bias
    )
    return dict(
        normed_one=normed_one,
        inverse_one=inverse_one,
        first_low=first_low,
        queries=queries,
        keys_all=keys_all,
        values_all=values_all,
        attn_probs=attn_probs,
        probs_low=probs_low,
        attn_mixed=attn_mixed,
        normed_two=normed_two,
        inverse_two=inverse_two,
        second_low=second_low,
        hidden_pre=hidden_pre,
        hidden_low=hidden_low,
        result=result,
    )


def layer_backward(upstream, saved, small, weights):
    ln1_gain, ln1_bias, qv_bias, out_bias, ln2_gain, ln2_bias, fc_bias, proj_bias = small
    qkv_weight, out_weight, fc_weight, proj_weight = weights
    row_count = upstream.shape[0]
    width_all = upstream.shape[1]
    proj_in = upstream.astype(jnp.bfloat16)
    grad_proj_b = jnp.sum(to_float(proj_in), axis=0)
    hidden_grad = jnp.einsum("td,fd->tf", proj_in, proj_weight, preferred_element_type=jnp.float32)
    _, gelu_pull = jax.vjp(lambda value: jax.nn.gelu(value, approximate=True), saved["hidden_pre"])
    pre_grad = gelu_pull(hidden_grad)[0].astype(jnp.bfloat16)
    grad_fc_b = jnp.sum(to_float(pre_grad), axis=0)
    second_grad = jnp.einsum("tf,df->td", pre_grad, fc_weight, preferred_element_type=jnp.float32)
    norm_part, grad_ln2_g, grad_ln2_b = norm_back(
        second_grad, saved["normed_two"], saved["inverse_two"], ln2_gain
    )
    residual_grad = upstream + norm_part
    branch_in = residual_grad.astype(jnp.bfloat16)
    grad_out_b = jnp.sum(to_float(branch_in), axis=0)
    mixed_grad = jnp.einsum("td,cd->tc", branch_in, out_weight, preferred_element_type=jnp.float32)
    mixed_grad = mixed_grad.astype(jnp.bfloat16).reshape(row_count, HEADS, HEAD)
    prob_grad = jnp.einsum(
        "qhd,khd->hqk", mixed_grad, saved["values_all"], preferred_element_type=jnp.float32
    )
    value_grad = jnp.einsum(
        "hqk,qhd->khd", saved["probs_low"], mixed_grad, preferred_element_type=jnp.float32
    )
    attn_probs = saved["attn_probs"]
    row_delta = jnp.sum(attn_probs * prob_grad, axis=-1, keepdims=True)
    score_grad = (attn_probs * (prob_grad - row_delta)).astype(jnp.bfloat16)
    query_grad = jnp.einsum(
        "hqk,khd->qhd", score_grad, saved["keys_all"], preferred_element_type=jnp.float32
    ) * HEAD ** (-0.5)
    key_grad = jnp.einsum(
        "hqk,qhd->khd", score_grad, saved["queries"], preferred_element_type=jnp.float32
    ) * HEAD ** (-0.5)
    joined_grad = jnp.concatenate(
        [
            query_grad.reshape(row_count, width_all),
            key_grad.reshape(row_count, width_all),
            value_grad.reshape(row_count, width_all),
        ],
        axis=1,
    ).astype(jnp.bfloat16)
    column_sums = jnp.sum(to_float(joined_grad), axis=0)
    grad_qv_b = jnp.concatenate([column_sums[:width_all], column_sums[2 * width_all :]])
    first_grad = jnp.einsum(
        "te,ce->tc", joined_grad, qkv_weight, preferred_element_type=jnp.float32
    )
    norm_first, grad_ln1_g, grad_ln1_b = norm_back(
        first_grad, saved["normed_one"], saved["inverse_one"], ln1_gain
    )
    small_grads = (
        grad_ln1_g,
        grad_ln1_b,
        grad_qv_b,
        grad_out_b,
        grad_ln2_g,
        grad_ln2_b,
        grad_fc_b,
        grad_proj_b,
    )
    pairs = (
        (saved["first_low"], joined_grad),
        (saved["attn_mixed"], branch_in),
        (saved["second_low"], pre_grad),
        (saved["hidden_low"], proj_in),
    )
    return (residual_grad + norm_first, small_grads, pairs)


def ring_position(shard_index, n):
    if n != 8:
        return shard_index
    y = shard_index % 2
    z = shard_index // 2
    return z * (1 - 2 * y) + 7 * y


def ring_shard(position, n):
    position = position % n
    if n != 8:
        return position
    y = position // 4
    z = (position % 4) * (1 - 2 * y) + 3 * y
    return z * 2 + y


FIRST_CORE_HALF = (0, 3)


X_ONLY = (2, 3)


def gather_kernel(n, count, *refs):
    local = refs[:count]
    full = refs[count : 2 * count]
    ring_send, ring_recv, pair_send, pair_recv, x_send, x_recv, relay_send, relay_recv = refs[2 * count :]
    rep = lax.axis_index("rep")
    shard = lax.axis_index("shard")
    core = rep % 2
    plane = rep // 2
    step_dir = 1 - 2 * core
    partner = (rep + step_dir, shard)
    x_partner = ((rep + 2) % 4, shard)
    here = ring_position(shard, n)
    target = (rep, ring_shard(here + step_dir, n))
    source = (rep, ring_shard(here - step_dir, n))
    steps = n // 2
    split_last = n % 2 == 0

    barrier = pltpu.get_barrier_semaphore()
    for peer in (target, source, partner, x_partner):
        pl.semaphore_signal(barrier, inc=1, device_id=peer, device_id_type=MESH)
    pl.semaphore_wait(barrier, 4)

    def both(a, b):
        if a is True:
            return b
        if b is True:
            return a
        return jnp.logical_and(a, b)

    def core_carries(k, w, which_core):
        if split_last and k == steps:
            return (which_core == 0) == (w in FIRST_CORE_HALF)
        return True

    def plane_carries(w, which_plane):
        if w == X_ONLY[0]:
            return which_plane == 0
        if w == X_ONLY[1]:
            return which_plane == 1
        return True

    def ring_in(k, w):
        return both(plane_carries(w, plane), core_carries(k, w, core))

    def x_out(k, w):
        if w not in X_ONLY:
            return False
        return both(plane_carries(w, plane), core_carries(k, w, core))

    def x_in(k, w):
        if w not in X_ONLY:
            return False
        return both(plane_carries(w, 1 - plane), core_carries(k, w, core))

    def partner_ring_in(k, w):
        return both(plane_carries(w, plane), core_carries(k, w, 1 - core))

    def partner_x_in(k, w):
        if w not in X_ONLY:
            return False
        return both(plane_carries(w, 1 - plane), core_carries(k, w, 1 - core))

    def guarded(cond, fn):
        if cond is False:
            return
        if cond is True:
            fn()
        else:
            pl.when(cond)(fn)

    def slot(position):
        return ring_shard(position, n)

    def remote(src, dst, ssem, rsem, device):
        return pltpu.make_async_remote_copy(
            src_ref=src, dst_ref=dst, send_sem=ssem, recv_sem=rsem, device_id=device, device_id_type=MESH
        )

    def ring_copy(k, w):
        src_pos = here - step_dir * (k - 1)
        src = local[w] if k == 1 else full[w].at[slot(src_pos)]
        return remote(src, full[w].at[slot(src_pos)], ring_send.at[k - 1, w], ring_recv.at[k - 1, w], target)

    def incoming_ring(k, w):
        pos = slot(here - step_dir * k)
        return remote(full[w].at[pos], full[w].at[pos], ring_send.at[k - 1, w], ring_recv.at[k - 1, w], source)

    def pair_copy(k, w, pos):
        src = local[w] if k == 0 else full[w].at[slot(pos)]
        return remote(src, full[w].at[slot(pos)], pair_send.at[k, w], pair_recv.at[k, w], partner)

    def x_copy(k, w):
        pos = slot(here - step_dir * k)
        return remote(full[w].at[pos], full[w].at[pos], x_send.at[k - 1, w], x_recv.at[k - 1, w], x_partner)

    def relay_copy(k, w, pos):
        pos = slot(pos)
        return remote(full[w].at[pos], full[w].at[pos], relay_send.at[k - 1, w], relay_recv.at[k - 1, w], partner)

    for w in range(count):
        pair_copy(0, w, here).start()
    for w in range(count):
        guarded(ring_in(1, w), lambda w=w: ring_copy(1, w).start())
    for k in range(1, steps + 1):
        for w in range(count):
            def arrived(k=k, w=w):
                incoming_ring(k, w).wait_recv()
                if k < steps:
                    guarded(ring_in(k + 1, w), lambda: ring_copy(k + 1, w).start())
                guarded(x_out(k, w), lambda: x_copy(k, w).start())
                pair_copy(k, w, here - step_dir * k).start()
            guarded(ring_in(k, w), arrived)
        for w in range(count):
            def crossed(k=k, w=w):
                x_copy(k, w).wait_recv()
                relay_copy(k, w, here - step_dir * k).start()
            guarded(x_in(k, w), crossed)
    for w in range(count):
        pair_copy(0, w, here).wait_recv()
    for k in range(1, steps + 1):
        for w in range(count):
            guarded(partner_ring_in(k, w), lambda k=k, w=w: pair_copy(k, w, here + step_dir * k).wait_recv())
            guarded(partner_x_in(k, w), lambda k=k, w=w: relay_copy(k, w, here + step_dir * k).wait_recv())
    for w in range(count):
        pair_copy(0, w, here).wait_send()
    for k in range(1, steps + 1):
        for w in range(count):
            def sent(k=k, w=w):
                ring_copy(k, w).wait_send()
                pair_copy(k, w, here - step_dir * k).wait_send()
            guarded(ring_in(k, w), sent)
            guarded(x_out(k, w), lambda k=k, w=w: x_copy(k, w).wait_send())
            guarded(x_in(k, w), lambda k=k, w=w: relay_copy(k, w, here - step_dir * k).wait_send())


def gather_weights(locals_, n):
    count = len(locals_)
    steps = n // 2
    dma = pltpu.SemaphoreType.DMA
    return pl.pallas_call(
        functools.partial(gather_kernel, n, count),
        out_shape=[jax.ShapeDtypeStruct((n,) + a.shape, a.dtype) for a in locals_],
        in_specs=[pl.BlockSpec(memory_space=pl.ANY)] * count,
        out_specs=[pl.BlockSpec(memory_space=pl.ANY)] * count,
        scratch_shapes=[
            dma((steps, count)),
            dma((steps, count)),
            dma((steps + 1, count)),
            dma((steps + 1, count)),
            dma((steps, count)),
            dma((steps, count)),
            dma((steps, count)),
            dma((steps, count)),
        ],
        compiler_params=pltpu.CompilerParams(collective_id=0, has_side_effects=True),
    )(*locals_)


def add_rows(dst, parts, rows, chunk):
    def body(i, carry):
        window = pl.ds(pl.multiple_of(i * chunk, chunk), chunk)
        total = parts[0][window, :]
        for part in parts[1:]:
            total = total + part[window, :]
        dst[window, :] = total
        return carry

    lax.fori_loop(0, rows // chunk, body, 0)


def reduce_kernel(n, count, mm, *refs):
    xt = refs[:mm]
    dy = refs[mm : 2 * mm]
    contrib = (None,) * mm + refs[2 * mm : mm + count]
    refs = refs[mm + count :]
    out = refs[:count]
    land, send, other, own, xland = (refs[count + i * count : count + (i + 1) * count] for i in range(5))
    (load_sem, own_sem, ring_send, ring_recv, pair_send, pair_recv, x_send, x_recv, back_send, back_recv) = refs[
        6 * count :
    ]
    rep = lax.axis_index("rep")
    shard = lax.axis_index("shard")
    core = rep % 2
    step_dir = 1 - 2 * core
    partner = (rep + step_dir, shard)
    x_partner = ((rep + 2) % 4, shard)
    here = ring_position(shard, n)
    target = (rep, ring_shard(here + step_dir, n))
    source = (rep, ring_shard(here - step_dir, n))
    steps = n // 2
    split_first = n % 2 == 0

    def carried(k, w):
        if split_first and k == 1:
            return (core == 0) == (w in FIRST_CORE_HALF)
        return True

    def guarded(cond, fn):
        if cond is True:
            fn()
        else:
            pl.when(cond)(fn)

    def block_at(k):
        return here + step_dir * (steps - k + 1)

    def load(k, w):
        return pltpu.make_async_copy(contrib[w].at[ring_shard(block_at(k), n)], send[w].at[k - 1], load_sem.at[k - 1, w])

    def load_own(w):
        return pltpu.make_async_copy(contrib[w].at[shard], own[w], own_sem.at[w])

    def remote(src, dst, ssem, rsem, device):
        return pltpu.make_async_remote_copy(
            src_ref=src, dst_ref=dst, send_sem=ssem, recv_sem=rsem, device_id=device, device_id_type=MESH
        )

    def ring_copy(k, w, device):
        return remote(send[w].at[k - 1], land[w].at[k - 1], ring_send.at[k - 1, w], ring_recv.at[k - 1, w], device)

    def pair_copy(w):
        return remote(land[w].at[steps - 1], other[w], pair_send.at[w], pair_recv.at[w], partner)

    def x_copy(w):
        return remote(own[w], xland[w], x_send.at[w], x_recv.at[w], x_partner)

    def back_copy(w):
        return remote(out[w], out[w], back_send.at[w], back_recv.at[w], partner)

    def owner(w):
        return core == w % 2

    def contribute(dst, w, position):
        block = ring_shard(position, n)
        width = 256

        def body(i, carry):
            window = pl.ds(pl.multiple_of(i * width, width), width)
            dst[:, window] = jnp.dot(xt[w][block], dy[w][:, window], preferred_element_type=jnp.float32)
            return carry

        lax.fori_loop(0, dy[w].shape[1] // width, body, 0)

    for w in range(mm, count):
        load_own(w).start()
    for k in range(1, steps + 1):
        for w in range(mm, count):
            guarded(carried(k, w), lambda k=k, w=w: load(k, w).start())

    barrier = pltpu.get_barrier_semaphore()
    for peer in (target, source, partner, x_partner):
        pl.semaphore_signal(barrier, inc=1, device_id=peer, device_id_type=MESH)
    pl.semaphore_wait(barrier, 4)

    def add_into(dst, parts):
        rows = dst.shape[0]
        chunk = 8 if rows % 8 == 0 else rows
        add_rows(dst, parts, rows, chunk)

    def step(k, w):
        if w < mm:
            contribute(send[w].at[k - 1], w, block_at(k))
        else:
            load(k, w).wait()
        if k > 1:
            def accumulate():
                ring_copy(k - 1, w, source).wait_recv()
                add_into(send[w].at[k - 1], [send[w].at[k - 1], land[w].at[k - 2]])
            guarded(carried(k - 1, w), accumulate)
        ring_copy(k, w, target).start()

    def arrive(w):
        ring_copy(steps, w, source).wait_recv()
        pl.when(jnp.logical_not(owner(w)))(lambda: pair_copy(w).start())
        mine = land[w].at[steps - 1]

        def plane():
            if w < mm:
                contribute(own[w], w, here)
            else:
                load_own(w).wait()
            pair_copy(w).wait_recv()

            @pl.when(core == 0)
            def _():
                add_into(own[w], [own[w], mine, other[w]])

            @pl.when(core == 1)
            def _():
                add_into(own[w], [own[w], other[w], mine])

            x_copy(w).start()

        pl.when(owner(w))(plane)

    def total(w):
        x_copy(w).wait_recv()
        add_into(out[w], [own[w], xland[w]])
        back_copy(w).start()

    slots = steps + count - 1
    for t in range(slots + 1):
        for w in range(count):
            k = t - w + 1
            if 1 <= k <= steps:
                guarded(carried(k, w), lambda k=k, w=w: step(k, w))
        for w in range(count):
            if steps + w == t:
                arrive(w)
    for w in range(count):
        pl.when(owner(w))(lambda w=w: total(w))

    for w in range(count):
        def not_owner(w=w):
            if w >= mm:
                load_own(w).wait()
            back_copy(w).wait_recv()
            pair_copy(w).wait_send()

        def was_owner(w=w):
            x_copy(w).wait_send()
            back_copy(w).wait_send()

        pl.when(owner(w))(was_owner)
        pl.when(jnp.logical_not(owner(w)))(not_owner)
    for k in range(1, steps + 1):
        for w in range(count):
            guarded(carried(k, w), lambda k=k, w=w: ring_copy(k, w, target).wait_send())


def reduce_gradients(pairs_t, contribs, n):
    mm = len(pairs_t)
    count = mm + len(contribs)
    steps = n // 2
    blocks = [(xt.shape[1], dy.shape[1]) for xt, dy in pairs_t] + [c.shape[1:] for c in contribs]
    vmem = lambda shape: pltpu.VMEM(shape, jnp.float32)
    dma = pltpu.SemaphoreType.DMA
    return pl.pallas_call(
        functools.partial(reduce_kernel, n, count, mm),
        out_shape=[jax.ShapeDtypeStruct(b, jnp.float32) for b in blocks],
        in_specs=[pl.BlockSpec(memory_space=pltpu.VMEM)] * (2 * mm)
        + [pl.BlockSpec(memory_space=pl.ANY)] * len(contribs),
        out_specs=[pl.BlockSpec(memory_space=pltpu.VMEM)] * count,
        scratch_shapes=[vmem((steps,) + b) for b in blocks]
        + [vmem((steps,) + b) for b in blocks]
        + [vmem(b) for b in blocks]
        + [vmem(b) for b in blocks]
        + [vmem(b) for b in blocks]
        + [
            dma((steps, count)),
            dma((count,)),
            dma((steps, count)),
            dma((steps, count)),
            dma((count,)),
            dma((count,)),
            dma((count,)),
            dma((count,)),
            dma((count,)),
            dma((count,)),
        ],
        compiler_params=pltpu.CompilerParams(
            collective_id=1, has_side_effects=True, vmem_limit_bytes=62 * 1024 * 1024
        ),
    )(*[xt for xt, _ in pairs_t], *[dy for _, dy in pairs_t], *contribs)


def swap_core(value):
    rep = lax.axis_size("rep")
    return lax.ppermute(value, "rep", perm=[(i, i ^ 1) for i in range(rep)])


def swap_x(value):
    rep = lax.axis_size("rep")
    return lax.ppermute(value, "rep", perm=[(i, i ^ 2) for i in range(rep)])


def join_halves(mine, theirs, core, axis):
    first = jnp.where(core == 0, mine, theirs)
    second = jnp.where(core == 0, theirs, mine)
    return jnp.concatenate([first, second], axis=axis)


def take_half(value, core, axis):
    half = value.shape[axis] // 2
    return lax.dynamic_slice_in_dim(value, core * half, half, axis=axis)


def per_device(
    tokens,
    segment_ids,
    cotangent,
    ln1_gain,
    ln1_bias,
    qkv_weight,
    qv_bias,
    out_weight,
    out_bias,
    ln2_gain,
    ln2_bias,
    fc_weight,
    fc_bias,
    proj_weight,
    proj_bias,
):
    rep = lax.axis_size("rep")
    assert rep == 4
    core = lax.axis_index("rep") % 2
    row_count = tokens.shape[0]
    positions = jnp.arange(row_count)
    allowed = (segment_ids[:, None] == segment_ids[None, :]) & (
        positions[None, :] <= positions[:, None]
    )
    layer_index = 0
    shard = lax.axis_size("shard")
    small_local = (ln1_gain, ln1_bias, qv_bias, out_bias, ln2_gain, ln2_bias, fc_bias, proj_bias)
    small_local = [v[layer_index] for v in small_local]
    widths = [v.shape[0] for v in small_local]
    local_weights = (
        qkv_weight[layer_index],
        out_weight[layer_index],
        fc_weight[layer_index],
        proj_weight[layer_index],
    )
    rows_local = local_weights[0].shape[0]
    small_row = jnp.concatenate(small_local).reshape(1, -1)
    fulls = gather_weights(list(local_weights) + [small_row], shard)
    weights = tuple(f.reshape(-1, f.shape[-1]) for f in fulls[:4])
    halves = [take_half(w, core, 1) for w in local_weights]
    half_widths = [h.size // rows_local for h in halves]
    packed_all = fulls[4].reshape(shard, -1)
    small = []
    start = 0
    for width in widths:
        small.append(to_float(packed_all[:, start : start + width].reshape(-1)))
        start += width
    small = tuple(small)

    residual = to_float(tokens)
    saved = layer_forward(residual, allowed, small, weights)
    out_tokens = saved["result"].astype(jnp.bfloat16)
    upstream = to_float(cotangent)
    input_grad, small_grads, pairs = layer_backward(upstream, saved, small, weights)

    outgoing = jnp.concatenate([x for x, _ in pairs] + [dy for _, dy in pairs], axis=1)
    incoming = swap_core(outgoing)
    small_mine = jnp.concatenate([g.reshape(shard, -1) for g in small_grads], axis=1)
    small_theirs = swap_core(small_mine)
    small_chip = jnp.where(core == 0, small_mine + small_theirs, small_theirs + small_mine)
    start = 0
    partner_x = []
    for x, _ in pairs:
        partner_x.append(incoming[:, start : start + x.shape[1]])
        start += x.shape[1]
    pairs_t = []
    for (x, dy), px in zip(pairs, partner_x):
        pdy = incoming[:, start : start + dy.shape[1]]
        start += dy.shape[1]
        rows_t = jnp.concatenate([x, px], axis=0).T
        pairs_t.append((rows_t.reshape(shard, -1, rows_t.shape[1]), jnp.concatenate([dy, pdy], axis=0)))
    totals = reduce_gradients(pairs_t, [small_chip.reshape(shard, 1, -1)], shard)
    small_share = totals[4]
    owned = [t[None] for t in totals[:4]]
    small_owned = []
    start = 0
    for g in small_grads:
        width = g.shape[0] // shard
        small_owned.append(small_share[:, start : start + width])
        start += width

    (g_ln1_g, g_ln1_b, g_qv_b, g_out_b, g_ln2_g, g_ln2_b, g_fc_b, g_proj_b) = small_owned
    g_qkv, g_out, g_fc, g_proj = owned
    return (
        out_tokens,
        input_grad,
        g_ln1_g,
        g_ln1_b,
        g_qkv,
        g_qv_b,
        g_out,
        g_out_b,
        g_ln2_g,
        g_ln2_b,
        g_fc,
        g_fc_b,
        g_proj,
        g_proj_b,
    )


def solution(mesh):
    placed = (
        P(("rep", "shard"), None),
        P(("rep", "shard")),
        P(("rep", "shard"), None),
        P(None, "shard"),
        P(None, "shard"),
        P(None, "shard", None),
        P(None, "shard"),
        P(None, "shard", None),
        P(None, "shard"),
        P(None, "shard"),
        P(None, "shard"),
        P(None, "shard", None),
        P(None, "shard"),
        P(None, "shard", None),
        P(None, "shard"),
    )
    return jax.shard_map(
        per_device,
        mesh=mesh,
        in_specs=placed,
        out_specs=(
            P(("rep", "shard"), None),
            P(("rep", "shard"), None),
            P(None, "shard"),
            P(None, "shard"),
            P(None, "shard", None),
            P(None, "shard"),
            P(None, "shard", None),
            P(None, "shard"),
            P(None, "shard"),
            P(None, "shard"),
            P(None, "shard", None),
            P(None, "shard"),
            P(None, "shard", None),
            P(None, "shard"),
        ),
        check_vma=False,
    )
```

```python
import functools

import jax
import jax.numpy as jnp
from jax import lax
from jax.experimental import pallas as pl
from jax.experimental.pallas import tpu as pltpu
from jax.sharding import PartitionSpec as P

MESH = pl.DeviceIdType.MESH

HEADS = 12
HEAD = 64
LAYERS = 1

epsilon = 1e-05

def to_float(value):
    return value.astype(jnp.float32)


def layer_norm(inputs, norm_gain, norm_shift):
    center = inputs - jnp.mean(inputs, axis=-1, keepdims=True)
    inverse_std = lax.rsqrt(jnp.mean(center * center, axis=-1, keepdims=True) + epsilon)
    normed = center * inverse_std
    return (normed * norm_gain + norm_shift, normed, inverse_std)


def norm_back(upstream, normed, inverse_std, norm_gain):
    scaled = upstream * norm_gain
    inner_term = scaled - jnp.mean(scaled, axis=-1, keepdims=True)
    inner_term = inner_term - normed * jnp.mean(scaled * normed, axis=-1, keepdims=True)
    return (inverse_std * inner_term, jnp.sum(upstream * normed, axis=0), jnp.sum(upstream, axis=0))


def layer_forward(inputs, allowed, small, weights):
    ln1_gain, ln1_bias, qv_bias, out_bias, ln2_gain, ln2_bias, fc_bias, proj_bias = small
    qkv_weight, out_weight, fc_weight, proj_weight = weights
    row_count = inputs.shape[0]
    width_all = inputs.shape[1]
    first_norm, normed_one, inverse_one = layer_norm(inputs, ln1_gain, ln1_bias)
    first_low = first_norm.astype(jnp.bfloat16)
    offset = jnp.concatenate(
        [qv_bias[:width_all], jnp.zeros((width_all,), jnp.float32), qv_bias[width_all:]]
    )
    projected = (
        jnp.dot(first_low, qkv_weight, preferred_element_type=jnp.float32) + offset
    ).astype(jnp.bfloat16)
    queries = projected[:, :width_all].reshape(row_count, HEADS, HEAD)
    keys_all = projected[:, width_all : 2 * width_all].reshape(row_count, HEADS, HEAD)
    values_all = projected[:, 2 * width_all :].reshape(row_count, HEADS, HEAD)
    scores = jnp.einsum(
        "qhd,khd->hqk", queries, keys_all, preferred_element_type=jnp.float32
    ) * HEAD ** (-0.5)
    scores = jnp.where(allowed[None], scores, -1e30)
    row_max = jnp.max(scores, axis=-1, keepdims=True)
    log_total = row_max + jnp.log(jnp.sum(jnp.exp(scores - row_max), axis=-1, keepdims=True))
    attn_probs = jnp.exp(scores - log_total)
    probs_low = attn_probs.astype(jnp.bfloat16)
    attn_mixed = jnp.einsum(
        "hqk,khd->qhd", probs_low, values_all, preferred_element_type=jnp.float32
    )
    attn_mixed = attn_mixed.reshape(row_count, width_all).astype(jnp.bfloat16)
    after_attn = (
        inputs + jnp.dot(attn_mixed, out_weight, preferred_element_type=jnp.float32) + out_bias
    )
    second_norm, normed_two, inverse_two = layer_norm(after_attn, ln2_gain, ln2_bias)
    second_low = second_norm.astype(jnp.bfloat16)
    hidden_pre = jnp.dot(second_low, fc_weight, preferred_element_type=jnp.float32) + fc_bias
    hidden_low = jax.nn.gelu(hidden_pre, approximate=True).astype(jnp.bfloat16)
    result = (
        after_attn + jnp.dot(hidden_low, proj_weight, preferred_element_type=jnp.float32) + proj_bias
    )
    return dict(
        normed_one=normed_one,
        inverse_one=inverse_one,
        first_low=first_low,
        queries=queries,
        keys_all=keys_all,
        values_all=values_all,
        attn_probs=attn_probs,
        probs_low=probs_low,
        attn_mixed=attn_mixed,
        normed_two=normed_two,
        inverse_two=inverse_two,
        second_low=second_low,
        hidden_pre=hidden_pre,
        hidden_low=hidden_low,
        result=result,
    )


def layer_backward(upstream, saved, small, weights):
    ln1_gain, ln1_bias, qv_bias, out_bias, ln2_gain, ln2_bias, fc_bias, proj_bias = small
    qkv_weight, out_weight, fc_weight, proj_weight = weights
    row_count = upstream.shape[0]
    width_all = upstream.shape[1]
    proj_in = upstream.astype(jnp.bfloat16)
    grad_proj_b = jnp.sum(to_float(proj_in), axis=0)
    hidden_grad = jnp.einsum("td,fd->tf", proj_in, proj_weight, preferred_element_type=jnp.float32)
    _, gelu_pull = jax.vjp(lambda value: jax.nn.gelu(value, approximate=True), saved["hidden_pre"])
    pre_grad = gelu_pull(hidden_grad)[0].astype(jnp.bfloat16)
    grad_fc_b = jnp.sum(to_float(pre_grad), axis=0)
    second_grad = jnp.einsum("tf,df->td", pre_grad, fc_weight, preferred_element_type=jnp.float32)
    norm_part, grad_ln2_g, grad_ln2_b = norm_back(
        second_grad, saved["normed_two"], saved["inverse_two"], ln2_gain
    )
    residual_grad = upstream + norm_part
    branch_in = residual_grad.astype(jnp.bfloat16)
    grad_out_b = jnp.sum(to_float(branch_in), axis=0)
    mixed_grad = jnp.einsum("td,cd->tc", branch_in, out_weight, preferred_element_type=jnp.float32)
    mixed_grad = mixed_grad.astype(jnp.bfloat16).reshape(row_count, HEADS, HEAD)
    prob_grad = jnp.einsum(
        "qhd,khd->hqk", mixed_grad, saved["values_all"], preferred_element_type=jnp.float32
    )
    value_grad = jnp.einsum(
        "hqk,qhd->khd", saved["probs_low"], mixed_grad, preferred_element_type=jnp.float32
    )
    attn_probs = saved["attn_probs"]
    row_delta = jnp.sum(attn_probs * prob_grad, axis=-1, keepdims=True)
    score_grad = (attn_probs * (prob_grad - row_delta)).astype(jnp.bfloat16)
    query_grad = jnp.einsum(
        "hqk,khd->qhd", score_grad, saved["keys_all"], preferred_element_type=jnp.float32
    ) * HEAD ** (-0.5)
    key_grad = jnp.einsum(
        "hqk,qhd->khd", score_grad, saved["queries"], preferred_element_type=jnp.float32
    ) * HEAD ** (-0.5)
    joined_grad = jnp.concatenate(
        [
            query_grad.reshape(row_count, width_all),
            key_grad.reshape(row_count, width_all),
            value_grad.reshape(row_count, width_all),
        ],
        axis=1,
    ).astype(jnp.bfloat16)
    column_sums = jnp.sum(to_float(joined_grad), axis=0)
    grad_qv_b = jnp.concatenate([column_sums[:width_all], column_sums[2 * width_all :]])
    first_grad = jnp.einsum(
        "te,ce->tc", joined_grad, qkv_weight, preferred_element_type=jnp.float32
    )
    norm_first, grad_ln1_g, grad_ln1_b = norm_back(
        first_grad, saved["normed_one"], saved["inverse_one"], ln1_gain
    )
    small_grads = (
        grad_ln1_g,
        grad_ln1_b,
        grad_qv_b,
        grad_out_b,
        grad_ln2_g,
        grad_ln2_b,
        grad_fc_b,
        grad_proj_b,
    )
    pairs = (
        (saved["first_low"], joined_grad),
        (saved["attn_mixed"], branch_in),
        (saved["second_low"], pre_grad),
        (saved["hidden_low"], proj_in),
    )
    return (residual_grad + norm_first, small_grads, pairs)


def ring_position(shard_index, n):
    if n != 8:
        return shard_index
    y = shard_index % 2
    z = shard_index // 2
    return z * (1 - 2 * y) + 7 * y


def ring_shard(position, n):
    position = position % n
    if n != 8:
        return position
    y = position // 4
    z = (position % 4) * (1 - 2 * y) + 3 * y
    return z * 2 + y


FIRST_CORE_HALF = (0, 3)


X_ONLY = (2, 3)


def gather_kernel(n, count, *refs):
    local = refs[:count]
    full = refs[count : 2 * count]
    ring_send, ring_recv, pair_send, pair_recv, x_send, x_recv, relay_send, relay_recv = refs[2 * count :]
    rep = lax.axis_index("rep")
    shard = lax.axis_index("shard")
    core = rep % 2
    plane = rep // 2
    step_dir = 1 - 2 * core
    partner = (rep + step_dir, shard)
    x_partner = ((rep + 2) % 4, shard)
    here = ring_position(shard, n)
    target = (rep, ring_shard(here + step_dir, n))
    source = (rep, ring_shard(here - step_dir, n))
    steps = n // 2
    split_last = n % 2 == 0

    barrier = pltpu.get_barrier_semaphore()
    for peer in (target, source, partner, x_partner):
        pl.semaphore_signal(barrier, inc=1, device_id=peer, device_id_type=MESH)
    pl.semaphore_wait(barrier, 4)

    def both(a, b):
        if a is True:
            return b
        if b is True:
            return a
        return jnp.logical_and(a, b)

    def core_carries(k, w, which_core):
        if split_last and k == steps:
            return (which_core == 0) == (w in FIRST_CORE_HALF)
        return True

    def plane_carries(w, which_plane):
        if w == X_ONLY[0]:
            return which_plane == 0
        if w == X_ONLY[1]:
            return which_plane == 1
        return True

    def ring_in(k, w):
        return both(plane_carries(w, plane), core_carries(k, w, core))

    def x_out(k, w):
        if w not in X_ONLY:
            return False
        return both(plane_carries(w, plane), core_carries(k, w, core))

    def x_in(k, w):
        if w not in X_ONLY:
            return False
        return both(plane_carries(w, 1 - plane), core_carries(k, w, core))

    def partner_ring_in(k, w):
        return both(plane_carries(w, plane), core_carries(k, w, 1 - core))

    def partner_x_in(k, w):
        if w not in X_ONLY:
            return False
        return both(plane_carries(w, 1 - plane), core_carries(k, w, 1 - core))

    def guarded(cond, fn):
        if cond is False:
            return
        if cond is True:
            fn()
        else:
            pl.when(cond)(fn)

    def slot(position):
        return ring_shard(position, n)

    def remote(src, dst, ssem, rsem, device):
        return pltpu.make_async_remote_copy(
            src_ref=src, dst_ref=dst, send_sem=ssem, recv_sem=rsem, device_id=device, device_id_type=MESH
        )

    def ring_copy(k, w):
        src_pos = here - step_dir * (k - 1)
        src = local[w] if k == 1 else full[w].at[slot(src_pos)]
        return remote(src, full[w].at[slot(src_pos)], ring_send.at[k - 1, w], ring_recv.at[k - 1, w], target)

    def incoming_ring(k, w):
        pos = slot(here - step_dir * k)
        return remote(full[w].at[pos], full[w].at[pos], ring_send.at[k - 1, w], ring_recv.at[k - 1, w], source)

    def pair_copy(k, w, pos):
        src = local[w] if k == 0 else full[w].at[slot(pos)]
        return remote(src, full[w].at[slot(pos)], pair_send.at[k, w], pair_recv.at[k, w], partner)

    def x_copy(k, w):
        pos = slot(here - step_dir * k)
        return remote(full[w].at[pos], full[w].at[pos], x_send.at[k - 1, w], x_recv.at[k - 1, w], x_partner)

    def relay_copy(k, w, pos):
        pos = slot(pos)
        return remote(full[w].at[pos], full[w].at[pos], relay_send.at[k - 1, w], relay_recv.at[k - 1, w], partner)

    for w in range(count):
        pair_copy(0, w, here).start()
    for w in range(count):
        guarded(ring_in(1, w), lambda w=w: ring_copy(1, w).start())
    for k in range(1, steps + 1):
        for w in range(count):
            def arrived(k=k, w=w):
                incoming_ring(k, w).wait_recv()
                if k < steps:
                    guarded(ring_in(k + 1, w), lambda: ring_copy(k + 1, w).start())
                guarded(x_out(k, w), lambda: x_copy(k, w).start())
                pair_copy(k, w, here - step_dir * k).start()
            guarded(ring_in(k, w), arrived)
        for w in range(count):
            def crossed(k=k, w=w):
                x_copy(k, w).wait_recv()
                relay_copy(k, w, here - step_dir * k).start()
            guarded(x_in(k, w), crossed)
    for w in range(count):
        pair_copy(0, w, here).wait_recv()
    for k in range(1, steps + 1):
        for w in range(count):
            guarded(partner_ring_in(k, w), lambda k=k, w=w: pair_copy(k, w, here + step_dir * k).wait_recv())
            guarded(partner_x_in(k, w), lambda k=k, w=w: relay_copy(k, w, here + step_dir * k).wait_recv())
    for w in range(count):
        pair_copy(0, w, here).wait_send()
    for k in range(1, steps + 1):
        for w in range(count):
            def sent(k=k, w=w):
                ring_copy(k, w).wait_send()
                pair_copy(k, w, here - step_dir * k).wait_send()
            guarded(ring_in(k, w), sent)
            guarded(x_out(k, w), lambda k=k, w=w: x_copy(k, w).wait_send())
            guarded(x_in(k, w), lambda k=k, w=w: relay_copy(k, w, here - step_dir * k).wait_send())


def gather_weights(locals_, n):
    count = len(locals_)
    steps = n // 2
    dma = pltpu.SemaphoreType.DMA
    return pl.pallas_call(
        functools.partial(gather_kernel, n, count),
        out_shape=[jax.ShapeDtypeStruct((n,) + a.shape, a.dtype) for a in locals_],
        in_specs=[pl.BlockSpec(memory_space=pl.ANY)] * count,
        out_specs=[pl.BlockSpec(memory_space=pl.ANY)] * count,
        scratch_shapes=[
            dma((steps, count)),
            dma((steps, count)),
            dma((steps + 1, count)),
            dma((steps + 1, count)),
            dma((steps, count)),
            dma((steps, count)),
            dma((steps, count)),
            dma((steps, count)),
        ],
        compiler_params=pltpu.CompilerParams(collective_id=0, has_side_effects=True),
    )(*locals_)


def add_rows(dst, parts, rows, chunk):
    def body(i, carry):
        window = pl.ds(pl.multiple_of(i * chunk, chunk), chunk)
        total = parts[0][window, :].astype(jnp.float32)
        for part in parts[1:]:
            total = total + part[window, :].astype(jnp.float32)
        dst[window, :] = total.astype(dst.dtype)
        return carry

    lax.fori_loop(0, rows // chunk, body, 0)


def reduce_kernel(n, count, mm, *refs):
    xt = refs[:mm]
    dy = refs[mm : 2 * mm]
    contrib = (None,) * mm + refs[2 * mm : mm + count]
    refs = refs[mm + count :]
    out = refs[:count]
    land, send, other, own, xland, stage = (refs[count + i * count : count + (i + 1) * count] for i in range(6))
    (load_sem, own_sem, ring_send, ring_recv, pair_send, pair_recv, x_send, x_recv, back_send, back_recv) = refs[
        7 * count :
    ]
    rep = lax.axis_index("rep")
    shard = lax.axis_index("shard")
    core = rep % 2
    step_dir = 1 - 2 * core
    partner = (rep + step_dir, shard)
    x_partner = ((rep + 2) % 4, shard)
    here = ring_position(shard, n)
    target = (rep, ring_shard(here + step_dir, n))
    source = (rep, ring_shard(here - step_dir, n))
    steps = n // 2
    split_first = n % 2 == 0

    def carried(k, w):
        if split_first and k == 1:
            return (core == 0) == (w in FIRST_CORE_HALF)
        return True

    def guarded(cond, fn):
        if cond is True:
            fn()
        else:
            pl.when(cond)(fn)

    def block_at(k):
        return here + step_dir * (steps - k + 1)

    def load(k, w):
        return pltpu.make_async_copy(contrib[w].at[ring_shard(block_at(k), n)], send[w].at[k - 1], load_sem.at[k - 1, w])

    def load_own(w):
        return pltpu.make_async_copy(contrib[w].at[shard], own[w], own_sem.at[w])

    def remote(src, dst, ssem, rsem, device):
        return pltpu.make_async_remote_copy(
            src_ref=src, dst_ref=dst, send_sem=ssem, recv_sem=rsem, device_id=device, device_id_type=MESH
        )

    def ring_copy(k, w, device):
        return remote(send[w].at[k - 1], land[w].at[k - 1], ring_send.at[k - 1, w], ring_recv.at[k - 1, w], device)

    def pair_copy(w):
        return remote(land[w].at[steps - 1], other[w], pair_send.at[w], pair_recv.at[w], partner)

    def x_copy(w):
        return remote(own[w], xland[w], x_send.at[w], x_recv.at[w], x_partner)

    def back_copy(w):
        return remote(out[w], out[w], back_send.at[w], back_recv.at[w], partner)

    def owner(w):
        return core == w % 2

    def contribute(dst, w, position):
        block = ring_shard(position, n)
        width = 256

        def body(i, carry):
            window = pl.ds(pl.multiple_of(i * width, width), width)
            dst[:, window] = jnp.dot(xt[w][block], dy[w][:, window], preferred_element_type=jnp.float32)
            return carry

        lax.fori_loop(0, dy[w].shape[1] // width, body, 0)

    for w in range(mm, count):
        load_own(w).start()
    for k in range(1, steps + 1):
        for w in range(mm, count):
            guarded(carried(k, w), lambda k=k, w=w: load(k, w).start())

    barrier = pltpu.get_barrier_semaphore()
    for peer in (target, source, partner, x_partner):
        pl.semaphore_signal(barrier, inc=1, device_id=peer, device_id_type=MESH)
    pl.semaphore_wait(barrier, 4)

    def add_into(dst, parts):
        rows = dst.shape[0]
        chunk = 16 if rows % 16 == 0 else rows
        add_rows(dst, parts, rows, chunk)

    def step(k, w):
        if w < mm:
            contribute(stage[w], w, block_at(k))
            if k > 1:
                def accumulate():
                    ring_copy(k - 1, w, source).wait_recv()
                    add_into(send[w].at[k - 1], [stage[w], land[w].at[k - 2]])

                def start_chain():
                    add_into(send[w].at[k - 1], [stage[w]])

                cond = carried(k - 1, w)
                if cond is True:
                    accumulate()
                else:
                    pl.when(cond)(accumulate)
                    pl.when(jnp.logical_not(cond))(start_chain)
            else:
                add_into(send[w].at[k - 1], [stage[w]])
        else:
            load(k, w).wait()
            if k > 1:
                def accumulate():
                    ring_copy(k - 1, w, source).wait_recv()
                    add_into(send[w].at[k - 1], [send[w].at[k - 1], land[w].at[k - 2]])
                guarded(carried(k - 1, w), accumulate)
        ring_copy(k, w, target).start()

    def arrive(w):
        ring_copy(steps, w, source).wait_recv()
        pl.when(jnp.logical_not(owner(w)))(lambda: pair_copy(w).start())
        mine = land[w].at[steps - 1]

        def plane():
            if w < mm:
                contribute(own[w], w, here)
            else:
                load_own(w).wait()
            pair_copy(w).wait_recv()

            @pl.when(core == 0)
            def _():
                add_into(own[w], [own[w], mine, other[w]])

            @pl.when(core == 1)
            def _():
                add_into(own[w], [own[w], other[w], mine])

            x_copy(w).start()

        pl.when(owner(w))(plane)

    def total(w):
        x_copy(w).wait_recv()
        add_into(out[w], [own[w], xland[w]])
        back_copy(w).start()

    slots = steps + count - 1
    for t in range(slots + 1):
        for w in range(count):
            k = t - w + 1
            if 1 <= k <= steps:
                guarded(carried(k, w), lambda k=k, w=w: step(k, w))
        for w in range(count):
            if steps + w == t:
                arrive(w)
    for w in range(count):
        pl.when(owner(w))(lambda w=w: total(w))

    for w in range(count):
        def not_owner(w=w):
            if w >= mm:
                load_own(w).wait()
            back_copy(w).wait_recv()
            pair_copy(w).wait_send()

        def was_owner(w=w):
            x_copy(w).wait_send()
            back_copy(w).wait_send()

        pl.when(owner(w))(was_owner)
        pl.when(jnp.logical_not(owner(w)))(not_owner)
    for k in range(1, steps + 1):
        for w in range(count):
            guarded(carried(k, w), lambda k=k, w=w: ring_copy(k, w, target).wait_send())


def reduce_gradients(pairs_t, contribs, n):
    mm = len(pairs_t)
    count = mm + len(contribs)
    steps = n // 2
    blocks = [(xt.shape[1], dy.shape[1]) for xt, dy in pairs_t] + [c.shape[1:] for c in contribs]
    ring_types = [jnp.bfloat16] * mm + [jnp.float32] * len(contribs)
    vmem = lambda shape, dtype=jnp.float32: pltpu.VMEM(shape, dtype)
    dma = pltpu.SemaphoreType.DMA
    return pl.pallas_call(
        functools.partial(reduce_kernel, n, count, mm),
        out_shape=[jax.ShapeDtypeStruct(b, jnp.float32) for b in blocks],
        in_specs=[pl.BlockSpec(memory_space=pltpu.VMEM)] * (2 * mm)
        + [pl.BlockSpec(memory_space=pl.ANY)] * len(contribs),
        out_specs=[pl.BlockSpec(memory_space=pltpu.VMEM)] * count,
        scratch_shapes=[vmem((steps,) + b, t) for b, t in zip(blocks, ring_types)]
        + [vmem((steps,) + b, t) for b, t in zip(blocks, ring_types)]
        + [vmem(b, t) for b, t in zip(blocks, ring_types)]
        + [vmem(b) for b in blocks]
        + [vmem(b) for b in blocks]
        + [vmem(b) for b in blocks]
        + [
            dma((steps, count)),
            dma((count,)),
            dma((steps, count)),
            dma((steps, count)),
            dma((count,)),
            dma((count,)),
            dma((count,)),
            dma((count,)),
            dma((count,)),
            dma((count,)),
        ],
        compiler_params=pltpu.CompilerParams(
            collective_id=1, has_side_effects=True, vmem_limit_bytes=62 * 1024 * 1024
        ),
    )(*[xt for xt, _ in pairs_t], *[dy for _, dy in pairs_t], *contribs)


def swap_core(value):
    rep = lax.axis_size("rep")
    return lax.ppermute(value, "rep", perm=[(i, i ^ 1) for i in range(rep)])


def swap_x(value):
    rep = lax.axis_size("rep")
    return lax.ppermute(value, "rep", perm=[(i, i ^ 2) for i in range(rep)])


def join_halves(mine, theirs, core, axis):
    first = jnp.where(core == 0, mine, theirs)
    second = jnp.where(core == 0, theirs, mine)
    return jnp.concatenate([first, second], axis=axis)


def take_half(value, core, axis):
    half = value.shape[axis] // 2
    return lax.dynamic_slice_in_dim(value, core * half, half, axis=axis)


def per_device(
    tokens,
    segment_ids,
    cotangent,
    ln1_gain,
    ln1_bias,
    qkv_weight,
    qv_bias,
    out_weight,
    out_bias,
    ln2_gain,
    ln2_bias,
    fc_weight,
    fc_bias,
    proj_weight,
    proj_bias,
):
    rep = lax.axis_size("rep")
    assert rep == 4
    core = lax.axis_index("rep") % 2
    row_count = tokens.shape[0]
    positions = jnp.arange(row_count)
    allowed = (segment_ids[:, None] == segment_ids[None, :]) & (
        positions[None, :] <= positions[:, None]
    )
    layer_index = 0
    shard = lax.axis_size("shard")
    small_local = (ln1_gain, ln1_bias, qv_bias, out_bias, ln2_gain, ln2_bias, fc_bias, proj_bias)
    small_local = [v[layer_index] for v in small_local]
    widths = [v.shape[0] for v in small_local]
    local_weights = (
        qkv_weight[layer_index],
        out_weight[layer_index],
        fc_weight[layer_index],
        proj_weight[layer_index],
    )
    rows_local = local_weights[0].shape[0]
    small_row = jnp.concatenate(small_local).reshape(1, -1)
    fulls = gather_weights(list(local_weights) + [small_row], shard)
    weights = tuple(f.reshape(-1, f.shape[-1]) for f in fulls[:4])
    halves = [take_half(w, core, 1) for w in local_weights]
    half_widths = [h.size // rows_local for h in halves]
    packed_all = fulls[4].reshape(shard, -1)
    small = []
    start = 0
    for width in widths:
        small.append(to_float(packed_all[:, start : start + width].reshape(-1)))
        start += width
    small = tuple(small)

    residual = to_float(tokens)
    saved = layer_forward(residual, allowed, small, weights)
    out_tokens = saved["result"].astype(jnp.bfloat16)
    upstream = to_float(cotangent)
    input_grad, small_grads, pairs = layer_backward(upstream, saved, small, weights)

    outgoing = jnp.concatenate([x for x, _ in pairs] + [dy for _, dy in pairs], axis=1)
    incoming = swap_core(outgoing)
    small_mine = jnp.concatenate([g.reshape(shard, -1) for g in small_grads], axis=1)
    small_theirs = swap_core(small_mine)
    small_chip = jnp.where(core == 0, small_mine + small_theirs, small_theirs + small_mine)
    start = 0
    partner_x = []
    for x, _ in pairs:
        partner_x.append(incoming[:, start : start + x.shape[1]])
        start += x.shape[1]
    pairs_t = []
    for (x, dy), px in zip(pairs, partner_x):
        pdy = incoming[:, start : start + dy.shape[1]]
        start += dy.shape[1]
        rows_t = jnp.concatenate([x, px], axis=0).T
        pairs_t.append((rows_t.reshape(shard, -1, rows_t.shape[1]), jnp.concatenate([dy, pdy], axis=0)))
    totals = reduce_gradients(pairs_t, [small_chip.reshape(shard, 1, -1)], shard)
    small_share = totals[4]
    owned = [t[None] for t in totals[:4]]
    small_owned = []
    start = 0
    for g in small_grads:
        width = g.shape[0] // shard
        small_owned.append(small_share[:, start : start + width])
        start += width

    (g_ln1_g, g_ln1_b, g_qv_b, g_out_b, g_ln2_g, g_ln2_b, g_fc_b, g_proj_b) = small_owned
    g_qkv, g_out, g_fc, g_proj = owned
    return (
        out_tokens,
        input_grad,
        g_ln1_g,
        g_ln1_b,
        g_qkv,
        g_qv_b,
        g_out,
        g_out_b,
        g_ln2_g,
        g_ln2_b,
        g_fc,
        g_fc_b,
        g_proj,
        g_proj_b,
    )


def solution(mesh):
    placed = (
        P(("rep", "shard"), None),
        P(("rep", "shard")),
        P(("rep", "shard"), None),
        P(None, "shard"),
        P(None, "shard"),
        P(None, "shard", None),
        P(None, "shard"),
        P(None, "shard", None),
        P(None, "shard"),
        P(None, "shard"),
        P(None, "shard"),
        P(None, "shard", None),
        P(None, "shard"),
        P(None, "shard", None),
        P(None, "shard"),
    )
    return jax.shard_map(
        per_device,
        mesh=mesh,
        in_specs=placed,
        out_specs=(
            P(("rep", "shard"), None),
            P(("rep", "shard"), None),
            P(None, "shard"),
            P(None, "shard"),
            P(None, "shard", None),
            P(None, "shard"),
            P(None, "shard", None),
            P(None, "shard"),
            P(None, "shard"),
            P(None, "shard"),
            P(None, "shard", None),
            P(None, "shard"),
            P(None, "shard", None),
            P(None, "shard"),
        ),
        check_vma=False,
    )
```

```python
import functools

import jax
import jax.numpy as jnp
from jax import lax
from jax.experimental import pallas as pl
from jax.experimental.pallas import tpu as pltpu
from jax.sharding import PartitionSpec as P

MESH = pl.DeviceIdType.MESH

HEADS = 12
HEAD = 64
LAYERS = 1

epsilon = 1e-05

def to_float(value):
    return value.astype(jnp.float32)


def layer_norm(inputs, norm_gain, norm_shift):
    center = inputs - jnp.mean(inputs, axis=-1, keepdims=True)
    inverse_std = lax.rsqrt(jnp.mean(center * center, axis=-1, keepdims=True) + epsilon)
    normed = center * inverse_std
    return (normed * norm_gain + norm_shift, normed, inverse_std)


def norm_back(upstream, normed, inverse_std, norm_gain):
    scaled = upstream * norm_gain
    inner_term = scaled - jnp.mean(scaled, axis=-1, keepdims=True)
    inner_term = inner_term - normed * jnp.mean(scaled * normed, axis=-1, keepdims=True)
    return (inverse_std * inner_term, jnp.sum(upstream * normed, axis=0), jnp.sum(upstream, axis=0))


def layer_forward(inputs, allowed, small, weights):
    ln1_gain, ln1_bias, qv_bias, out_bias, ln2_gain, ln2_bias, fc_bias, proj_bias = small
    qkv_weight, out_weight, fc_weight, proj_weight = weights
    row_count = inputs.shape[0]
    width_all = inputs.shape[1]
    first_norm, normed_one, inverse_one = layer_norm(inputs, ln1_gain, ln1_bias)
    first_low = first_norm.astype(jnp.bfloat16)
    offset = jnp.concatenate(
        [qv_bias[:width_all], jnp.zeros((width_all,), jnp.float32), qv_bias[width_all:]]
    )
    projected = (
        jnp.dot(first_low, qkv_weight, preferred_element_type=jnp.float32) + offset
    ).astype(jnp.bfloat16)
    queries = projected[:, :width_all].reshape(row_count, HEADS, HEAD)
    keys_all = projected[:, width_all : 2 * width_all].reshape(row_count, HEADS, HEAD)
    values_all = projected[:, 2 * width_all :].reshape(row_count, HEADS, HEAD)
    scores = jnp.einsum(
        "qhd,khd->hqk", queries, keys_all, preferred_element_type=jnp.float32
    ) * HEAD ** (-0.5)
    scores = jnp.where(allowed[None], scores, -1e30)
    row_max = jnp.max(scores, axis=-1, keepdims=True)
    log_total = row_max + jnp.log(jnp.sum(jnp.exp(scores - row_max), axis=-1, keepdims=True))
    attn_probs = jnp.exp(scores - log_total)
    probs_low = attn_probs.astype(jnp.bfloat16)
    attn_mixed = jnp.einsum(
        "hqk,khd->qhd", probs_low, values_all, preferred_element_type=jnp.float32
    )
    attn_mixed = attn_mixed.reshape(row_count, width_all).astype(jnp.bfloat16)
    after_attn = (
        inputs + jnp.dot(attn_mixed, out_weight, preferred_element_type=jnp.float32) + out_bias
    )
    second_norm, normed_two, inverse_two = layer_norm(after_attn, ln2_gain, ln2_bias)
    second_low = second_norm.astype(jnp.bfloat16)
    hidden_pre = jnp.dot(second_low, fc_weight, preferred_element_type=jnp.float32) + fc_bias
    hidden_low = jax.nn.gelu(hidden_pre, approximate=True).astype(jnp.bfloat16)
    result = (
        after_attn + jnp.dot(hidden_low, proj_weight, preferred_element_type=jnp.float32) + proj_bias
    )
    return dict(
        normed_one=normed_one,
        inverse_one=inverse_one,
        first_low=first_low,
        queries=queries,
        keys_all=keys_all,
        values_all=values_all,
        attn_probs=attn_probs,
        probs_low=probs_low,
        attn_mixed=attn_mixed,
        normed_two=normed_two,
        inverse_two=inverse_two,
        second_low=second_low,
        hidden_pre=hidden_pre,
        hidden_low=hidden_low,
        result=result,
    )


def layer_backward(upstream, saved, small, weights):
    ln1_gain, ln1_bias, qv_bias, out_bias, ln2_gain, ln2_bias, fc_bias, proj_bias = small
    qkv_weight, out_weight, fc_weight, proj_weight = weights
    row_count = upstream.shape[0]
    width_all = upstream.shape[1]
    proj_in = upstream.astype(jnp.bfloat16)
    grad_proj_b = jnp.sum(to_float(proj_in), axis=0)
    hidden_grad = jnp.einsum("td,fd->tf", proj_in, proj_weight, preferred_element_type=jnp.float32)
    _, gelu_pull = jax.vjp(lambda value: jax.nn.gelu(value, approximate=True), saved["hidden_pre"])
    pre_grad = gelu_pull(hidden_grad)[0].astype(jnp.bfloat16)
    grad_fc_b = jnp.sum(to_float(pre_grad), axis=0)
    second_grad = jnp.einsum("tf,df->td", pre_grad, fc_weight, preferred_element_type=jnp.float32)
    norm_part, grad_ln2_g, grad_ln2_b = norm_back(
        second_grad, saved["normed_two"], saved["inverse_two"], ln2_gain
    )
    residual_grad = upstream + norm_part
    branch_in = residual_grad.astype(jnp.bfloat16)
    grad_out_b = jnp.sum(to_float(branch_in), axis=0)
    mixed_grad = jnp.einsum("td,cd->tc", branch_in, out_weight, preferred_element_type=jnp.float32)
    mixed_grad = mixed_grad.astype(jnp.bfloat16).reshape(row_count, HEADS, HEAD)
    prob_grad = jnp.einsum(
        "qhd,khd->hqk", mixed_grad, saved["values_all"], preferred_element_type=jnp.float32
    )
    value_grad = jnp.einsum(
        "hqk,qhd->khd", saved["probs_low"], mixed_grad, preferred_element_type=jnp.float32
    )
    attn_probs = saved["attn_probs"]
    row_delta = jnp.sum(attn_probs * prob_grad, axis=-1, keepdims=True)
    score_grad = (attn_probs * (prob_grad - row_delta)).astype(jnp.bfloat16)
    query_grad = jnp.einsum(
        "hqk,khd->qhd", score_grad, saved["keys_all"], preferred_element_type=jnp.float32
    ) * HEAD ** (-0.5)
    key_grad = jnp.einsum(
        "hqk,qhd->khd", score_grad, saved["queries"], preferred_element_type=jnp.float32
    ) * HEAD ** (-0.5)
    joined_grad = jnp.concatenate(
        [
            query_grad.reshape(row_count, width_all),
            key_grad.reshape(row_count, width_all),
            value_grad.reshape(row_count, width_all),
        ],
        axis=1,
    ).astype(jnp.bfloat16)
    column_sums = jnp.sum(to_float(joined_grad), axis=0)
    grad_qv_b = jnp.concatenate([column_sums[:width_all], column_sums[2 * width_all :]])
    first_grad = jnp.einsum(
        "te,ce->tc", joined_grad, qkv_weight, preferred_element_type=jnp.float32
    )
    norm_first, grad_ln1_g, grad_ln1_b = norm_back(
        first_grad, saved["normed_one"], saved["inverse_one"], ln1_gain
    )
    small_grads = (
        grad_ln1_g,
        grad_ln1_b,
        grad_qv_b,
        grad_out_b,
        grad_ln2_g,
        grad_ln2_b,
        grad_fc_b,
        grad_proj_b,
    )
    pairs = (
        (saved["first_low"], joined_grad),
        (saved["attn_mixed"], branch_in),
        (saved["second_low"], pre_grad),
        (saved["hidden_low"], proj_in),
    )
    return (residual_grad + norm_first, small_grads, pairs)


def ring_position(shard_index, n):
    if n != 8:
        return shard_index
    y = shard_index % 2
    z = shard_index // 2
    return z * (1 - 2 * y) + 7 * y


def ring_shard(position, n):
    position = position % n
    if n != 8:
        return position
    y = position // 4
    z = (position % 4) * (1 - 2 * y) + 3 * y
    return z * 2 + y


FIRST_CORE_HALF = (0, 3)


CHAIN_RANK = (2, 3, 0, 1, 4)
CHAIN_LAG = 2


X_ONLY = (2, 3)


def gather_kernel(n, count, *refs):
    local = refs[:count]
    full = refs[count : 2 * count]
    ring_send, ring_recv, pair_send, pair_recv, x_send, x_recv, relay_send, relay_recv = refs[2 * count :]
    rep = lax.axis_index("rep")
    shard = lax.axis_index("shard")
    core = rep % 2
    plane = rep // 2
    step_dir = 1 - 2 * core
    partner = (rep + step_dir, shard)
    x_partner = ((rep + 2) % 4, shard)
    here = ring_position(shard, n)
    target = (rep, ring_shard(here + step_dir, n))
    source = (rep, ring_shard(here - step_dir, n))
    steps = n // 2
    split_last = n % 2 == 0

    barrier = pltpu.get_barrier_semaphore()
    for peer in (target, source, partner, x_partner):
        pl.semaphore_signal(barrier, inc=1, device_id=peer, device_id_type=MESH)
    pl.semaphore_wait(barrier, 4)

    def both(a, b):
        if a is True:
            return b
        if b is True:
            return a
        return jnp.logical_and(a, b)

    def core_carries(k, w, which_core):
        if split_last and k == steps:
            return (which_core == 0) == (w in FIRST_CORE_HALF)
        return True

    def plane_carries(w, which_plane):
        if w == X_ONLY[0]:
            return which_plane == 0
        if w == X_ONLY[1]:
            return which_plane == 1
        return True

    def ring_in(k, w):
        return both(plane_carries(w, plane), core_carries(k, w, core))

    def x_out(k, w):
        if w not in X_ONLY:
            return False
        return both(plane_carries(w, plane), core_carries(k, w, core))

    def x_in(k, w):
        if w not in X_ONLY:
            return False
        return both(plane_carries(w, 1 - plane), core_carries(k, w, core))

    def partner_ring_in(k, w):
        return both(plane_carries(w, plane), core_carries(k, w, 1 - core))

    def partner_x_in(k, w):
        if w not in X_ONLY:
            return False
        return both(plane_carries(w, 1 - plane), core_carries(k, w, 1 - core))

    def guarded(cond, fn):
        if cond is False:
            return
        if cond is True:
            fn()
        else:
            pl.when(cond)(fn)

    def slot(position):
        return ring_shard(position, n)

    def remote(src, dst, ssem, rsem, device):
        return pltpu.make_async_remote_copy(
            src_ref=src, dst_ref=dst, send_sem=ssem, recv_sem=rsem, device_id=device, device_id_type=MESH
        )

    def ring_copy(k, w):
        src_pos = here - step_dir * (k - 1)
        src = local[w] if k == 1 else full[w].at[slot(src_pos)]
        return remote(src, full[w].at[slot(src_pos)], ring_send.at[k - 1, w], ring_recv.at[k - 1, w], target)

    def incoming_ring(k, w):
        pos = slot(here - step_dir * k)
        return remote(full[w].at[pos], full[w].at[pos], ring_send.at[k - 1, w], ring_recv.at[k - 1, w], source)

    def pair_copy(k, w, pos):
        src = local[w] if k == 0 else full[w].at[slot(pos)]
        return remote(src, full[w].at[slot(pos)], pair_send.at[k, w], pair_recv.at[k, w], partner)

    def x_copy(k, w):
        pos = slot(here - step_dir * k)
        return remote(full[w].at[pos], full[w].at[pos], x_send.at[k - 1, w], x_recv.at[k - 1, w], x_partner)

    def relay_copy(k, w, pos):
        pos = slot(pos)
        return remote(full[w].at[pos], full[w].at[pos], relay_send.at[k - 1, w], relay_recv.at[k - 1, w], partner)

    for w in range(count):
        pair_copy(0, w, here).start()
    for w in range(count):
        guarded(ring_in(1, w), lambda w=w: ring_copy(1, w).start())
    for k in range(1, steps + 1):
        for w in range(count):
            def arrived(k=k, w=w):
                incoming_ring(k, w).wait_recv()
                if k < steps:
                    guarded(ring_in(k + 1, w), lambda: ring_copy(k + 1, w).start())
                guarded(x_out(k, w), lambda: x_copy(k, w).start())
                pair_copy(k, w, here - step_dir * k).start()
            guarded(ring_in(k, w), arrived)
        for w in range(count):
            def crossed(k=k, w=w):
                x_copy(k, w).wait_recv()
                relay_copy(k, w, here - step_dir * k).start()
            guarded(x_in(k, w), crossed)
    for w in range(count):
        pair_copy(0, w, here).wait_recv()
    for k in range(1, steps + 1):
        for w in range(count):
            guarded(partner_ring_in(k, w), lambda k=k, w=w: pair_copy(k, w, here + step_dir * k).wait_recv())
            guarded(partner_x_in(k, w), lambda k=k, w=w: relay_copy(k, w, here + step_dir * k).wait_recv())
    for w in range(count):
        pair_copy(0, w, here).wait_send()
    for k in range(1, steps + 1):
        for w in range(count):
            def sent(k=k, w=w):
                ring_copy(k, w).wait_send()
                pair_copy(k, w, here - step_dir * k).wait_send()
            guarded(ring_in(k, w), sent)
            guarded(x_out(k, w), lambda k=k, w=w: x_copy(k, w).wait_send())
            guarded(x_in(k, w), lambda k=k, w=w: relay_copy(k, w, here - step_dir * k).wait_send())


def gather_weights(locals_, n):
    count = len(locals_)
    steps = n // 2
    dma = pltpu.SemaphoreType.DMA
    return pl.pallas_call(
        functools.partial(gather_kernel, n, count),
        out_shape=[jax.ShapeDtypeStruct((n,) + a.shape, a.dtype) for a in locals_],
        in_specs=[pl.BlockSpec(memory_space=pl.ANY)] * count,
        out_specs=[pl.BlockSpec(memory_space=pl.ANY)] * count,
        scratch_shapes=[
            dma((steps, count)),
            dma((steps, count)),
            dma((steps + 1, count)),
            dma((steps + 1, count)),
            dma((steps, count)),
            dma((steps, count)),
            dma((steps, count)),
            dma((steps, count)),
        ],
        compiler_params=pltpu.CompilerParams(collective_id=0, has_side_effects=True),
    )(*locals_)


def add_rows(dst, parts, rows, chunk):
    def body(i, carry):
        window = pl.ds(pl.multiple_of(i * chunk, chunk), chunk)
        total = parts[0][window, :].astype(jnp.float32)
        for part in parts[1:]:
            total = total + part[window, :].astype(jnp.float32)
        dst[window, :] = total.astype(dst.dtype)
        return carry

    lax.fori_loop(0, rows // chunk, body, 0)


def reduce_kernel(n, count, mm, *refs):
    xt = refs[:mm]
    dy = refs[mm : 2 * mm]
    contrib = (None,) * mm + refs[2 * mm : mm + count]
    refs = refs[mm + count :]
    out = refs[:count]
    land, send, other, own, xland, stage = (refs[count + i * count : count + (i + 1) * count] for i in range(6))
    (load_sem, own_sem, ring_send, ring_recv, pair_send, pair_recv, x_send, x_recv, back_send, back_recv) = refs[
        7 * count :
    ]
    rep = lax.axis_index("rep")
    shard = lax.axis_index("shard")
    core = rep % 2
    step_dir = 1 - 2 * core
    partner = (rep + step_dir, shard)
    x_partner = ((rep + 2) % 4, shard)
    here = ring_position(shard, n)
    target = (rep, ring_shard(here + step_dir, n))
    source = (rep, ring_shard(here - step_dir, n))
    steps = n // 2
    split_first = n % 2 == 0

    def carried(k, w):
        if split_first and k == 1:
            return (core == 0) == (w in FIRST_CORE_HALF)
        return True

    def guarded(cond, fn):
        if cond is True:
            fn()
        else:
            pl.when(cond)(fn)

    def block_at(k):
        return here + step_dir * (steps - k + 1)

    def load(k, w):
        return pltpu.make_async_copy(contrib[w].at[ring_shard(block_at(k), n)], send[w].at[k - 1], load_sem.at[k - 1, w])

    def load_own(w):
        return pltpu.make_async_copy(contrib[w].at[shard], own[w], own_sem.at[w])

    def remote(src, dst, ssem, rsem, device):
        return pltpu.make_async_remote_copy(
            src_ref=src, dst_ref=dst, send_sem=ssem, recv_sem=rsem, device_id=device, device_id_type=MESH
        )

    def ring_copy(k, w, device):
        return remote(send[w].at[k - 1], land[w].at[k - 1], ring_send.at[k - 1, w], ring_recv.at[k - 1, w], device)

    def pair_copy(w):
        return remote(land[w].at[steps - 1], other[w], pair_send.at[w], pair_recv.at[w], partner)

    def x_copy(w):
        return remote(own[w], xland[w], x_send.at[w], x_recv.at[w], x_partner)

    def back_copy(w):
        return remote(out[w], out[w], back_send.at[w], back_recv.at[w], partner)

    def owner(w):
        return core == w % 2

    def contribute(dst, w, position):
        block = ring_shard(position, n)
        width = 256

        def body(i, carry):
            window = pl.ds(pl.multiple_of(i * width, width), width)
            dst[:, window] = jnp.dot(xt[w][block], dy[w][:, window], preferred_element_type=jnp.float32)
            return carry

        lax.fori_loop(0, dy[w].shape[1] // width, body, 0)

    for w in range(mm, count):
        load_own(w).start()
    for k in range(1, steps + 1):
        for w in range(mm, count):
            guarded(carried(k, w), lambda k=k, w=w: load(k, w).start())

    barrier = pltpu.get_barrier_semaphore()
    for peer in (target, source, partner, x_partner):
        pl.semaphore_signal(barrier, inc=1, device_id=peer, device_id_type=MESH)
    pl.semaphore_wait(barrier, 4)

    def add_into(dst, parts):
        rows = dst.shape[0]
        chunk = 16 if rows % 16 == 0 else rows
        add_rows(dst, parts, rows, chunk)

    def step(k, w):
        if w < mm:
            contribute(stage[w], w, block_at(k))
            if k > 1:
                def accumulate():
                    ring_copy(k - 1, w, source).wait_recv()
                    add_into(send[w].at[k - 1], [stage[w], land[w].at[k - 2]])

                def start_chain():
                    add_into(send[w].at[k - 1], [stage[w]])

                cond = carried(k - 1, w)
                if cond is True:
                    accumulate()
                else:
                    pl.when(cond)(accumulate)
                    pl.when(jnp.logical_not(cond))(start_chain)
            else:
                add_into(send[w].at[k - 1], [stage[w]])
        else:
            load(k, w).wait()
            if k > 1:
                def accumulate():
                    ring_copy(k - 1, w, source).wait_recv()
                    add_into(send[w].at[k - 1], [send[w].at[k - 1], land[w].at[k - 2]])
                guarded(carried(k - 1, w), accumulate)
        ring_copy(k, w, target).start()

    def arrive(w):
        ring_copy(steps, w, source).wait_recv()
        pl.when(jnp.logical_not(owner(w)))(lambda: pair_copy(w).start())
        mine = land[w].at[steps - 1]

        def plane():
            if w < mm:
                contribute(own[w], w, here)
            else:
                load_own(w).wait()
            pair_copy(w).wait_recv()

            @pl.when(core == 0)
            def _():
                add_into(own[w], [own[w], mine, other[w]])

            @pl.when(core == 1)
            def _():
                add_into(own[w], [own[w], other[w], mine])

            x_copy(w).start()

        pl.when(owner(w))(plane)

    def total(w):
        x_copy(w).wait_recv()
        add_into(out[w], [own[w], xland[w]])
        back_copy(w).start()

    rank = [CHAIN_RANK[w] if w < len(CHAIN_RANK) else w for w in range(count)]
    slots = steps + CHAIN_LAG * (count - 1)
    by_rank = sorted(range(count), key=lambda w: rank[w])
    for t in range(slots + 1):
        for w in by_rank:
            k = t - CHAIN_LAG * rank[w] + 1
            if 1 <= k <= steps:
                guarded(carried(k, w), lambda k=k, w=w: step(k, w))
        for w in by_rank:
            if steps + CHAIN_LAG * rank[w] == t:
                arrive(w)
    for w in range(count):
        pl.when(owner(w))(lambda w=w: total(w))

    for w in range(count):
        def not_owner(w=w):
            if w >= mm:
                load_own(w).wait()
            back_copy(w).wait_recv()
            pair_copy(w).wait_send()

        def was_owner(w=w):
            x_copy(w).wait_send()
            back_copy(w).wait_send()

        pl.when(owner(w))(was_owner)
        pl.when(jnp.logical_not(owner(w)))(not_owner)
    for k in range(1, steps + 1):
        for w in range(count):
            guarded(carried(k, w), lambda k=k, w=w: ring_copy(k, w, target).wait_send())


def reduce_gradients(pairs_t, contribs, n):
    mm = len(pairs_t)
    count = mm + len(contribs)
    steps = n // 2
    blocks = [(xt.shape[1], dy.shape[1]) for xt, dy in pairs_t] + [c.shape[1:] for c in contribs]
    ring_types = [jnp.bfloat16] * mm + [jnp.float32] * len(contribs)
    vmem = lambda shape, dtype=jnp.float32: pltpu.VMEM(shape, dtype)
    dma = pltpu.SemaphoreType.DMA
    return pl.pallas_call(
        functools.partial(reduce_kernel, n, count, mm),
        out_shape=[jax.ShapeDtypeStruct(b, jnp.float32) for b in blocks],
        in_specs=[pl.BlockSpec(memory_space=pltpu.VMEM)] * (2 * mm)
        + [pl.BlockSpec(memory_space=pl.ANY)] * len(contribs),
        out_specs=[pl.BlockSpec(memory_space=pltpu.VMEM)] * count,
        scratch_shapes=[vmem((steps,) + b, t) for b, t in zip(blocks, ring_types)]
        + [vmem((steps,) + b, t) for b, t in zip(blocks, ring_types)]
        + [vmem(b, t) for b, t in zip(blocks, ring_types)]
        + [vmem(b) for b in blocks]
        + [vmem(b) for b in blocks]
        + [vmem(b) for b in blocks]
        + [
            dma((steps, count)),
            dma((count,)),
            dma((steps, count)),
            dma((steps, count)),
            dma((count,)),
            dma((count,)),
            dma((count,)),
            dma((count,)),
            dma((count,)),
            dma((count,)),
        ],
        compiler_params=pltpu.CompilerParams(
            collective_id=1, has_side_effects=True, vmem_limit_bytes=62 * 1024 * 1024
        ),
    )(*[xt for xt, _ in pairs_t], *[dy for _, dy in pairs_t], *contribs)


def swap_core(value):
    rep = lax.axis_size("rep")
    return lax.ppermute(value, "rep", perm=[(i, i ^ 1) for i in range(rep)])


def swap_x(value):
    rep = lax.axis_size("rep")
    return lax.ppermute(value, "rep", perm=[(i, i ^ 2) for i in range(rep)])


def join_halves(mine, theirs, core, axis):
    first = jnp.where(core == 0, mine, theirs)
    second = jnp.where(core == 0, theirs, mine)
    return jnp.concatenate([first, second], axis=axis)


def take_half(value, core, axis):
    half = value.shape[axis] // 2
    return lax.dynamic_slice_in_dim(value, core * half, half, axis=axis)


def per_device(
    tokens,
    segment_ids,
    cotangent,
    ln1_gain,
    ln1_bias,
    qkv_weight,
    qv_bias,
    out_weight,
    out_bias,
    ln2_gain,
    ln2_bias,
    fc_weight,
    fc_bias,
    proj_weight,
    proj_bias,
):
    rep = lax.axis_size("rep")
    assert rep == 4
    core = lax.axis_index("rep") % 2
    row_count = tokens.shape[0]
    positions = jnp.arange(row_count)
    allowed = (segment_ids[:, None] == segment_ids[None, :]) & (
        positions[None, :] <= positions[:, None]
    )
    layer_index = 0
    shard = lax.axis_size("shard")
    small_local = (ln1_gain, ln1_bias, qv_bias, out_bias, ln2_gain, ln2_bias, fc_bias, proj_bias)
    small_local = [v[layer_index] for v in small_local]
    widths = [v.shape[0] for v in small_local]
    local_weights = (
        qkv_weight[layer_index],
        out_weight[layer_index],
        fc_weight[layer_index],
        proj_weight[layer_index],
    )
    rows_local = local_weights[0].shape[0]
    small_row = jnp.concatenate(small_local).reshape(1, -1)
    fulls = gather_weights(list(local_weights) + [small_row], shard)
    weights = tuple(f.reshape(-1, f.shape[-1]) for f in fulls[:4])
    halves = [take_half(w, core, 1) for w in local_weights]
    half_widths = [h.size // rows_local for h in halves]
    packed_all = fulls[4].reshape(shard, -1)
    small = []
    start = 0
    for width in widths:
        small.append(to_float(packed_all[:, start : start + width].reshape(-1)))
        start += width
    small = tuple(small)

    residual = to_float(tokens)
    saved = layer_forward(residual, allowed, small, weights)
    out_tokens = saved["result"].astype(jnp.bfloat16)
    upstream = to_float(cotangent)
    input_grad, small_grads, pairs = layer_backward(upstream, saved, small, weights)

    outgoing = jnp.concatenate([x for x, _ in pairs] + [dy for _, dy in pairs], axis=1)
    incoming = swap_core(outgoing)
    small_mine = jnp.concatenate([g.reshape(shard, -1) for g in small_grads], axis=1)
    small_theirs = swap_core(small_mine)
    small_chip = jnp.where(core == 0, small_mine + small_theirs, small_theirs + small_mine)
    start = 0
    partner_x = []
    for x, _ in pairs:
        partner_x.append(incoming[:, start : start + x.shape[1]])
        start += x.shape[1]
    pairs_t = []
    for (x, dy), px in zip(pairs, partner_x):
        pdy = incoming[:, start : start + dy.shape[1]]
        start += dy.shape[1]
        rows_t = jnp.concatenate([x, px], axis=0).T
        pairs_t.append((rows_t.reshape(shard, -1, rows_t.shape[1]), jnp.concatenate([dy, pdy], axis=0)))
    totals = reduce_gradients(pairs_t, [small_chip.reshape(shard, 1, -1)], shard)
    small_share = totals[4]
    owned = [t[None] for t in totals[:4]]
    small_owned = []
    start = 0
    for g in small_grads:
        width = g.shape[0] // shard
        small_owned.append(small_share[:, start : start + width])
        start += width

    (g_ln1_g, g_ln1_b, g_qv_b, g_out_b, g_ln2_g, g_ln2_b, g_fc_b, g_proj_b) = small_owned
    g_qkv, g_out, g_fc, g_proj = owned
    return (
        out_tokens,
        input_grad,
        g_ln1_g,
        g_ln1_b,
        g_qkv,
        g_qv_b,
        g_out,
        g_out_b,
        g_ln2_g,
        g_ln2_b,
        g_fc,
        g_fc_b,
        g_proj,
        g_proj_b,
    )


def solution(mesh):
    placed = (
        P(("rep", "shard"), None),
        P(("rep", "shard")),
        P(("rep", "shard"), None),
        P(None, "shard"),
        P(None, "shard"),
        P(None, "shard", None),
        P(None, "shard"),
        P(None, "shard", None),
        P(None, "shard"),
        P(None, "shard"),
        P(None, "shard"),
        P(None, "shard", None),
        P(None, "shard"),
        P(None, "shard", None),
        P(None, "shard"),
    )
    return jax.shard_map(
        per_device,
        mesh=mesh,
        in_specs=placed,
        out_specs=(
            P(("rep", "shard"), None),
            P(("rep", "shard"), None),
            P(None, "shard"),
            P(None, "shard"),
            P(None, "shard", None),
            P(None, "shard"),
            P(None, "shard", None),
            P(None, "shard"),
            P(None, "shard"),
            P(None, "shard"),
            P(None, "shard", None),
            P(None, "shard"),
            P(None, "shard", None),
            P(None, "shard"),
        ),
        check_vma=False,
    )
```

```python
import functools

import jax
import jax.numpy as jnp
from jax import lax
from jax.experimental import pallas as pl
from jax.experimental.pallas import tpu as pltpu
from jax.sharding import PartitionSpec as P

MESH = pl.DeviceIdType.MESH

HEADS = 12
HEAD = 64
LAYERS = 1

epsilon = 1e-05

def to_float(value):
    return value.astype(jnp.float32)


def layer_norm(inputs, norm_gain, norm_shift):
    center = inputs - jnp.mean(inputs, axis=-1, keepdims=True)
    inverse_std = lax.rsqrt(jnp.mean(center * center, axis=-1, keepdims=True) + epsilon)
    normed = center * inverse_std
    return (normed * norm_gain + norm_shift, normed, inverse_std)


def norm_back(upstream, normed, inverse_std, norm_gain):
    scaled = upstream * norm_gain
    inner_term = scaled - jnp.mean(scaled, axis=-1, keepdims=True)
    inner_term = inner_term - normed * jnp.mean(scaled * normed, axis=-1, keepdims=True)
    return (inverse_std * inner_term, jnp.sum(upstream * normed, axis=0), jnp.sum(upstream, axis=0))


def layer_forward(inputs, allowed, small, weights):
    ln1_gain, ln1_bias, qv_bias, out_bias, ln2_gain, ln2_bias, fc_bias, proj_bias = small
    qkv_weight, out_weight, fc_weight, proj_weight = weights
    row_count = inputs.shape[0]
    width_all = inputs.shape[1]
    first_norm, normed_one, inverse_one = layer_norm(inputs, ln1_gain, ln1_bias)
    first_low = first_norm.astype(jnp.bfloat16)
    offset = jnp.concatenate(
        [qv_bias[:width_all], jnp.zeros((width_all,), jnp.float32), qv_bias[width_all:]]
    )
    projected = (
        jnp.dot(first_low, qkv_weight, preferred_element_type=jnp.float32) + offset
    ).astype(jnp.bfloat16)
    queries = projected[:, :width_all].reshape(row_count, HEADS, HEAD)
    keys_all = projected[:, width_all : 2 * width_all].reshape(row_count, HEADS, HEAD)
    values_all = projected[:, 2 * width_all :].reshape(row_count, HEADS, HEAD)
    scores = jnp.einsum(
        "qhd,khd->hqk", queries, keys_all, preferred_element_type=jnp.float32
    ) * HEAD ** (-0.5)
    scores = jnp.where(allowed[None], scores, -1e30)
    row_max = jnp.max(scores, axis=-1, keepdims=True)
    log_total = row_max + jnp.log(jnp.sum(jnp.exp(scores - row_max), axis=-1, keepdims=True))
    attn_probs = jnp.exp(scores - log_total)
    probs_low = attn_probs.astype(jnp.bfloat16)
    attn_mixed = jnp.einsum(
        "hqk,khd->qhd", probs_low, values_all, preferred_element_type=jnp.float32
    )
    attn_mixed = attn_mixed.reshape(row_count, width_all).astype(jnp.bfloat16)
    after_attn = (
        inputs + jnp.dot(attn_mixed, out_weight, preferred_element_type=jnp.float32) + out_bias
    )
    second_norm, normed_two, inverse_two = layer_norm(after_attn, ln2_gain, ln2_bias)
    second_low = second_norm.astype(jnp.bfloat16)
    hidden_pre = jnp.dot(second_low, fc_weight, preferred_element_type=jnp.float32) + fc_bias
    hidden_low = jax.nn.gelu(hidden_pre, approximate=True).astype(jnp.bfloat16)
    result = (
        after_attn + jnp.dot(hidden_low, proj_weight, preferred_element_type=jnp.float32) + proj_bias
    )
    return dict(
        normed_one=normed_one,
        inverse_one=inverse_one,
        first_low=first_low,
        queries=queries,
        keys_all=keys_all,
        values_all=values_all,
        attn_probs=attn_probs,
        probs_low=probs_low,
        attn_mixed=attn_mixed,
        normed_two=normed_two,
        inverse_two=inverse_two,
        second_low=second_low,
        hidden_pre=hidden_pre,
        hidden_low=hidden_low,
        result=result,
    )


def layer_backward(upstream, saved, small, weights):
    ln1_gain, ln1_bias, qv_bias, out_bias, ln2_gain, ln2_bias, fc_bias, proj_bias = small
    qkv_weight, out_weight, fc_weight, proj_weight = weights
    row_count = upstream.shape[0]
    width_all = upstream.shape[1]
    proj_in = upstream.astype(jnp.bfloat16)
    grad_proj_b = jnp.sum(to_float(proj_in), axis=0)
    hidden_grad = jnp.einsum("td,fd->tf", proj_in, proj_weight, preferred_element_type=jnp.float32)
    _, gelu_pull = jax.vjp(lambda value: jax.nn.gelu(value, approximate=True), saved["hidden_pre"])
    pre_grad = gelu_pull(hidden_grad)[0].astype(jnp.bfloat16)
    grad_fc_b = jnp.sum(to_float(pre_grad), axis=0)
    second_grad = jnp.einsum("tf,df->td", pre_grad, fc_weight, preferred_element_type=jnp.float32)
    norm_part, grad_ln2_g, grad_ln2_b = norm_back(
        second_grad, saved["normed_two"], saved["inverse_two"], ln2_gain
    )
    residual_grad = upstream + norm_part
    branch_in = residual_grad.astype(jnp.bfloat16)
    grad_out_b = jnp.sum(to_float(branch_in), axis=0)
    mixed_grad = jnp.einsum("td,cd->tc", branch_in, out_weight, preferred_element_type=jnp.float32)
    mixed_grad = mixed_grad.astype(jnp.bfloat16).reshape(row_count, HEADS, HEAD)
    prob_grad = jnp.einsum(
        "qhd,khd->hqk", mixed_grad, saved["values_all"], preferred_element_type=jnp.float32
    )
    value_grad = jnp.einsum(
        "hqk,qhd->khd", saved["probs_low"], mixed_grad, preferred_element_type=jnp.float32
    )
    attn_probs = saved["attn_probs"]
    row_delta = jnp.sum(attn_probs * prob_grad, axis=-1, keepdims=True)
    score_grad = (attn_probs * (prob_grad - row_delta)).astype(jnp.bfloat16)
    query_grad = jnp.einsum(
        "hqk,khd->qhd", score_grad, saved["keys_all"], preferred_element_type=jnp.float32
    ) * HEAD ** (-0.5)
    key_grad = jnp.einsum(
        "hqk,qhd->khd", score_grad, saved["queries"], preferred_element_type=jnp.float32
    ) * HEAD ** (-0.5)
    joined_grad = jnp.concatenate(
        [
            query_grad.reshape(row_count, width_all),
            key_grad.reshape(row_count, width_all),
            value_grad.reshape(row_count, width_all),
        ],
        axis=1,
    ).astype(jnp.bfloat16)
    column_sums = jnp.sum(to_float(joined_grad), axis=0)
    grad_qv_b = jnp.concatenate([column_sums[:width_all], column_sums[2 * width_all :]])
    first_grad = jnp.einsum(
        "te,ce->tc", joined_grad, qkv_weight, preferred_element_type=jnp.float32
    )
    norm_first, grad_ln1_g, grad_ln1_b = norm_back(
        first_grad, saved["normed_one"], saved["inverse_one"], ln1_gain
    )
    small_grads = (
        grad_ln1_g,
        grad_ln1_b,
        grad_qv_b,
        grad_out_b,
        grad_ln2_g,
        grad_ln2_b,
        grad_fc_b,
        grad_proj_b,
    )
    pairs = (
        (saved["first_low"], joined_grad),
        (saved["attn_mixed"], branch_in),
        (saved["second_low"], pre_grad),
        (saved["hidden_low"], proj_in),
    )
    return (residual_grad + norm_first, small_grads, pairs)


def ring_position(shard_index, n):
    if n != 8:
        return shard_index
    y = shard_index % 2
    z = shard_index // 2
    return z * (1 - 2 * y) + 7 * y


def ring_shard(position, n):
    position = position % n
    if n != 8:
        return position
    y = position // 4
    z = (position % 4) * (1 - 2 * y) + 3 * y
    return z * 2 + y


FIRST_CORE_HALF = (0, 3)


CHAIN_RANK = (2, 3, 0, 1, 4)
CHAIN_LAG = 2


X_ONLY = (2, 3)


def gather_kernel(n, count, *refs):
    local = refs[:count]
    full = refs[count : 2 * count]
    ring_send, ring_recv, pair_send, pair_recv, x_send, x_recv, relay_send, relay_recv = refs[2 * count :]
    rep = lax.axis_index("rep")
    shard = lax.axis_index("shard")
    core = rep % 2
    plane = rep // 2
    step_dir = 1 - 2 * core
    partner = (rep + step_dir, shard)
    x_partner = ((rep + 2) % 4, shard)
    here = ring_position(shard, n)
    target = (rep, ring_shard(here + step_dir, n))
    source = (rep, ring_shard(here - step_dir, n))
    steps = n // 2
    split_last = n % 2 == 0

    barrier = pltpu.get_barrier_semaphore()
    for peer in (target, source, partner, x_partner):
        pl.semaphore_signal(barrier, inc=1, device_id=peer, device_id_type=MESH)
    pl.semaphore_wait(barrier, 4)

    def both(a, b):
        if a is True:
            return b
        if b is True:
            return a
        return jnp.logical_and(a, b)

    def core_carries(k, w, which_core):
        if split_last and k == steps:
            return (which_core == 0) == (w in FIRST_CORE_HALF)
        return True

    def plane_carries(w, which_plane):
        if w == X_ONLY[0]:
            return which_plane == 0
        if w == X_ONLY[1]:
            return which_plane == 1
        return True

    def ring_in(k, w):
        return both(plane_carries(w, plane), core_carries(k, w, core))

    def x_out(k, w):
        if w not in X_ONLY:
            return False
        return both(plane_carries(w, plane), core_carries(k, w, core))

    def x_in(k, w):
        if w not in X_ONLY:
            return False
        return both(plane_carries(w, 1 - plane), core_carries(k, w, core))

    def partner_ring_in(k, w):
        return both(plane_carries(w, plane), core_carries(k, w, 1 - core))

    def partner_x_in(k, w):
        if w not in X_ONLY:
            return False
        return both(plane_carries(w, 1 - plane), core_carries(k, w, 1 - core))

    def guarded(cond, fn):
        if cond is False:
            return
        if cond is True:
            fn()
        else:
            pl.when(cond)(fn)

    def slot(position):
        return ring_shard(position, n)

    def remote(src, dst, ssem, rsem, device):
        return pltpu.make_async_remote_copy(
            src_ref=src, dst_ref=dst, send_sem=ssem, recv_sem=rsem, device_id=device, device_id_type=MESH
        )

    def ring_copy(k, w):
        src_pos = here - step_dir * (k - 1)
        src = local[w] if k == 1 else full[w].at[slot(src_pos)]
        return remote(src, full[w].at[slot(src_pos)], ring_send.at[k - 1, w], ring_recv.at[k - 1, w], target)

    def incoming_ring(k, w):
        pos = slot(here - step_dir * k)
        return remote(full[w].at[pos], full[w].at[pos], ring_send.at[k - 1, w], ring_recv.at[k - 1, w], source)

    def pair_copy(k, w, pos):
        src = local[w] if k == 0 else full[w].at[slot(pos)]
        return remote(src, full[w].at[slot(pos)], pair_send.at[k, w], pair_recv.at[k, w], partner)

    def x_copy(k, w):
        pos = slot(here - step_dir * k)
        return remote(full[w].at[pos], full[w].at[pos], x_send.at[k - 1, w], x_recv.at[k - 1, w], x_partner)

    def relay_copy(k, w, pos):
        pos = slot(pos)
        return remote(full[w].at[pos], full[w].at[pos], relay_send.at[k - 1, w], relay_recv.at[k - 1, w], partner)

    for w in range(count):
        pair_copy(0, w, here).start()
    for w in range(count):
        guarded(ring_in(1, w), lambda w=w: ring_copy(1, w).start())
    for k in range(1, steps + 1):
        for w in range(count):
            def arrived(k=k, w=w):
                incoming_ring(k, w).wait_recv()
                if k < steps:
                    guarded(ring_in(k + 1, w), lambda: ring_copy(k + 1, w).start())
                guarded(x_out(k, w), lambda: x_copy(k, w).start())
                pair_copy(k, w, here - step_dir * k).start()
            guarded(ring_in(k, w), arrived)
        for w in range(count):
            def crossed(k=k, w=w):
                x_copy(k, w).wait_recv()
                relay_copy(k, w, here - step_dir * k).start()
            guarded(x_in(k, w), crossed)
    for w in range(count):
        pair_copy(0, w, here).wait_recv()
    for k in range(1, steps + 1):
        for w in range(count):
            guarded(partner_ring_in(k, w), lambda k=k, w=w: pair_copy(k, w, here + step_dir * k).wait_recv())
            guarded(partner_x_in(k, w), lambda k=k, w=w: relay_copy(k, w, here + step_dir * k).wait_recv())
    for w in range(count):
        pair_copy(0, w, here).wait_send()
    for k in range(1, steps + 1):
        for w in range(count):
            def sent(k=k, w=w):
                ring_copy(k, w).wait_send()
                pair_copy(k, w, here - step_dir * k).wait_send()
            guarded(ring_in(k, w), sent)
            guarded(x_out(k, w), lambda k=k, w=w: x_copy(k, w).wait_send())
            guarded(x_in(k, w), lambda k=k, w=w: relay_copy(k, w, here - step_dir * k).wait_send())


def gather_weights(locals_, n):
    count = len(locals_)
    steps = n // 2
    dma = pltpu.SemaphoreType.DMA
    return pl.pallas_call(
        functools.partial(gather_kernel, n, count),
        out_shape=[jax.ShapeDtypeStruct((n,) + a.shape, a.dtype) for a in locals_],
        in_specs=[pl.BlockSpec(memory_space=pl.ANY)] * count,
        out_specs=[pl.BlockSpec(memory_space=pl.ANY)] * count,
        scratch_shapes=[
            dma((steps, count)),
            dma((steps, count)),
            dma((steps + 1, count)),
            dma((steps + 1, count)),
            dma((steps, count)),
            dma((steps, count)),
            dma((steps, count)),
            dma((steps, count)),
        ],
        compiler_params=pltpu.CompilerParams(collective_id=0, has_side_effects=True),
    )(*locals_)


def add_rows(dst, parts, rows, chunk):
    def body(i, carry):
        window = pl.ds(pl.multiple_of(i * chunk, chunk), chunk)
        total = parts[0][window, :].astype(jnp.float32)
        for part in parts[1:]:
            total = total + part[window, :].astype(jnp.float32)
        dst[window, :] = total.astype(dst.dtype)
        return carry

    lax.fori_loop(0, rows // chunk, body, 0)


def reduce_kernel(n, count, mm, *refs):
    xt = refs[:mm]
    dy = refs[mm : 2 * mm]
    contrib = (None,) * mm + refs[2 * mm : mm + count]
    refs = refs[mm + count :]
    out = refs[:count]
    land, send, other, own, xland, stage, xsend = (refs[count + i * count : count + (i + 1) * count] for i in range(7))
    (load_sem, own_sem, ring_send, ring_recv, pair_send, pair_recv, x_send, x_recv, back_send, back_recv) = refs[
        8 * count :
    ]
    rep = lax.axis_index("rep")
    shard = lax.axis_index("shard")
    core = rep % 2
    plane = rep // 2
    step_dir = 1 - 2 * core
    partner = (rep + step_dir, shard)
    x_partner = ((rep + 2) % 4, shard)
    here = ring_position(shard, n)
    target = (rep, ring_shard(here + step_dir, n))
    source = (rep, ring_shard(here - step_dir, n))
    steps = n // 2
    split_first = n % 2 == 0

    def carried(k, w):
        if split_first and k == 1:
            return (core == 0) == (w in FIRST_CORE_HALF)
        return True

    def guarded(cond, fn):
        if cond is True:
            fn()
        else:
            pl.when(cond)(fn)

    def block_at(k):
        return here + step_dir * (steps - k + 1)

    def load(k, w):
        return pltpu.make_async_copy(contrib[w].at[ring_shard(block_at(k), n)], send[w].at[k - 1], load_sem.at[k - 1, w])

    def load_own(w):
        return pltpu.make_async_copy(contrib[w].at[shard], own[w], own_sem.at[w])

    def remote(src, dst, ssem, rsem, device):
        return pltpu.make_async_remote_copy(
            src_ref=src, dst_ref=dst, send_sem=ssem, recv_sem=rsem, device_id=device, device_id_type=MESH
        )

    def ring_copy(k, w, device):
        return remote(send[w].at[k - 1], land[w].at[k - 1], ring_send.at[k - 1, w], ring_recv.at[k - 1, w], device)

    def pair_copy(w):
        return remote(land[w].at[steps - 1], other[w], pair_send.at[w], pair_recv.at[w], partner)

    def x_copy(w):
        return remote(xsend[w], xland[w], x_send.at[w], x_recv.at[w], x_partner)

    def back_copy(w):
        return remote(out[w], out[w], back_send.at[w], back_recv.at[w], partner)

    def owner(w):
        return core == w % 2

    def contribute(dst, w, position):
        block = ring_shard(position, n)
        width = 256

        def body(i, carry):
            window = pl.ds(pl.multiple_of(i * width, width), width)
            dst[:, window] = jnp.dot(xt[w][block], dy[w][:, window], preferred_element_type=jnp.float32)
            return carry

        lax.fori_loop(0, dy[w].shape[1] // width, body, 0)

    for w in range(mm, count):
        load_own(w).start()
    for k in range(1, steps + 1):
        for w in range(mm, count):
            guarded(carried(k, w), lambda k=k, w=w: load(k, w).start())

    barrier = pltpu.get_barrier_semaphore()
    for peer in (target, source, partner, x_partner):
        pl.semaphore_signal(barrier, inc=1, device_id=peer, device_id_type=MESH)
    pl.semaphore_wait(barrier, 4)

    def add_into(dst, parts):
        rows = dst.shape[0]
        chunk = 16 if rows % 16 == 0 else rows
        add_rows(dst, parts, rows, chunk)

    def step(k, w):
        if w < mm:
            contribute(stage[w], w, block_at(k))
            if k > 1:
                def accumulate():
                    ring_copy(k - 1, w, source).wait_recv()
                    add_into(send[w].at[k - 1], [stage[w], land[w].at[k - 2]])

                def start_chain():
                    add_into(send[w].at[k - 1], [stage[w]])

                cond = carried(k - 1, w)
                if cond is True:
                    accumulate()
                else:
                    pl.when(cond)(accumulate)
                    pl.when(jnp.logical_not(cond))(start_chain)
            else:
                add_into(send[w].at[k - 1], [stage[w]])
        else:
            load(k, w).wait()
            if k > 1:
                def accumulate():
                    ring_copy(k - 1, w, source).wait_recv()
                    add_into(send[w].at[k - 1], [send[w].at[k - 1], land[w].at[k - 2]])
                guarded(carried(k - 1, w), accumulate)
        ring_copy(k, w, target).start()

    def arrive(w):
        ring_copy(steps, w, source).wait_recv()
        pl.when(jnp.logical_not(owner(w)))(lambda: pair_copy(w).start())
        mine = land[w].at[steps - 1]

        def plane():
            if w < mm:
                contribute(own[w], w, here)
            else:
                load_own(w).wait()
            pair_copy(w).wait_recv()

            @pl.when(core == 0)
            def _():
                add_into(own[w], [own[w], mine, other[w]])

            @pl.when(core == 1)
            def _():
                add_into(own[w], [own[w], other[w], mine])

            add_into(xsend[w], [own[w]])
            x_copy(w).start()

        pl.when(owner(w))(plane)

    def total(w):
        x_copy(w).wait_recv()

        @pl.when(plane == 0)
        def _():
            add_into(out[w], [xsend[w], xland[w]])

        @pl.when(plane == 1)
        def _():
            add_into(out[w], [xland[w], xsend[w]])
        back_copy(w).start()

    rank = [CHAIN_RANK[w] if w < len(CHAIN_RANK) else w for w in range(count)]
    slots = steps + CHAIN_LAG * (count - 1)
    by_rank = sorted(range(count), key=lambda w: rank[w])
    for t in range(slots + 1):
        for w in by_rank:
            k = t - CHAIN_LAG * rank[w] + 1
            if 1 <= k <= steps:
                guarded(carried(k, w), lambda k=k, w=w: step(k, w))
        for w in by_rank:
            if steps + CHAIN_LAG * rank[w] == t:
                arrive(w)
    for w in range(count):
        pl.when(owner(w))(lambda w=w: total(w))

    for w in range(count):
        def not_owner(w=w):
            if w >= mm:
                load_own(w).wait()
            back_copy(w).wait_recv()
            pair_copy(w).wait_send()

        def was_owner(w=w):
            x_copy(w).wait_send()
            back_copy(w).wait_send()

        pl.when(owner(w))(was_owner)
        pl.when(jnp.logical_not(owner(w)))(not_owner)
    for k in range(1, steps + 1):
        for w in range(count):
            guarded(carried(k, w), lambda k=k, w=w: ring_copy(k, w, target).wait_send())


def reduce_gradients(pairs_t, contribs, n):
    mm = len(pairs_t)
    count = mm + len(contribs)
    steps = n // 2
    blocks = [(xt.shape[1], dy.shape[1]) for xt, dy in pairs_t] + [c.shape[1:] for c in contribs]
    ring_types = [jnp.bfloat16] * mm + [jnp.float32] * len(contribs)
    vmem = lambda shape, dtype=jnp.float32: pltpu.VMEM(shape, dtype)
    dma = pltpu.SemaphoreType.DMA
    return pl.pallas_call(
        functools.partial(reduce_kernel, n, count, mm),
        out_shape=[jax.ShapeDtypeStruct(b, jnp.float32) for b in blocks],
        in_specs=[pl.BlockSpec(memory_space=pltpu.VMEM)] * (2 * mm)
        + [pl.BlockSpec(memory_space=pl.ANY)] * len(contribs),
        out_specs=[pl.BlockSpec(memory_space=pltpu.VMEM)] * count,
        scratch_shapes=[vmem((steps,) + b, t) for b, t in zip(blocks, ring_types)]
        + [vmem((steps,) + b, t) for b, t in zip(blocks, ring_types)]
        + [vmem(b, t) for b, t in zip(blocks, ring_types)]
        + [vmem(b) for b in blocks]
        + [vmem(b, t) for b, t in zip(blocks, ring_types)]
        + [vmem(b) for b in blocks]
        + [vmem(b, t) for b, t in zip(blocks, ring_types)]
        + [
            dma((steps, count)),
            dma((count,)),
            dma((steps, count)),
            dma((steps, count)),
            dma((count,)),
            dma((count,)),
            dma((count,)),
            dma((count,)),
            dma((count,)),
            dma((count,)),
        ],
        compiler_params=pltpu.CompilerParams(
            collective_id=1, has_side_effects=True, vmem_limit_bytes=62 * 1024 * 1024
        ),
    )(*[xt for xt, _ in pairs_t], *[dy for _, dy in pairs_t], *contribs)


def swap_core(value):
    rep = lax.axis_size("rep")
    return lax.ppermute(value, "rep", perm=[(i, i ^ 1) for i in range(rep)])


def swap_x(value):
    rep = lax.axis_size("rep")
    return lax.ppermute(value, "rep", perm=[(i, i ^ 2) for i in range(rep)])


def join_halves(mine, theirs, core, axis):
    first = jnp.where(core == 0, mine, theirs)
    second = jnp.where(core == 0, theirs, mine)
    return jnp.concatenate([first, second], axis=axis)


def take_half(value, core, axis):
    half = value.shape[axis] // 2
    return lax.dynamic_slice_in_dim(value, core * half, half, axis=axis)


def per_device(
    tokens,
    segment_ids,
    cotangent,
    ln1_gain,
    ln1_bias,
    qkv_weight,
    qv_bias,
    out_weight,
    out_bias,
    ln2_gain,
    ln2_bias,
    fc_weight,
    fc_bias,
    proj_weight,
    proj_bias,
):
    rep = lax.axis_size("rep")
    assert rep == 4
    core = lax.axis_index("rep") % 2
    row_count = tokens.shape[0]
    positions = jnp.arange(row_count)
    allowed = (segment_ids[:, None] == segment_ids[None, :]) & (
        positions[None, :] <= positions[:, None]
    )
    layer_index = 0
    shard = lax.axis_size("shard")
    small_local = (ln1_gain, ln1_bias, qv_bias, out_bias, ln2_gain, ln2_bias, fc_bias, proj_bias)
    widths = [v.shape[1] for v in small_local]
    local_weights = (
        qkv_weight[layer_index],
        out_weight[layer_index],
        fc_weight[layer_index],
        proj_weight[layer_index],
    )
    rows_local = local_weights[0].shape[0]
    small_row = jnp.concatenate(small_local, axis=1)
    fulls = gather_weights(list(local_weights) + [small_row], shard)
    weights = tuple(f.reshape(-1, f.shape[-1]) for f in fulls[:4])
    halves = [take_half(w, core, 1) for w in local_weights]
    half_widths = [h.size // rows_local for h in halves]
    packed_all = fulls[4].reshape(shard, -1)
    small = []
    start = 0
    for width in widths:
        small.append(to_float(packed_all[:, start : start + width].reshape(-1)))
        start += width
    small = tuple(small)

    residual = to_float(tokens)
    saved = layer_forward(residual, allowed, small, weights)
    out_tokens = saved["result"].astype(jnp.bfloat16)
    upstream = to_float(cotangent)
    input_grad, small_grads, pairs = layer_backward(upstream, saved, small, weights)

    outgoing = jnp.concatenate([x for x, _ in pairs] + [dy for _, dy in pairs], axis=1)
    incoming = swap_core(outgoing)
    small_mine = jnp.concatenate([g.reshape(shard, -1) for g in small_grads], axis=1)
    small_theirs = swap_core(small_mine)
    small_chip = jnp.where(core == 0, small_mine + small_theirs, small_theirs + small_mine)
    start = 0
    partner_x = []
    for x, _ in pairs:
        partner_x.append(incoming[:, start : start + x.shape[1]])
        start += x.shape[1]
    pairs_t = []
    for (x, dy), px in zip(pairs, partner_x):
        pdy = incoming[:, start : start + dy.shape[1]]
        start += dy.shape[1]
        rows_t = jnp.concatenate([x, px], axis=0).T
        pairs_t.append((rows_t.reshape(shard, -1, rows_t.shape[1]), jnp.concatenate([dy, pdy], axis=0)))
    totals = reduce_gradients(pairs_t, [small_chip.reshape(shard, 1, -1)], shard)
    small_share = totals[4]
    owned = [t[None] for t in totals[:4]]
    small_owned = []
    start = 0
    for g in small_grads:
        width = g.shape[0] // shard
        small_owned.append(small_share[:, start : start + width])
        start += width

    (g_ln1_g, g_ln1_b, g_qv_b, g_out_b, g_ln2_g, g_ln2_b, g_fc_b, g_proj_b) = small_owned
    g_qkv, g_out, g_fc, g_proj = owned
    return (
        out_tokens,
        input_grad,
        g_ln1_g,
        g_ln1_b,
        g_qkv,
        g_qv_b,
        g_out,
        g_out_b,
        g_ln2_g,
        g_ln2_b,
        g_fc,
        g_fc_b,
        g_proj,
        g_proj_b,
    )


def solution(mesh):
    placed = (
        P(("rep", "shard"), None),
        P(("rep", "shard")),
        P(("rep", "shard"), None),
        P(None, "shard"),
        P(None, "shard"),
        P(None, "shard", None),
        P(None, "shard"),
        P(None, "shard", None),
        P(None, "shard"),
        P(None, "shard"),
        P(None, "shard"),
        P(None, "shard", None),
        P(None, "shard"),
        P(None, "shard", None),
        P(None, "shard"),
    )
    return jax.shard_map(
        per_device,
        mesh=mesh,
        in_specs=placed,
        out_specs=(
            P(("rep", "shard"), None),
            P(("rep", "shard"), None),
            P(None, "shard"),
            P(None, "shard"),
            P(None, "shard", None),
            P(None, "shard"),
            P(None, "shard", None),
            P(None, "shard"),
            P(None, "shard"),
            P(None, "shard"),
            P(None, "shard", None),
            P(None, "shard"),
            P(None, "shard", None),
            P(None, "shard"),
        ),
        check_vma=False,
    )
```

```python
import functools

import jax
import jax.numpy as jnp
from jax import lax
from jax.experimental import pallas as pl
from jax.experimental.pallas import tpu as pltpu
from jax.sharding import PartitionSpec as P

MESH = pl.DeviceIdType.MESH

HEADS = 12
HEAD = 64
LAYERS = 1

epsilon = 1e-05

def to_float(value):
    return value.astype(jnp.float32)


def layer_norm(inputs, norm_gain, norm_shift):
    center = inputs - jnp.mean(inputs, axis=-1, keepdims=True)
    inverse_std = lax.rsqrt(jnp.mean(center * center, axis=-1, keepdims=True) + epsilon)
    normed = center * inverse_std
    return (normed * norm_gain + norm_shift, normed, inverse_std)


def norm_back(upstream, normed, inverse_std, norm_gain):
    scaled = upstream * norm_gain
    inner_term = scaled - jnp.mean(scaled, axis=-1, keepdims=True)
    inner_term = inner_term - normed * jnp.mean(scaled * normed, axis=-1, keepdims=True)
    return (inverse_std * inner_term, jnp.sum(upstream * normed, axis=0), jnp.sum(upstream, axis=0))


def layer_forward(inputs, allowed, small, weights):
    ln1_gain, ln1_bias, qv_bias, out_bias, ln2_gain, ln2_bias, fc_bias, proj_bias = small
    qkv_weight, out_weight, fc_weight, proj_weight = weights
    row_count = inputs.shape[0]
    width_all = inputs.shape[1]
    first_norm, normed_one, inverse_one = layer_norm(inputs, ln1_gain, ln1_bias)
    first_low = first_norm.astype(jnp.bfloat16)
    offset = jnp.concatenate(
        [qv_bias[:width_all], jnp.zeros((width_all,), jnp.float32), qv_bias[width_all:]]
    )
    projected = (
        jnp.dot(first_low, qkv_weight, preferred_element_type=jnp.float32) + offset
    ).astype(jnp.bfloat16)
    queries = projected[:, :width_all].reshape(row_count, HEADS, HEAD)
    keys_all = projected[:, width_all : 2 * width_all].reshape(row_count, HEADS, HEAD)
    values_all = projected[:, 2 * width_all :].reshape(row_count, HEADS, HEAD)
    scores = jnp.einsum(
        "qhd,khd->hqk", queries, keys_all, preferred_element_type=jnp.float32
    ) * HEAD ** (-0.5)
    scores = jnp.where(allowed[None], scores, -1e30)
    row_max = jnp.max(scores, axis=-1, keepdims=True)
    log_total = row_max + jnp.log(jnp.sum(jnp.exp(scores - row_max), axis=-1, keepdims=True))
    attn_probs = jnp.exp(scores - log_total)
    probs_low = attn_probs.astype(jnp.bfloat16)
    attn_mixed = jnp.einsum(
        "hqk,khd->qhd", probs_low, values_all, preferred_element_type=jnp.float32
    )
    attn_mixed = attn_mixed.reshape(row_count, width_all).astype(jnp.bfloat16)
    after_attn = (
        inputs + jnp.dot(attn_mixed, out_weight, preferred_element_type=jnp.float32) + out_bias
    )
    second_norm, normed_two, inverse_two = layer_norm(after_attn, ln2_gain, ln2_bias)
    second_low = second_norm.astype(jnp.bfloat16)
    hidden_pre = jnp.dot(second_low, fc_weight, preferred_element_type=jnp.float32) + fc_bias
    hidden_low = jax.nn.gelu(hidden_pre, approximate=True).astype(jnp.bfloat16)
    result = (
        after_attn + jnp.dot(hidden_low, proj_weight, preferred_element_type=jnp.float32) + proj_bias
    )
    return dict(
        normed_one=normed_one,
        inverse_one=inverse_one,
        first_low=first_low,
        queries=queries,
        keys_all=keys_all,
        values_all=values_all,
        attn_probs=attn_probs,
        probs_low=probs_low,
        attn_mixed=attn_mixed,
        normed_two=normed_two,
        inverse_two=inverse_two,
        second_low=second_low,
        hidden_pre=hidden_pre,
        hidden_low=hidden_low,
        result=result,
    )


def layer_backward(upstream, saved, small, weights):
    ln1_gain, ln1_bias, qv_bias, out_bias, ln2_gain, ln2_bias, fc_bias, proj_bias = small
    qkv_weight, out_weight, fc_weight, proj_weight = weights
    row_count = upstream.shape[0]
    width_all = upstream.shape[1]
    proj_in = upstream.astype(jnp.bfloat16)
    grad_proj_b = jnp.sum(to_float(proj_in), axis=0)
    hidden_grad = jnp.einsum("td,fd->tf", proj_in, proj_weight, preferred_element_type=jnp.float32)
    _, gelu_pull = jax.vjp(lambda value: jax.nn.gelu(value, approximate=True), saved["hidden_pre"])
    pre_grad = gelu_pull(hidden_grad)[0].astype(jnp.bfloat16)
    grad_fc_b = jnp.sum(to_float(pre_grad), axis=0)
    second_grad = jnp.einsum("tf,df->td", pre_grad, fc_weight, preferred_element_type=jnp.float32)
    norm_part, grad_ln2_g, grad_ln2_b = norm_back(
        second_grad, saved["normed_two"], saved["inverse_two"], ln2_gain
    )
    residual_grad = upstream + norm_part
    branch_in = residual_grad.astype(jnp.bfloat16)
    grad_out_b = jnp.sum(to_float(branch_in), axis=0)
    mixed_grad = jnp.einsum("td,cd->tc", branch_in, out_weight, preferred_element_type=jnp.float32)
    mixed_grad = mixed_grad.astype(jnp.bfloat16).reshape(row_count, HEADS, HEAD)
    prob_grad = jnp.einsum(
        "qhd,khd->hqk", mixed_grad, saved["values_all"], preferred_element_type=jnp.float32
    )
    value_grad = jnp.einsum(
        "hqk,qhd->khd", saved["probs_low"], mixed_grad, preferred_element_type=jnp.float32
    )
    attn_probs = saved["attn_probs"]
    row_delta = jnp.sum(attn_probs * prob_grad, axis=-1, keepdims=True)
    score_grad = (attn_probs * (prob_grad - row_delta)).astype(jnp.bfloat16)
    query_grad = jnp.einsum(
        "hqk,khd->qhd", score_grad, saved["keys_all"], preferred_element_type=jnp.float32
    ) * HEAD ** (-0.5)
    key_grad = jnp.einsum(
        "hqk,qhd->khd", score_grad, saved["queries"], preferred_element_type=jnp.float32
    ) * HEAD ** (-0.5)
    joined_grad = jnp.concatenate(
        [
            query_grad.reshape(row_count, width_all),
            key_grad.reshape(row_count, width_all),
            value_grad.reshape(row_count, width_all),
        ],
        axis=1,
    ).astype(jnp.bfloat16)
    column_sums = jnp.sum(to_float(joined_grad), axis=0)
    grad_qv_b = jnp.concatenate([column_sums[:width_all], column_sums[2 * width_all :]])
    first_grad = jnp.einsum(
        "te,ce->tc", joined_grad, qkv_weight, preferred_element_type=jnp.float32
    )
    norm_first, grad_ln1_g, grad_ln1_b = norm_back(
        first_grad, saved["normed_one"], saved["inverse_one"], ln1_gain
    )
    small_grads = (
        grad_ln1_g,
        grad_ln1_b,
        grad_qv_b,
        grad_out_b,
        grad_ln2_g,
        grad_ln2_b,
        grad_fc_b,
        grad_proj_b,
    )
    pairs = (
        (saved["first_low"], joined_grad),
        (saved["attn_mixed"], branch_in),
        (saved["second_low"], pre_grad),
        (saved["hidden_low"], proj_in),
    )
    return (residual_grad + norm_first, small_grads, pairs)


def ring_position(shard_index, n):
    if n != 8:
        return shard_index
    y = shard_index % 2
    z = shard_index // 2
    return z * (1 - 2 * y) + 7 * y


def ring_shard(position, n):
    position = position % n
    if n != 8:
        return position
    y = position // 4
    z = (position % 4) * (1 - 2 * y) + 3 * y
    return z * 2 + y


FIRST_CORE_HALF = (0, 3)


CHAIN_RANK = (2, 3, 0, 1, 4)
CHAIN_LAG = 2


X_ONLY = (2, 3)


def gather_kernel(n, count, *refs):
    local = refs[:count]
    full = refs[count : 2 * count]
    ring_send, ring_recv, pair_send, pair_recv, x_send, x_recv, relay_send, relay_recv = refs[2 * count :]
    rep = lax.axis_index("rep")
    shard = lax.axis_index("shard")
    core = rep % 2
    plane = rep // 2
    step_dir = 1 - 2 * core
    partner = (rep + step_dir, shard)
    x_partner = ((rep + 2) % 4, shard)
    here = ring_position(shard, n)
    target = (rep, ring_shard(here + step_dir, n))
    source = (rep, ring_shard(here - step_dir, n))
    steps = n // 2
    split_last = n % 2 == 0

    barrier = pltpu.get_barrier_semaphore()
    for peer in (target, source, partner, x_partner):
        pl.semaphore_signal(barrier, inc=1, device_id=peer, device_id_type=MESH)
    pl.semaphore_wait(barrier, 4)

    def both(a, b):
        if a is True:
            return b
        if b is True:
            return a
        return jnp.logical_and(a, b)

    def core_carries(k, w, which_core):
        if split_last and k == steps:
            return (which_core == 0) == (w in FIRST_CORE_HALF)
        return True

    def plane_carries(w, which_plane):
        if w == X_ONLY[0]:
            return which_plane == 0
        if w == X_ONLY[1]:
            return which_plane == 1
        return True

    def ring_in(k, w):
        return both(plane_carries(w, plane), core_carries(k, w, core))

    def x_out(k, w):
        if w not in X_ONLY:
            return False
        return both(plane_carries(w, plane), core_carries(k, w, core))

    def x_in(k, w):
        if w not in X_ONLY:
            return False
        return both(plane_carries(w, 1 - plane), core_carries(k, w, core))

    def partner_ring_in(k, w):
        return both(plane_carries(w, plane), core_carries(k, w, 1 - core))

    def partner_x_in(k, w):
        if w not in X_ONLY:
            return False
        return both(plane_carries(w, 1 - plane), core_carries(k, w, 1 - core))

    def guarded(cond, fn):
        if cond is False:
            return
        if cond is True:
            fn()
        else:
            pl.when(cond)(fn)

    def slot(position):
        return ring_shard(position, n)

    def remote(src, dst, ssem, rsem, device):
        return pltpu.make_async_remote_copy(
            src_ref=src, dst_ref=dst, send_sem=ssem, recv_sem=rsem, device_id=device, device_id_type=MESH
        )

    def ring_copy(k, w):
        src_pos = here - step_dir * (k - 1)
        src = local[w] if k == 1 else full[w].at[slot(src_pos)]
        return remote(src, full[w].at[slot(src_pos)], ring_send.at[k - 1, w], ring_recv.at[k - 1, w], target)

    def incoming_ring(k, w):
        pos = slot(here - step_dir * k)
        return remote(full[w].at[pos], full[w].at[pos], ring_send.at[k - 1, w], ring_recv.at[k - 1, w], source)

    def pair_copy(k, w, pos):
        src = local[w] if k == 0 else full[w].at[slot(pos)]
        return remote(src, full[w].at[slot(pos)], pair_send.at[k, w], pair_recv.at[k, w], partner)

    def x_copy(k, w):
        pos = slot(here - step_dir * k)
        return remote(full[w].at[pos], full[w].at[pos], x_send.at[k - 1, w], x_recv.at[k - 1, w], x_partner)

    def relay_copy(k, w, pos):
        pos = slot(pos)
        return remote(full[w].at[pos], full[w].at[pos], relay_send.at[k - 1, w], relay_recv.at[k - 1, w], partner)

    for w in range(count):
        pair_copy(0, w, here).start()
    for w in range(count):
        guarded(ring_in(1, w), lambda w=w: ring_copy(1, w).start())
    for k in range(1, steps + 1):
        for w in range(count):
            def arrived(k=k, w=w):
                incoming_ring(k, w).wait_recv()
                if k < steps:
                    guarded(ring_in(k + 1, w), lambda: ring_copy(k + 1, w).start())
                guarded(x_out(k, w), lambda: x_copy(k, w).start())
                pair_copy(k, w, here - step_dir * k).start()
            guarded(ring_in(k, w), arrived)
        for w in range(count):
            def crossed(k=k, w=w):
                x_copy(k, w).wait_recv()
                relay_copy(k, w, here - step_dir * k).start()
            guarded(x_in(k, w), crossed)
    for w in range(count):
        pair_copy(0, w, here).wait_recv()
    for k in range(1, steps + 1):
        for w in range(count):
            guarded(partner_ring_in(k, w), lambda k=k, w=w: pair_copy(k, w, here + step_dir * k).wait_recv())
            guarded(partner_x_in(k, w), lambda k=k, w=w: relay_copy(k, w, here + step_dir * k).wait_recv())
    for w in range(count):
        pair_copy(0, w, here).wait_send()
    for k in range(1, steps + 1):
        for w in range(count):
            def sent(k=k, w=w):
                ring_copy(k, w).wait_send()
                pair_copy(k, w, here - step_dir * k).wait_send()
            guarded(ring_in(k, w), sent)
            guarded(x_out(k, w), lambda k=k, w=w: x_copy(k, w).wait_send())
            guarded(x_in(k, w), lambda k=k, w=w: relay_copy(k, w, here - step_dir * k).wait_send())


def gather_weights(locals_, n):
    count = len(locals_)
    steps = n // 2
    dma = pltpu.SemaphoreType.DMA
    return pl.pallas_call(
        functools.partial(gather_kernel, n, count),
        out_shape=[jax.ShapeDtypeStruct((n,) + a.shape, a.dtype) for a in locals_],
        in_specs=[pl.BlockSpec(memory_space=pl.ANY)] * count,
        out_specs=[pl.BlockSpec(memory_space=pl.ANY)] * count,
        scratch_shapes=[
            dma((steps, count)),
            dma((steps, count)),
            dma((steps + 1, count)),
            dma((steps + 1, count)),
            dma((steps, count)),
            dma((steps, count)),
            dma((steps, count)),
            dma((steps, count)),
        ],
        compiler_params=pltpu.CompilerParams(collective_id=0, has_side_effects=True),
    )(*locals_)


def add_rows(dst, parts, rows, chunk):
    def body(i, carry):
        window = pl.ds(pl.multiple_of(i * chunk, chunk), chunk)
        total = parts[0][window, :].astype(jnp.float32)
        for part in parts[1:]:
            total = total + part[window, :].astype(jnp.float32)
        dst[window, :] = total.astype(dst.dtype)
        return carry

    lax.fori_loop(0, rows // chunk, body, 0)


def reduce_kernel(n, count, mm, *refs):
    xt = refs[:mm]
    dy = refs[mm : 2 * mm]
    contrib = (None,) * mm + refs[2 * mm : mm + count]
    refs = refs[mm + count :]
    out = refs[:count]
    land, send, other, own, xland, stage, xsend = (refs[count + i * count : count + (i + 1) * count] for i in range(7))
    (load_sem, own_sem, ring_send, ring_recv, pair_send, pair_recv, x_send, x_recv, back_send, back_recv) = refs[
        8 * count :
    ]
    rep = lax.axis_index("rep")
    shard = lax.axis_index("shard")
    core = rep % 2
    plane = rep // 2
    step_dir = 1 - 2 * core
    partner = (rep + step_dir, shard)
    x_partner = ((rep + 2) % 4, shard)
    here = ring_position(shard, n)
    target = (rep, ring_shard(here + step_dir, n))
    source = (rep, ring_shard(here - step_dir, n))
    steps = n // 2
    split_first = n % 2 == 0

    def carried(k, w):
        if split_first and k == 1:
            return (core == 0) == (w in FIRST_CORE_HALF)
        return True

    def guarded(cond, fn):
        if cond is True:
            fn()
        else:
            pl.when(cond)(fn)

    def block_at(k):
        return here + step_dir * (steps - k + 1)

    def load(k, w):
        return pltpu.make_async_copy(contrib[w].at[ring_shard(block_at(k), n)], send[w].at[k - 1], load_sem.at[k - 1, w])

    def load_own(w):
        return pltpu.make_async_copy(contrib[w].at[shard], own[w], own_sem.at[w])

    def remote(src, dst, ssem, rsem, device):
        return pltpu.make_async_remote_copy(
            src_ref=src, dst_ref=dst, send_sem=ssem, recv_sem=rsem, device_id=device, device_id_type=MESH
        )

    def ring_copy(k, w, device):
        return remote(send[w].at[k - 1], land[w].at[k - 1], ring_send.at[k - 1, w], ring_recv.at[k - 1, w], device)

    def pair_copy(w):
        return remote(land[w].at[steps - 1], other[w], pair_send.at[w], pair_recv.at[w], partner)

    def x_copy(w):
        return remote(xsend[w], xland[w], x_send.at[w], x_recv.at[w], x_partner)

    def back_copy(w):
        return remote(out[w], out[w], back_send.at[w], back_recv.at[w], partner)

    def owner(w):
        return core == w % 2

    def contribute(dst, w, position):
        block = ring_shard(position, n)
        width = 256

        def body(i, carry):
            window = pl.ds(pl.multiple_of(i * width, width), width)
            dst[:, window] = jnp.dot(xt[w][block], dy[w][:, window], preferred_element_type=jnp.float32)
            return carry

        lax.fori_loop(0, dy[w].shape[1] // width, body, 0)

    for w in range(mm, count):
        load_own(w).start()
    for k in range(1, steps + 1):
        for w in range(mm, count):
            guarded(carried(k, w), lambda k=k, w=w: load(k, w).start())

    barrier = pltpu.get_barrier_semaphore()
    for peer in (target, source, partner, x_partner):
        pl.semaphore_signal(barrier, inc=1, device_id=peer, device_id_type=MESH)
    pl.semaphore_wait(barrier, 4)

    def add_into(dst, parts):
        rows = dst.shape[0]
        chunk = 16 if rows % 16 == 0 else rows
        add_rows(dst, parts, rows, chunk)

    def step(k, w):
        if w < mm:
            if k == 1:
                contribute(stage[w], w, block_at(k))
            if k > 1:
                def accumulate():
                    ring_copy(k - 1, w, source).wait_recv()
                    add_into(send[w].at[k - 1], [stage[w], land[w].at[k - 2]])

                def start_chain():
                    contribute(stage[w], w, block_at(k))
                    add_into(send[w].at[k - 1], [stage[w]])

                cond = carried(k - 1, w)
                if cond is True:
                    accumulate()
                else:
                    pl.when(cond)(accumulate)
                    pl.when(jnp.logical_not(cond))(start_chain)
            else:
                add_into(send[w].at[k - 1], [stage[w]])
            ring_copy(k, w, target).start()
            if k < steps:
                contribute(stage[w], w, block_at(k + 1))
            else:
                pl.when(owner(w))(lambda: contribute(own[w], w, here))
        else:
            load(k, w).wait()
            if k > 1:
                def accumulate():
                    ring_copy(k - 1, w, source).wait_recv()
                    add_into(send[w].at[k - 1], [send[w].at[k - 1], land[w].at[k - 2]])
                guarded(carried(k - 1, w), accumulate)
            ring_copy(k, w, target).start()

    def arrive(w):
        ring_copy(steps, w, source).wait_recv()
        pl.when(jnp.logical_not(owner(w)))(lambda: pair_copy(w).start())
        mine = land[w].at[steps - 1]

        def plane():
            if w >= mm:
                load_own(w).wait()
            pair_copy(w).wait_recv()

            @pl.when(core == 0)
            def _():
                add_into(own[w], [own[w], mine, other[w]])

            @pl.when(core == 1)
            def _():
                add_into(own[w], [own[w], other[w], mine])

            add_into(xsend[w], [own[w]])
            x_copy(w).start()

        pl.when(owner(w))(plane)

    def total(w):
        x_copy(w).wait_recv()

        @pl.when(plane == 0)
        def _():
            add_into(out[w], [xsend[w], xland[w]])

        @pl.when(plane == 1)
        def _():
            add_into(out[w], [xland[w], xsend[w]])
        back_copy(w).start()

    rank = [CHAIN_RANK[w] if w < len(CHAIN_RANK) else w for w in range(count)]
    slots = steps + CHAIN_LAG * (count - 1)
    by_rank = sorted(range(count), key=lambda w: rank[w])
    for t in range(slots + 1):
        for w in by_rank:
            k = t - CHAIN_LAG * rank[w] + 1
            if 1 <= k <= steps:
                guarded(carried(k, w), lambda k=k, w=w: step(k, w))
        for w in by_rank:
            if steps + CHAIN_LAG * rank[w] == t:
                arrive(w)
    for w in range(count):
        pl.when(owner(w))(lambda w=w: total(w))

    for w in range(count):
        def not_owner(w=w):
            if w >= mm:
                load_own(w).wait()
            back_copy(w).wait_recv()
            pair_copy(w).wait_send()

        def was_owner(w=w):
            x_copy(w).wait_send()
            back_copy(w).wait_send()

        pl.when(owner(w))(was_owner)
        pl.when(jnp.logical_not(owner(w)))(not_owner)
    for k in range(1, steps + 1):
        for w in range(count):
            guarded(carried(k, w), lambda k=k, w=w: ring_copy(k, w, target).wait_send())


def reduce_gradients(pairs_t, contribs, n):
    mm = len(pairs_t)
    count = mm + len(contribs)
    steps = n // 2
    blocks = [(xt.shape[1], dy.shape[1]) for xt, dy in pairs_t] + [c.shape[1:] for c in contribs]
    ring_types = [jnp.bfloat16] * mm + [jnp.float32] * len(contribs)
    vmem = lambda shape, dtype=jnp.float32: pltpu.VMEM(shape, dtype)
    dma = pltpu.SemaphoreType.DMA
    return pl.pallas_call(
        functools.partial(reduce_kernel, n, count, mm),
        out_shape=[jax.ShapeDtypeStruct(b, jnp.float32) for b in blocks],
        in_specs=[pl.BlockSpec(memory_space=pltpu.VMEM)] * (2 * mm)
        + [pl.BlockSpec(memory_space=pl.ANY)] * len(contribs),
        out_specs=[pl.BlockSpec(memory_space=pltpu.VMEM)] * count,
        scratch_shapes=[vmem((steps,) + b, t) for b, t in zip(blocks, ring_types)]
        + [vmem((steps,) + b, t) for b, t in zip(blocks, ring_types)]
        + [vmem(b, t) for b, t in zip(blocks, ring_types)]
        + [vmem(b) for b in blocks]
        + [vmem(b, t) for b, t in zip(blocks, ring_types)]
        + [vmem(b) for b in blocks]
        + [vmem(b, t) for b, t in zip(blocks, ring_types)]
        + [
            dma((steps, count)),
            dma((count,)),
            dma((steps, count)),
            dma((steps, count)),
            dma((count,)),
            dma((count,)),
            dma((count,)),
            dma((count,)),
            dma((count,)),
            dma((count,)),
        ],
        compiler_params=pltpu.CompilerParams(
            collective_id=1, has_side_effects=True, vmem_limit_bytes=62 * 1024 * 1024
        ),
    )(*[xt for xt, _ in pairs_t], *[dy for _, dy in pairs_t], *contribs)


def swap_core(value):
    rep = lax.axis_size("rep")
    return lax.ppermute(value, "rep", perm=[(i, i ^ 1) for i in range(rep)])


def swap_x(value):
    rep = lax.axis_size("rep")
    return lax.ppermute(value, "rep", perm=[(i, i ^ 2) for i in range(rep)])


def join_halves(mine, theirs, core, axis):
    first = jnp.where(core == 0, mine, theirs)
    second = jnp.where(core == 0, theirs, mine)
    return jnp.concatenate([first, second], axis=axis)


def take_half(value, core, axis):
    half = value.shape[axis] // 2
    return lax.dynamic_slice_in_dim(value, core * half, half, axis=axis)


def per_device(
    tokens,
    segment_ids,
    cotangent,
    ln1_gain,
    ln1_bias,
    qkv_weight,
    qv_bias,
    out_weight,
    out_bias,
    ln2_gain,
    ln2_bias,
    fc_weight,
    fc_bias,
    proj_weight,
    proj_bias,
):
    rep = lax.axis_size("rep")
    assert rep == 4
    core = lax.axis_index("rep") % 2
    row_count = tokens.shape[0]
    positions = jnp.arange(row_count)
    allowed = (segment_ids[:, None] == segment_ids[None, :]) & (
        positions[None, :] <= positions[:, None]
    )
    layer_index = 0
    shard = lax.axis_size("shard")
    small_local = (ln1_gain, ln1_bias, qv_bias, out_bias, ln2_gain, ln2_bias, fc_bias, proj_bias)
    widths = [v.shape[1] for v in small_local]
    local_weights = (
        qkv_weight[layer_index],
        out_weight[layer_index],
        fc_weight[layer_index],
        proj_weight[layer_index],
    )
    rows_local = local_weights[0].shape[0]
    small_row = jnp.concatenate(small_local, axis=1)
    fulls = gather_weights(list(local_weights) + [small_row], shard)
    weights = tuple(f.reshape(-1, f.shape[-1]) for f in fulls[:4])
    halves = [take_half(w, core, 1) for w in local_weights]
    half_widths = [h.size // rows_local for h in halves]
    packed_all = fulls[4].reshape(shard, -1)
    small = []
    start = 0
    for width in widths:
        small.append(to_float(packed_all[:, start : start + width].reshape(-1)))
        start += width
    small = tuple(small)

    residual = to_float(tokens)
    saved = layer_forward(residual, allowed, small, weights)
    out_tokens = saved["result"].astype(jnp.bfloat16)
    upstream = to_float(cotangent)
    input_grad, small_grads, pairs = layer_backward(upstream, saved, small, weights)

    outgoing = jnp.concatenate([x for x, _ in pairs] + [dy for _, dy in pairs], axis=1)
    incoming = swap_core(outgoing)
    small_mine = jnp.concatenate([g.reshape(shard, -1) for g in small_grads], axis=1)
    small_theirs = swap_core(small_mine)
    small_chip = jnp.where(core == 0, small_mine + small_theirs, small_theirs + small_mine)
    start = 0
    partner_x = []
    for x, _ in pairs:
        partner_x.append(incoming[:, start : start + x.shape[1]])
        start += x.shape[1]
    pairs_t = []
    for (x, dy), px in zip(pairs, partner_x):
        pdy = incoming[:, start : start + dy.shape[1]]
        start += dy.shape[1]
        rows_t = jnp.concatenate([x, px], axis=0).T
        pairs_t.append((rows_t.reshape(shard, -1, rows_t.shape[1]), jnp.concatenate([dy, pdy], axis=0)))
    totals = reduce_gradients(pairs_t, [small_chip.reshape(shard, 1, -1)], shard)
    small_share = totals[4]
    owned = [t[None] for t in totals[:4]]
    small_owned = []
    start = 0
    for g in small_grads:
        width = g.shape[0] // shard
        small_owned.append(small_share[:, start : start + width])
        start += width

    (g_ln1_g, g_ln1_b, g_qv_b, g_out_b, g_ln2_g, g_ln2_b, g_fc_b, g_proj_b) = small_owned
    g_qkv, g_out, g_fc, g_proj = owned
    return (
        out_tokens,
        input_grad,
        g_ln1_g,
        g_ln1_b,
        g_qkv,
        g_qv_b,
        g_out,
        g_out_b,
        g_ln2_g,
        g_ln2_b,
        g_fc,
        g_fc_b,
        g_proj,
        g_proj_b,
    )


def solution(mesh):
    placed = (
        P(("rep", "shard"), None),
        P(("rep", "shard")),
        P(("rep", "shard"), None),
        P(None, "shard"),
        P(None, "shard"),
        P(None, "shard", None),
        P(None, "shard"),
        P(None, "shard", None),
        P(None, "shard"),
        P(None, "shard"),
        P(None, "shard"),
        P(None, "shard", None),
        P(None, "shard"),
        P(None, "shard", None),
        P(None, "shard"),
    )
    return jax.shard_map(
        per_device,
        mesh=mesh,
        in_specs=placed,
        out_specs=(
            P(("rep", "shard"), None),
            P(("rep", "shard"), None),
            P(None, "shard"),
            P(None, "shard"),
            P(None, "shard", None),
            P(None, "shard"),
            P(None, "shard", None),
            P(None, "shard"),
            P(None, "shard"),
            P(None, "shard"),
            P(None, "shard", None),
            P(None, "shard"),
            P(None, "shard", None),
            P(None, "shard"),
        ),
        check_vma=False,
    )
```

```python
import functools

import jax
import jax.numpy as jnp
from jax import lax
from jax.experimental import pallas as pl
from jax.experimental.pallas import tpu as pltpu
from jax.sharding import PartitionSpec as P

MESH = pl.DeviceIdType.MESH

HEADS = 12
HEAD = 64
LAYERS = 1

epsilon = 1e-05

def to_float(value):
    return value.astype(jnp.float32)


def layer_norm(inputs, norm_gain, norm_shift):
    center = inputs - jnp.mean(inputs, axis=-1, keepdims=True)
    inverse_std = lax.rsqrt(jnp.mean(center * center, axis=-1, keepdims=True) + epsilon)
    normed = center * inverse_std
    return (normed * norm_gain + norm_shift, normed, inverse_std)


def norm_back(upstream, normed, inverse_std, norm_gain):
    scaled = upstream * norm_gain
    inner_term = scaled - jnp.mean(scaled, axis=-1, keepdims=True)
    inner_term = inner_term - normed * jnp.mean(scaled * normed, axis=-1, keepdims=True)
    return (inverse_std * inner_term, jnp.sum(upstream * normed, axis=0), jnp.sum(upstream, axis=0))


def layer_forward(inputs, allowed, small, weights):
    ln1_gain, ln1_bias, qv_bias, out_bias, ln2_gain, ln2_bias, fc_bias, proj_bias = small
    qkv_weight, out_weight, fc_weight, proj_weight = weights
    row_count = inputs.shape[0]
    width_all = inputs.shape[1]
    first_norm, normed_one, inverse_one = layer_norm(inputs, ln1_gain, ln1_bias)
    first_low = first_norm.astype(jnp.bfloat16)
    offset = jnp.concatenate(
        [qv_bias[:width_all], jnp.zeros((width_all,), jnp.float32), qv_bias[width_all:]]
    )
    projected = (
        jnp.dot(first_low, qkv_weight, preferred_element_type=jnp.float32) + offset
    ).astype(jnp.bfloat16)
    queries = projected[:, :width_all].reshape(row_count, HEADS, HEAD)
    keys_all = projected[:, width_all : 2 * width_all].reshape(row_count, HEADS, HEAD)
    values_all = projected[:, 2 * width_all :].reshape(row_count, HEADS, HEAD)
    scores = jnp.einsum(
        "qhd,khd->hqk", queries, keys_all, preferred_element_type=jnp.float32
    ) * HEAD ** (-0.5)
    scores = jnp.where(allowed[None], scores, -1e30)
    row_max = jnp.max(scores, axis=-1, keepdims=True)
    log_total = row_max + jnp.log(jnp.sum(jnp.exp(scores - row_max), axis=-1, keepdims=True))
    attn_probs = jnp.exp(scores - log_total)
    probs_low = attn_probs.astype(jnp.bfloat16)
    attn_mixed = jnp.einsum(
        "hqk,khd->qhd", probs_low, values_all, preferred_element_type=jnp.float32
    )
    attn_mixed = attn_mixed.reshape(row_count, width_all).astype(jnp.bfloat16)
    after_attn = (
        inputs + jnp.dot(attn_mixed, out_weight, preferred_element_type=jnp.float32) + out_bias
    )
    second_norm, normed_two, inverse_two = layer_norm(after_attn, ln2_gain, ln2_bias)
    second_low = second_norm.astype(jnp.bfloat16)
    hidden_pre = jnp.dot(second_low, fc_weight, preferred_element_type=jnp.float32) + fc_bias
    hidden_low = jax.nn.gelu(hidden_pre, approximate=True).astype(jnp.bfloat16)
    result = (
        after_attn + jnp.dot(hidden_low, proj_weight, preferred_element_type=jnp.float32) + proj_bias
    )
    return dict(
        normed_one=normed_one,
        inverse_one=inverse_one,
        first_low=first_low,
        queries=queries,
        keys_all=keys_all,
        values_all=values_all,
        attn_probs=attn_probs,
        probs_low=probs_low,
        attn_mixed=attn_mixed,
        normed_two=normed_two,
        inverse_two=inverse_two,
        second_low=second_low,
        hidden_pre=hidden_pre,
        hidden_low=hidden_low,
        result=result,
    )


def layer_backward(upstream, saved, small, weights):
    ln1_gain, ln1_bias, qv_bias, out_bias, ln2_gain, ln2_bias, fc_bias, proj_bias = small
    qkv_weight, out_weight, fc_weight, proj_weight = weights
    row_count = upstream.shape[0]
    width_all = upstream.shape[1]
    proj_in = upstream.astype(jnp.bfloat16)
    grad_proj_b = jnp.sum(to_float(proj_in), axis=0)
    hidden_grad = jnp.einsum("td,fd->tf", proj_in, proj_weight, preferred_element_type=jnp.float32)
    _, gelu_pull = jax.vjp(lambda value: jax.nn.gelu(value, approximate=True), saved["hidden_pre"])
    pre_grad = gelu_pull(hidden_grad)[0].astype(jnp.bfloat16)
    grad_fc_b = jnp.sum(to_float(pre_grad), axis=0)
    second_grad = jnp.einsum("tf,df->td", pre_grad, fc_weight, preferred_element_type=jnp.float32)
    norm_part, grad_ln2_g, grad_ln2_b = norm_back(
        second_grad, saved["normed_two"], saved["inverse_two"], ln2_gain
    )
    residual_grad = upstream + norm_part
    branch_in = residual_grad.astype(jnp.bfloat16)
    grad_out_b = jnp.sum(to_float(branch_in), axis=0)
    mixed_grad = jnp.einsum("td,cd->tc", branch_in, out_weight, preferred_element_type=jnp.float32)
    mixed_grad = mixed_grad.astype(jnp.bfloat16).reshape(row_count, HEADS, HEAD)
    prob_grad = jnp.einsum(
        "qhd,khd->hqk", mixed_grad, saved["values_all"], preferred_element_type=jnp.float32
    )
    value_grad = jnp.einsum(
        "hqk,qhd->khd", saved["probs_low"], mixed_grad, preferred_element_type=jnp.float32
    )
    attn_probs = saved["attn_probs"]
    row_delta = jnp.sum(attn_probs * prob_grad, axis=-1, keepdims=True)
    score_grad = (attn_probs * (prob_grad - row_delta)).astype(jnp.bfloat16)
    query_grad = jnp.einsum(
        "hqk,khd->qhd", score_grad, saved["keys_all"], preferred_element_type=jnp.float32
    ) * HEAD ** (-0.5)
    key_grad = jnp.einsum(
        "hqk,qhd->khd", score_grad, saved["queries"], preferred_element_type=jnp.float32
    ) * HEAD ** (-0.5)
    joined_grad = jnp.concatenate(
        [
            query_grad.reshape(row_count, width_all),
            key_grad.reshape(row_count, width_all),
            value_grad.reshape(row_count, width_all),
        ],
        axis=1,
    ).astype(jnp.bfloat16)
    column_sums = jnp.sum(to_float(joined_grad), axis=0)
    grad_qv_b = jnp.concatenate([column_sums[:width_all], column_sums[2 * width_all :]])
    first_grad = jnp.einsum(
        "te,ce->tc", joined_grad, qkv_weight, preferred_element_type=jnp.float32
    )
    norm_first, grad_ln1_g, grad_ln1_b = norm_back(
        first_grad, saved["normed_one"], saved["inverse_one"], ln1_gain
    )
    small_grads = (
        grad_ln1_g,
        grad_ln1_b,
        grad_qv_b,
        grad_out_b,
        grad_ln2_g,
        grad_ln2_b,
        grad_fc_b,
        grad_proj_b,
    )
    pairs = (
        (saved["first_low"], joined_grad),
        (saved["attn_mixed"], branch_in),
        (saved["second_low"], pre_grad),
        (saved["hidden_low"], proj_in),
    )
    return (residual_grad + norm_first, small_grads, pairs)


def ring_position(shard_index, n):
    if n != 8:
        return shard_index
    y = shard_index % 2
    z = shard_index // 2
    return z * (1 - 2 * y) + 7 * y


def ring_shard(position, n):
    position = position % n
    if n != 8:
        return position
    y = position // 4
    z = (position % 4) * (1 - 2 * y) + 3 * y
    return z * 2 + y


FIRST_CORE_HALF = (0, 3)


CHAIN_RANK = (2, 3, 0, 1, 4)
CHAIN_LAG = 0


X_ONLY = (2, 3)


def gather_kernel(n, count, *refs):
    local = refs[:count]
    full = refs[count : 2 * count]
    ring_send, ring_recv, pair_send, pair_recv, x_send, x_recv, relay_send, relay_recv = refs[2 * count :]
    rep = lax.axis_index("rep")
    shard = lax.axis_index("shard")
    core = rep % 2
    plane = rep // 2
    step_dir = 1 - 2 * core
    partner = (rep + step_dir, shard)
    x_partner = ((rep + 2) % 4, shard)
    here = ring_position(shard, n)
    target = (rep, ring_shard(here + step_dir, n))
    source = (rep, ring_shard(here - step_dir, n))
    steps = n // 2
    split_last = n % 2 == 0

    barrier = pltpu.get_barrier_semaphore()
    for peer in (target, source, partner, x_partner):
        pl.semaphore_signal(barrier, inc=1, device_id=peer, device_id_type=MESH)
    pl.semaphore_wait(barrier, 4)

    def both(a, b):
        if a is True:
            return b
        if b is True:
            return a
        return jnp.logical_and(a, b)

    def core_carries(k, w, which_core):
        if split_last and k == steps:
            return (which_core == 0) == (w in FIRST_CORE_HALF)
        return True

    def plane_carries(w, which_plane):
        if w == X_ONLY[0]:
            return which_plane == 0
        if w == X_ONLY[1]:
            return which_plane == 1
        return True

    def ring_in(k, w):
        return both(plane_carries(w, plane), core_carries(k, w, core))

    def x_out(k, w):
        if w not in X_ONLY:
            return False
        return both(plane_carries(w, plane), core_carries(k, w, core))

    def x_in(k, w):
        if w not in X_ONLY:
            return False
        return both(plane_carries(w, 1 - plane), core_carries(k, w, core))

    def partner_ring_in(k, w):
        return both(plane_carries(w, plane), core_carries(k, w, 1 - core))

    def partner_x_in(k, w):
        if w not in X_ONLY:
            return False
        return both(plane_carries(w, 1 - plane), core_carries(k, w, 1 - core))

    def guarded(cond, fn):
        if cond is False:
            return
        if cond is True:
            fn()
        else:
            pl.when(cond)(fn)

    def slot(position):
        return ring_shard(position, n)

    def remote(src, dst, ssem, rsem, device):
        return pltpu.make_async_remote_copy(
            src_ref=src, dst_ref=dst, send_sem=ssem, recv_sem=rsem, device_id=device, device_id_type=MESH
        )

    def ring_copy(k, w):
        src_pos = here - step_dir * (k - 1)
        src = local[w] if k == 1 else full[w].at[slot(src_pos)]
        return remote(src, full[w].at[slot(src_pos)], ring_send.at[k - 1, w], ring_recv.at[k - 1, w], target)

    def incoming_ring(k, w):
        pos = slot(here - step_dir * k)
        return remote(full[w].at[pos], full[w].at[pos], ring_send.at[k - 1, w], ring_recv.at[k - 1, w], source)

    def pair_copy(k, w, pos):
        src = local[w] if k == 0 else full[w].at[slot(pos)]
        return remote(src, full[w].at[slot(pos)], pair_send.at[k, w], pair_recv.at[k, w], partner)

    def x_copy(k, w):
        pos = slot(here - step_dir * k)
        return remote(full[w].at[pos], full[w].at[pos], x_send.at[k - 1, w], x_recv.at[k - 1, w], x_partner)

    def relay_copy(k, w, pos):
        pos = slot(pos)
        return remote(full[w].at[pos], full[w].at[pos], relay_send.at[k - 1, w], relay_recv.at[k - 1, w], partner)

    for w in range(count):
        pair_copy(0, w, here).start()
    for w in range(count):
        guarded(ring_in(1, w), lambda w=w: ring_copy(1, w).start())
    for k in range(1, steps + 1):
        for w in range(count):
            def arrived(k=k, w=w):
                incoming_ring(k, w).wait_recv()
                if k < steps:
                    guarded(ring_in(k + 1, w), lambda: ring_copy(k + 1, w).start())
                guarded(x_out(k, w), lambda: x_copy(k, w).start())
                pair_copy(k, w, here - step_dir * k).start()
            guarded(ring_in(k, w), arrived)
        for w in range(count):
            def crossed(k=k, w=w):
                x_copy(k, w).wait_recv()
                relay_copy(k, w, here - step_dir * k).start()
            guarded(x_in(k, w), crossed)
    for w in range(count):
        pair_copy(0, w, here).wait_recv()
    for k in range(1, steps + 1):
        for w in range(count):
            guarded(partner_ring_in(k, w), lambda k=k, w=w: pair_copy(k, w, here + step_dir * k).wait_recv())
            guarded(partner_x_in(k, w), lambda k=k, w=w: relay_copy(k, w, here + step_dir * k).wait_recv())
    for w in range(count):
        pair_copy(0, w, here).wait_send()
    for k in range(1, steps + 1):
        for w in range(count):
            def sent(k=k, w=w):
                ring_copy(k, w).wait_send()
                pair_copy(k, w, here - step_dir * k).wait_send()
            guarded(ring_in(k, w), sent)
            guarded(x_out(k, w), lambda k=k, w=w: x_copy(k, w).wait_send())
            guarded(x_in(k, w), lambda k=k, w=w: relay_copy(k, w, here - step_dir * k).wait_send())


def gather_weights(locals_, n):
    count = len(locals_)
    steps = n // 2
    dma = pltpu.SemaphoreType.DMA
    return pl.pallas_call(
        functools.partial(gather_kernel, n, count),
        out_shape=[jax.ShapeDtypeStruct((n,) + a.shape, a.dtype) for a in locals_],
        in_specs=[pl.BlockSpec(memory_space=pl.ANY)] * count,
        out_specs=[pl.BlockSpec(memory_space=pl.ANY)] * count,
        scratch_shapes=[
            dma((steps, count)),
            dma((steps, count)),
            dma((steps + 1, count)),
            dma((steps + 1, count)),
            dma((steps, count)),
            dma((steps, count)),
            dma((steps, count)),
            dma((steps, count)),
        ],
        compiler_params=pltpu.CompilerParams(collective_id=0, has_side_effects=True),
    )(*locals_)


def add_rows(dst, parts, rows, chunk):
    def body(i, carry):
        window = pl.ds(pl.multiple_of(i * chunk, chunk), chunk)
        total = parts[0][window, :].astype(jnp.float32)
        for part in parts[1:]:
            total = total + part[window, :].astype(jnp.float32)
        dst[window, :] = total.astype(dst.dtype)
        return carry

    lax.fori_loop(0, rows // chunk, body, 0)


def reduce_kernel(n, count, mm, *refs):
    xt = refs[:mm]
    dy = refs[mm : 2 * mm]
    contrib = (None,) * mm + refs[2 * mm : mm + count]
    refs = refs[mm + count :]
    out = refs[:count]
    land, send, other, own, xland, stage, xsend = (refs[count + i * count : count + (i + 1) * count] for i in range(7))
    (load_sem, own_sem, ring_send, ring_recv, pair_send, pair_recv, x_send, x_recv, back_send, back_recv) = refs[
        8 * count :
    ]
    rep = lax.axis_index("rep")
    shard = lax.axis_index("shard")
    core = rep % 2
    plane = rep // 2
    step_dir = 1 - 2 * core
    partner = (rep + step_dir, shard)
    x_partner = ((rep + 2) % 4, shard)
    here = ring_position(shard, n)
    target = (rep, ring_shard(here + step_dir, n))
    source = (rep, ring_shard(here - step_dir, n))
    steps = n // 2
    split_first = n % 2 == 0

    def carried(k, w):
        if split_first and k == 1:
            return (core == 0) == (w in FIRST_CORE_HALF)
        return True

    def guarded(cond, fn):
        if cond is True:
            fn()
        else:
            pl.when(cond)(fn)

    def block_at(k):
        return here + step_dir * (steps - k + 1)

    def load(k, w):
        return pltpu.make_async_copy(contrib[w].at[ring_shard(block_at(k), n)], send[w].at[k - 1], load_sem.at[k - 1, w])

    def load_own(w):
        return pltpu.make_async_copy(contrib[w].at[shard], own[w], own_sem.at[w])

    def remote(src, dst, ssem, rsem, device):
        return pltpu.make_async_remote_copy(
            src_ref=src, dst_ref=dst, send_sem=ssem, recv_sem=rsem, device_id=device, device_id_type=MESH
        )

    def ring_copy(k, w, device):
        return remote(send[w].at[k - 1], land[w].at[k - 1], ring_send.at[k - 1, w], ring_recv.at[k - 1, w], device)

    def pair_copy(w):
        return remote(land[w].at[steps - 1], other[w], pair_send.at[w], pair_recv.at[w], partner)

    def x_copy(w):
        return remote(xsend[w], xland[w], x_send.at[w], x_recv.at[w], x_partner)

    def back_copy(w):
        return remote(out[w], out[w], back_send.at[w], back_recv.at[w], partner)

    def owner(w):
        return core == w % 2

    def contribute(dst, w, position):
        block = ring_shard(position, n)
        width = 256

        def body(i, carry):
            window = pl.ds(pl.multiple_of(i * width, width), width)
            dst[:, window] = jnp.dot(xt[w][block], dy[w][:, window], preferred_element_type=jnp.float32)
            return carry

        lax.fori_loop(0, dy[w].shape[1] // width, body, 0)

    for w in range(mm, count):
        load_own(w).start()
    for k in range(1, steps + 1):
        for w in range(mm, count):
            guarded(carried(k, w), lambda k=k, w=w: load(k, w).start())

    barrier = pltpu.get_barrier_semaphore()
    for peer in (target, source, partner, x_partner):
        pl.semaphore_signal(barrier, inc=1, device_id=peer, device_id_type=MESH)
    pl.semaphore_wait(barrier, 4)

    def add_into(dst, parts):
        rows = dst.shape[0]
        chunk = 16 if rows % 16 == 0 else rows
        add_rows(dst, parts, rows, chunk)

    def step(k, w):
        if w < mm:
            if k == 1:
                contribute(stage[w], w, block_at(k))
            if k > 1:
                def accumulate():
                    ring_copy(k - 1, w, source).wait_recv()
                    add_into(send[w].at[k - 1], [stage[w], land[w].at[k - 2]])

                def start_chain():
                    contribute(stage[w], w, block_at(k))
                    add_into(send[w].at[k - 1], [stage[w]])

                cond = carried(k - 1, w)
                if cond is True:
                    accumulate()
                else:
                    pl.when(cond)(accumulate)
                    pl.when(jnp.logical_not(cond))(start_chain)
            else:
                add_into(send[w].at[k - 1], [stage[w]])
            ring_copy(k, w, target).start()
            if k < steps:
                contribute(stage[w], w, block_at(k + 1))
            else:
                pl.when(owner(w))(lambda: contribute(own[w], w, here))
        else:
            load(k, w).wait()
            if k > 1:
                def accumulate():
                    ring_copy(k - 1, w, source).wait_recv()
                    add_into(send[w].at[k - 1], [send[w].at[k - 1], land[w].at[k - 2]])
                guarded(carried(k - 1, w), accumulate)
            ring_copy(k, w, target).start()

    def arrive(w):
        ring_copy(steps, w, source).wait_recv()
        pl.when(jnp.logical_not(owner(w)))(lambda: pair_copy(w).start())
        mine = land[w].at[steps - 1]

        def plane():
            if w >= mm:
                load_own(w).wait()
            pair_copy(w).wait_recv()

            @pl.when(core == 0)
            def _():
                add_into(own[w], [own[w], mine, other[w]])

            @pl.when(core == 1)
            def _():
                add_into(own[w], [own[w], other[w], mine])

            add_into(xsend[w], [own[w]])
            x_copy(w).start()

        pl.when(owner(w))(plane)

    def total(w):
        x_copy(w).wait_recv()

        @pl.when(plane == 0)
        def _():
            add_into(out[w], [xsend[w], xland[w]])

        @pl.when(plane == 1)
        def _():
            add_into(out[w], [xland[w], xsend[w]])
        back_copy(w).start()

    rank = [CHAIN_RANK[w] if w < len(CHAIN_RANK) else w for w in range(count)]
    slots = steps + CHAIN_LAG * (count - 1)
    by_rank = sorted(range(count), key=lambda w: rank[w])
    for t in range(slots + 1):
        for w in by_rank:
            k = t - CHAIN_LAG * rank[w] + 1
            if 1 <= k <= steps:
                guarded(carried(k, w), lambda k=k, w=w: step(k, w))
        for w in by_rank:
            if steps + CHAIN_LAG * rank[w] == t:
                arrive(w)
    for w in range(count):
        pl.when(owner(w))(lambda w=w: total(w))

    for w in range(count):
        def not_owner(w=w):
            if w >= mm:
                load_own(w).wait()
            back_copy(w).wait_recv()
            pair_copy(w).wait_send()

        def was_owner(w=w):
            x_copy(w).wait_send()
            back_copy(w).wait_send()

        pl.when(owner(w))(was_owner)
        pl.when(jnp.logical_not(owner(w)))(not_owner)
    for k in range(1, steps + 1):
        for w in range(count):
            guarded(carried(k, w), lambda k=k, w=w: ring_copy(k, w, target).wait_send())


def reduce_gradients(pairs_t, contribs, n):
    mm = len(pairs_t)
    count = mm + len(contribs)
    steps = n // 2
    blocks = [(xt.shape[1], dy.shape[1]) for xt, dy in pairs_t] + [c.shape[1:] for c in contribs]
    ring_types = [jnp.bfloat16] * mm + [jnp.float32] * len(contribs)
    vmem = lambda shape, dtype=jnp.float32: pltpu.VMEM(shape, dtype)
    dma = pltpu.SemaphoreType.DMA
    return pl.pallas_call(
        functools.partial(reduce_kernel, n, count, mm),
        out_shape=[jax.ShapeDtypeStruct(b, jnp.float32) for b in blocks],
        in_specs=[pl.BlockSpec(memory_space=pltpu.VMEM)] * (2 * mm)
        + [pl.BlockSpec(memory_space=pl.ANY)] * len(contribs),
        out_specs=[pl.BlockSpec(memory_space=pltpu.VMEM)] * count,
        scratch_shapes=[vmem((steps,) + b, t) for b, t in zip(blocks, ring_types)]
        + [vmem((steps,) + b, t) for b, t in zip(blocks, ring_types)]
        + [vmem(b, t) for b, t in zip(blocks, ring_types)]
        + [vmem(b) for b in blocks]
        + [vmem(b, t) for b, t in zip(blocks, ring_types)]
        + [vmem(b) for b in blocks]
        + [vmem(b, t) for b, t in zip(blocks, ring_types)]
        + [
            dma((steps, count)),
            dma((count,)),
            dma((steps, count)),
            dma((steps, count)),
            dma((count,)),
            dma((count,)),
            dma((count,)),
            dma((count,)),
            dma((count,)),
            dma((count,)),
        ],
        compiler_params=pltpu.CompilerParams(
            collective_id=1, has_side_effects=True, vmem_limit_bytes=62 * 1024 * 1024
        ),
    )(*[xt for xt, _ in pairs_t], *[dy for _, dy in pairs_t], *contribs)


def swap_core(value):
    rep = lax.axis_size("rep")
    return lax.ppermute(value, "rep", perm=[(i, i ^ 1) for i in range(rep)])


def swap_x(value):
    rep = lax.axis_size("rep")
    return lax.ppermute(value, "rep", perm=[(i, i ^ 2) for i in range(rep)])


def join_halves(mine, theirs, core, axis):
    first = jnp.where(core == 0, mine, theirs)
    second = jnp.where(core == 0, theirs, mine)
    return jnp.concatenate([first, second], axis=axis)


def take_half(value, core, axis):
    half = value.shape[axis] // 2
    return lax.dynamic_slice_in_dim(value, core * half, half, axis=axis)


def per_device(
    tokens,
    segment_ids,
    cotangent,
    ln1_gain,
    ln1_bias,
    qkv_weight,
    qv_bias,
    out_weight,
    out_bias,
    ln2_gain,
    ln2_bias,
    fc_weight,
    fc_bias,
    proj_weight,
    proj_bias,
):
    rep = lax.axis_size("rep")
    assert rep == 4
    core = lax.axis_index("rep") % 2
    row_count = tokens.shape[0]
    positions = jnp.arange(row_count)
    allowed = (segment_ids[:, None] == segment_ids[None, :]) & (
        positions[None, :] <= positions[:, None]
    )
    layer_index = 0
    shard = lax.axis_size("shard")
    small_local = (ln1_gain, ln1_bias, qv_bias, out_bias, ln2_gain, ln2_bias, fc_bias, proj_bias)
    widths = [v.shape[1] for v in small_local]
    local_weights = (
        qkv_weight[layer_index],
        out_weight[layer_index],
        fc_weight[layer_index],
        proj_weight[layer_index],
    )
    rows_local = local_weights[0].shape[0]
    small_row = jnp.concatenate(small_local, axis=1)
    fulls = gather_weights(list(local_weights) + [small_row], shard)
    weights = tuple(f.reshape(-1, f.shape[-1]) for f in fulls[:4])
    halves = [take_half(w, core, 1) for w in local_weights]
    half_widths = [h.size // rows_local for h in halves]
    packed_all = fulls[4].reshape(shard, -1)
    small = []
    start = 0
    for width in widths:
        small.append(to_float(packed_all[:, start : start + width].reshape(-1)))
        start += width
    small = tuple(small)

    residual = to_float(tokens)
    saved = layer_forward(residual, allowed, small, weights)
    out_tokens = saved["result"].astype(jnp.bfloat16)
    upstream = to_float(cotangent)
    input_grad, small_grads, pairs = layer_backward(upstream, saved, small, weights)

    outgoing = jnp.concatenate([x for x, _ in pairs] + [dy for _, dy in pairs], axis=1)
    incoming = swap_core(outgoing)
    small_mine = jnp.concatenate([g.reshape(shard, -1) for g in small_grads], axis=1)
    small_theirs = swap_core(small_mine)
    small_chip = jnp.where(core == 0, small_mine + small_theirs, small_theirs + small_mine)
    start = 0
    partner_x = []
    for x, _ in pairs:
        partner_x.append(incoming[:, start : start + x.shape[1]])
        start += x.shape[1]
    pairs_t = []
    for (x, dy), px in zip(pairs, partner_x):
        pdy = incoming[:, start : start + dy.shape[1]]
        start += dy.shape[1]
        rows_t = jnp.concatenate([x, px], axis=0).T
        pairs_t.append((rows_t.reshape(shard, -1, rows_t.shape[1]), jnp.concatenate([dy, pdy], axis=0)))
    totals = reduce_gradients(pairs_t, [small_chip.reshape(shard, 1, -1)], shard)
    small_share = totals[4]
    owned = [t[None] for t in totals[:4]]
    small_owned = []
    start = 0
    for g in small_grads:
        width = g.shape[0] // shard
        small_owned.append(small_share[:, start : start + width])
        start += width

    (g_ln1_g, g_ln1_b, g_qv_b, g_out_b, g_ln2_g, g_ln2_b, g_fc_b, g_proj_b) = small_owned
    g_qkv, g_out, g_fc, g_proj = owned
    return (
        out_tokens,
        input_grad,
        g_ln1_g,
        g_ln1_b,
        g_qkv,
        g_qv_b,
        g_out,
        g_out_b,
        g_ln2_g,
        g_ln2_b,
        g_fc,
        g_fc_b,
        g_proj,
        g_proj_b,
    )


def solution(mesh):
    placed = (
        P(("rep", "shard"), None),
        P(("rep", "shard")),
        P(("rep", "shard"), None),
        P(None, "shard"),
        P(None, "shard"),
        P(None, "shard", None),
        P(None, "shard"),
        P(None, "shard", None),
        P(None, "shard"),
        P(None, "shard"),
        P(None, "shard"),
        P(None, "shard", None),
        P(None, "shard"),
        P(None, "shard", None),
        P(None, "shard"),
    )
    return jax.shard_map(
        per_device,
        mesh=mesh,
        in_specs=placed,
        out_specs=(
            P(("rep", "shard"), None),
            P(("rep", "shard"), None),
            P(None, "shard"),
            P(None, "shard"),
            P(None, "shard", None),
            P(None, "shard"),
            P(None, "shard", None),
            P(None, "shard"),
            P(None, "shard"),
            P(None, "shard"),
            P(None, "shard", None),
            P(None, "shard"),
            P(None, "shard", None),
            P(None, "shard"),
        ),
        check_vma=False,
    )
```

```python
import functools

import jax
import jax.numpy as jnp
from jax import lax
from jax.experimental import pallas as pl
from jax.experimental.pallas import tpu as pltpu
from jax.sharding import PartitionSpec as P

MESH = pl.DeviceIdType.MESH

HEADS = 12
HEAD = 64
LAYERS = 1

epsilon = 1e-05

def to_float(value):
    return value.astype(jnp.float32)


def layer_norm(inputs, norm_gain, norm_shift):
    center = inputs - jnp.mean(inputs, axis=-1, keepdims=True)
    inverse_std = lax.rsqrt(jnp.mean(center * center, axis=-1, keepdims=True) + epsilon)
    normed = center * inverse_std
    return (normed * norm_gain + norm_shift, normed, inverse_std)


def norm_back(upstream, normed, inverse_std, norm_gain):
    scaled = upstream * norm_gain
    inner_term = scaled - jnp.mean(scaled, axis=-1, keepdims=True)
    inner_term = inner_term - normed * jnp.mean(scaled * normed, axis=-1, keepdims=True)
    return (inverse_std * inner_term, jnp.sum(upstream * normed, axis=0), jnp.sum(upstream, axis=0))


def layer_forward(inputs, allowed, small, weights):
    ln1_gain, ln1_bias, qv_bias, out_bias, ln2_gain, ln2_bias, fc_bias, proj_bias = small
    qkv_weight, out_weight, fc_weight, proj_weight = weights
    row_count = inputs.shape[0]
    width_all = inputs.shape[1]
    first_norm, normed_one, inverse_one = layer_norm(inputs, ln1_gain, ln1_bias)
    first_low = first_norm.astype(jnp.bfloat16)
    offset = jnp.concatenate(
        [qv_bias[:width_all], jnp.zeros((width_all,), jnp.float32), qv_bias[width_all:]]
    )
    projected = (
        jnp.dot(first_low, qkv_weight, preferred_element_type=jnp.float32) + offset
    ).astype(jnp.bfloat16)
    queries = projected[:, :width_all].reshape(row_count, HEADS, HEAD)
    keys_all = projected[:, width_all : 2 * width_all].reshape(row_count, HEADS, HEAD)
    values_all = projected[:, 2 * width_all :].reshape(row_count, HEADS, HEAD)
    scores = jnp.einsum(
        "qhd,khd->hqk", queries, keys_all, preferred_element_type=jnp.float32
    ) * HEAD ** (-0.5)
    scores = jnp.where(allowed[None], scores, -1e30)
    row_max = jnp.max(scores, axis=-1, keepdims=True)
    log_total = row_max + jnp.log(jnp.sum(jnp.exp(scores - row_max), axis=-1, keepdims=True))
    attn_probs = jnp.exp(scores - log_total)
    probs_low = attn_probs.astype(jnp.bfloat16)
    attn_mixed = jnp.einsum(
        "hqk,khd->qhd", probs_low, values_all, preferred_element_type=jnp.float32
    )
    attn_mixed = attn_mixed.reshape(row_count, width_all).astype(jnp.bfloat16)
    after_attn = (
        inputs + jnp.dot(attn_mixed, out_weight, preferred_element_type=jnp.float32) + out_bias
    )
    second_norm, normed_two, inverse_two = layer_norm(after_attn, ln2_gain, ln2_bias)
    second_low = second_norm.astype(jnp.bfloat16)
    hidden_pre = jnp.dot(second_low, fc_weight, preferred_element_type=jnp.float32) + fc_bias
    hidden_low = jax.nn.gelu(hidden_pre, approximate=True).astype(jnp.bfloat16)
    result = (
        after_attn + jnp.dot(hidden_low, proj_weight, preferred_element_type=jnp.float32) + proj_bias
    )
    return dict(
        normed_one=normed_one,
        inverse_one=inverse_one,
        first_low=first_low,
        queries=queries,
        keys_all=keys_all,
        values_all=values_all,
        attn_probs=attn_probs,
        probs_low=probs_low,
        attn_mixed=attn_mixed,
        normed_two=normed_two,
        inverse_two=inverse_two,
        second_low=second_low,
        hidden_pre=hidden_pre,
        hidden_low=hidden_low,
        result=result,
    )


def layer_backward(upstream, saved, small, weights):
    ln1_gain, ln1_bias, qv_bias, out_bias, ln2_gain, ln2_bias, fc_bias, proj_bias = small
    qkv_weight, out_weight, fc_weight, proj_weight = weights
    row_count = upstream.shape[0]
    width_all = upstream.shape[1]
    proj_in = upstream.astype(jnp.bfloat16)
    grad_proj_b = jnp.sum(to_float(proj_in), axis=0)
    hidden_grad = jnp.einsum("td,fd->tf", proj_in, proj_weight, preferred_element_type=jnp.float32)
    _, gelu_pull = jax.vjp(lambda value: jax.nn.gelu(value, approximate=True), saved["hidden_pre"])
    pre_grad = gelu_pull(hidden_grad)[0].astype(jnp.bfloat16)
    grad_fc_b = jnp.sum(to_float(pre_grad), axis=0)
    second_grad = jnp.einsum("tf,df->td", pre_grad, fc_weight, preferred_element_type=jnp.float32)
    norm_part, grad_ln2_g, grad_ln2_b = norm_back(
        second_grad, saved["normed_two"], saved["inverse_two"], ln2_gain
    )
    residual_grad = upstream + norm_part
    branch_in = residual_grad.astype(jnp.bfloat16)
    grad_out_b = jnp.sum(to_float(branch_in), axis=0)
    mixed_grad = jnp.einsum("td,cd->tc", branch_in, out_weight, preferred_element_type=jnp.float32)
    mixed_grad = mixed_grad.astype(jnp.bfloat16).reshape(row_count, HEADS, HEAD)
    prob_grad = jnp.einsum(
        "qhd,khd->hqk", mixed_grad, saved["values_all"], preferred_element_type=jnp.float32
    )
    value_grad = jnp.einsum(
        "hqk,qhd->khd", saved["probs_low"], mixed_grad, preferred_element_type=jnp.float32
    )
    attn_probs = saved["attn_probs"]
    row_delta = jnp.sum(attn_probs * prob_grad, axis=-1, keepdims=True)
    score_grad = (attn_probs * (prob_grad - row_delta)).astype(jnp.bfloat16)
    query_grad = jnp.einsum(
        "hqk,khd->qhd", score_grad, saved["keys_all"], preferred_element_type=jnp.float32
    ) * HEAD ** (-0.5)
    key_grad = jnp.einsum(
        "hqk,qhd->khd", score_grad, saved["queries"], preferred_element_type=jnp.float32
    ) * HEAD ** (-0.5)
    joined_grad = jnp.concatenate(
        [
            query_grad.reshape(row_count, width_all),
            key_grad.reshape(row_count, width_all),
            value_grad.reshape(row_count, width_all),
        ],
        axis=1,
    ).astype(jnp.bfloat16)
    column_sums = jnp.sum(to_float(joined_grad), axis=0)
    grad_qv_b = jnp.concatenate([column_sums[:width_all], column_sums[2 * width_all :]])
    first_grad = jnp.einsum(
        "te,ce->tc", joined_grad, qkv_weight, preferred_element_type=jnp.float32
    )
    norm_first, grad_ln1_g, grad_ln1_b = norm_back(
        first_grad, saved["normed_one"], saved["inverse_one"], ln1_gain
    )
    small_grads = (
        grad_ln1_g,
        grad_ln1_b,
        grad_qv_b,
        grad_out_b,
        grad_ln2_g,
        grad_ln2_b,
        grad_fc_b,
        grad_proj_b,
    )
    pairs = (
        (saved["first_low"], joined_grad),
        (saved["attn_mixed"], branch_in),
        (saved["second_low"], pre_grad),
        (saved["hidden_low"], proj_in),
    )
    return (residual_grad + norm_first, small_grads, pairs)


def ring_position(shard_index, n):
    if n != 8:
        return shard_index
    y = shard_index % 2
    z = shard_index // 2
    return z * (1 - 2 * y) + 7 * y


def ring_shard(position, n):
    position = position % n
    if n != 8:
        return position
    y = position // 4
    z = (position % 4) * (1 - 2 * y) + 3 * y
    return z * 2 + y


FIRST_CORE_HALF = (0, 3)


CHAIN_RANK = (2, 3, 0, 1, 4)
CHAIN_LAG = 0


def gather_kernel(n, count, parts, plane_only, first_core, *refs):
    local = refs[:count]
    full = refs[count : 2 * count]
    ring_send, ring_recv, pair_send, pair_recv, x_send, x_recv, relay_send, relay_recv = refs[2 * count :]
    count = len(parts)

    def lview(w):
        array, row, rows = parts[w]
        return local[array] if rows is None else local[array].at[pl.ds(row, rows)]

    def fview(w, pos):
        array, row, rows = parts[w]
        return full[array].at[pos] if rows is None else full[array].at[pos, pl.ds(row, rows)]
    rep = lax.axis_index("rep")
    shard = lax.axis_index("shard")
    core = rep % 2
    plane = rep // 2
    step_dir = 1 - 2 * core
    partner = (rep + step_dir, shard)
    x_partner = ((rep + 2) % 4, shard)
    here = ring_position(shard, n)
    target = (rep, ring_shard(here + step_dir, n))
    source = (rep, ring_shard(here - step_dir, n))
    steps = n // 2
    split_last = n % 2 == 0

    barrier = pltpu.get_barrier_semaphore()
    for peer in (target, source, partner, x_partner):
        pl.semaphore_signal(barrier, inc=1, device_id=peer, device_id_type=MESH)
    pl.semaphore_wait(barrier, 4)

    def both(a, b):
        if a is True:
            return b
        if b is True:
            return a
        return jnp.logical_and(a, b)

    def core_carries(k, w, which_core):
        if split_last and k == steps:
            return (which_core == 0) == (w in first_core)
        return True

    def plane_carries(w, which_plane):
        for only, sole in enumerate(plane_only):
            if w in sole:
                return which_plane == only
        return True

    def ring_in(k, w):
        return both(plane_carries(w, plane), core_carries(k, w, core))

    def x_out(k, w):
        if not any(w in sole for sole in plane_only):
            return False
        return both(plane_carries(w, plane), core_carries(k, w, core))

    def x_in(k, w):
        if not any(w in sole for sole in plane_only):
            return False
        return both(plane_carries(w, 1 - plane), core_carries(k, w, core))

    def partner_ring_in(k, w):
        return both(plane_carries(w, plane), core_carries(k, w, 1 - core))

    def partner_x_in(k, w):
        if not any(w in sole for sole in plane_only):
            return False
        return both(plane_carries(w, 1 - plane), core_carries(k, w, 1 - core))

    def guarded(cond, fn):
        if cond is False:
            return
        if cond is True:
            fn()
        else:
            pl.when(cond)(fn)

    def slot(position):
        return ring_shard(position, n)

    def remote(src, dst, ssem, rsem, device):
        return pltpu.make_async_remote_copy(
            src_ref=src, dst_ref=dst, send_sem=ssem, recv_sem=rsem, device_id=device, device_id_type=MESH
        )

    def ring_copy(k, w):
        src_pos = here - step_dir * (k - 1)
        src = lview(w) if k == 1 else fview(w, slot(src_pos))
        return remote(src, fview(w, slot(src_pos)), ring_send.at[k - 1, w], ring_recv.at[k - 1, w], target)

    def incoming_ring(k, w):
        pos = slot(here - step_dir * k)
        return remote(fview(w, pos), fview(w, pos), ring_send.at[k - 1, w], ring_recv.at[k - 1, w], source)

    def pair_copy(k, w, pos):
        src = lview(w) if k == 0 else fview(w, slot(pos))
        return remote(src, fview(w, slot(pos)), pair_send.at[k, w], pair_recv.at[k, w], partner)

    def x_copy(k, w):
        pos = slot(here - step_dir * k)
        return remote(fview(w, pos), fview(w, pos), x_send.at[k - 1, w], x_recv.at[k - 1, w], x_partner)

    def relay_copy(k, w, pos):
        pos = slot(pos)
        return remote(fview(w, pos), fview(w, pos), relay_send.at[k - 1, w], relay_recv.at[k - 1, w], partner)

    for w in range(count):
        pair_copy(0, w, here).start()
    for w in range(count):
        guarded(ring_in(1, w), lambda w=w: ring_copy(1, w).start())
    for k in range(1, steps + 1):
        for w in range(count):
            def arrived(k=k, w=w):
                incoming_ring(k, w).wait_recv()
                if k < steps:
                    guarded(ring_in(k + 1, w), lambda: ring_copy(k + 1, w).start())
                guarded(x_out(k, w), lambda: x_copy(k, w).start())
                pair_copy(k, w, here - step_dir * k).start()
            guarded(ring_in(k, w), arrived)
        for w in range(count):
            def crossed(k=k, w=w):
                x_copy(k, w).wait_recv()
                relay_copy(k, w, here - step_dir * k).start()
            guarded(x_in(k, w), crossed)
    for w in range(count):
        pair_copy(0, w, here).wait_recv()
    for k in range(1, steps + 1):
        for w in range(count):
            guarded(partner_ring_in(k, w), lambda k=k, w=w: pair_copy(k, w, here + step_dir * k).wait_recv())
            guarded(partner_x_in(k, w), lambda k=k, w=w: relay_copy(k, w, here + step_dir * k).wait_recv())
    for w in range(count):
        pair_copy(0, w, here).wait_send()
    for k in range(1, steps + 1):
        for w in range(count):
            def sent(k=k, w=w):
                ring_copy(k, w).wait_send()
                pair_copy(k, w, here - step_dir * k).wait_send()
            guarded(ring_in(k, w), sent)
            guarded(x_out(k, w), lambda k=k, w=w: x_copy(k, w).wait_send())
            guarded(x_in(k, w), lambda k=k, w=w: relay_copy(k, w, here - step_dir * k).wait_send())


def gather_weights(locals_, n):
    count = len(locals_)
    steps = n // 2
    rows = locals_[2].shape[0]
    if n == 8 and rows % 32 == 0:
        half = rows // 2
        parts = ((0, 0, None), (1, 0, None), (2, 0, half), (2, half, half), (3, 0, None), (4, 0, None))
        plane_only = ((0,), (1, 2))
        first_core = (1, 4)
    else:
        parts = tuple((a, 0, None) for a in range(count))
        plane_only = ((),)
        first_core = FIRST_CORE_HALF
    pieces = len(parts)
    dma = pltpu.SemaphoreType.DMA
    return pl.pallas_call(
        functools.partial(gather_kernel, n, count, parts, plane_only, first_core),
        out_shape=[jax.ShapeDtypeStruct((n,) + a.shape, a.dtype) for a in locals_],
        in_specs=[pl.BlockSpec(memory_space=pl.ANY)] * count,
        out_specs=[pl.BlockSpec(memory_space=pl.ANY)] * count,
        scratch_shapes=[
            dma((steps, pieces)),
            dma((steps, pieces)),
            dma((steps + 1, pieces)),
            dma((steps + 1, pieces)),
            dma((steps, pieces)),
            dma((steps, pieces)),
            dma((steps, pieces)),
            dma((steps, pieces)),
        ],
        compiler_params=pltpu.CompilerParams(collective_id=0, has_side_effects=True),
    )(*locals_)


def add_rows(dst, parts, rows, chunk):
    def body(i, carry):
        window = pl.ds(pl.multiple_of(i * chunk, chunk), chunk)
        total = parts[0][window, :].astype(jnp.float32)
        for part in parts[1:]:
            total = total + part[window, :].astype(jnp.float32)
        dst[window, :] = total.astype(dst.dtype)
        return carry

    lax.fori_loop(0, rows // chunk, body, 0)


def reduce_kernel(n, count, mm, *refs):
    xt = refs[:mm]
    dy = refs[mm : 2 * mm]
    contrib = (None,) * mm + refs[2 * mm : mm + count]
    refs = refs[mm + count :]
    out = refs[:count]
    land, send, other, own, xland, stage, xsend = (refs[count + i * count : count + (i + 1) * count] for i in range(7))
    (load_sem, own_sem, ring_send, ring_recv, pair_send, pair_recv, x_send, x_recv, back_send, back_recv) = refs[
        8 * count :
    ]
    rep = lax.axis_index("rep")
    shard = lax.axis_index("shard")
    core = rep % 2
    plane = rep // 2
    step_dir = 1 - 2 * core
    partner = (rep + step_dir, shard)
    x_partner = ((rep + 2) % 4, shard)
    here = ring_position(shard, n)
    target = (rep, ring_shard(here + step_dir, n))
    source = (rep, ring_shard(here - step_dir, n))
    steps = n // 2
    split_first = n % 2 == 0

    def carried(k, w):
        if split_first and k == 1:
            return (core == 0) == (w in FIRST_CORE_HALF)
        return True

    def guarded(cond, fn):
        if cond is True:
            fn()
        else:
            pl.when(cond)(fn)

    def block_at(k):
        return here + step_dir * (steps - k + 1)

    def load(k, w):
        return pltpu.make_async_copy(contrib[w].at[ring_shard(block_at(k), n)], send[w].at[k - 1], load_sem.at[k - 1, w])

    def load_own(w):
        return pltpu.make_async_copy(contrib[w].at[shard], own[w], own_sem.at[w])

    def remote(src, dst, ssem, rsem, device):
        return pltpu.make_async_remote_copy(
            src_ref=src, dst_ref=dst, send_sem=ssem, recv_sem=rsem, device_id=device, device_id_type=MESH
        )

    def ring_copy(k, w, device):
        return remote(send[w].at[k - 1], land[w].at[k - 1], ring_send.at[k - 1, w], ring_recv.at[k - 1, w], device)

    def pair_copy(w):
        return remote(land[w].at[steps - 1], other[w], pair_send.at[w], pair_recv.at[w], partner)

    def x_copy(w):
        return remote(xsend[w], xland[w], x_send.at[w], x_recv.at[w], x_partner)

    def back_copy(w):
        return remote(out[w], out[w], back_send.at[w], back_recv.at[w], partner)

    def owner(w):
        return core == w % 2

    def contribute(dst, w, position):
        block = ring_shard(position, n)
        width = 256

        def body(i, carry):
            window = pl.ds(pl.multiple_of(i * width, width), width)
            dst[:, window] = jnp.dot(xt[w][block], dy[w][:, window], preferred_element_type=jnp.float32)
            return carry

        lax.fori_loop(0, dy[w].shape[1] // width, body, 0)

    for w in range(mm, count):
        load_own(w).start()
    for k in range(1, steps + 1):
        for w in range(mm, count):
            guarded(carried(k, w), lambda k=k, w=w: load(k, w).start())

    barrier = pltpu.get_barrier_semaphore()
    for peer in (target, source, partner, x_partner):
        pl.semaphore_signal(barrier, inc=1, device_id=peer, device_id_type=MESH)
    pl.semaphore_wait(barrier, 4)

    def add_into(dst, parts):
        rows = dst.shape[0]
        chunk = 16 if rows % 16 == 0 else rows
        add_rows(dst, parts, rows, chunk)

    def step(k, w):
        if w < mm:
            if k == 1:
                contribute(stage[w], w, block_at(k))
            if k > 1:
                def accumulate():
                    ring_copy(k - 1, w, source).wait_recv()
                    add_into(send[w].at[k - 1], [stage[w], land[w].at[k - 2]])

                def start_chain():
                    contribute(stage[w], w, block_at(k))
                    add_into(send[w].at[k - 1], [stage[w]])

                cond = carried(k - 1, w)
                if cond is True:
                    accumulate()
                else:
                    pl.when(cond)(accumulate)
                    pl.when(jnp.logical_not(cond))(start_chain)
            else:
                add_into(send[w].at[k - 1], [stage[w]])
            ring_copy(k, w, target).start()
            if k < steps:
                contribute(stage[w], w, block_at(k + 1))
            else:
                pl.when(owner(w))(lambda: contribute(own[w], w, here))
        else:
            load(k, w).wait()
            if k > 1:
                def accumulate():
                    ring_copy(k - 1, w, source).wait_recv()
                    add_into(send[w].at[k - 1], [send[w].at[k - 1], land[w].at[k - 2]])
                guarded(carried(k - 1, w), accumulate)
            ring_copy(k, w, target).start()

    def arrive(w):
        ring_copy(steps, w, source).wait_recv()
        pl.when(jnp.logical_not(owner(w)))(lambda: pair_copy(w).start())
        mine = land[w].at[steps - 1]

        def plane():
            if w >= mm:
                load_own(w).wait()
            pair_copy(w).wait_recv()

            @pl.when(core == 0)
            def _():
                add_into(own[w], [own[w], mine, other[w]])

            @pl.when(core == 1)
            def _():
                add_into(own[w], [own[w], other[w], mine])

            add_into(xsend[w], [own[w]])
            x_copy(w).start()

        pl.when(owner(w))(plane)

    def total(w):
        x_copy(w).wait_recv()

        @pl.when(plane == 0)
        def _():
            add_into(out[w], [xsend[w], xland[w]])

        @pl.when(plane == 1)
        def _():
            add_into(out[w], [xland[w], xsend[w]])
        back_copy(w).start()

    rank = [CHAIN_RANK[w] if w < len(CHAIN_RANK) else w for w in range(count)]
    slots = steps + CHAIN_LAG * (count - 1)
    by_rank = sorted(range(count), key=lambda w: rank[w])
    for t in range(slots + 1):
        for w in by_rank:
            k = t - CHAIN_LAG * rank[w] + 1
            if 1 <= k <= steps:
                guarded(carried(k, w), lambda k=k, w=w: step(k, w))
        for w in by_rank:
            if steps + CHAIN_LAG * rank[w] == t:
                arrive(w)
    for w in range(count):
        pl.when(owner(w))(lambda w=w: total(w))

    for w in range(count):
        def not_owner(w=w):
            if w >= mm:
                load_own(w).wait()
            back_copy(w).wait_recv()
            pair_copy(w).wait_send()

        def was_owner(w=w):
            x_copy(w).wait_send()
            back_copy(w).wait_send()

        pl.when(owner(w))(was_owner)
        pl.when(jnp.logical_not(owner(w)))(not_owner)
    for k in range(1, steps + 1):
        for w in range(count):
            guarded(carried(k, w), lambda k=k, w=w: ring_copy(k, w, target).wait_send())


def reduce_gradients(pairs_t, contribs, n):
    mm = len(pairs_t)
    count = mm + len(contribs)
    steps = n // 2
    blocks = [(xt.shape[1], dy.shape[1]) for xt, dy in pairs_t] + [c.shape[1:] for c in contribs]
    ring_types = [jnp.bfloat16] * mm + [jnp.float32] * len(contribs)
    vmem = lambda shape, dtype=jnp.float32: pltpu.VMEM(shape, dtype)
    dma = pltpu.SemaphoreType.DMA
    return pl.pallas_call(
        functools.partial(reduce_kernel, n, count, mm),
        out_shape=[jax.ShapeDtypeStruct(b, jnp.float32) for b in blocks],
        in_specs=[pl.BlockSpec(memory_space=pltpu.VMEM)] * (2 * mm)
        + [pl.BlockSpec(memory_space=pl.ANY)] * len(contribs),
        out_specs=[pl.BlockSpec(memory_space=pltpu.VMEM)] * count,
        scratch_shapes=[vmem((steps,) + b, t) for b, t in zip(blocks, ring_types)]
        + [vmem((steps,) + b, t) for b, t in zip(blocks, ring_types)]
        + [vmem(b, t) for b, t in zip(blocks, ring_types)]
        + [vmem(b) for b in blocks]
        + [vmem(b, t) for b, t in zip(blocks, ring_types)]
        + [vmem(b) for b in blocks]
        + [vmem(b, t) for b, t in zip(blocks, ring_types)]
        + [
            dma((steps, count)),
            dma((count,)),
            dma((steps, count)),
            dma((steps, count)),
            dma((count,)),
            dma((count,)),
            dma((count,)),
            dma((count,)),
            dma((count,)),
            dma((count,)),
        ],
        compiler_params=pltpu.CompilerParams(
            collective_id=1, has_side_effects=True, vmem_limit_bytes=62 * 1024 * 1024
        ),
    )(*[xt for xt, _ in pairs_t], *[dy for _, dy in pairs_t], *contribs)


def swap_core(value):
    rep = lax.axis_size("rep")
    return lax.ppermute(value, "rep", perm=[(i, i ^ 1) for i in range(rep)])


def swap_x(value):
    rep = lax.axis_size("rep")
    return lax.ppermute(value, "rep", perm=[(i, i ^ 2) for i in range(rep)])


def join_halves(mine, theirs, core, axis):
    first = jnp.where(core == 0, mine, theirs)
    second = jnp.where(core == 0, theirs, mine)
    return jnp.concatenate([first, second], axis=axis)


def take_half(value, core, axis):
    half = value.shape[axis] // 2
    return lax.dynamic_slice_in_dim(value, core * half, half, axis=axis)


def per_device(
    tokens,
    segment_ids,
    cotangent,
    ln1_gain,
    ln1_bias,
    qkv_weight,
    qv_bias,
    out_weight,
    out_bias,
    ln2_gain,
    ln2_bias,
    fc_weight,
    fc_bias,
    proj_weight,
    proj_bias,
):
    rep = lax.axis_size("rep")
    assert rep == 4
    core = lax.axis_index("rep") % 2
    row_count = tokens.shape[0]
    positions = jnp.arange(row_count)
    allowed = (segment_ids[:, None] == segment_ids[None, :]) & (
        positions[None, :] <= positions[:, None]
    )
    layer_index = 0
    shard = lax.axis_size("shard")
    small_local = (ln1_gain, ln1_bias, qv_bias, out_bias, ln2_gain, ln2_bias, fc_bias, proj_bias)
    widths = [v.shape[1] for v in small_local]
    local_weights = (
        qkv_weight[layer_index],
        out_weight[layer_index],
        fc_weight[layer_index],
        proj_weight[layer_index],
    )
    rows_local = local_weights[0].shape[0]
    small_row = jnp.concatenate(small_local, axis=1)
    fulls = gather_weights(list(local_weights) + [small_row], shard)
    weights = tuple(f.reshape(-1, f.shape[-1]) for f in fulls[:4])
    halves = [take_half(w, core, 1) for w in local_weights]
    half_widths = [h.size // rows_local for h in halves]
    packed_all = fulls[4].reshape(shard, -1)
    small = []
    start = 0
    for width in widths:
        small.append(to_float(packed_all[:, start : start + width].reshape(-1)))
        start += width
    small = tuple(small)

    residual = to_float(tokens)
    saved = layer_forward(residual, allowed, small, weights)
    out_tokens = saved["result"].astype(jnp.bfloat16)
    upstream = to_float(cotangent)
    input_grad, small_grads, pairs = layer_backward(upstream, saved, small, weights)

    outgoing = jnp.concatenate([x for x, _ in pairs] + [dy for _, dy in pairs], axis=1)
    incoming = swap_core(outgoing)
    small_mine = jnp.concatenate([g.reshape(shard, -1) for g in small_grads], axis=1)
    small_theirs = swap_core(small_mine)
    small_chip = jnp.where(core == 0, small_mine + small_theirs, small_theirs + small_mine)
    start = 0
    partner_x = []
    for x, _ in pairs:
        partner_x.append(incoming[:, start : start + x.shape[1]])
        start += x.shape[1]
    pairs_t = []
    for (x, dy), px in zip(pairs, partner_x):
        pdy = incoming[:, start : start + dy.shape[1]]
        start += dy.shape[1]
        rows_t = jnp.concatenate([x, px], axis=0).T
        pairs_t.append((rows_t.reshape(shard, -1, rows_t.shape[1]), jnp.concatenate([dy, pdy], axis=0)))
    totals = reduce_gradients(pairs_t, [small_chip.reshape(shard, 1, -1)], shard)
    small_share = totals[4]
    owned = [t[None] for t in totals[:4]]
    small_owned = []
    start = 0
    for g in small_grads:
        width = g.shape[0] // shard
        small_owned.append(small_share[:, start : start + width])
        start += width

    (g_ln1_g, g_ln1_b, g_qv_b, g_out_b, g_ln2_g, g_ln2_b, g_fc_b, g_proj_b) = small_owned
    g_qkv, g_out, g_fc, g_proj = owned
    return (
        out_tokens,
        input_grad,
        g_ln1_g,
        g_ln1_b,
        g_qkv,
        g_qv_b,
        g_out,
        g_out_b,
        g_ln2_g,
        g_ln2_b,
        g_fc,
        g_fc_b,
        g_proj,
        g_proj_b,
    )


def solution(mesh):
    placed = (
        P(("rep", "shard"), None),
        P(("rep", "shard")),
        P(("rep", "shard"), None),
        P(None, "shard"),
        P(None, "shard"),
        P(None, "shard", None),
        P(None, "shard"),
        P(None, "shard", None),
        P(None, "shard"),
        P(None, "shard"),
        P(None, "shard"),
        P(None, "shard", None),
        P(None, "shard"),
        P(None, "shard", None),
        P(None, "shard"),
    )
    return jax.shard_map(
        per_device,
        mesh=mesh,
        in_specs=placed,
        out_specs=(
            P(("rep", "shard"), None),
            P(("rep", "shard"), None),
            P(None, "shard"),
            P(None, "shard"),
            P(None, "shard", None),
            P(None, "shard"),
            P(None, "shard", None),
            P(None, "shard"),
            P(None, "shard"),
            P(None, "shard"),
            P(None, "shard", None),
            P(None, "shard"),
            P(None, "shard", None),
            P(None, "shard"),
        ),
        check_vma=False,
    )
```

```python
import functools

import jax
import jax.numpy as jnp
from jax import lax
from jax.experimental import pallas as pl
from jax.experimental.pallas import tpu as pltpu
from jax.sharding import PartitionSpec as P

MESH = pl.DeviceIdType.MESH

HEADS = 12
HEAD = 64
LAYERS = 1

epsilon = 1e-05

def to_float(value):
    return value.astype(jnp.float32)


def layer_norm(inputs, norm_gain, norm_shift):
    center = inputs - jnp.mean(inputs, axis=-1, keepdims=True)
    inverse_std = lax.rsqrt(jnp.mean(center * center, axis=-1, keepdims=True) + epsilon)
    normed = center * inverse_std
    return (normed * norm_gain + norm_shift, normed, inverse_std)


def norm_back(upstream, normed, inverse_std, norm_gain):
    scaled = upstream * norm_gain
    inner_term = scaled - jnp.mean(scaled, axis=-1, keepdims=True)
    inner_term = inner_term - normed * jnp.mean(scaled * normed, axis=-1, keepdims=True)
    return (inverse_std * inner_term, jnp.sum(upstream * normed, axis=0), jnp.sum(upstream, axis=0))


def layer_forward(inputs, allowed, small, weights):
    ln1_gain, ln1_bias, qv_bias, out_bias, ln2_gain, ln2_bias, fc_bias, proj_bias = small
    qkv_weight, out_weight, fc_weight, proj_weight = weights
    row_count = inputs.shape[0]
    width_all = inputs.shape[1]
    first_norm, normed_one, inverse_one = layer_norm(inputs, ln1_gain, ln1_bias)
    first_low = first_norm.astype(jnp.bfloat16)
    offset = jnp.concatenate(
        [qv_bias[:width_all], jnp.zeros((width_all,), jnp.float32), qv_bias[width_all:]]
    )
    projected = (
        jnp.dot(first_low, qkv_weight, preferred_element_type=jnp.float32) + offset
    ).astype(jnp.bfloat16)
    queries = projected[:, :width_all].reshape(row_count, HEADS, HEAD)
    keys_all = projected[:, width_all : 2 * width_all].reshape(row_count, HEADS, HEAD)
    values_all = projected[:, 2 * width_all :].reshape(row_count, HEADS, HEAD)
    scores = jnp.einsum(
        "qhd,khd->hqk", queries, keys_all, preferred_element_type=jnp.float32
    ) * HEAD ** (-0.5)
    scores = jnp.where(allowed[None], scores, -1e30)
    row_max = jnp.max(scores, axis=-1, keepdims=True)
    log_total = row_max + jnp.log(jnp.sum(jnp.exp(scores - row_max), axis=-1, keepdims=True))
    attn_probs = jnp.exp(scores - log_total)
    probs_low = attn_probs.astype(jnp.bfloat16)
    attn_mixed = jnp.einsum(
        "hqk,khd->qhd", probs_low, values_all, preferred_element_type=jnp.float32
    )
    attn_mixed = attn_mixed.reshape(row_count, width_all).astype(jnp.bfloat16)
    after_attn = (
        inputs + jnp.dot(attn_mixed, out_weight, preferred_element_type=jnp.float32) + out_bias
    )
    second_norm, normed_two, inverse_two = layer_norm(after_attn, ln2_gain, ln2_bias)
    second_low = second_norm.astype(jnp.bfloat16)
    hidden_pre = jnp.dot(second_low, fc_weight, preferred_element_type=jnp.float32) + fc_bias
    hidden_low = jax.nn.gelu(hidden_pre, approximate=True).astype(jnp.bfloat16)
    result = (
        after_attn + jnp.dot(hidden_low, proj_weight, preferred_element_type=jnp.float32) + proj_bias
    )
    return dict(
        normed_one=normed_one,
        inverse_one=inverse_one,
        first_low=first_low,
        queries=queries,
        keys_all=keys_all,
        values_all=values_all,
        attn_probs=attn_probs,
        probs_low=probs_low,
        attn_mixed=attn_mixed,
        normed_two=normed_two,
        inverse_two=inverse_two,
        second_low=second_low,
        hidden_pre=hidden_pre,
        hidden_low=hidden_low,
        result=result,
    )


def layer_backward(upstream, saved, small, weights):
    ln1_gain, ln1_bias, qv_bias, out_bias, ln2_gain, ln2_bias, fc_bias, proj_bias = small
    qkv_weight, out_weight, fc_weight, proj_weight = weights
    row_count = upstream.shape[0]
    width_all = upstream.shape[1]
    proj_in = upstream.astype(jnp.bfloat16)
    grad_proj_b = jnp.sum(to_float(proj_in), axis=0)
    hidden_grad = jnp.einsum("td,fd->tf", proj_in, proj_weight, preferred_element_type=jnp.float32)
    _, gelu_pull = jax.vjp(lambda value: jax.nn.gelu(value, approximate=True), saved["hidden_pre"])
    pre_grad = gelu_pull(hidden_grad)[0].astype(jnp.bfloat16)
    grad_fc_b = jnp.sum(to_float(pre_grad), axis=0)
    second_grad = jnp.einsum("tf,df->td", pre_grad, fc_weight, preferred_element_type=jnp.float32)
    norm_part, grad_ln2_g, grad_ln2_b = norm_back(
        second_grad, saved["normed_two"], saved["inverse_two"], ln2_gain
    )
    residual_grad = upstream + norm_part
    branch_in = residual_grad.astype(jnp.bfloat16)
    grad_out_b = jnp.sum(to_float(branch_in), axis=0)
    mixed_grad = jnp.einsum("td,cd->tc", branch_in, out_weight, preferred_element_type=jnp.float32)
    mixed_grad = mixed_grad.astype(jnp.bfloat16).reshape(row_count, HEADS, HEAD)
    prob_grad = jnp.einsum(
        "qhd,khd->hqk", mixed_grad, saved["values_all"], preferred_element_type=jnp.float32
    )
    value_grad = jnp.einsum(
        "hqk,qhd->khd", saved["probs_low"], mixed_grad, preferred_element_type=jnp.float32
    )
    attn_probs = saved["attn_probs"]
    row_delta = jnp.sum(attn_probs * prob_grad, axis=-1, keepdims=True)
    score_grad = (attn_probs * (prob_grad - row_delta)).astype(jnp.bfloat16)
    query_grad = jnp.einsum(
        "hqk,khd->qhd", score_grad, saved["keys_all"], preferred_element_type=jnp.float32
    ) * HEAD ** (-0.5)
    key_grad = jnp.einsum(
        "hqk,qhd->khd", score_grad, saved["queries"], preferred_element_type=jnp.float32
    ) * HEAD ** (-0.5)
    joined_grad = jnp.concatenate(
        [
            query_grad.reshape(row_count, width_all),
            key_grad.reshape(row_count, width_all),
            value_grad.reshape(row_count, width_all),
        ],
        axis=1,
    ).astype(jnp.bfloat16)
    column_sums = jnp.sum(to_float(joined_grad), axis=0)
    grad_qv_b = jnp.concatenate([column_sums[:width_all], column_sums[2 * width_all :]])
    first_grad = jnp.einsum(
        "te,ce->tc", joined_grad, qkv_weight, preferred_element_type=jnp.float32
    )
    norm_first, grad_ln1_g, grad_ln1_b = norm_back(
        first_grad, saved["normed_one"], saved["inverse_one"], ln1_gain
    )
    small_grads = (
        grad_ln1_g,
        grad_ln1_b,
        grad_qv_b,
        grad_out_b,
        grad_ln2_g,
        grad_ln2_b,
        grad_fc_b,
        grad_proj_b,
    )
    pairs = (
        (saved["first_low"], joined_grad),
        (saved["attn_mixed"], branch_in),
        (saved["second_low"], pre_grad),
        (saved["hidden_low"], proj_in),
    )
    return (residual_grad + norm_first, small_grads, pairs)


def ring_position(shard_index, n):
    if n != 8:
        return shard_index
    y = shard_index % 2
    z = shard_index // 2
    return z * (1 - 2 * y) + 7 * y


def ring_shard(position, n):
    position = position % n
    if n != 8:
        return position
    y = position // 4
    z = (position % 4) * (1 - 2 * y) + 3 * y
    return z * 2 + y


FIRST_CORE_HALF = (0, 3)


CHAIN_RANK = (2, 3, 0, 1, 4)
CHAIN_LAG = 0


def gather_kernel(n, count, parts, plane_only, first_core, *refs):
    local = refs[:count]
    full = refs[count : 2 * count]
    ring_send, ring_recv, pair_send, pair_recv, x_send, x_recv, relay_send, relay_recv = refs[2 * count :]
    count = len(parts)

    def lview(w):
        array, row, rows = parts[w]
        return local[array] if rows is None else local[array].at[pl.ds(row, rows)]

    def fview(w, pos):
        array, row, rows = parts[w]
        return full[array].at[pos] if rows is None else full[array].at[pos, pl.ds(row, rows)]
    rep = lax.axis_index("rep")
    shard = lax.axis_index("shard")
    core = rep % 2
    plane = rep // 2
    step_dir = 1 - 2 * core
    partner = (rep + step_dir, shard)
    x_partner = ((rep + 2) % 4, shard)
    here = ring_position(shard, n)
    target = (rep, ring_shard(here + step_dir, n))
    source = (rep, ring_shard(here - step_dir, n))
    steps = n // 2
    split_last = n % 2 == 0

    barrier = pltpu.get_barrier_semaphore()
    for peer in (target, source, partner, x_partner):
        pl.semaphore_signal(barrier, inc=1, device_id=peer, device_id_type=MESH)
    pl.semaphore_wait(barrier, 4)

    def both(a, b):
        if a is True:
            return b
        if b is True:
            return a
        return jnp.logical_and(a, b)

    def core_carries(k, w, which_core):
        if split_last and k == steps:
            return (which_core == 0) == (w in first_core)
        return True

    def plane_carries(w, which_plane):
        for only, sole in enumerate(plane_only):
            if w in sole:
                return which_plane == only
        return True

    def ring_in(k, w):
        return both(plane_carries(w, plane), core_carries(k, w, core))

    def x_out(k, w):
        if not any(w in sole for sole in plane_only):
            return False
        return both(plane_carries(w, plane), core_carries(k, w, core))

    def x_in(k, w):
        if not any(w in sole for sole in plane_only):
            return False
        return both(plane_carries(w, 1 - plane), core_carries(k, w, core))

    def partner_ring_in(k, w):
        return both(plane_carries(w, plane), core_carries(k, w, 1 - core))

    def partner_x_in(k, w):
        if not any(w in sole for sole in plane_only):
            return False
        return both(plane_carries(w, 1 - plane), core_carries(k, w, 1 - core))

    def guarded(cond, fn):
        if cond is False:
            return
        if cond is True:
            fn()
        else:
            pl.when(cond)(fn)

    def slot(position):
        return ring_shard(position, n)

    def remote(src, dst, ssem, rsem, device):
        return pltpu.make_async_remote_copy(
            src_ref=src, dst_ref=dst, send_sem=ssem, recv_sem=rsem, device_id=device, device_id_type=MESH
        )

    def ring_copy(k, w):
        src_pos = here - step_dir * (k - 1)
        src = lview(w) if k == 1 else fview(w, slot(src_pos))
        return remote(src, fview(w, slot(src_pos)), ring_send.at[k - 1, w], ring_recv.at[k - 1, w], target)

    def incoming_ring(k, w):
        pos = slot(here - step_dir * k)
        return remote(fview(w, pos), fview(w, pos), ring_send.at[k - 1, w], ring_recv.at[k - 1, w], source)

    def pair_copy(k, w, pos):
        src = lview(w) if k == 0 else fview(w, slot(pos))
        return remote(src, fview(w, slot(pos)), pair_send.at[k, w], pair_recv.at[k, w], partner)

    def x_copy(k, w):
        pos = slot(here - step_dir * k)
        return remote(fview(w, pos), fview(w, pos), x_send.at[k - 1, w], x_recv.at[k - 1, w], x_partner)

    def relay_copy(k, w, pos):
        pos = slot(pos)
        return remote(fview(w, pos), fview(w, pos), relay_send.at[k - 1, w], relay_recv.at[k - 1, w], partner)

    for w in range(count):
        pair_copy(0, w, here).start()
    for w in range(count):
        guarded(ring_in(1, w), lambda w=w: ring_copy(1, w).start())
    for k in range(1, steps + 1):
        for w in range(count):
            def arrived(k=k, w=w):
                incoming_ring(k, w).wait_recv()
                if k < steps:
                    guarded(ring_in(k + 1, w), lambda: ring_copy(k + 1, w).start())
                guarded(x_out(k, w), lambda: x_copy(k, w).start())
                pair_copy(k, w, here - step_dir * k).start()
            guarded(ring_in(k, w), arrived)
        for w in range(count):
            def crossed(k=k, w=w):
                x_copy(k, w).wait_recv()
                relay_copy(k, w, here - step_dir * k).start()
            guarded(x_in(k, w), crossed)
    for w in range(count):
        pair_copy(0, w, here).wait_recv()
    for k in range(1, steps + 1):
        for w in range(count):
            guarded(partner_ring_in(k, w), lambda k=k, w=w: pair_copy(k, w, here + step_dir * k).wait_recv())
            guarded(partner_x_in(k, w), lambda k=k, w=w: relay_copy(k, w, here + step_dir * k).wait_recv())
    for w in range(count):
        pair_copy(0, w, here).wait_send()
    for k in range(1, steps + 1):
        for w in range(count):
            def sent(k=k, w=w):
                ring_copy(k, w).wait_send()
                pair_copy(k, w, here - step_dir * k).wait_send()
            guarded(ring_in(k, w), sent)
            guarded(x_out(k, w), lambda k=k, w=w: x_copy(k, w).wait_send())
            guarded(x_in(k, w), lambda k=k, w=w: relay_copy(k, w, here - step_dir * k).wait_send())


def gather_weights(locals_, n):
    count = len(locals_)
    steps = n // 2
    rows = locals_[2].shape[0]
    if n == 8 and rows % 32 == 0:
        half = rows // 2
        parts = ((0, 0, None), (1, 0, None), (2, 0, half), (2, half, half), (3, 0, None), (4, 0, None))
        plane_only = ((0,), (1, 2))
        first_core = (1, 4)
    else:
        parts = tuple((a, 0, None) for a in range(count))
        plane_only = ((),)
        first_core = FIRST_CORE_HALF
    pieces = len(parts)
    dma = pltpu.SemaphoreType.DMA
    return pl.pallas_call(
        functools.partial(gather_kernel, n, count, parts, plane_only, first_core),
        out_shape=[jax.ShapeDtypeStruct((n,) + a.shape, a.dtype) for a in locals_],
        in_specs=[pl.BlockSpec(memory_space=pl.ANY)] * count,
        out_specs=[pl.BlockSpec(memory_space=pl.ANY)] * count,
        scratch_shapes=[
            dma((steps, pieces)),
            dma((steps, pieces)),
            dma((steps + 1, pieces)),
            dma((steps + 1, pieces)),
            dma((steps, pieces)),
            dma((steps, pieces)),
            dma((steps, pieces)),
            dma((steps, pieces)),
        ],
        compiler_params=pltpu.CompilerParams(collective_id=0, has_side_effects=True),
    )(*locals_)


def add_rows(dst, parts, rows, chunk):
    def body(i, carry):
        window = pl.ds(pl.multiple_of(i * chunk, chunk), chunk)
        total = parts[0][window, :].astype(jnp.float32)
        for part in parts[1:]:
            total = total + part[window, :].astype(jnp.float32)
        dst[window, :] = total.astype(dst.dtype)
        return carry

    lax.fori_loop(0, rows // chunk, body, 0)


def reduce_kernel(n, count, mm, *refs):
    xt = refs[:mm]
    dy = refs[mm : 2 * mm]
    xtp = refs[2 * mm : 3 * mm]
    dyp = refs[3 * mm : 4 * mm]
    contrib = (None,) * mm + refs[4 * mm : 3 * mm + count]
    refs = refs[3 * mm + count :]
    out = refs[:count]
    land, send, other, own, xland, stage, xsend = (refs[count + i * count : count + (i + 1) * count] for i in range(7))
    (load_sem, own_sem, ring_send, ring_recv, pair_send, pair_recv, x_send, x_recv, back_send, back_recv) = refs[
        8 * count :
    ]
    rep = lax.axis_index("rep")
    shard = lax.axis_index("shard")
    core = rep % 2
    plane = rep // 2
    step_dir = 1 - 2 * core
    partner = (rep + step_dir, shard)
    x_partner = ((rep + 2) % 4, shard)
    here = ring_position(shard, n)
    target = (rep, ring_shard(here + step_dir, n))
    source = (rep, ring_shard(here - step_dir, n))
    steps = n // 2
    split_first = n % 2 == 0

    def carried(k, w):
        if split_first and k == 1:
            return (core == 0) == (w in FIRST_CORE_HALF)
        return True

    def guarded(cond, fn):
        if cond is True:
            fn()
        else:
            pl.when(cond)(fn)

    def block_at(k):
        return here + step_dir * (steps - k + 1)

    def load(k, w):
        return pltpu.make_async_copy(contrib[w].at[ring_shard(block_at(k), n)], send[w].at[k - 1], load_sem.at[k - 1, w])

    def load_own(w):
        return pltpu.make_async_copy(contrib[w].at[shard], own[w], own_sem.at[w])

    def remote(src, dst, ssem, rsem, device):
        return pltpu.make_async_remote_copy(
            src_ref=src, dst_ref=dst, send_sem=ssem, recv_sem=rsem, device_id=device, device_id_type=MESH
        )

    def ring_copy(k, w, device):
        return remote(send[w].at[k - 1], land[w].at[k - 1], ring_send.at[k - 1, w], ring_recv.at[k - 1, w], device)

    def pair_copy(w):
        return remote(land[w].at[steps - 1], other[w], pair_send.at[w], pair_recv.at[w], partner)

    def x_copy(w):
        return remote(xsend[w], xland[w], x_send.at[w], x_recv.at[w], x_partner)

    def back_copy(w):
        return remote(out[w], out[w], back_send.at[w], back_recv.at[w], partner)

    def owner(w):
        return core == w % 2

    def contribute(dst, w, position):
        block = ring_shard(position, n)
        width = 256

        def body(i, carry):
            window = pl.ds(pl.multiple_of(i * width, width), width)
            dst[:, window] = jnp.dot(
                xt[w][block], dy[w][:, window], preferred_element_type=jnp.float32
            ) + jnp.dot(xtp[w][block], dyp[w][:, window], preferred_element_type=jnp.float32)
            return carry

        lax.fori_loop(0, dy[w].shape[1] // width, body, 0)

    for w in range(mm, count):
        load_own(w).start()
    for k in range(1, steps + 1):
        for w in range(mm, count):
            guarded(carried(k, w), lambda k=k, w=w: load(k, w).start())

    barrier = pltpu.get_barrier_semaphore()
    for peer in (target, source, partner, x_partner):
        pl.semaphore_signal(barrier, inc=1, device_id=peer, device_id_type=MESH)
    pl.semaphore_wait(barrier, 4)

    def add_into(dst, parts):
        rows = dst.shape[0]
        chunk = 16 if rows % 16 == 0 else rows
        add_rows(dst, parts, rows, chunk)

    def step(k, w):
        if w < mm:
            if k == 1:
                contribute(stage[w], w, block_at(k))
            if k > 1:
                def accumulate():
                    ring_copy(k - 1, w, source).wait_recv()
                    add_into(send[w].at[k - 1], [stage[w], land[w].at[k - 2]])

                def start_chain():
                    contribute(stage[w], w, block_at(k))
                    add_into(send[w].at[k - 1], [stage[w]])

                cond = carried(k - 1, w)
                if cond is True:
                    accumulate()
                else:
                    pl.when(cond)(accumulate)
                    pl.when(jnp.logical_not(cond))(start_chain)
            else:
                add_into(send[w].at[k - 1], [stage[w]])
            ring_copy(k, w, target).start()
            if k < steps:
                contribute(stage[w], w, block_at(k + 1))
            else:
                pl.when(owner(w))(lambda: contribute(own[w], w, here))
        else:
            load(k, w).wait()
            if k > 1:
                def accumulate():
                    ring_copy(k - 1, w, source).wait_recv()
                    add_into(send[w].at[k - 1], [send[w].at[k - 1], land[w].at[k - 2]])
                guarded(carried(k - 1, w), accumulate)
            ring_copy(k, w, target).start()

    def arrive(w):
        ring_copy(steps, w, source).wait_recv()
        pl.when(jnp.logical_not(owner(w)))(lambda: pair_copy(w).start())
        mine = land[w].at[steps - 1]

        def plane():
            if w >= mm:
                load_own(w).wait()
            pair_copy(w).wait_recv()

            @pl.when(core == 0)
            def _():
                add_into(own[w], [own[w], mine, other[w]])

            @pl.when(core == 1)
            def _():
                add_into(own[w], [own[w], other[w], mine])

            add_into(xsend[w], [own[w]])
            x_copy(w).start()

        pl.when(owner(w))(plane)

    def total(w):
        x_copy(w).wait_recv()

        @pl.when(plane == 0)
        def _():
            add_into(out[w], [xsend[w], xland[w]])

        @pl.when(plane == 1)
        def _():
            add_into(out[w], [xland[w], xsend[w]])
        back_copy(w).start()

    rank = [CHAIN_RANK[w] if w < len(CHAIN_RANK) else w for w in range(count)]
    slots = steps + CHAIN_LAG * (count - 1)
    by_rank = sorted(range(count), key=lambda w: rank[w])
    for t in range(slots + 1):
        for w in by_rank:
            k = t - CHAIN_LAG * rank[w] + 1
            if 1 <= k <= steps:
                guarded(carried(k, w), lambda k=k, w=w: step(k, w))
        for w in by_rank:
            if steps + CHAIN_LAG * rank[w] == t:
                arrive(w)
    for w in range(count):
        pl.when(owner(w))(lambda w=w: total(w))

    for w in range(count):
        def not_owner(w=w):
            if w >= mm:
                load_own(w).wait()
            back_copy(w).wait_recv()
            pair_copy(w).wait_send()

        def was_owner(w=w):
            x_copy(w).wait_send()
            back_copy(w).wait_send()

        pl.when(owner(w))(was_owner)
        pl.when(jnp.logical_not(owner(w)))(not_owner)
    for k in range(1, steps + 1):
        for w in range(count):
            guarded(carried(k, w), lambda k=k, w=w: ring_copy(k, w, target).wait_send())


def reduce_gradients(pairs_t, contribs, n):
    mm = len(pairs_t)
    count = mm + len(contribs)
    steps = n // 2
    blocks = [(xt.shape[1], dy.shape[1]) for xt, dy, _, _ in pairs_t] + [c.shape[1:] for c in contribs]
    ring_types = [jnp.bfloat16] * mm + [jnp.float32] * len(contribs)
    vmem = lambda shape, dtype=jnp.float32: pltpu.VMEM(shape, dtype)
    dma = pltpu.SemaphoreType.DMA
    return pl.pallas_call(
        functools.partial(reduce_kernel, n, count, mm),
        out_shape=[jax.ShapeDtypeStruct(b, jnp.float32) for b in blocks],
        in_specs=[pl.BlockSpec(memory_space=pltpu.VMEM)] * (4 * mm)
        + [pl.BlockSpec(memory_space=pl.ANY)] * len(contribs),
        out_specs=[pl.BlockSpec(memory_space=pltpu.VMEM)] * count,
        scratch_shapes=[vmem((steps,) + b, t) for b, t in zip(blocks, ring_types)]
        + [vmem((steps,) + b, t) for b, t in zip(blocks, ring_types)]
        + [vmem(b, t) for b, t in zip(blocks, ring_types)]
        + [vmem(b) for b in blocks]
        + [vmem(b, t) for b, t in zip(blocks, ring_types)]
        + [vmem(b) for b in blocks]
        + [vmem(b, t) for b, t in zip(blocks, ring_types)]
        + [
            dma((steps, count)),
            dma((count,)),
            dma((steps, count)),
            dma((steps, count)),
            dma((count,)),
            dma((count,)),
            dma((count,)),
            dma((count,)),
            dma((count,)),
            dma((count,)),
        ],
        compiler_params=pltpu.CompilerParams(
            collective_id=1, has_side_effects=True, vmem_limit_bytes=62 * 1024 * 1024
        ),
    )(*[p[0] for p in pairs_t], *[p[1] for p in pairs_t], *[p[2] for p in pairs_t], *[p[3] for p in pairs_t], *contribs)


def swap_core(value):
    rep = lax.axis_size("rep")
    return lax.ppermute(value, "rep", perm=[(i, i ^ 1) for i in range(rep)])


def swap_x(value):
    rep = lax.axis_size("rep")
    return lax.ppermute(value, "rep", perm=[(i, i ^ 2) for i in range(rep)])


def join_halves(mine, theirs, core, axis):
    first = jnp.where(core == 0, mine, theirs)
    second = jnp.where(core == 0, theirs, mine)
    return jnp.concatenate([first, second], axis=axis)


def take_half(value, core, axis):
    half = value.shape[axis] // 2
    return lax.dynamic_slice_in_dim(value, core * half, half, axis=axis)


def per_device(
    tokens,
    segment_ids,
    cotangent,
    ln1_gain,
    ln1_bias,
    qkv_weight,
    qv_bias,
    out_weight,
    out_bias,
    ln2_gain,
    ln2_bias,
    fc_weight,
    fc_bias,
    proj_weight,
    proj_bias,
):
    rep = lax.axis_size("rep")
    assert rep == 4
    core = lax.axis_index("rep") % 2
    row_count = tokens.shape[0]
    positions = jnp.arange(row_count)
    allowed = (segment_ids[:, None] == segment_ids[None, :]) & (
        positions[None, :] <= positions[:, None]
    )
    layer_index = 0
    shard = lax.axis_size("shard")
    small_local = (ln1_gain, ln1_bias, qv_bias, out_bias, ln2_gain, ln2_bias, fc_bias, proj_bias)
    widths = [v.shape[1] for v in small_local]
    local_weights = (
        qkv_weight[layer_index],
        out_weight[layer_index],
        fc_weight[layer_index],
        proj_weight[layer_index],
    )
    rows_local = local_weights[0].shape[0]
    small_row = jnp.concatenate(small_local, axis=1)
    fulls = gather_weights(list(local_weights) + [small_row], shard)
    weights = tuple(f.reshape(-1, f.shape[-1]) for f in fulls[:4])
    halves = [take_half(w, core, 1) for w in local_weights]
    half_widths = [h.size // rows_local for h in halves]
    packed_all = fulls[4].reshape(shard, -1)
    small = []
    start = 0
    for width in widths:
        small.append(to_float(packed_all[:, start : start + width].reshape(-1)))
        start += width
    small = tuple(small)

    residual = to_float(tokens)
    saved = layer_forward(residual, allowed, small, weights)
    out_tokens = saved["result"].astype(jnp.bfloat16)
    upstream = to_float(cotangent)
    input_grad, small_grads, pairs = layer_backward(upstream, saved, small, weights)

    small_mine = jnp.concatenate([g.reshape(shard, -1) for g in small_grads], axis=1)
    small_theirs = swap_core(small_mine)
    small_chip = jnp.where(core == 0, small_mine + small_theirs, small_theirs + small_mine)
    pairs_t = []
    for x, dy in pairs:
        rows_t = x.T.reshape(shard, -1, x.shape[0])
        pairs_t.append((rows_t, dy, swap_core(rows_t), swap_core(dy)))
    totals = reduce_gradients(pairs_t, [small_chip.reshape(shard, 1, -1)], shard)
    small_share = totals[4]
    owned = [t[None] for t in totals[:4]]
    small_owned = []
    start = 0
    for g in small_grads:
        width = g.shape[0] // shard
        small_owned.append(small_share[:, start : start + width])
        start += width

    (g_ln1_g, g_ln1_b, g_qv_b, g_out_b, g_ln2_g, g_ln2_b, g_fc_b, g_proj_b) = small_owned
    g_qkv, g_out, g_fc, g_proj = owned
    return (
        out_tokens,
        input_grad,
        g_ln1_g,
        g_ln1_b,
        g_qkv,
        g_qv_b,
        g_out,
        g_out_b,
        g_ln2_g,
        g_ln2_b,
        g_fc,
        g_fc_b,
        g_proj,
        g_proj_b,
    )


def solution(mesh):
    placed = (
        P(("rep", "shard"), None),
        P(("rep", "shard")),
        P(("rep", "shard"), None),
        P(None, "shard"),
        P(None, "shard"),
        P(None, "shard", None),
        P(None, "shard"),
        P(None, "shard", None),
        P(None, "shard"),
        P(None, "shard"),
        P(None, "shard"),
        P(None, "shard", None),
        P(None, "shard"),
        P(None, "shard", None),
        P(None, "shard"),
    )
    return jax.shard_map(
        per_device,
        mesh=mesh,
        in_specs=placed,
        out_specs=(
            P(("rep", "shard"), None),
            P(("rep", "shard"), None),
            P(None, "shard"),
            P(None, "shard"),
            P(None, "shard", None),
            P(None, "shard"),
            P(None, "shard", None),
            P(None, "shard"),
            P(None, "shard"),
            P(None, "shard"),
            P(None, "shard", None),
            P(None, "shard"),
            P(None, "shard", None),
            P(None, "shard"),
        ),
        check_vma=False,
    )
```

```python
import functools

import jax
import jax.numpy as jnp
from jax import lax
from jax.experimental import pallas as pl
from jax.experimental.pallas import tpu as pltpu
from jax.sharding import PartitionSpec as P

MESH = pl.DeviceIdType.MESH

HEADS = 12
HEAD = 64
LAYERS = 1

epsilon = 1e-05

def to_float(value):
    return value.astype(jnp.float32)


def layer_norm(inputs, norm_gain, norm_shift):
    center = inputs - jnp.mean(inputs, axis=-1, keepdims=True)
    inverse_std = lax.rsqrt(jnp.mean(center * center, axis=-1, keepdims=True) + epsilon)
    normed = center * inverse_std
    return (normed * norm_gain + norm_shift, normed, inverse_std)


def norm_back(upstream, normed, inverse_std, norm_gain):
    scaled = upstream * norm_gain
    inner_term = scaled - jnp.mean(scaled, axis=-1, keepdims=True)
    inner_term = inner_term - normed * jnp.mean(scaled * normed, axis=-1, keepdims=True)
    return (inverse_std * inner_term, jnp.sum(upstream * normed, axis=0), jnp.sum(upstream, axis=0))


def layer_forward(inputs, allowed, small, weights):
    ln1_gain, ln1_bias, qv_bias, out_bias, ln2_gain, ln2_bias, fc_bias, proj_bias = small
    qkv_weight, out_weight, fc_weight, proj_weight = weights
    row_count = inputs.shape[0]
    width_all = inputs.shape[1]
    first_norm, normed_one, inverse_one = layer_norm(inputs, ln1_gain, ln1_bias)
    first_low = first_norm.astype(jnp.bfloat16)
    offset = jnp.concatenate(
        [qv_bias[:width_all], jnp.zeros((width_all,), jnp.float32), qv_bias[width_all:]]
    )
    projected = (
        jnp.dot(first_low, qkv_weight, preferred_element_type=jnp.float32) + offset
    ).astype(jnp.bfloat16)
    queries = projected[:, :width_all].reshape(row_count, HEADS, HEAD)
    keys_all = projected[:, width_all : 2 * width_all].reshape(row_count, HEADS, HEAD)
    values_all = projected[:, 2 * width_all :].reshape(row_count, HEADS, HEAD)
    scores = jnp.einsum(
        "qhd,khd->hqk", queries, keys_all, preferred_element_type=jnp.float32
    ) * HEAD ** (-0.5)
    scores = jnp.where(allowed[None], scores, -1e30)
    row_max = jnp.max(scores, axis=-1, keepdims=True)
    log_total = row_max + jnp.log(jnp.sum(jnp.exp(scores - row_max), axis=-1, keepdims=True))
    attn_probs = jnp.exp(scores - log_total)
    probs_low = attn_probs.astype(jnp.bfloat16)
    attn_mixed = jnp.einsum(
        "hqk,khd->qhd", probs_low, values_all, preferred_element_type=jnp.float32
    )
    attn_mixed = attn_mixed.reshape(row_count, width_all).astype(jnp.bfloat16)
    after_attn = (
        inputs + jnp.dot(attn_mixed, out_weight, preferred_element_type=jnp.float32) + out_bias
    )
    second_norm, normed_two, inverse_two = layer_norm(after_attn, ln2_gain, ln2_bias)
    second_low = second_norm.astype(jnp.bfloat16)
    hidden_pre = jnp.dot(second_low, fc_weight, preferred_element_type=jnp.float32) + fc_bias
    hidden_low = jax.nn.gelu(hidden_pre, approximate=True).astype(jnp.bfloat16)
    result = (
        after_attn + jnp.dot(hidden_low, proj_weight, preferred_element_type=jnp.float32) + proj_bias
    )
    return dict(
        normed_one=normed_one,
        inverse_one=inverse_one,
        first_low=first_low,
        queries=queries,
        keys_all=keys_all,
        values_all=values_all,
        attn_probs=attn_probs,
        probs_low=probs_low,
        attn_mixed=attn_mixed,
        normed_two=normed_two,
        inverse_two=inverse_two,
        second_low=second_low,
        hidden_pre=hidden_pre,
        hidden_low=hidden_low,
        result=result,
    )


def layer_backward(upstream, saved, small, weights):
    ln1_gain, ln1_bias, qv_bias, out_bias, ln2_gain, ln2_bias, fc_bias, proj_bias = small
    qkv_weight, out_weight, fc_weight, proj_weight = weights
    row_count = upstream.shape[0]
    width_all = upstream.shape[1]
    proj_in = upstream.astype(jnp.bfloat16)
    grad_proj_b = jnp.sum(to_float(proj_in), axis=0)
    hidden_grad = jnp.einsum("td,fd->tf", proj_in, proj_weight, preferred_element_type=jnp.float32)
    _, gelu_pull = jax.vjp(lambda value: jax.nn.gelu(value, approximate=True), saved["hidden_pre"])
    pre_grad = gelu_pull(hidden_grad)[0].astype(jnp.bfloat16)
    grad_fc_b = jnp.sum(to_float(pre_grad), axis=0)
    second_grad = jnp.einsum("tf,df->td", pre_grad, fc_weight, preferred_element_type=jnp.float32)
    norm_part, grad_ln2_g, grad_ln2_b = norm_back(
        second_grad, saved["normed_two"], saved["inverse_two"], ln2_gain
    )
    residual_grad = upstream + norm_part
    branch_in = residual_grad.astype(jnp.bfloat16)
    grad_out_b = jnp.sum(to_float(branch_in), axis=0)
    mixed_grad = jnp.einsum("td,cd->tc", branch_in, out_weight, preferred_element_type=jnp.float32)
    mixed_grad = mixed_grad.astype(jnp.bfloat16).reshape(row_count, HEADS, HEAD)
    prob_grad = jnp.einsum(
        "qhd,khd->hqk", mixed_grad, saved["values_all"], preferred_element_type=jnp.float32
    )
    attn_probs = saved["attn_probs"]
    row_delta = jnp.sum(attn_probs * prob_grad, axis=-1, keepdims=True)
    score_grad = (attn_probs * (prob_grad - row_delta)).astype(jnp.bfloat16)
    query_grad = jnp.einsum(
        "hqk,khd->hqd", score_grad, saved["keys_all"], preferred_element_type=jnp.float32
    ) * HEAD ** (-0.5)
    key_grad = jnp.einsum(
        "hqk,qhd->hkd", score_grad, saved["queries"], preferred_element_type=jnp.float32
    ) * HEAD ** (-0.5)
    value_grad = jnp.einsum(
        "hqk,qhd->hkd", saved["probs_low"], mixed_grad, preferred_element_type=jnp.float32
    )
    joined_grad = (
        jnp.stack([query_grad, key_grad, value_grad])
        .transpose(2, 0, 1, 3)
        .reshape(row_count, 3 * width_all)
        .astype(jnp.bfloat16)
    )
    column_sums = jnp.sum(to_float(joined_grad), axis=0)
    grad_qv_b = jnp.concatenate([column_sums[:width_all], column_sums[2 * width_all :]])
    first_grad = jnp.einsum(
        "te,ce->tc", joined_grad, qkv_weight, preferred_element_type=jnp.float32
    )
    norm_first, grad_ln1_g, grad_ln1_b = norm_back(
        first_grad, saved["normed_one"], saved["inverse_one"], ln1_gain
    )
    small_grads = (
        grad_ln1_g,
        grad_ln1_b,
        grad_qv_b,
        grad_out_b,
        grad_ln2_g,
        grad_ln2_b,
        grad_fc_b,
        grad_proj_b,
    )
    pairs = (
        (saved["first_low"], joined_grad),
        (saved["attn_mixed"], branch_in),
        (saved["second_low"], pre_grad),
        (saved["hidden_low"], proj_in),
    )
    return (residual_grad + norm_first, small_grads, pairs)


def ring_position(shard_index, n):
    if n != 8:
        return shard_index
    y = shard_index % 2
    z = shard_index // 2
    return z * (1 - 2 * y) + 7 * y


def ring_shard(position, n):
    position = position % n
    if n != 8:
        return position
    y = position // 4
    z = (position % 4) * (1 - 2 * y) + 3 * y
    return z * 2 + y


FIRST_CORE_HALF = (0, 3)


CHAIN_RANK = (2, 3, 0, 1, 4)
CHAIN_LAG = 0


def gather_kernel(n, count, parts, plane_only, first_core, *refs):
    local = refs[:count]
    full = refs[count : 2 * count]
    ring_send, ring_recv, pair_send, pair_recv, x_send, x_recv, relay_send, relay_recv = refs[2 * count :]
    count = len(parts)

    def lview(w):
        array, row, rows = parts[w]
        return local[array] if rows is None else local[array].at[pl.ds(row, rows)]

    def fview(w, pos):
        array, row, rows = parts[w]
        return full[array].at[pos] if rows is None else full[array].at[pos, pl.ds(row, rows)]
    rep = lax.axis_index("rep")
    shard = lax.axis_index("shard")
    core = rep % 2
    plane = rep // 2
    step_dir = 1 - 2 * core
    partner = (rep + step_dir, shard)
    x_partner = ((rep + 2) % 4, shard)
    here = ring_position(shard, n)
    target = (rep, ring_shard(here + step_dir, n))
    source = (rep, ring_shard(here - step_dir, n))
    steps = n // 2
    split_last = n % 2 == 0

    barrier = pltpu.get_barrier_semaphore()
    for peer in (target, source, partner, x_partner):
        pl.semaphore_signal(barrier, inc=1, device_id=peer, device_id_type=MESH)
    pl.semaphore_wait(barrier, 4)

    def both(a, b):
        if a is True:
            return b
        if b is True:
            return a
        return jnp.logical_and(a, b)

    def core_carries(k, w, which_core):
        if split_last and k == steps:
            return (which_core == 0) == (w in first_core)
        return True

    def plane_carries(w, which_plane):
        for only, sole in enumerate(plane_only):
            if w in sole:
                return which_plane == only
        return True

    def ring_in(k, w):
        return both(plane_carries(w, plane), core_carries(k, w, core))

    def x_out(k, w):
        if not any(w in sole for sole in plane_only):
            return False
        return both(plane_carries(w, plane), core_carries(k, w, core))

    def x_in(k, w):
        if not any(w in sole for sole in plane_only):
            return False
        return both(plane_carries(w, 1 - plane), core_carries(k, w, core))

    def partner_ring_in(k, w):
        return both(plane_carries(w, plane), core_carries(k, w, 1 - core))

    def partner_x_in(k, w):
        if not any(w in sole for sole in plane_only):
            return False
        return both(plane_carries(w, 1 - plane), core_carries(k, w, 1 - core))

    def guarded(cond, fn):
        if cond is False:
            return
        if cond is True:
            fn()
        else:
            pl.when(cond)(fn)

    def slot(position):
        return ring_shard(position, n)

    def remote(src, dst, ssem, rsem, device):
        return pltpu.make_async_remote_copy(
            src_ref=src, dst_ref=dst, send_sem=ssem, recv_sem=rsem, device_id=device, device_id_type=MESH
        )

    def ring_copy(k, w):
        src_pos = here - step_dir * (k - 1)
        src = lview(w) if k == 1 else fview(w, slot(src_pos))
        return remote(src, fview(w, slot(src_pos)), ring_send.at[k - 1, w], ring_recv.at[k - 1, w], target)

    def incoming_ring(k, w):
        pos = slot(here - step_dir * k)
        return remote(fview(w, pos), fview(w, pos), ring_send.at[k - 1, w], ring_recv.at[k - 1, w], source)

    def pair_copy(k, w, pos):
        src = lview(w) if k == 0 else fview(w, slot(pos))
        return remote(src, fview(w, slot(pos)), pair_send.at[k, w], pair_recv.at[k, w], partner)

    def x_copy(k, w):
        pos = slot(here - step_dir * k)
        return remote(fview(w, pos), fview(w, pos), x_send.at[k - 1, w], x_recv.at[k - 1, w], x_partner)

    def relay_copy(k, w, pos):
        pos = slot(pos)
        return remote(fview(w, pos), fview(w, pos), relay_send.at[k - 1, w], relay_recv.at[k - 1, w], partner)

    for w in range(count):
        pair_copy(0, w, here).start()
    for w in range(count):
        guarded(ring_in(1, w), lambda w=w: ring_copy(1, w).start())
    for k in range(1, steps + 1):
        for w in range(count):
            def arrived(k=k, w=w):
                incoming_ring(k, w).wait_recv()
                if k < steps:
                    guarded(ring_in(k + 1, w), lambda: ring_copy(k + 1, w).start())
                guarded(x_out(k, w), lambda: x_copy(k, w).start())
                pair_copy(k, w, here - step_dir * k).start()
            guarded(ring_in(k, w), arrived)
        for w in range(count):
            def crossed(k=k, w=w):
                x_copy(k, w).wait_recv()
                relay_copy(k, w, here - step_dir * k).start()
            guarded(x_in(k, w), crossed)
    for w in range(count):
        pair_copy(0, w, here).wait_recv()
    for k in range(1, steps + 1):
        for w in range(count):
            guarded(partner_ring_in(k, w), lambda k=k, w=w: pair_copy(k, w, here + step_dir * k).wait_recv())
            guarded(partner_x_in(k, w), lambda k=k, w=w: relay_copy(k, w, here + step_dir * k).wait_recv())
    for w in range(count):
        pair_copy(0, w, here).wait_send()
    for k in range(1, steps + 1):
        for w in range(count):
            def sent(k=k, w=w):
                ring_copy(k, w).wait_send()
                pair_copy(k, w, here - step_dir * k).wait_send()
            guarded(ring_in(k, w), sent)
            guarded(x_out(k, w), lambda k=k, w=w: x_copy(k, w).wait_send())
            guarded(x_in(k, w), lambda k=k, w=w: relay_copy(k, w, here - step_dir * k).wait_send())


def gather_weights(locals_, n):
    count = len(locals_)
    steps = n // 2
    rows = locals_[2].shape[0]
    if n == 8 and rows % 32 == 0:
        half = rows // 2
        parts = ((0, 0, None), (1, 0, None), (2, 0, half), (2, half, half), (3, 0, None), (4, 0, None))
        plane_only = ((0,), (1, 2))
        first_core = (1, 4)
    else:
        parts = tuple((a, 0, None) for a in range(count))
        plane_only = ((),)
        first_core = FIRST_CORE_HALF
    pieces = len(parts)
    dma = pltpu.SemaphoreType.DMA
    return pl.pallas_call(
        functools.partial(gather_kernel, n, count, parts, plane_only, first_core),
        out_shape=[jax.ShapeDtypeStruct((n,) + a.shape, a.dtype) for a in locals_],
        in_specs=[pl.BlockSpec(memory_space=pl.ANY)] * count,
        out_specs=[pl.BlockSpec(memory_space=pl.ANY)] * count,
        scratch_shapes=[
            dma((steps, pieces)),
            dma((steps, pieces)),
            dma((steps + 1, pieces)),
            dma((steps + 1, pieces)),
            dma((steps, pieces)),
            dma((steps, pieces)),
            dma((steps, pieces)),
            dma((steps, pieces)),
        ],
        compiler_params=pltpu.CompilerParams(collective_id=0, has_side_effects=True),
    )(*locals_)


def add_rows(dst, parts, rows, chunk):
    def body(i, carry):
        window = pl.ds(pl.multiple_of(i * chunk, chunk), chunk)
        total = parts[0][window, :].astype(jnp.float32)
        for part in parts[1:]:
            total = total + part[window, :].astype(jnp.float32)
        dst[window, :] = total.astype(dst.dtype)
        return carry

    lax.fori_loop(0, rows // chunk, body, 0)


def reduce_kernel(n, count, mm, *refs):
    xt = refs[:mm]
    dy = refs[mm : 2 * mm]
    xtp = refs[2 * mm : 3 * mm]
    dyp = refs[3 * mm : 4 * mm]
    contrib = (None,) * mm + refs[4 * mm : 3 * mm + count]
    refs = refs[3 * mm + count :]
    out = refs[:count]
    land, send, other, own, xland, stage, xsend = (refs[count + i * count : count + (i + 1) * count] for i in range(7))
    (load_sem, own_sem, ring_send, ring_recv, pair_send, pair_recv, x_send, x_recv, back_send, back_recv) = refs[
        8 * count :
    ]
    rep = lax.axis_index("rep")
    shard = lax.axis_index("shard")
    core = rep % 2
    plane = rep // 2
    step_dir = 1 - 2 * core
    partner = (rep + step_dir, shard)
    x_partner = ((rep + 2) % 4, shard)
    here = ring_position(shard, n)
    target = (rep, ring_shard(here + step_dir, n))
    source = (rep, ring_shard(here - step_dir, n))
    steps = n // 2
    split_first = n % 2 == 0

    def carried(k, w):
        if split_first and k == 1:
            return (core == 0) == (w in FIRST_CORE_HALF)
        return True

    def guarded(cond, fn):
        if cond is True:
            fn()
        else:
            pl.when(cond)(fn)

    def block_at(k):
        return here + step_dir * (steps - k + 1)

    def load(k, w):
        return pltpu.make_async_copy(contrib[w].at[ring_shard(block_at(k), n)], send[w].at[k - 1], load_sem.at[k - 1, w])

    def load_own(w):
        return pltpu.make_async_copy(contrib[w].at[shard], own[w], own_sem.at[w])

    def remote(src, dst, ssem, rsem, device):
        return pltpu.make_async_remote_copy(
            src_ref=src, dst_ref=dst, send_sem=ssem, recv_sem=rsem, device_id=device, device_id_type=MESH
        )

    def ring_copy(k, w, device):
        return remote(send[w].at[k - 1], land[w].at[k - 1], ring_send.at[k - 1, w], ring_recv.at[k - 1, w], device)

    def pair_copy(w):
        return remote(land[w].at[steps - 1], other[w], pair_send.at[w], pair_recv.at[w], partner)

    def x_copy(w):
        return remote(xsend[w], xland[w], x_send.at[w], x_recv.at[w], x_partner)

    def back_copy(w):
        return remote(out[w], out[w], back_send.at[w], back_recv.at[w], partner)

    def owner(w):
        return core == w % 2

    def contribute(dst, w, position):
        block = ring_shard(position, n)
        width = 256

        def body(i, carry):
            window = pl.ds(pl.multiple_of(i * width, width), width)
            dst[:, window] = jnp.dot(
                xt[w][block], dy[w][:, window], preferred_element_type=jnp.float32
            ) + jnp.dot(xtp[w][block], dyp[w][:, window], preferred_element_type=jnp.float32)
            return carry

        lax.fori_loop(0, dy[w].shape[1] // width, body, 0)

    for w in range(mm, count):
        load_own(w).start()
    for k in range(1, steps + 1):
        for w in range(mm, count):
            guarded(carried(k, w), lambda k=k, w=w: load(k, w).start())

    barrier = pltpu.get_barrier_semaphore()
    for peer in (target, source, partner, x_partner):
        pl.semaphore_signal(barrier, inc=1, device_id=peer, device_id_type=MESH)
    pl.semaphore_wait(barrier, 4)

    def add_into(dst, parts):
        rows = dst.shape[0]
        chunk = 16 if rows % 16 == 0 else rows
        add_rows(dst, parts, rows, chunk)

    def step(k, w):
        if w < mm:
            if k == 1:
                contribute(stage[w], w, block_at(k))
            if k > 1:
                def accumulate():
                    ring_copy(k - 1, w, source).wait_recv()
                    add_into(send[w].at[k - 1], [stage[w], land[w].at[k - 2]])

                def start_chain():
                    contribute(stage[w], w, block_at(k))
                    add_into(send[w].at[k - 1], [stage[w]])

                cond = carried(k - 1, w)
                if cond is True:
                    accumulate()
                else:
                    pl.when(cond)(accumulate)
                    pl.when(jnp.logical_not(cond))(start_chain)
            else:
                add_into(send[w].at[k - 1], [stage[w]])
            ring_copy(k, w, target).start()
            if k < steps:
                contribute(stage[w], w, block_at(k + 1))
            else:
                pl.when(owner(w))(lambda: contribute(own[w], w, here))
        else:
            load(k, w).wait()
            if k > 1:
                def accumulate():
                    ring_copy(k - 1, w, source).wait_recv()
                    add_into(send[w].at[k - 1], [send[w].at[k - 1], land[w].at[k - 2]])
                guarded(carried(k - 1, w), accumulate)
            ring_copy(k, w, target).start()

    def arrive(w):
        ring_copy(steps, w, source).wait_recv()
        pl.when(jnp.logical_not(owner(w)))(lambda: pair_copy(w).start())
        mine = land[w].at[steps - 1]

        def plane():
            if w >= mm:
                load_own(w).wait()
            pair_copy(w).wait_recv()

            @pl.when(core == 0)
            def _():
                add_into(own[w], [own[w], mine, other[w]])

            @pl.when(core == 1)
            def _():
                add_into(own[w], [own[w], other[w], mine])

            add_into(xsend[w], [own[w]])
            x_copy(w).start()

        pl.when(owner(w))(plane)

    def total(w):
        x_copy(w).wait_recv()

        @pl.when(plane == 0)
        def _():
            add_into(out[w], [xsend[w], xland[w]])

        @pl.when(plane == 1)
        def _():
            add_into(out[w], [xland[w], xsend[w]])
        back_copy(w).start()

    rank = [CHAIN_RANK[w] if w < len(CHAIN_RANK) else w for w in range(count)]
    slots = steps + CHAIN_LAG * (count - 1)
    by_rank = sorted(range(count), key=lambda w: rank[w])
    for t in range(slots + 1):
        for w in by_rank:
            k = t - CHAIN_LAG * rank[w] + 1
            if 1 <= k <= steps:
                guarded(carried(k, w), lambda k=k, w=w: step(k, w))
        for w in by_rank:
            if steps + CHAIN_LAG * rank[w] == t:
                arrive(w)
    for w in range(count):
        pl.when(owner(w))(lambda w=w: total(w))

    for w in range(count):
        def not_owner(w=w):
            if w >= mm:
                load_own(w).wait()
            back_copy(w).wait_recv()
            pair_copy(w).wait_send()

        def was_owner(w=w):
            x_copy(w).wait_send()
            back_copy(w).wait_send()

        pl.when(owner(w))(was_owner)
        pl.when(jnp.logical_not(owner(w)))(not_owner)
    for k in range(1, steps + 1):
        for w in range(count):
            guarded(carried(k, w), lambda k=k, w=w: ring_copy(k, w, target).wait_send())


def reduce_gradients(pairs_t, contribs, n):
    mm = len(pairs_t)
    count = mm + len(contribs)
    steps = n // 2
    blocks = [(xt.shape[1], dy.shape[1]) for xt, dy, _, _ in pairs_t] + [c.shape[1:] for c in contribs]
    ring_types = [jnp.bfloat16] * mm + [jnp.float32] * len(contribs)
    vmem = lambda shape, dtype=jnp.float32: pltpu.VMEM(shape, dtype)
    dma = pltpu.SemaphoreType.DMA
    return pl.pallas_call(
        functools.partial(reduce_kernel, n, count, mm),
        out_shape=[jax.ShapeDtypeStruct(b, jnp.float32) for b in blocks],
        in_specs=[pl.BlockSpec(memory_space=pltpu.VMEM)] * (4 * mm)
        + [pl.BlockSpec(memory_space=pl.ANY)] * len(contribs),
        out_specs=[pl.BlockSpec(memory_space=pltpu.VMEM)] * count,
        scratch_shapes=[vmem((steps,) + b, t) for b, t in zip(blocks, ring_types)]
        + [vmem((steps,) + b, t) for b, t in zip(blocks, ring_types)]
        + [vmem(b, t) for b, t in zip(blocks, ring_types)]
        + [vmem(b) for b in blocks]
        + [vmem(b, t) for b, t in zip(blocks, ring_types)]
        + [vmem(b) for b in blocks]
        + [vmem(b, t) for b, t in zip(blocks, ring_types)]
        + [
            dma((steps, count)),
            dma((count,)),
            dma((steps, count)),
            dma((steps, count)),
            dma((count,)),
            dma((count,)),
            dma((count,)),
            dma((count,)),
            dma((count,)),
            dma((count,)),
        ],
        compiler_params=pltpu.CompilerParams(
            collective_id=1, has_side_effects=True, vmem_limit_bytes=62 * 1024 * 1024
        ),
    )(*[p[0] for p in pairs_t], *[p[1] for p in pairs_t], *[p[2] for p in pairs_t], *[p[3] for p in pairs_t], *contribs)


def swap_core(value):
    rep = lax.axis_size("rep")
    return lax.ppermute(value, "rep", perm=[(i, i ^ 1) for i in range(rep)])


def swap_x(value):
    rep = lax.axis_size("rep")
    return lax.ppermute(value, "rep", perm=[(i, i ^ 2) for i in range(rep)])


def join_halves(mine, theirs, core, axis):
    first = jnp.where(core == 0, mine, theirs)
    second = jnp.where(core == 0, theirs, mine)
    return jnp.concatenate([first, second], axis=axis)


def take_half(value, core, axis):
    half = value.shape[axis] // 2
    return lax.dynamic_slice_in_dim(value, core * half, half, axis=axis)


def per_device(
    tokens,
    segment_ids,
    cotangent,
    ln1_gain,
    ln1_bias,
    qkv_weight,
    qv_bias,
    out_weight,
    out_bias,
    ln2_gain,
    ln2_bias,
    fc_weight,
    fc_bias,
    proj_weight,
    proj_bias,
):
    rep = lax.axis_size("rep")
    assert rep == 4
    core = lax.axis_index("rep") % 2
    row_count = tokens.shape[0]
    positions = jnp.arange(row_count)
    allowed = (segment_ids[:, None] == segment_ids[None, :]) & (
        positions[None, :] <= positions[:, None]
    )
    layer_index = 0
    shard = lax.axis_size("shard")
    small_local = (ln1_gain, ln1_bias, qv_bias, out_bias, ln2_gain, ln2_bias, fc_bias, proj_bias)
    widths = [v.shape[1] for v in small_local]
    local_weights = (
        qkv_weight[layer_index],
        out_weight[layer_index],
        fc_weight[layer_index],
        proj_weight[layer_index],
    )
    rows_local = local_weights[0].shape[0]
    small_row = jnp.concatenate(small_local, axis=1)
    fulls = gather_weights(list(local_weights) + [small_row], shard)
    weights = tuple(f.reshape(-1, f.shape[-1]) for f in fulls[:4])
    halves = [take_half(w, core, 1) for w in local_weights]
    half_widths = [h.size // rows_local for h in halves]
    packed_all = fulls[4].reshape(shard, -1)
    small = []
    start = 0
    for width in widths:
        small.append(to_float(packed_all[:, start : start + width].reshape(-1)))
        start += width
    small = tuple(small)

    residual = to_float(tokens)
    saved = layer_forward(residual, allowed, small, weights)
    out_tokens = saved["result"].astype(jnp.bfloat16)
    upstream = to_float(cotangent)
    input_grad, small_grads, pairs = layer_backward(upstream, saved, small, weights)

    small_mine = jnp.concatenate([g.reshape(shard, -1) for g in small_grads], axis=1)
    small_theirs = swap_core(small_mine)
    small_chip = jnp.where(core == 0, small_mine + small_theirs, small_theirs + small_mine)
    pairs_t = []
    for x, dy in pairs:
        rows_t = x.T.reshape(shard, -1, x.shape[0])
        pairs_t.append((rows_t, dy, swap_core(rows_t), swap_core(dy)))
    totals = reduce_gradients(pairs_t, [small_chip.reshape(shard, 1, -1)], shard)
    small_share = totals[4]
    owned = [t[None] for t in totals[:4]]
    small_owned = []
    start = 0
    for g in small_grads:
        width = g.shape[0] // shard
        small_owned.append(small_share[:, start : start + width])
        start += width

    (g_ln1_g, g_ln1_b, g_qv_b, g_out_b, g_ln2_g, g_ln2_b, g_fc_b, g_proj_b) = small_owned
    g_qkv, g_out, g_fc, g_proj = owned
    return (
        out_tokens,
        input_grad,
        g_ln1_g,
        g_ln1_b,
        g_qkv,
        g_qv_b,
        g_out,
        g_out_b,
        g_ln2_g,
        g_ln2_b,
        g_fc,
        g_fc_b,
        g_proj,
        g_proj_b,
    )


def solution(mesh):
    placed = (
        P(("rep", "shard"), None),
        P(("rep", "shard")),
        P(("rep", "shard"), None),
        P(None, "shard"),
        P(None, "shard"),
        P(None, "shard", None),
        P(None, "shard"),
        P(None, "shard", None),
        P(None, "shard"),
        P(None, "shard"),
        P(None, "shard"),
        P(None, "shard", None),
        P(None, "shard"),
        P(None, "shard", None),
        P(None, "shard"),
    )
    return jax.shard_map(
        per_device,
        mesh=mesh,
        in_specs=placed,
        out_specs=(
            P(("rep", "shard"), None),
            P(("rep", "shard"), None),
            P(None, "shard"),
            P(None, "shard"),
            P(None, "shard", None),
            P(None, "shard"),
            P(None, "shard", None),
            P(None, "shard"),
            P(None, "shard"),
            P(None, "shard"),
            P(None, "shard", None),
            P(None, "shard"),
            P(None, "shard", None),
            P(None, "shard"),
        ),
        check_vma=False,
    )
```

```python
import functools

import jax
import jax.numpy as jnp
from jax import lax
from jax.experimental import pallas as pl
from jax.experimental.pallas import tpu as pltpu
from jax.sharding import PartitionSpec as P

MESH = pl.DeviceIdType.MESH

HEADS = 12
HEAD = 64
LAYERS = 1

epsilon = 1e-05

def to_float(value):
    return value.astype(jnp.float32)


def layer_norm(inputs, norm_gain, norm_shift):
    center = inputs - jnp.mean(inputs, axis=-1, keepdims=True)
    inverse_std = lax.rsqrt(jnp.mean(center * center, axis=-1, keepdims=True) + epsilon)
    normed = center * inverse_std
    return (normed * norm_gain + norm_shift, normed, inverse_std)


def norm_back(upstream, normed, inverse_std, norm_gain):
    scaled = upstream * norm_gain
    inner_term = scaled - jnp.mean(scaled, axis=-1, keepdims=True)
    inner_term = inner_term - normed * jnp.mean(scaled * normed, axis=-1, keepdims=True)
    return (inverse_std * inner_term, jnp.sum(upstream * normed, axis=0), jnp.sum(upstream, axis=0))


def layer_forward(inputs, allowed, small, weights):
    ln1_gain, ln1_bias, qv_bias, out_bias, ln2_gain, ln2_bias, fc_bias, proj_bias = small
    qkv_weight, out_weight, fc_weight, proj_weight = weights
    row_count = inputs.shape[0]
    width_all = inputs.shape[1]
    first_norm, normed_one, inverse_one = layer_norm(inputs, ln1_gain, ln1_bias)
    first_low = first_norm.astype(jnp.bfloat16)
    offset = jnp.concatenate(
        [qv_bias[:width_all], jnp.zeros((width_all,), jnp.float32), qv_bias[width_all:]]
    )
    projected = (
        jnp.dot(first_low, qkv_weight, preferred_element_type=jnp.float32) + offset
    ).astype(jnp.bfloat16)
    queries = projected[:, :width_all].reshape(row_count, HEADS, HEAD)
    keys_all = projected[:, width_all : 2 * width_all].reshape(row_count, HEADS, HEAD)
    values_all = projected[:, 2 * width_all :].reshape(row_count, HEADS, HEAD)
    scores = jnp.einsum(
        "qhd,khd->hqk", queries, keys_all, preferred_element_type=jnp.float32
    ) * HEAD ** (-0.5)
    scores = jnp.where(allowed[None], scores, -1e30)
    row_max = jnp.max(scores, axis=-1, keepdims=True)
    log_total = row_max + jnp.log(jnp.sum(jnp.exp(scores - row_max), axis=-1, keepdims=True))
    attn_probs = jnp.exp(scores - log_total)
    probs_low = attn_probs.astype(jnp.bfloat16)
    attn_mixed = jnp.einsum(
        "hqk,khd->qhd", probs_low, values_all, preferred_element_type=jnp.float32
    )
    attn_mixed = attn_mixed.reshape(row_count, width_all).astype(jnp.bfloat16)
    after_attn = (
        inputs + jnp.dot(attn_mixed, out_weight, preferred_element_type=jnp.float32) + out_bias
    )
    second_norm, normed_two, inverse_two = layer_norm(after_attn, ln2_gain, ln2_bias)
    second_low = second_norm.astype(jnp.bfloat16)
    hidden_pre = jnp.dot(second_low, fc_weight, preferred_element_type=jnp.float32) + fc_bias
    hidden_low = jax.nn.gelu(hidden_pre, approximate=True).astype(jnp.bfloat16)
    result = (
        after_attn + jnp.dot(hidden_low, proj_weight, preferred_element_type=jnp.float32) + proj_bias
    )
    return dict(
        normed_one=normed_one,
        inverse_one=inverse_one,
        first_low=first_low,
        queries=queries,
        keys_all=keys_all,
        values_all=values_all,
        attn_probs=attn_probs,
        probs_low=probs_low,
        attn_mixed=attn_mixed,
        normed_two=normed_two,
        inverse_two=inverse_two,
        second_low=second_low,
        hidden_pre=hidden_pre,
        hidden_low=hidden_low,
        result=result,
    )


def layer_backward(upstream, saved, small, weights):
    ln1_gain, ln1_bias, qv_bias, out_bias, ln2_gain, ln2_bias, fc_bias, proj_bias = small
    qkv_weight, out_weight, fc_weight, proj_weight = weights
    row_count = upstream.shape[0]
    width_all = upstream.shape[1]
    proj_in = upstream.astype(jnp.bfloat16)
    grad_proj_b = jnp.sum(to_float(proj_in), axis=0)
    hidden_grad = jnp.einsum("td,fd->tf", proj_in, proj_weight, preferred_element_type=jnp.float32)
    _, gelu_pull = jax.vjp(lambda value: jax.nn.gelu(value, approximate=True), saved["hidden_pre"])
    pre_grad = gelu_pull(hidden_grad)[0].astype(jnp.bfloat16)
    grad_fc_b = jnp.sum(to_float(pre_grad), axis=0)
    second_grad = jnp.einsum("tf,df->td", pre_grad, fc_weight, preferred_element_type=jnp.float32)
    norm_part, grad_ln2_g, grad_ln2_b = norm_back(
        second_grad, saved["normed_two"], saved["inverse_two"], ln2_gain
    )
    residual_grad = upstream + norm_part
    branch_in = residual_grad.astype(jnp.bfloat16)
    grad_out_b = jnp.sum(to_float(branch_in), axis=0)
    mixed_grad = jnp.einsum("td,cd->tc", branch_in, out_weight, preferred_element_type=jnp.float32)
    mixed_grad = mixed_grad.astype(jnp.bfloat16).reshape(row_count, HEADS, HEAD)
    prob_grad = jnp.einsum(
        "qhd,khd->hqk", mixed_grad, saved["values_all"], preferred_element_type=jnp.float32
    )
    attn_probs = saved["attn_probs"]
    row_delta = jnp.sum(attn_probs * prob_grad, axis=-1, keepdims=True)
    score_grad = (attn_probs * (prob_grad - row_delta)).astype(jnp.bfloat16)
    query_grad = jnp.einsum(
        "hqk,khd->hqd", score_grad, saved["keys_all"], preferred_element_type=jnp.float32
    ) * HEAD ** (-0.5)
    key_grad = jnp.einsum(
        "hqk,qhd->hkd", score_grad, saved["queries"], preferred_element_type=jnp.float32
    ) * HEAD ** (-0.5)
    value_grad = jnp.einsum(
        "hqk,qhd->hkd", saved["probs_low"], mixed_grad, preferred_element_type=jnp.float32
    )
    joined_grad = (
        jnp.stack([query_grad, key_grad, value_grad])
        .transpose(2, 0, 1, 3)
        .reshape(row_count, 3 * width_all)
        .astype(jnp.bfloat16)
    )
    column_sums = jnp.sum(to_float(joined_grad), axis=0)
    grad_qv_b = jnp.concatenate([column_sums[:width_all], column_sums[2 * width_all :]])
    first_grad = jnp.einsum(
        "te,ce->tc", joined_grad, qkv_weight, preferred_element_type=jnp.float32
    )
    norm_first, grad_ln1_g, grad_ln1_b = norm_back(
        first_grad, saved["normed_one"], saved["inverse_one"], ln1_gain
    )
    small_grads = (
        grad_ln1_g,
        grad_ln1_b,
        grad_qv_b,
        grad_out_b,
        grad_ln2_g,
        grad_ln2_b,
        grad_fc_b,
        grad_proj_b,
    )
    pairs = (
        (saved["first_low"], joined_grad),
        (saved["attn_mixed"], branch_in),
        (saved["second_low"], pre_grad),
        (saved["hidden_low"], proj_in),
    )
    return (residual_grad + norm_first, small_grads, pairs)


def ring_position(shard_index, n):
    if n != 8:
        return shard_index
    y = shard_index % 2
    z = shard_index // 2
    return z * (1 - 2 * y) + 7 * y


def ring_shard(position, n):
    position = position % n
    if n != 8:
        return position
    y = position // 4
    z = (position % 4) * (1 - 2 * y) + 3 * y
    return z * 2 + y


FIRST_CORE_HALF = (0, 3)


CHAIN_RANK = (2, 3, 0, 1, 4)
CHAIN_LAG = 0


def gather_kernel(n, count, parts, plane_only, first_core, *refs):
    local = refs[:count]
    full = refs[count : 2 * count]
    ring_send, ring_recv, pair_send, pair_recv, x_send, x_recv, relay_send, relay_recv = refs[2 * count :]
    count = len(parts)

    def lview(w):
        array, row, rows = parts[w]
        return local[array] if rows is None else local[array].at[pl.ds(row, rows)]

    def fview(w, pos):
        array, row, rows = parts[w]
        return full[array].at[pos] if rows is None else full[array].at[pos, pl.ds(row, rows)]
    rep = lax.axis_index("rep")
    shard = lax.axis_index("shard")
    core = rep % 2
    plane = rep // 2
    step_dir = 1 - 2 * core
    partner = (rep + step_dir, shard)
    x_partner = ((rep + 2) % 4, shard)
    here = ring_position(shard, n)
    target = (rep, ring_shard(here + step_dir, n))
    source = (rep, ring_shard(here - step_dir, n))
    steps = n // 2
    split_last = n % 2 == 0

    barrier = pltpu.get_barrier_semaphore()
    for peer in (target, source, partner, x_partner):
        pl.semaphore_signal(barrier, inc=1, device_id=peer, device_id_type=MESH)
    pl.semaphore_wait(barrier, 4)

    def both(a, b):
        if a is True:
            return b
        if b is True:
            return a
        return jnp.logical_and(a, b)

    def core_carries(k, w, which_core):
        if split_last and k == steps:
            return (which_core == 0) == (w in first_core)
        return True

    def plane_carries(w, which_plane):
        for only, sole in enumerate(plane_only):
            if w in sole:
                return which_plane == only
        return True

    def ring_in(k, w):
        return both(plane_carries(w, plane), core_carries(k, w, core))

    def x_out(k, w):
        if not any(w in sole for sole in plane_only):
            return False
        return both(plane_carries(w, plane), core_carries(k, w, core))

    def x_in(k, w):
        if not any(w in sole for sole in plane_only):
            return False
        return both(plane_carries(w, 1 - plane), core_carries(k, w, core))

    def partner_ring_in(k, w):
        return both(plane_carries(w, plane), core_carries(k, w, 1 - core))

    def partner_x_in(k, w):
        if not any(w in sole for sole in plane_only):
            return False
        return both(plane_carries(w, 1 - plane), core_carries(k, w, 1 - core))

    def guarded(cond, fn):
        if cond is False:
            return
        if cond is True:
            fn()
        else:
            pl.when(cond)(fn)

    def slot(position):
        return ring_shard(position, n)

    def remote(src, dst, ssem, rsem, device):
        return pltpu.make_async_remote_copy(
            src_ref=src, dst_ref=dst, send_sem=ssem, recv_sem=rsem, device_id=device, device_id_type=MESH
        )

    def ring_copy(k, w):
        src_pos = here - step_dir * (k - 1)
        src = lview(w) if k == 1 else fview(w, slot(src_pos))
        return remote(src, fview(w, slot(src_pos)), ring_send.at[k - 1, w], ring_recv.at[k - 1, w], target)

    def incoming_ring(k, w):
        pos = slot(here - step_dir * k)
        return remote(fview(w, pos), fview(w, pos), ring_send.at[k - 1, w], ring_recv.at[k - 1, w], source)

    def pair_copy(k, w, pos):
        src = lview(w) if k == 0 else fview(w, slot(pos))
        return remote(src, fview(w, slot(pos)), pair_send.at[k, w], pair_recv.at[k, w], partner)

    def x_copy(k, w):
        pos = slot(here - step_dir * k)
        return remote(fview(w, pos), fview(w, pos), x_send.at[k - 1, w], x_recv.at[k - 1, w], x_partner)

    def relay_copy(k, w, pos):
        pos = slot(pos)
        return remote(fview(w, pos), fview(w, pos), relay_send.at[k - 1, w], relay_recv.at[k - 1, w], partner)

    for w in range(count):
        pair_copy(0, w, here).start()
    for w in range(count):
        guarded(ring_in(1, w), lambda w=w: ring_copy(1, w).start())
    for k in range(1, steps + 1):
        for w in range(count):
            def arrived(k=k, w=w):
                incoming_ring(k, w).wait_recv()
                if k < steps:
                    guarded(ring_in(k + 1, w), lambda: ring_copy(k + 1, w).start())
                guarded(x_out(k, w), lambda: x_copy(k, w).start())
                pair_copy(k, w, here - step_dir * k).start()
            guarded(ring_in(k, w), arrived)
        for w in range(count):
            def crossed(k=k, w=w):
                x_copy(k, w).wait_recv()
                relay_copy(k, w, here - step_dir * k).start()
            guarded(x_in(k, w), crossed)
    for w in range(count):
        pair_copy(0, w, here).wait_recv()
    for k in range(1, steps + 1):
        for w in range(count):
            guarded(partner_ring_in(k, w), lambda k=k, w=w: pair_copy(k, w, here + step_dir * k).wait_recv())
            guarded(partner_x_in(k, w), lambda k=k, w=w: relay_copy(k, w, here + step_dir * k).wait_recv())
    for w in range(count):
        pair_copy(0, w, here).wait_send()
    for k in range(1, steps + 1):
        for w in range(count):
            def sent(k=k, w=w):
                ring_copy(k, w).wait_send()
                pair_copy(k, w, here - step_dir * k).wait_send()
            guarded(ring_in(k, w), sent)
            guarded(x_out(k, w), lambda k=k, w=w: x_copy(k, w).wait_send())
            guarded(x_in(k, w), lambda k=k, w=w: relay_copy(k, w, here - step_dir * k).wait_send())


def gather_weights(locals_, n):
    count = len(locals_)
    steps = n // 2
    rows = locals_[2].shape[0]
    if n == 8 and rows % 32 == 0:
        half = rows // 2
        parts = ((0, 0, None), (1, 0, None), (2, 0, half), (2, half, half), (3, 0, None), (4, 0, None))
        plane_only = ((0,), (1, 2))
        first_core = (1, 4)
    else:
        parts = tuple((a, 0, None) for a in range(count))
        plane_only = ((),)
        first_core = FIRST_CORE_HALF
    pieces = len(parts)
    dma = pltpu.SemaphoreType.DMA
    return pl.pallas_call(
        functools.partial(gather_kernel, n, count, parts, plane_only, first_core),
        out_shape=[jax.ShapeDtypeStruct((n,) + a.shape, a.dtype) for a in locals_],
        in_specs=[pl.BlockSpec(memory_space=pl.ANY)] * count,
        out_specs=[pl.BlockSpec(memory_space=pltpu.VMEM)] * count,
        scratch_shapes=[
            dma((steps, pieces)),
            dma((steps, pieces)),
            dma((steps + 1, pieces)),
            dma((steps + 1, pieces)),
            dma((steps, pieces)),
            dma((steps, pieces)),
            dma((steps, pieces)),
            dma((steps, pieces)),
        ],
        compiler_params=pltpu.CompilerParams(
            collective_id=0, has_side_effects=True, vmem_limit_bytes=40 * 1024 * 1024
        ),
    )(*locals_)


def add_rows(dst, parts, rows, chunk):
    def body(i, carry):
        window = pl.ds(pl.multiple_of(i * chunk, chunk), chunk)
        total = parts[0][window, :].astype(jnp.float32)
        for part in parts[1:]:
            total = total + part[window, :].astype(jnp.float32)
        dst[window, :] = total.astype(dst.dtype)
        return carry

    lax.fori_loop(0, rows // chunk, body, 0)


def reduce_kernel(n, count, mm, *refs):
    xt = refs[:mm]
    dy = refs[mm : 2 * mm]
    xtp = refs[2 * mm : 3 * mm]
    dyp = refs[3 * mm : 4 * mm]
    contrib = (None,) * mm + refs[4 * mm : 3 * mm + count]
    refs = refs[3 * mm + count :]
    out = refs[:count]
    land, send, other, own, xland, stage, xsend = (refs[count + i * count : count + (i + 1) * count] for i in range(7))
    (load_sem, own_sem, ring_send, ring_recv, pair_send, pair_recv, x_send, x_recv, back_send, back_recv) = refs[
        8 * count :
    ]
    rep = lax.axis_index("rep")
    shard = lax.axis_index("shard")
    core = rep % 2
    plane = rep // 2
    step_dir = 1 - 2 * core
    partner = (rep + step_dir, shard)
    x_partner = ((rep + 2) % 4, shard)
    here = ring_position(shard, n)
    target = (rep, ring_shard(here + step_dir, n))
    source = (rep, ring_shard(here - step_dir, n))
    steps = n // 2
    split_first = n % 2 == 0

    def carried(k, w):
        if split_first and k == 1:
            return (core == 0) == (w in FIRST_CORE_HALF)
        return True

    def guarded(cond, fn):
        if cond is True:
            fn()
        else:
            pl.when(cond)(fn)

    def block_at(k):
        return here + step_dir * (steps - k + 1)

    def load(k, w):
        return pltpu.make_async_copy(contrib[w].at[ring_shard(block_at(k), n)], send[w].at[k - 1], load_sem.at[k - 1, w])

    def load_own(w):
        return pltpu.make_async_copy(contrib[w].at[shard], own[w], own_sem.at[w])

    def remote(src, dst, ssem, rsem, device):
        return pltpu.make_async_remote_copy(
            src_ref=src, dst_ref=dst, send_sem=ssem, recv_sem=rsem, device_id=device, device_id_type=MESH
        )

    def ring_copy(k, w, device):
        return remote(send[w].at[k - 1], land[w].at[k - 1], ring_send.at[k - 1, w], ring_recv.at[k - 1, w], device)

    def pair_copy(w):
        return remote(land[w].at[steps - 1], other[w], pair_send.at[w], pair_recv.at[w], partner)

    def x_copy(w):
        return remote(xsend[w], xland[w], x_send.at[w], x_recv.at[w], x_partner)

    def back_copy(w):
        return remote(out[w], out[w], back_send.at[w], back_recv.at[w], partner)

    def owner(w):
        return core == w % 2

    def contribute(dst, w, position):
        block = ring_shard(position, n)
        width = 256

        def body(i, carry):
            window = pl.ds(pl.multiple_of(i * width, width), width)
            dst[:, window] = jnp.dot(
                xt[w][block], dy[w][:, window], preferred_element_type=jnp.float32
            ) + jnp.dot(xtp[w][block], dyp[w][:, window], preferred_element_type=jnp.float32)
            return carry

        lax.fori_loop(0, dy[w].shape[1] // width, body, 0)

    for w in range(mm, count):
        load_own(w).start()
    for k in range(1, steps + 1):
        for w in range(mm, count):
            guarded(carried(k, w), lambda k=k, w=w: load(k, w).start())

    barrier = pltpu.get_barrier_semaphore()
    for peer in (target, source, partner, x_partner):
        pl.semaphore_signal(barrier, inc=1, device_id=peer, device_id_type=MESH)
    pl.semaphore_wait(barrier, 4)

    def add_into(dst, parts):
        rows = dst.shape[0]
        chunk = 16 if rows % 16 == 0 else rows
        add_rows(dst, parts, rows, chunk)

    def step(k, w):
        if w < mm:
            if k == 1:
                contribute(stage[w], w, block_at(k))
            if k > 1:
                def accumulate():
                    ring_copy(k - 1, w, source).wait_recv()
                    add_into(send[w].at[k - 1], [stage[w], land[w].at[k - 2]])

                def start_chain():
                    contribute(stage[w], w, block_at(k))
                    add_into(send[w].at[k - 1], [stage[w]])

                cond = carried(k - 1, w)
                if cond is True:
                    accumulate()
                else:
                    pl.when(cond)(accumulate)
                    pl.when(jnp.logical_not(cond))(start_chain)
            else:
                add_into(send[w].at[k - 1], [stage[w]])
            ring_copy(k, w, target).start()
            if k < steps:
                contribute(stage[w], w, block_at(k + 1))
            else:
                pl.when(owner(w))(lambda: contribute(own[w], w, here))
        else:
            load(k, w).wait()
            if k > 1:
                def accumulate():
                    ring_copy(k - 1, w, source).wait_recv()
                    add_into(send[w].at[k - 1], [send[w].at[k - 1], land[w].at[k - 2]])
                guarded(carried(k - 1, w), accumulate)
            ring_copy(k, w, target).start()

    def arrive(w):
        ring_copy(steps, w, source).wait_recv()
        pl.when(jnp.logical_not(owner(w)))(lambda: pair_copy(w).start())
        mine = land[w].at[steps - 1]

        def plane():
            if w >= mm:
                load_own(w).wait()
            pair_copy(w).wait_recv()

            @pl.when(core == 0)
            def _():
                add_into(own[w], [own[w], mine, other[w]])

            @pl.when(core == 1)
            def _():
                add_into(own[w], [own[w], other[w], mine])

            add_into(xsend[w], [own[w]])
            x_copy(w).start()

        pl.when(owner(w))(plane)

    def total(w):
        x_copy(w).wait_recv()

        @pl.when(plane == 0)
        def _():
            add_into(out[w], [xsend[w], xland[w]])

        @pl.when(plane == 1)
        def _():
            add_into(out[w], [xland[w], xsend[w]])
        back_copy(w).start()

    rank = [CHAIN_RANK[w] if w < len(CHAIN_RANK) else w for w in range(count)]
    slots = steps + CHAIN_LAG * (count - 1)
    by_rank = sorted(range(count), key=lambda w: rank[w])
    for t in range(slots + 1):
        for w in by_rank:
            k = t - CHAIN_LAG * rank[w] + 1
            if 1 <= k <= steps:
                guarded(carried(k, w), lambda k=k, w=w: step(k, w))
        for w in by_rank:
            if steps + CHAIN_LAG * rank[w] == t:
                arrive(w)
    for w in range(count):
        pl.when(owner(w))(lambda w=w: total(w))

    for w in range(count):
        def not_owner(w=w):
            if w >= mm:
                load_own(w).wait()
            back_copy(w).wait_recv()
            pair_copy(w).wait_send()

        def was_owner(w=w):
            x_copy(w).wait_send()
            back_copy(w).wait_send()

        pl.when(owner(w))(was_owner)
        pl.when(jnp.logical_not(owner(w)))(not_owner)
    for k in range(1, steps + 1):
        for w in range(count):
            guarded(carried(k, w), lambda k=k, w=w: ring_copy(k, w, target).wait_send())


def reduce_gradients(pairs_t, contribs, n):
    mm = len(pairs_t)
    count = mm + len(contribs)
    steps = n // 2
    blocks = [(xt.shape[1], dy.shape[1]) for xt, dy, _, _ in pairs_t] + [c.shape[1:] for c in contribs]
    ring_types = [jnp.bfloat16] * mm + [jnp.float32] * len(contribs)
    vmem = lambda shape, dtype=jnp.float32: pltpu.VMEM(shape, dtype)
    dma = pltpu.SemaphoreType.DMA
    return pl.pallas_call(
        functools.partial(reduce_kernel, n, count, mm),
        out_shape=[jax.ShapeDtypeStruct(b, jnp.float32) for b in blocks],
        in_specs=[pl.BlockSpec(memory_space=pltpu.VMEM)] * (4 * mm)
        + [pl.BlockSpec(memory_space=pl.ANY)] * len(contribs),
        out_specs=[pl.BlockSpec(memory_space=pltpu.VMEM)] * count,
        scratch_shapes=[vmem((steps,) + b, t) for b, t in zip(blocks, ring_types)]
        + [vmem((steps,) + b, t) for b, t in zip(blocks, ring_types)]
        + [vmem(b, t) for b, t in zip(blocks, ring_types)]
        + [vmem(b) for b in blocks]
        + [vmem(b, t) for b, t in zip(blocks, ring_types)]
        + [vmem(b) for b in blocks]
        + [vmem(b, t) for b, t in zip(blocks, ring_types)]
        + [
            dma((steps, count)),
            dma((count,)),
            dma((steps, count)),
            dma((steps, count)),
            dma((count,)),
            dma((count,)),
            dma((count,)),
            dma((count,)),
            dma((count,)),
            dma((count,)),
        ],
        compiler_params=pltpu.CompilerParams(
            collective_id=1, has_side_effects=True, vmem_limit_bytes=62 * 1024 * 1024
        ),
    )(*[p[0] for p in pairs_t], *[p[1] for p in pairs_t], *[p[2] for p in pairs_t], *[p[3] for p in pairs_t], *contribs)


def swap_core(value):
    rep = lax.axis_size("rep")
    return lax.ppermute(value, "rep", perm=[(i, i ^ 1) for i in range(rep)])


def swap_x(value):
    rep = lax.axis_size("rep")
    return lax.ppermute(value, "rep", perm=[(i, i ^ 2) for i in range(rep)])


def join_halves(mine, theirs, core, axis):
    first = jnp.where(core == 0, mine, theirs)
    second = jnp.where(core == 0, theirs, mine)
    return jnp.concatenate([first, second], axis=axis)


def take_half(value, core, axis):
    half = value.shape[axis] // 2
    return lax.dynamic_slice_in_dim(value, core * half, half, axis=axis)


def per_device(
    tokens,
    segment_ids,
    cotangent,
    ln1_gain,
    ln1_bias,
    qkv_weight,
    qv_bias,
    out_weight,
    out_bias,
    ln2_gain,
    ln2_bias,
    fc_weight,
    fc_bias,
    proj_weight,
    proj_bias,
):
    rep = lax.axis_size("rep")
    assert rep == 4
    core = lax.axis_index("rep") % 2
    row_count = tokens.shape[0]
    positions = jnp.arange(row_count)
    allowed = (segment_ids[:, None] == segment_ids[None, :]) & (
        positions[None, :] <= positions[:, None]
    )
    layer_index = 0
    shard = lax.axis_size("shard")
    small_local = (ln1_gain, ln1_bias, qv_bias, out_bias, ln2_gain, ln2_bias, fc_bias, proj_bias)
    widths = [v.shape[1] for v in small_local]
    local_weights = (
        qkv_weight[layer_index],
        out_weight[layer_index],
        fc_weight[layer_index],
        proj_weight[layer_index],
    )
    rows_local = local_weights[0].shape[0]
    small_row = jnp.concatenate(small_local, axis=1)
    fulls = gather_weights(list(local_weights) + [small_row], shard)
    weights = tuple(f.reshape(-1, f.shape[-1]) for f in fulls[:4])
    halves = [take_half(w, core, 1) for w in local_weights]
    half_widths = [h.size // rows_local for h in halves]
    packed_all = fulls[4].reshape(shard, -1)
    small = []
    start = 0
    for width in widths:
        small.append(to_float(packed_all[:, start : start + width].reshape(-1)))
        start += width
    small = tuple(small)

    residual = to_float(tokens)
    saved = layer_forward(residual, allowed, small, weights)
    out_tokens = saved["result"].astype(jnp.bfloat16)
    upstream = to_float(cotangent)
    input_grad, small_grads, pairs = layer_backward(upstream, saved, small, weights)

    small_mine = jnp.concatenate([g.reshape(shard, -1) for g in small_grads], axis=1)
    small_theirs = swap_core(small_mine)
    small_chip = jnp.where(core == 0, small_mine + small_theirs, small_theirs + small_mine)
    pairs_t = []
    for x, dy in pairs:
        rows_t = x.T.reshape(shard, -1, x.shape[0])
        pairs_t.append((rows_t, dy, swap_core(rows_t), swap_core(dy)))
    totals = reduce_gradients(pairs_t, [small_chip.reshape(shard, 1, -1)], shard)
    small_share = totals[4]
    owned = [t[None] for t in totals[:4]]
    small_owned = []
    start = 0
    for g in small_grads:
        width = g.shape[0] // shard
        small_owned.append(small_share[:, start : start + width])
        start += width

    (g_ln1_g, g_ln1_b, g_qv_b, g_out_b, g_ln2_g, g_ln2_b, g_fc_b, g_proj_b) = small_owned
    g_qkv, g_out, g_fc, g_proj = owned
    return (
        out_tokens,
        input_grad,
        g_ln1_g,
        g_ln1_b,
        g_qkv,
        g_qv_b,
        g_out,
        g_out_b,
        g_ln2_g,
        g_ln2_b,
        g_fc,
        g_fc_b,
        g_proj,
        g_proj_b,
    )


def solution(mesh):
    placed = (
        P(("rep", "shard"), None),
        P(("rep", "shard")),
        P(("rep", "shard"), None),
        P(None, "shard"),
        P(None, "shard"),
        P(None, "shard", None),
        P(None, "shard"),
        P(None, "shard", None),
        P(None, "shard"),
        P(None, "shard"),
        P(None, "shard"),
        P(None, "shard", None),
        P(None, "shard"),
        P(None, "shard", None),
        P(None, "shard"),
    )
    return jax.shard_map(
        per_device,
        mesh=mesh,
        in_specs=placed,
        out_specs=(
            P(("rep", "shard"), None),
            P(("rep", "shard"), None),
            P(None, "shard"),
            P(None, "shard"),
            P(None, "shard", None),
            P(None, "shard"),
            P(None, "shard", None),
            P(None, "shard"),
            P(None, "shard"),
            P(None, "shard"),
            P(None, "shard", None),
            P(None, "shard"),
            P(None, "shard", None),
            P(None, "shard"),
        ),
        check_vma=False,
    )
```

```python
import functools

import jax
import jax.numpy as jnp
from jax import lax
from jax.experimental import pallas as pl
from jax.experimental.pallas import tpu as pltpu
from jax.sharding import PartitionSpec as P

MESH = pl.DeviceIdType.MESH

HEADS = 12
HEAD = 64
LAYERS = 1

epsilon = 1e-05

def to_float(value):
    return value.astype(jnp.float32)


def layer_norm(inputs, norm_gain, norm_shift):
    center = inputs - jnp.mean(inputs, axis=-1, keepdims=True)
    inverse_std = lax.rsqrt(jnp.mean(center * center, axis=-1, keepdims=True) + epsilon)
    normed = center * inverse_std
    return (normed * norm_gain + norm_shift, normed, inverse_std)


def norm_back(upstream, normed, inverse_std, norm_gain):
    scaled = upstream * norm_gain
    inner_term = scaled - jnp.mean(scaled, axis=-1, keepdims=True)
    inner_term = inner_term - normed * jnp.mean(scaled * normed, axis=-1, keepdims=True)
    return (inverse_std * inner_term, jnp.sum(upstream * normed, axis=0), jnp.sum(upstream, axis=0))


def layer_forward(inputs, allowed, small, weights):
    ln1_gain, ln1_bias, qv_bias, out_bias, ln2_gain, ln2_bias, fc_bias, proj_bias = small
    qkv_weight, out_weight, fc_weight, proj_weight = weights
    row_count = inputs.shape[0]
    width_all = inputs.shape[1]
    first_norm, normed_one, inverse_one = layer_norm(inputs, ln1_gain, ln1_bias)
    first_low = first_norm.astype(jnp.bfloat16)
    offset = jnp.concatenate(
        [qv_bias[:width_all], jnp.zeros((width_all,), jnp.float32), qv_bias[width_all:]]
    )
    projected = (
        jnp.dot(first_low, qkv_weight, preferred_element_type=jnp.float32) + offset
    ).astype(jnp.bfloat16)
    queries = projected[:, :width_all].reshape(row_count, HEADS, HEAD)
    keys_all = projected[:, width_all : 2 * width_all].reshape(row_count, HEADS, HEAD)
    values_all = projected[:, 2 * width_all :].reshape(row_count, HEADS, HEAD)
    scores = jnp.einsum(
        "qhd,khd->hqk", queries, keys_all, preferred_element_type=jnp.float32
    ) * HEAD ** (-0.5)
    scores = jnp.where(allowed[None], scores, -1e30)
    row_max = jnp.max(scores, axis=-1, keepdims=True)
    log_total = row_max + jnp.log(jnp.sum(jnp.exp(scores - row_max), axis=-1, keepdims=True))
    attn_probs = jnp.exp(scores - log_total)
    probs_low = attn_probs.astype(jnp.bfloat16)
    attn_mixed = jnp.einsum(
        "hqk,khd->qhd", probs_low, values_all, preferred_element_type=jnp.float32
    )
    attn_mixed = attn_mixed.reshape(row_count, width_all).astype(jnp.bfloat16)
    after_attn = (
        inputs + jnp.dot(attn_mixed, out_weight, preferred_element_type=jnp.float32) + out_bias
    )
    second_norm, normed_two, inverse_two = layer_norm(after_attn, ln2_gain, ln2_bias)
    second_low = second_norm.astype(jnp.bfloat16)
    hidden_pre = jnp.dot(second_low, fc_weight, preferred_element_type=jnp.float32) + fc_bias
    hidden_low = jax.nn.gelu(hidden_pre, approximate=True).astype(jnp.bfloat16)
    return dict(
        normed_one=normed_one,
        inverse_one=inverse_one,
        first_low=first_low,
        queries=queries,
        keys_all=keys_all,
        values_all=values_all,
        attn_probs=attn_probs,
        probs_low=probs_low,
        attn_mixed=attn_mixed,
        normed_two=normed_two,
        inverse_two=inverse_two,
        second_low=second_low,
        hidden_pre=hidden_pre,
        hidden_low=hidden_low,
        after_attn=after_attn,
    )


def layer_backward(upstream, saved, small, weights):
    ln1_gain, ln1_bias, qv_bias, out_bias, ln2_gain, ln2_bias, fc_bias, proj_bias = small
    qkv_weight, out_weight, fc_weight, proj_weight = weights
    row_count = upstream.shape[0]
    width_all = upstream.shape[1]
    proj_in = upstream.astype(jnp.bfloat16)
    grad_proj_b = jnp.sum(to_float(proj_in), axis=0)
    hidden_grad = jnp.einsum("td,fd->tf", proj_in, proj_weight, preferred_element_type=jnp.float32)
    _, gelu_pull = jax.vjp(lambda value: jax.nn.gelu(value, approximate=True), saved["hidden_pre"])
    pre_grad = gelu_pull(hidden_grad)[0].astype(jnp.bfloat16)
    grad_fc_b = jnp.sum(to_float(pre_grad), axis=0)
    second_grad = jnp.einsum("tf,df->td", pre_grad, fc_weight, preferred_element_type=jnp.float32)
    norm_part, grad_ln2_g, grad_ln2_b = norm_back(
        second_grad, saved["normed_two"], saved["inverse_two"], ln2_gain
    )
    residual_grad = upstream + norm_part
    branch_in = residual_grad.astype(jnp.bfloat16)
    grad_out_b = jnp.sum(to_float(branch_in), axis=0)
    mixed_grad = jnp.einsum("td,cd->tc", branch_in, out_weight, preferred_element_type=jnp.float32)
    mixed_grad = mixed_grad.astype(jnp.bfloat16).reshape(row_count, HEADS, HEAD)
    prob_grad = jnp.einsum(
        "qhd,khd->hqk", mixed_grad, saved["values_all"], preferred_element_type=jnp.float32
    )
    attn_probs = saved["attn_probs"]
    row_delta = jnp.sum(attn_probs * prob_grad, axis=-1, keepdims=True)
    score_grad = (attn_probs * (prob_grad - row_delta)).astype(jnp.bfloat16)
    query_grad = jnp.einsum(
        "hqk,khd->hqd", score_grad, saved["keys_all"], preferred_element_type=jnp.float32
    ) * HEAD ** (-0.5)
    key_grad = jnp.einsum(
        "hqk,qhd->hkd", score_grad, saved["queries"], preferred_element_type=jnp.float32
    ) * HEAD ** (-0.5)
    value_grad = jnp.einsum(
        "hqk,qhd->hkd", saved["probs_low"], mixed_grad, preferred_element_type=jnp.float32
    )
    joined_grad = (
        jnp.stack([query_grad, key_grad, value_grad])
        .transpose(2, 0, 1, 3)
        .reshape(row_count, 3 * width_all)
        .astype(jnp.bfloat16)
    )
    column_sums = jnp.sum(to_float(joined_grad), axis=0)
    grad_qv_b = jnp.concatenate([column_sums[:width_all], column_sums[2 * width_all :]])
    first_grad = jnp.einsum(
        "te,ce->tc", joined_grad, qkv_weight, preferred_element_type=jnp.float32
    )
    norm_first, grad_ln1_g, grad_ln1_b = norm_back(
        first_grad, saved["normed_one"], saved["inverse_one"], ln1_gain
    )
    small_grads = (
        grad_ln1_g,
        grad_ln1_b,
        grad_qv_b,
        grad_out_b,
        grad_ln2_g,
        grad_ln2_b,
        grad_fc_b,
        grad_proj_b,
    )
    pairs = (
        (saved["first_low"], joined_grad),
        (saved["attn_mixed"], branch_in),
        (saved["second_low"], pre_grad),
        (saved["hidden_low"], proj_in),
    )
    return (residual_grad + norm_first, small_grads, pairs)


def ring_position(shard_index, n):
    if n != 8:
        return shard_index
    y = shard_index % 2
    z = shard_index // 2
    return z * (1 - 2 * y) + 7 * y


def ring_shard(position, n):
    position = position % n
    if n != 8:
        return position
    y = position // 4
    z = (position % 4) * (1 - 2 * y) + 3 * y
    return z * 2 + y


FIRST_CORE_HALF = (0, 3)


CHAIN_RANK = (2, 3, 0, 1, 4)
CHAIN_LAG = 0


def gather_kernel(n, count, parts, plane_only, first_core, *refs):
    local = refs[:count]
    full = refs[count : 2 * count]
    ring_send, ring_recv, pair_send, pair_recv, x_send, x_recv, relay_send, relay_recv = refs[2 * count :]
    count = len(parts)

    def lview(w):
        array, row, rows = parts[w]
        return local[array] if rows is None else local[array].at[pl.ds(row, rows)]

    def fview(w, pos):
        array, row, rows = parts[w]
        return full[array].at[pos] if rows is None else full[array].at[pos, pl.ds(row, rows)]
    rep = lax.axis_index("rep")
    shard = lax.axis_index("shard")
    core = rep % 2
    plane = rep // 2
    step_dir = 1 - 2 * core
    partner = (rep + step_dir, shard)
    x_partner = ((rep + 2) % 4, shard)
    here = ring_position(shard, n)
    target = (rep, ring_shard(here + step_dir, n))
    source = (rep, ring_shard(here - step_dir, n))
    steps = n // 2
    split_last = n % 2 == 0

    barrier = pltpu.get_barrier_semaphore()
    for peer in (target, source, partner, x_partner):
        pl.semaphore_signal(barrier, inc=1, device_id=peer, device_id_type=MESH)
    pl.semaphore_wait(barrier, 4)

    def both(a, b):
        if a is True:
            return b
        if b is True:
            return a
        return jnp.logical_and(a, b)

    def core_carries(k, w, which_core):
        if split_last and k == steps:
            return (which_core == 0) == (w in first_core)
        return True

    def plane_carries(w, which_plane):
        for only, sole in enumerate(plane_only):
            if w in sole:
                return which_plane == only
        return True

    def ring_in(k, w):
        return both(plane_carries(w, plane), core_carries(k, w, core))

    def x_out(k, w):
        if not any(w in sole for sole in plane_only):
            return False
        return both(plane_carries(w, plane), core_carries(k, w, core))

    def x_in(k, w):
        if not any(w in sole for sole in plane_only):
            return False
        return both(plane_carries(w, 1 - plane), core_carries(k, w, core))

    def partner_ring_in(k, w):
        return both(plane_carries(w, plane), core_carries(k, w, 1 - core))

    def partner_x_in(k, w):
        if not any(w in sole for sole in plane_only):
            return False
        return both(plane_carries(w, 1 - plane), core_carries(k, w, 1 - core))

    def guarded(cond, fn):
        if cond is False:
            return
        if cond is True:
            fn()
        else:
            pl.when(cond)(fn)

    def slot(position):
        return ring_shard(position, n)

    def remote(src, dst, ssem, rsem, device):
        return pltpu.make_async_remote_copy(
            src_ref=src, dst_ref=dst, send_sem=ssem, recv_sem=rsem, device_id=device, device_id_type=MESH
        )

    def ring_copy(k, w):
        src_pos = here - step_dir * (k - 1)
        src = lview(w) if k == 1 else fview(w, slot(src_pos))
        return remote(src, fview(w, slot(src_pos)), ring_send.at[k - 1, w], ring_recv.at[k - 1, w], target)

    def incoming_ring(k, w):
        pos = slot(here - step_dir * k)
        return remote(fview(w, pos), fview(w, pos), ring_send.at[k - 1, w], ring_recv.at[k - 1, w], source)

    def pair_copy(k, w, pos):
        src = lview(w) if k == 0 else fview(w, slot(pos))
        return remote(src, fview(w, slot(pos)), pair_send.at[k, w], pair_recv.at[k, w], partner)

    def x_copy(k, w):
        pos = slot(here - step_dir * k)
        return remote(fview(w, pos), fview(w, pos), x_send.at[k - 1, w], x_recv.at[k - 1, w], x_partner)

    def relay_copy(k, w, pos):
        pos = slot(pos)
        return remote(fview(w, pos), fview(w, pos), relay_send.at[k - 1, w], relay_recv.at[k - 1, w], partner)

    for w in range(count):
        pair_copy(0, w, here).start()
    for w in range(count):
        guarded(ring_in(1, w), lambda w=w: ring_copy(1, w).start())
    for k in range(1, steps + 1):
        for w in range(count):
            def arrived(k=k, w=w):
                incoming_ring(k, w).wait_recv()
                if k < steps:
                    guarded(ring_in(k + 1, w), lambda: ring_copy(k + 1, w).start())
                guarded(x_out(k, w), lambda: x_copy(k, w).start())
                pair_copy(k, w, here - step_dir * k).start()
            guarded(ring_in(k, w), arrived)
        for w in range(count):
            def crossed(k=k, w=w):
                x_copy(k, w).wait_recv()
                relay_copy(k, w, here - step_dir * k).start()
            guarded(x_in(k, w), crossed)
    for w in range(count):
        pair_copy(0, w, here).wait_recv()
    for k in range(1, steps + 1):
        for w in range(count):
            guarded(partner_ring_in(k, w), lambda k=k, w=w: pair_copy(k, w, here + step_dir * k).wait_recv())
            guarded(partner_x_in(k, w), lambda k=k, w=w: relay_copy(k, w, here + step_dir * k).wait_recv())
    for w in range(count):
        pair_copy(0, w, here).wait_send()
    for k in range(1, steps + 1):
        for w in range(count):
            def sent(k=k, w=w):
                ring_copy(k, w).wait_send()
                pair_copy(k, w, here - step_dir * k).wait_send()
            guarded(ring_in(k, w), sent)
            guarded(x_out(k, w), lambda k=k, w=w: x_copy(k, w).wait_send())
            guarded(x_in(k, w), lambda k=k, w=w: relay_copy(k, w, here - step_dir * k).wait_send())


def gather_weights(locals_, n):
    count = len(locals_)
    steps = n // 2
    rows = locals_[2].shape[0]
    if n == 8 and rows % 32 == 0:
        half = rows // 2
        parts = ((0, 0, None), (1, 0, None), (2, 0, half), (2, half, half), (3, 0, None), (4, 0, None))
        plane_only = ((0,), (1, 2))
        first_core = (1, 4)
    else:
        parts = tuple((a, 0, None) for a in range(count))
        plane_only = ((),)
        first_core = FIRST_CORE_HALF
    pieces = len(parts)
    dma = pltpu.SemaphoreType.DMA
    return pl.pallas_call(
        functools.partial(gather_kernel, n, count, parts, plane_only, first_core),
        out_shape=[jax.ShapeDtypeStruct((n,) + a.shape, a.dtype) for a in locals_],
        in_specs=[pl.BlockSpec(memory_space=pl.ANY)] * count,
        out_specs=[pl.BlockSpec(memory_space=pl.ANY)] * count,
        scratch_shapes=[
            dma((steps, pieces)),
            dma((steps, pieces)),
            dma((steps + 1, pieces)),
            dma((steps + 1, pieces)),
            dma((steps, pieces)),
            dma((steps, pieces)),
            dma((steps, pieces)),
            dma((steps, pieces)),
        ],
        compiler_params=pltpu.CompilerParams(collective_id=0, has_side_effects=True),
    )(*locals_)


def add_rows(dst, parts, rows, chunk):
    def body(i, carry):
        window = pl.ds(pl.multiple_of(i * chunk, chunk), chunk)
        total = parts[0][window, :].astype(jnp.float32)
        for part in parts[1:]:
            total = total + part[window, :].astype(jnp.float32)
        dst[window, :] = total.astype(dst.dtype)
        return carry

    lax.fori_loop(0, rows // chunk, body, 0)


def reduce_kernel(n, count, mm, *refs):
    xt = refs[:mm]
    dy = refs[mm : 2 * mm]
    xtp = refs[2 * mm : 3 * mm]
    dyp = refs[3 * mm : 4 * mm]
    contrib = (None,) * mm + refs[4 * mm : 3 * mm + count]
    refs = refs[3 * mm + count :]
    hidden, residual, bias, weight = refs[:4]
    refs = refs[4:]
    out = refs[:count]
    tokens = refs[count]
    refs = refs[count + 1 :]
    land, send, other, own, xland, stage, xsend = (refs[i * count : (i + 1) * count] for i in range(7))
    (load_sem, own_sem, ring_send, ring_recv, pair_send, pair_recv, x_send, x_recv, back_send, back_recv) = refs[
        7 * count : 7 * count + 10
    ]
    weight_vmem, weight_sem = refs[7 * count + 10 :]
    rep = lax.axis_index("rep")
    shard = lax.axis_index("shard")
    core = rep % 2
    plane = rep // 2
    step_dir = 1 - 2 * core
    partner = (rep + step_dir, shard)
    x_partner = ((rep + 2) % 4, shard)
    here = ring_position(shard, n)
    target = (rep, ring_shard(here + step_dir, n))
    source = (rep, ring_shard(here - step_dir, n))
    steps = n // 2
    split_first = n % 2 == 0

    def carried(k, w):
        if split_first and k == 1:
            return (core == 0) == (w in FIRST_CORE_HALF)
        return True

    def guarded(cond, fn):
        if cond is True:
            fn()
        else:
            pl.when(cond)(fn)

    def block_at(k):
        return here + step_dir * (steps - k + 1)

    def load(k, w):
        return pltpu.make_async_copy(contrib[w].at[ring_shard(block_at(k), n)], send[w].at[k - 1], load_sem.at[k - 1, w])

    def load_own(w):
        return pltpu.make_async_copy(contrib[w].at[shard], own[w], own_sem.at[w])

    def remote(src, dst, ssem, rsem, device):
        return pltpu.make_async_remote_copy(
            src_ref=src, dst_ref=dst, send_sem=ssem, recv_sem=rsem, device_id=device, device_id_type=MESH
        )

    def ring_copy(k, w, device):
        return remote(send[w].at[k - 1], land[w].at[k - 1], ring_send.at[k - 1, w], ring_recv.at[k - 1, w], device)

    def pair_copy(w):
        return remote(land[w].at[steps - 1], other[w], pair_send.at[w], pair_recv.at[w], partner)

    def x_copy(w):
        return remote(xsend[w], xland[w], x_send.at[w], x_recv.at[w], x_partner)

    def back_copy(w):
        return remote(out[w], out[w], back_send.at[w], back_recv.at[w], partner)

    def owner(w):
        return core == w % 2

    def contribute(dst, w, position):
        block = ring_shard(position, n)
        width = 256

        def body(i, carry):
            window = pl.ds(pl.multiple_of(i * width, width), width)
            dst[:, window] = jnp.dot(
                xt[w][block], dy[w][:, window], preferred_element_type=jnp.float32
            ) + jnp.dot(xtp[w][block], dyp[w][:, window], preferred_element_type=jnp.float32)
            return carry

        lax.fori_loop(0, dy[w].shape[1] // width, body, 0)

    weight_copy = pltpu.make_async_copy(weight, weight_vmem, weight_sem)
    weight_copy.start()
    for w in range(mm, count):
        load_own(w).start()
    for k in range(1, steps + 1):
        for w in range(mm, count):
            guarded(carried(k, w), lambda k=k, w=w: load(k, w).start())

    barrier = pltpu.get_barrier_semaphore()
    for peer in (target, source, partner, x_partner):
        pl.semaphore_signal(barrier, inc=1, device_id=peer, device_id_type=MESH)
    pl.semaphore_wait(barrier, 4)

    def add_into(dst, parts):
        rows = dst.shape[0]
        chunk = 16 if rows % 16 == 0 else rows
        add_rows(dst, parts, rows, chunk)

    def step(k, w):
        if w < mm:
            if k == 1:
                contribute(stage[w], w, block_at(k))
            if k > 1:
                def accumulate():
                    ring_copy(k - 1, w, source).wait_recv()
                    add_into(send[w].at[k - 1], [stage[w], land[w].at[k - 2]])

                def start_chain():
                    contribute(stage[w], w, block_at(k))
                    add_into(send[w].at[k - 1], [stage[w]])

                cond = carried(k - 1, w)
                if cond is True:
                    accumulate()
                else:
                    pl.when(cond)(accumulate)
                    pl.when(jnp.logical_not(cond))(start_chain)
            else:
                add_into(send[w].at[k - 1], [stage[w]])
            ring_copy(k, w, target).start()
            if k < steps:
                contribute(stage[w], w, block_at(k + 1))
            else:
                pl.when(owner(w))(lambda: contribute(own[w], w, here))
        else:
            load(k, w).wait()
            if k > 1:
                def accumulate():
                    ring_copy(k - 1, w, source).wait_recv()
                    add_into(send[w].at[k - 1], [send[w].at[k - 1], land[w].at[k - 2]])
                guarded(carried(k - 1, w), accumulate)
            ring_copy(k, w, target).start()

    def arrive(w):
        ring_copy(steps, w, source).wait_recv()
        pl.when(jnp.logical_not(owner(w)))(lambda: pair_copy(w).start())
        mine = land[w].at[steps - 1]

        def plane():
            if w >= mm:
                load_own(w).wait()
            pair_copy(w).wait_recv()

            @pl.when(core == 0)
            def _():
                add_into(own[w], [own[w], mine, other[w]])

            @pl.when(core == 1)
            def _():
                add_into(own[w], [own[w], other[w], mine])

            add_into(xsend[w], [own[w]])
            x_copy(w).start()

        pl.when(owner(w))(plane)

    def total(w):
        x_copy(w).wait_recv()

        @pl.when(plane == 0)
        def _():
            add_into(out[w], [xsend[w], xland[w]])

        @pl.when(plane == 1)
        def _():
            add_into(out[w], [xland[w], xsend[w]])
        back_copy(w).start()

    rank = [CHAIN_RANK[w] if w < len(CHAIN_RANK) else w for w in range(count)]
    slots = steps + CHAIN_LAG * (count - 1)
    by_rank = sorted(range(count), key=lambda w: rank[w])
    for t in range(slots + 1):
        for w in by_rank:
            k = t - CHAIN_LAG * rank[w] + 1
            if 1 <= k <= steps:
                guarded(carried(k, w), lambda k=k, w=w: step(k, w))
        for w in by_rank:
            if steps + CHAIN_LAG * rank[w] == t:
                arrive(w)
        if t == 0:
            weight_copy.wait()
            width = 256

            def project(i, carry):
                window = pl.ds(pl.multiple_of(i * width, width), width)
                product = jnp.dot(hidden[...], weight_vmem[:, window], preferred_element_type=jnp.float32)
                tokens[:, window] = (residual[:, window] + product + bias[:, window]).astype(tokens.dtype)
                return carry

            lax.fori_loop(0, weight_vmem.shape[1] // width, project, 0)
    for w in range(count):
        pl.when(owner(w))(lambda w=w: total(w))

    for w in range(count):
        def not_owner(w=w):
            if w >= mm:
                load_own(w).wait()
            back_copy(w).wait_recv()
            pair_copy(w).wait_send()

        def was_owner(w=w):
            x_copy(w).wait_send()
            back_copy(w).wait_send()

        pl.when(owner(w))(was_owner)
        pl.when(jnp.logical_not(owner(w)))(not_owner)
    for k in range(1, steps + 1):
        for w in range(count):
            guarded(carried(k, w), lambda k=k, w=w: ring_copy(k, w, target).wait_send())


def reduce_gradients(pairs_t, contribs, head, n):
    mm = len(pairs_t)
    count = mm + len(contribs)
    steps = n // 2
    blocks = [(xt.shape[1], dy.shape[1]) for xt, dy, _, _ in pairs_t] + [c.shape[1:] for c in contribs]
    ring_types = [jnp.bfloat16] * mm + [jnp.float32] * len(contribs)
    vmem = lambda shape, dtype=jnp.float32: pltpu.VMEM(shape, dtype)
    dma = pltpu.SemaphoreType.DMA
    return pl.pallas_call(
        functools.partial(reduce_kernel, n, count, mm),
        out_shape=[jax.ShapeDtypeStruct(b, jnp.float32) for b in blocks]
        + [jax.ShapeDtypeStruct(head[1].shape, jnp.bfloat16)],
        in_specs=[pl.BlockSpec(memory_space=pltpu.VMEM)] * (4 * mm)
        + [pl.BlockSpec(memory_space=pl.ANY)] * len(contribs)
        + [pl.BlockSpec(memory_space=pltpu.VMEM)] * 3
        + [pl.BlockSpec(memory_space=pl.ANY)],
        out_specs=[pl.BlockSpec(memory_space=pltpu.VMEM)] * (count + 1),
        scratch_shapes=[vmem((steps,) + b, t) for b, t in zip(blocks, ring_types)]
        + [vmem((steps,) + b, t) for b, t in zip(blocks, ring_types)]
        + [vmem(b, t) for b, t in zip(blocks, ring_types)]
        + [vmem(b) for b in blocks]
        + [vmem(b, t) for b, t in zip(blocks, ring_types)]
        + [vmem(b) for b in blocks]
        + [vmem(b, t) for b, t in zip(blocks, ring_types)]
        + [
            dma((steps, count)),
            dma((count,)),
            dma((steps, count)),
            dma((steps, count)),
            dma((count,)),
            dma((count,)),
            dma((count,)),
            dma((count,)),
            dma((count,)),
            dma((count,)),
            pltpu.VMEM(head[3].shape, head[3].dtype),
            dma(()),
        ],
        compiler_params=pltpu.CompilerParams(
            collective_id=1, has_side_effects=True, vmem_limit_bytes=62 * 1024 * 1024
        ),
    )(*[p[0] for p in pairs_t], *[p[1] for p in pairs_t], *[p[2] for p in pairs_t], *[p[3] for p in pairs_t], *contribs, *head)


def swap_core(value):
    rep = lax.axis_size("rep")
    return lax.ppermute(value, "rep", perm=[(i, i ^ 1) for i in range(rep)])


def swap_x(value):
    rep = lax.axis_size("rep")
    return lax.ppermute(value, "rep", perm=[(i, i ^ 2) for i in range(rep)])


def join_halves(mine, theirs, core, axis):
    first = jnp.where(core == 0, mine, theirs)
    second = jnp.where(core == 0, theirs, mine)
    return jnp.concatenate([first, second], axis=axis)


def take_half(value, core, axis):
    half = value.shape[axis] // 2
    return lax.dynamic_slice_in_dim(value, core * half, half, axis=axis)


def per_device(
    tokens,
    segment_ids,
    cotangent,
    ln1_gain,
    ln1_bias,
    qkv_weight,
    qv_bias,
    out_weight,
    out_bias,
    ln2_gain,
    ln2_bias,
    fc_weight,
    fc_bias,
    proj_weight,
    proj_bias,
):
    rep = lax.axis_size("rep")
    assert rep == 4
    core = lax.axis_index("rep") % 2
    row_count = tokens.shape[0]
    positions = jnp.arange(row_count)
    allowed = (segment_ids[:, None] == segment_ids[None, :]) & (
        positions[None, :] <= positions[:, None]
    )
    layer_index = 0
    shard = lax.axis_size("shard")
    small_local = (ln1_gain, ln1_bias, qv_bias, out_bias, ln2_gain, ln2_bias, fc_bias, proj_bias)
    widths = [v.shape[1] for v in small_local]
    local_weights = (
        qkv_weight[layer_index],
        out_weight[layer_index],
        fc_weight[layer_index],
        proj_weight[layer_index],
    )
    rows_local = local_weights[0].shape[0]
    small_row = jnp.concatenate(small_local, axis=1)
    fulls = gather_weights(list(local_weights) + [small_row], shard)
    weights = tuple(f.reshape(-1, f.shape[-1]) for f in fulls[:4])
    halves = [take_half(w, core, 1) for w in local_weights]
    half_widths = [h.size // rows_local for h in halves]
    packed_all = fulls[4].reshape(shard, -1)
    small = []
    start = 0
    for width in widths:
        small.append(to_float(packed_all[:, start : start + width].reshape(-1)))
        start += width
    small = tuple(small)

    residual = to_float(tokens)
    saved = layer_forward(residual, allowed, small, weights)
    upstream = to_float(cotangent)
    input_grad, small_grads, pairs = layer_backward(upstream, saved, small, weights)

    small_mine = jnp.concatenate([g.reshape(shard, -1) for g in small_grads], axis=1)
    small_theirs = swap_core(small_mine)
    small_chip = jnp.where(core == 0, small_mine + small_theirs, small_theirs + small_mine)
    pairs_t = []
    for x, dy in pairs:
        rows_t = x.T.reshape(shard, -1, x.shape[0])
        pairs_t.append((rows_t, dy, swap_core(rows_t), swap_core(dy)))
    head = (saved["hidden_low"], saved["after_attn"], small[7].reshape(1, -1), weights[3])
    *totals, out_tokens = reduce_gradients(pairs_t, [small_chip.reshape(shard, 1, -1)], head, shard)
    small_share = totals[4]
    owned = [t[None] for t in totals[:4]]
    small_owned = []
    start = 0
    for g in small_grads:
        width = g.shape[0] // shard
        small_owned.append(small_share[:, start : start + width])
        start += width

    (g_ln1_g, g_ln1_b, g_qv_b, g_out_b, g_ln2_g, g_ln2_b, g_fc_b, g_proj_b) = small_owned
    g_qkv, g_out, g_fc, g_proj = owned
    return (
        out_tokens,
        input_grad,
        g_ln1_g,
        g_ln1_b,
        g_qkv,
        g_qv_b,
        g_out,
        g_out_b,
        g_ln2_g,
        g_ln2_b,
        g_fc,
        g_fc_b,
        g_proj,
        g_proj_b,
    )


def solution(mesh):
    placed = (
        P(("rep", "shard"), None),
        P(("rep", "shard")),
        P(("rep", "shard"), None),
        P(None, "shard"),
        P(None, "shard"),
        P(None, "shard", None),
        P(None, "shard"),
        P(None, "shard", None),
        P(None, "shard"),
        P(None, "shard"),
        P(None, "shard"),
        P(None, "shard", None),
        P(None, "shard"),
        P(None, "shard", None),
        P(None, "shard"),
    )
    return jax.shard_map(
        per_device,
        mesh=mesh,
        in_specs=placed,
        out_specs=(
            P(("rep", "shard"), None),
            P(("rep", "shard"), None),
            P(None, "shard"),
            P(None, "shard"),
            P(None, "shard", None),
            P(None, "shard"),
            P(None, "shard", None),
            P(None, "shard"),
            P(None, "shard"),
            P(None, "shard"),
            P(None, "shard", None),
            P(None, "shard"),
            P(None, "shard", None),
            P(None, "shard"),
        ),
        check_vma=False,
    )
```

```python
import functools

import jax
import jax.numpy as jnp
from jax import lax
from jax.experimental import pallas as pl
from jax.experimental.pallas import tpu as pltpu
from jax.sharding import PartitionSpec as P

MESH = pl.DeviceIdType.MESH

HEADS = 12
HEAD = 64
LAYERS = 1

epsilon = 1e-05

def to_float(value):
    return value.astype(jnp.float32)


def layer_norm(inputs, norm_gain, norm_shift):
    center = inputs - jnp.mean(inputs, axis=-1, keepdims=True)
    inverse_std = lax.rsqrt(jnp.mean(center * center, axis=-1, keepdims=True) + epsilon)
    normed = center * inverse_std
    return (normed * norm_gain + norm_shift, normed, inverse_std)


def norm_back(upstream, normed, inverse_std, norm_gain):
    scaled = upstream * norm_gain
    inner_term = scaled - jnp.mean(scaled, axis=-1, keepdims=True)
    inner_term = inner_term - normed * jnp.mean(scaled * normed, axis=-1, keepdims=True)
    return (inverse_std * inner_term, jnp.sum(upstream * normed, axis=0), jnp.sum(upstream, axis=0))


def layer_forward(inputs, allowed, small, weights):
    ln1_gain, ln1_bias, qv_bias, out_bias, ln2_gain, ln2_bias, fc_bias, proj_bias = small
    qkv_weight, out_weight, fc_weight, proj_weight = weights
    row_count = inputs.shape[0]
    width_all = inputs.shape[1]
    first_norm, normed_one, inverse_one = layer_norm(inputs, ln1_gain, ln1_bias)
    first_low = first_norm.astype(jnp.bfloat16)
    offset = jnp.concatenate(
        [qv_bias[:width_all], jnp.zeros((width_all,), jnp.float32), qv_bias[width_all:]]
    )
    projected = (
        jnp.dot(first_low, qkv_weight, preferred_element_type=jnp.float32) + offset
    ).astype(jnp.bfloat16)
    queries = projected[:, :width_all].reshape(row_count, HEADS, HEAD)
    keys_all = projected[:, width_all : 2 * width_all].reshape(row_count, HEADS, HEAD)
    values_all = projected[:, 2 * width_all :].reshape(row_count, HEADS, HEAD)
    scores = jnp.einsum(
        "qhd,khd->hqk", queries, keys_all, preferred_element_type=jnp.float32
    ) * HEAD ** (-0.5)
    scores = jnp.where(allowed[None], scores, -1e30)
    row_max = jnp.max(scores, axis=-1, keepdims=True)
    log_total = row_max + jnp.log(jnp.sum(jnp.exp(scores - row_max), axis=-1, keepdims=True))
    attn_probs = jnp.exp(scores - log_total)
    probs_low = attn_probs.astype(jnp.bfloat16)
    attn_mixed = jnp.einsum(
        "hqk,khd->qhd", probs_low, values_all, preferred_element_type=jnp.float32
    )
    attn_mixed = attn_mixed.reshape(row_count, width_all).astype(jnp.bfloat16)
    after_attn = (
        inputs + jnp.dot(attn_mixed, out_weight, preferred_element_type=jnp.float32) + out_bias
    )
    second_norm, normed_two, inverse_two = layer_norm(after_attn, ln2_gain, ln2_bias)
    second_low = second_norm.astype(jnp.bfloat16)
    hidden_pre = jnp.dot(second_low, fc_weight, preferred_element_type=jnp.float32) + fc_bias
    hidden_low = jax.nn.gelu(hidden_pre, approximate=True).astype(jnp.bfloat16)
    return dict(
        normed_one=normed_one,
        inverse_one=inverse_one,
        first_low=first_low,
        queries=queries,
        keys_all=keys_all,
        values_all=values_all,
        attn_probs=attn_probs,
        probs_low=probs_low,
        attn_mixed=attn_mixed,
        normed_two=normed_two,
        inverse_two=inverse_two,
        second_low=second_low,
        hidden_pre=hidden_pre,
        hidden_low=hidden_low,
        after_attn=after_attn,
    )


def layer_backward(upstream, saved, small, weights):
    ln1_gain, ln1_bias, qv_bias, out_bias, ln2_gain, ln2_bias, fc_bias, proj_bias = small
    qkv_weight, out_weight, fc_weight, proj_weight = weights
    row_count = upstream.shape[0]
    width_all = upstream.shape[1]
    proj_in = upstream.astype(jnp.bfloat16)
    grad_proj_b = jnp.sum(to_float(proj_in), axis=0)
    hidden_grad = jnp.einsum("td,fd->tf", proj_in, proj_weight, preferred_element_type=jnp.float32)
    _, gelu_pull = jax.vjp(lambda value: jax.nn.gelu(value, approximate=True), saved["hidden_pre"])
    pre_grad = gelu_pull(hidden_grad)[0].astype(jnp.bfloat16)
    grad_fc_b = jnp.sum(to_float(pre_grad), axis=0)
    second_grad = jnp.einsum("tf,df->td", pre_grad, fc_weight, preferred_element_type=jnp.float32)
    norm_part, grad_ln2_g, grad_ln2_b = norm_back(
        second_grad, saved["normed_two"], saved["inverse_two"], ln2_gain
    )
    residual_grad = upstream + norm_part
    branch_in = residual_grad.astype(jnp.bfloat16)
    grad_out_b = jnp.sum(to_float(branch_in), axis=0)
    mixed_grad = jnp.einsum("td,cd->tc", branch_in, out_weight, preferred_element_type=jnp.float32)
    mixed_grad = mixed_grad.astype(jnp.bfloat16).reshape(row_count, HEADS, HEAD)
    prob_grad = jnp.einsum(
        "qhd,khd->hqk", mixed_grad, saved["values_all"], preferred_element_type=jnp.float32
    )
    attn_probs = saved["attn_probs"]
    row_delta = jnp.sum(attn_probs * prob_grad, axis=-1, keepdims=True)
    score_grad = (attn_probs * (prob_grad - row_delta)).astype(jnp.bfloat16)
    query_grad = jnp.einsum(
        "hqk,khd->hqd", score_grad, saved["keys_all"], preferred_element_type=jnp.float32
    ) * HEAD ** (-0.5)
    key_grad = jnp.einsum(
        "hqk,qhd->hkd", score_grad, saved["queries"], preferred_element_type=jnp.float32
    ) * HEAD ** (-0.5)
    value_grad = jnp.einsum(
        "hqk,qhd->hkd", saved["probs_low"], mixed_grad, preferred_element_type=jnp.float32
    )
    joined_grad = (
        jnp.stack([query_grad, key_grad, value_grad])
        .transpose(2, 0, 1, 3)
        .reshape(row_count, 3 * width_all)
        .astype(jnp.bfloat16)
    )
    column_sums = jnp.sum(to_float(joined_grad), axis=0)
    grad_qv_b = jnp.concatenate([column_sums[:width_all], column_sums[2 * width_all :]])
    first_grad = jnp.einsum(
        "te,ce->tc", joined_grad, qkv_weight, preferred_element_type=jnp.float32
    )
    norm_first, grad_ln1_g, grad_ln1_b = norm_back(
        first_grad, saved["normed_one"], saved["inverse_one"], ln1_gain
    )
    small_grads = (
        grad_ln1_g,
        grad_ln1_b,
        grad_qv_b,
        grad_out_b,
        grad_ln2_g,
        grad_ln2_b,
        grad_fc_b,
        grad_proj_b,
    )
    pairs = (
        (saved["first_low"], joined_grad),
        (saved["attn_mixed"], branch_in),
        (saved["second_low"], pre_grad),
        (saved["hidden_low"], proj_in),
    )
    return (residual_grad + norm_first, small_grads, pairs)


def ring_position(shard_index, n):
    if n != 8:
        return shard_index
    y = shard_index % 2
    z = shard_index // 2
    return z * (1 - 2 * y) + 7 * y


def ring_shard(position, n):
    position = position % n
    if n != 8:
        return position
    y = position // 4
    z = (position % 4) * (1 - 2 * y) + 3 * y
    return z * 2 + y


FIRST_CORE_HALF = (0, 3)


CHAIN_RANK = (2, 3, 0, 1, 4)
CHAIN_LAG = 0


def gather_kernel(n, count, parts, plane_only, first_core, *refs):
    local = refs[:count]
    full = refs[count : 2 * count]
    ring_send, ring_recv, pair_send, pair_recv, x_send, x_recv, relay_send, relay_recv = refs[2 * count :]
    count = len(parts)

    def lview(w):
        array, row, rows = parts[w]
        return local[array] if rows is None else local[array].at[pl.ds(row, rows)]

    def fview(w, pos):
        array, row, rows = parts[w]
        return full[array].at[pos] if rows is None else full[array].at[pos, pl.ds(row, rows)]
    rep = lax.axis_index("rep")
    shard = lax.axis_index("shard")
    core = rep % 2
    plane = rep // 2
    step_dir = 1 - 2 * core
    partner = (rep + step_dir, shard)
    x_partner = ((rep + 2) % 4, shard)
    here = ring_position(shard, n)
    target = (rep, ring_shard(here + step_dir, n))
    source = (rep, ring_shard(here - step_dir, n))
    steps = n // 2
    split_last = n % 2 == 0

    barrier = pltpu.get_barrier_semaphore()
    for peer in (target, source, partner, x_partner):
        pl.semaphore_signal(barrier, inc=1, device_id=peer, device_id_type=MESH)
    pl.semaphore_wait(barrier, 4)

    def both(a, b):
        if a is True:
            return b
        if b is True:
            return a
        return jnp.logical_and(a, b)

    def core_carries(k, w, which_core):
        if split_last and k == steps:
            return (which_core == 0) == (w in first_core)
        return True

    def plane_carries(w, which_plane):
        for only, sole in enumerate(plane_only):
            if w in sole:
                return which_plane == only
        return True

    def ring_in(k, w):
        return both(plane_carries(w, plane), core_carries(k, w, core))

    def x_out(k, w):
        if not any(w in sole for sole in plane_only):
            return False
        return both(plane_carries(w, plane), core_carries(k, w, core))

    def x_in(k, w):
        if not any(w in sole for sole in plane_only):
            return False
        return both(plane_carries(w, 1 - plane), core_carries(k, w, core))

    def partner_ring_in(k, w):
        return both(plane_carries(w, plane), core_carries(k, w, 1 - core))

    def partner_x_in(k, w):
        if not any(w in sole for sole in plane_only):
            return False
        return both(plane_carries(w, 1 - plane), core_carries(k, w, 1 - core))

    def guarded(cond, fn):
        if cond is False:
            return
        if cond is True:
            fn()
        else:
            pl.when(cond)(fn)

    def slot(position):
        return ring_shard(position, n)

    def remote(src, dst, ssem, rsem, device):
        return pltpu.make_async_remote_copy(
            src_ref=src, dst_ref=dst, send_sem=ssem, recv_sem=rsem, device_id=device, device_id_type=MESH
        )

    def ring_copy(k, w):
        src_pos = here - step_dir * (k - 1)
        src = lview(w) if k == 1 else fview(w, slot(src_pos))
        return remote(src, fview(w, slot(src_pos)), ring_send.at[k - 1, w], ring_recv.at[k - 1, w], target)

    def incoming_ring(k, w):
        pos = slot(here - step_dir * k)
        return remote(fview(w, pos), fview(w, pos), ring_send.at[k - 1, w], ring_recv.at[k - 1, w], source)

    def pair_copy(k, w, pos):
        src = lview(w) if k == 0 else fview(w, slot(pos))
        return remote(src, fview(w, slot(pos)), pair_send.at[k, w], pair_recv.at[k, w], partner)

    def x_copy(k, w):
        pos = slot(here - step_dir * k)
        return remote(fview(w, pos), fview(w, pos), x_send.at[k - 1, w], x_recv.at[k - 1, w], x_partner)

    def relay_copy(k, w, pos):
        pos = slot(pos)
        return remote(fview(w, pos), fview(w, pos), relay_send.at[k - 1, w], relay_recv.at[k - 1, w], partner)

    for w in range(count):
        pair_copy(0, w, here).start()
    for w in range(count):
        guarded(ring_in(1, w), lambda w=w: ring_copy(1, w).start())
    for k in range(1, steps + 1):
        for w in range(count):
            def arrived(k=k, w=w):
                incoming_ring(k, w).wait_recv()
                if k < steps:
                    guarded(ring_in(k + 1, w), lambda: ring_copy(k + 1, w).start())
                guarded(x_out(k, w), lambda: x_copy(k, w).start())
                pair_copy(k, w, here - step_dir * k).start()
            guarded(ring_in(k, w), arrived)
        for w in range(count):
            def crossed(k=k, w=w):
                x_copy(k, w).wait_recv()
                relay_copy(k, w, here - step_dir * k).start()
            guarded(x_in(k, w), crossed)
    for w in range(count):
        pair_copy(0, w, here).wait_recv()
    for k in range(1, steps + 1):
        for w in range(count):
            guarded(partner_ring_in(k, w), lambda k=k, w=w: pair_copy(k, w, here + step_dir * k).wait_recv())
            guarded(partner_x_in(k, w), lambda k=k, w=w: relay_copy(k, w, here + step_dir * k).wait_recv())
    for w in range(count):
        pair_copy(0, w, here).wait_send()
    for k in range(1, steps + 1):
        for w in range(count):
            def sent(k=k, w=w):
                ring_copy(k, w).wait_send()
                pair_copy(k, w, here - step_dir * k).wait_send()
            guarded(ring_in(k, w), sent)
            guarded(x_out(k, w), lambda k=k, w=w: x_copy(k, w).wait_send())
            guarded(x_in(k, w), lambda k=k, w=w: relay_copy(k, w, here - step_dir * k).wait_send())


def gather_weights(locals_, n):
    count = len(locals_)
    steps = n // 2
    rows = locals_[2].shape[0]
    if n == 8 and rows % 32 == 0:
        half = rows // 2
        parts = ((0, 0, None), (1, 0, None), (2, 0, half), (2, half, half), (3, 0, None), (4, 0, None))
        plane_only = ((0,), (1, 2))
        first_core = (1, 4)
    else:
        parts = tuple((a, 0, None) for a in range(count))
        plane_only = ((),)
        first_core = FIRST_CORE_HALF
    pieces = len(parts)
    dma = pltpu.SemaphoreType.DMA
    return pl.pallas_call(
        functools.partial(gather_kernel, n, count, parts, plane_only, first_core),
        out_shape=[jax.ShapeDtypeStruct((n,) + a.shape, a.dtype) for a in locals_],
        in_specs=[pl.BlockSpec(memory_space=pl.ANY)] * count,
        out_specs=[pl.BlockSpec(memory_space=pl.ANY)] * count,
        scratch_shapes=[
            dma((steps, pieces)),
            dma((steps, pieces)),
            dma((steps + 1, pieces)),
            dma((steps + 1, pieces)),
            dma((steps, pieces)),
            dma((steps, pieces)),
            dma((steps, pieces)),
            dma((steps, pieces)),
        ],
        compiler_params=pltpu.CompilerParams(collective_id=0, has_side_effects=True),
    )(*locals_)


def add_rows(dst, parts, rows, chunk):
    def body(i, carry):
        window = pl.ds(pl.multiple_of(i * chunk, chunk), chunk)
        total = parts[0][window, :].astype(jnp.float32)
        for part in parts[1:]:
            total = total + part[window, :].astype(jnp.float32)
        dst[window, :] = total.astype(dst.dtype)
        return carry

    lax.fori_loop(0, rows // chunk, body, 0)


def reduce_kernel(n, count, mm, *refs):
    xt = refs[:mm]
    dy = refs[mm : 2 * mm]
    xtp = refs[2 * mm : 3 * mm]
    dyp = refs[3 * mm : 4 * mm]
    contrib = (None,) * mm + refs[4 * mm : 3 * mm + count]
    refs = refs[3 * mm + count :]
    hidden, residual, bias, weight = refs[:4]
    refs = refs[4:]
    out = refs[:count]
    tokens = refs[count]
    refs = refs[count + 1 :]
    land, send, other, own, xland, stage, xsend = (refs[i * count : (i + 1) * count] for i in range(7))
    (load_sem, own_sem, ring_send, ring_recv, pair_send, pair_recv, x_send, x_recv, back_send, back_recv) = refs[
        7 * count : 7 * count + 10
    ]
    weight_vmem, weight_sem = refs[7 * count + 10 :]
    rep = lax.axis_index("rep")
    shard = lax.axis_index("shard")
    core = rep % 2
    plane = rep // 2
    step_dir = 1 - 2 * core
    partner = (rep + step_dir, shard)
    x_partner = ((rep + 2) % 4, shard)
    here = ring_position(shard, n)
    target = (rep, ring_shard(here + step_dir, n))
    source = (rep, ring_shard(here - step_dir, n))
    steps = n // 2
    split_first = n % 2 == 0

    def carried(k, w):
        if split_first and k == 1:
            return (core == 0) == (w in FIRST_CORE_HALF)
        return True

    def guarded(cond, fn):
        if cond is True:
            fn()
        else:
            pl.when(cond)(fn)

    def block_at(k):
        return here + step_dir * (steps - k + 1)

    def load(k, w):
        return pltpu.make_async_copy(contrib[w].at[ring_shard(block_at(k), n)], send[w].at[k - 1], load_sem.at[k - 1, w])

    def load_own(w):
        return pltpu.make_async_copy(contrib[w].at[shard], own[w], own_sem.at[w])

    def remote(src, dst, ssem, rsem, device):
        return pltpu.make_async_remote_copy(
            src_ref=src, dst_ref=dst, send_sem=ssem, recv_sem=rsem, device_id=device, device_id_type=MESH
        )

    def ring_copy(k, w, device):
        return remote(send[w].at[k - 1], land[w].at[k - 1], ring_send.at[k - 1, w], ring_recv.at[k - 1, w], device)

    def pair_copy(w):
        return remote(land[w].at[steps - 1], other[w], pair_send.at[w], pair_recv.at[w], partner)

    def x_copy(w):
        return remote(xsend[w], xland[w], x_send.at[w], x_recv.at[w], x_partner)

    def back_copy(w):
        return remote(out[w], out[w], back_send.at[w], back_recv.at[w], partner)

    def owner(w):
        return core == w % 2

    def contribute(dst, w, position):
        block = ring_shard(position, n)
        width = 256

        def body(i, carry):
            window = pl.ds(pl.multiple_of(i * width, width), width)
            dst[:, window] = jnp.dot(
                xt[w][block], dy[w][:, window], preferred_element_type=jnp.float32
            ) + jnp.dot(xtp[w][block], dyp[w][:, window], preferred_element_type=jnp.float32)
            return carry

        lax.fori_loop(0, dy[w].shape[1] // width, body, 0)

    weight_copy = pltpu.make_async_copy(weight, weight_vmem, weight_sem)
    weight_copy.start()
    for w in range(mm, count):
        load_own(w).start()
    for k in range(1, steps + 1):
        for w in range(mm, count):
            guarded(carried(k, w), lambda k=k, w=w: load(k, w).start())

    barrier = pltpu.get_barrier_semaphore()
    for peer in (target, source, partner, x_partner):
        pl.semaphore_signal(barrier, inc=1, device_id=peer, device_id_type=MESH)
    pl.semaphore_wait(barrier, 4)

    def add_into(dst, parts):
        rows = dst.shape[0]
        chunk = 16 if rows % 16 == 0 else rows
        add_rows(dst, parts, rows, chunk)

    def step(k, w):
        if w < mm:
            if k == 1:
                contribute(stage[w], w, block_at(k))
            if k > 1:
                def accumulate():
                    ring_copy(k - 1, w, source).wait_recv()
                    add_into(send[w].at[k - 1], [stage[w], land[w].at[k - 2]])

                def start_chain():
                    contribute(stage[w], w, block_at(k))
                    add_into(send[w].at[k - 1], [stage[w]])

                cond = carried(k - 1, w)
                if cond is True:
                    accumulate()
                else:
                    pl.when(cond)(accumulate)
                    pl.when(jnp.logical_not(cond))(start_chain)
            else:
                add_into(send[w].at[k - 1], [stage[w]])
            ring_copy(k, w, target).start()
            if k < steps:
                contribute(stage[w], w, block_at(k + 1))
            else:
                pl.when(owner(w))(lambda: contribute(own[w], w, here))
        else:
            load(k, w).wait()
            if k > 1:
                def accumulate():
                    ring_copy(k - 1, w, source).wait_recv()
                    add_into(send[w].at[k - 1], [send[w].at[k - 1], land[w].at[k - 2]])
                guarded(carried(k - 1, w), accumulate)
            ring_copy(k, w, target).start()

    def arrive(w):
        ring_copy(steps, w, source).wait_recv()
        pl.when(jnp.logical_not(owner(w)))(lambda: pair_copy(w).start())
        mine = land[w].at[steps - 1]

        def plane():
            if w >= mm:
                load_own(w).wait()
            pair_copy(w).wait_recv()

            @pl.when(core == 0)
            def _():
                add_into(xsend[w], [own[w], mine, other[w]])

            @pl.when(core == 1)
            def _():
                add_into(xsend[w], [own[w], other[w], mine])

            x_copy(w).start()

        pl.when(owner(w))(plane)

    def total(w):
        x_copy(w).wait_recv()

        @pl.when(plane == 0)
        def _():
            add_into(out[w], [xsend[w], xland[w]])

        @pl.when(plane == 1)
        def _():
            add_into(out[w], [xland[w], xsend[w]])
        back_copy(w).start()

    rank = [CHAIN_RANK[w] if w < len(CHAIN_RANK) else w for w in range(count)]
    slots = steps + CHAIN_LAG * (count - 1)
    by_rank = sorted(range(count), key=lambda w: rank[w])
    for t in range(slots + 1):
        for w in by_rank:
            k = t - CHAIN_LAG * rank[w] + 1
            if 1 <= k <= steps:
                guarded(carried(k, w), lambda k=k, w=w: step(k, w))
        for w in by_rank:
            if steps + CHAIN_LAG * rank[w] == t:
                arrive(w)
        if t == 0:
            weight_copy.wait()
            width = 256

            def project(i, carry):
                window = pl.ds(pl.multiple_of(i * width, width), width)
                product = jnp.dot(hidden[...], weight_vmem[:, window], preferred_element_type=jnp.float32)
                tokens[:, window] = (residual[:, window] + product + bias[:, window]).astype(tokens.dtype)
                return carry

            lax.fori_loop(0, weight_vmem.shape[1] // width, project, 0)
    for w in range(count):
        pl.when(owner(w))(lambda w=w: total(w))

    for w in range(count):
        def not_owner(w=w):
            if w >= mm:
                load_own(w).wait()
            back_copy(w).wait_recv()
            pair_copy(w).wait_send()

        def was_owner(w=w):
            x_copy(w).wait_send()
            back_copy(w).wait_send()

        pl.when(owner(w))(was_owner)
        pl.when(jnp.logical_not(owner(w)))(not_owner)
    for k in range(1, steps + 1):
        for w in range(count):
            guarded(carried(k, w), lambda k=k, w=w: ring_copy(k, w, target).wait_send())


def reduce_gradients(pairs_t, contribs, head, n):
    mm = len(pairs_t)
    count = mm + len(contribs)
    steps = n // 2
    blocks = [(xt.shape[1], dy.shape[1]) for xt, dy, _, _ in pairs_t] + [c.shape[1:] for c in contribs]
    ring_types = [jnp.bfloat16] * mm + [jnp.float32] * len(contribs)
    vmem = lambda shape, dtype=jnp.float32: pltpu.VMEM(shape, dtype)
    dma = pltpu.SemaphoreType.DMA
    return pl.pallas_call(
        functools.partial(reduce_kernel, n, count, mm),
        out_shape=[jax.ShapeDtypeStruct(b, jnp.float32) for b in blocks]
        + [jax.ShapeDtypeStruct(head[1].shape, jnp.bfloat16)],
        in_specs=[pl.BlockSpec(memory_space=pltpu.VMEM)] * (4 * mm)
        + [pl.BlockSpec(memory_space=pl.ANY)] * len(contribs)
        + [pl.BlockSpec(memory_space=pltpu.VMEM)] * 3
        + [pl.BlockSpec(memory_space=pl.ANY)],
        out_specs=[pl.BlockSpec(memory_space=pltpu.VMEM)] * (count + 1),
        scratch_shapes=[vmem((steps,) + b, t) for b, t in zip(blocks, ring_types)]
        + [vmem((steps,) + b, t) for b, t in zip(blocks, ring_types)]
        + [vmem(b, t) for b, t in zip(blocks, ring_types)]
        + [vmem(b) for b in blocks]
        + [vmem(b, t) for b, t in zip(blocks, ring_types)]
        + [vmem(b) for b in blocks]
        + [vmem(b, t) for b, t in zip(blocks, ring_types)]
        + [
            dma((steps, count)),
            dma((count,)),
            dma((steps, count)),
            dma((steps, count)),
            dma((count,)),
            dma((count,)),
            dma((count,)),
            dma((count,)),
            dma((count,)),
            dma((count,)),
            pltpu.VMEM(head[3].shape, head[3].dtype),
            dma(()),
        ],
        compiler_params=pltpu.CompilerParams(
            collective_id=1, has_side_effects=True, vmem_limit_bytes=62 * 1024 * 1024
        ),
    )(*[p[0] for p in pairs_t], *[p[1] for p in pairs_t], *[p[2] for p in pairs_t], *[p[3] for p in pairs_t], *contribs, *head)


def swap_core(value):
    rep = lax.axis_size("rep")
    return lax.ppermute(value, "rep", perm=[(i, i ^ 1) for i in range(rep)])


def swap_x(value):
    rep = lax.axis_size("rep")
    return lax.ppermute(value, "rep", perm=[(i, i ^ 2) for i in range(rep)])


def join_halves(mine, theirs, core, axis):
    first = jnp.where(core == 0, mine, theirs)
    second = jnp.where(core == 0, theirs, mine)
    return jnp.concatenate([first, second], axis=axis)


def take_half(value, core, axis):
    half = value.shape[axis] // 2
    return lax.dynamic_slice_in_dim(value, core * half, half, axis=axis)


def per_device(
    tokens,
    segment_ids,
    cotangent,
    ln1_gain,
    ln1_bias,
    qkv_weight,
    qv_bias,
    out_weight,
    out_bias,
    ln2_gain,
    ln2_bias,
    fc_weight,
    fc_bias,
    proj_weight,
    proj_bias,
):
    rep = lax.axis_size("rep")
    assert rep == 4
    core = lax.axis_index("rep") % 2
    row_count = tokens.shape[0]
    positions = jnp.arange(row_count)
    allowed = (segment_ids[:, None] == segment_ids[None, :]) & (
        positions[None, :] <= positions[:, None]
    )
    layer_index = 0
    shard = lax.axis_size("shard")
    small_local = (ln1_gain, ln1_bias, qv_bias, out_bias, ln2_gain, ln2_bias, fc_bias, proj_bias)
    widths = [v.shape[1] for v in small_local]
    local_weights = (
        qkv_weight[layer_index],
        out_weight[layer_index],
        fc_weight[layer_index],
        proj_weight[layer_index],
    )
    rows_local = local_weights[0].shape[0]
    small_row = jnp.concatenate(small_local, axis=1)
    fulls = gather_weights(list(local_weights) + [small_row], shard)
    weights = tuple(f.reshape(-1, f.shape[-1]) for f in fulls[:4])
    halves = [take_half(w, core, 1) for w in local_weights]
    half_widths = [h.size // rows_local for h in halves]
    packed_all = fulls[4].reshape(shard, -1)
    small = []
    start = 0
    for width in widths:
        small.append(to_float(packed_all[:, start : start + width].reshape(-1)))
        start += width
    small = tuple(small)

    residual = to_float(tokens)
    saved = layer_forward(residual, allowed, small, weights)
    upstream = to_float(cotangent)
    input_grad, small_grads, pairs = layer_backward(upstream, saved, small, weights)

    small_mine = jnp.concatenate([g.reshape(shard, -1) for g in small_grads], axis=1)
    small_theirs = swap_core(small_mine)
    small_chip = jnp.where(core == 0, small_mine + small_theirs, small_theirs + small_mine)
    pairs_t = []
    for x, dy in pairs:
        rows_t = x.T.reshape(shard, -1, x.shape[0])
        pairs_t.append((rows_t, dy, swap_core(rows_t), swap_core(dy)))
    head = (saved["hidden_low"], saved["after_attn"], small[7].reshape(1, -1), weights[3])
    *totals, out_tokens = reduce_gradients(pairs_t, [small_chip.reshape(shard, 1, -1)], head, shard)
    small_share = totals[4]
    owned = [t[None] for t in totals[:4]]
    small_owned = []
    start = 0
    for g in small_grads:
        width = g.shape[0] // shard
        small_owned.append(small_share[:, start : start + width])
        start += width

    (g_ln1_g, g_ln1_b, g_qv_b, g_out_b, g_ln2_g, g_ln2_b, g_fc_b, g_proj_b) = small_owned
    g_qkv, g_out, g_fc, g_proj = owned
    return (
        out_tokens,
        input_grad,
        g_ln1_g,
        g_ln1_b,
        g_qkv,
        g_qv_b,
        g_out,
        g_out_b,
        g_ln2_g,
        g_ln2_b,
        g_fc,
        g_fc_b,
        g_proj,
        g_proj_b,
    )


def solution(mesh):
    placed = (
        P(("rep", "shard"), None),
        P(("rep", "shard")),
        P(("rep", "shard"), None),
        P(None, "shard"),
        P(None, "shard"),
        P(None, "shard", None),
        P(None, "shard"),
        P(None, "shard", None),
        P(None, "shard"),
        P(None, "shard"),
        P(None, "shard"),
        P(None, "shard", None),
        P(None, "shard"),
        P(None, "shard", None),
        P(None, "shard"),
    )
    return jax.shard_map(
        per_device,
        mesh=mesh,
        in_specs=placed,
        out_specs=(
            P(("rep", "shard"), None),
            P(("rep", "shard"), None),
            P(None, "shard"),
            P(None, "shard"),
            P(None, "shard", None),
            P(None, "shard"),
            P(None, "shard", None),
            P(None, "shard"),
            P(None, "shard"),
            P(None, "shard"),
            P(None, "shard", None),
            P(None, "shard"),
            P(None, "shard", None),
            P(None, "shard"),
        ),
        check_vma=False,
    )
```

```python
import functools

import jax
import jax.numpy as jnp
from jax import lax
from jax.experimental import pallas as pl
from jax.experimental.pallas import tpu as pltpu
from jax.sharding import PartitionSpec as P

MESH = pl.DeviceIdType.MESH

HEADS = 12
HEAD = 64
LAYERS = 1

epsilon = 1e-05

def to_float(value):
    return value.astype(jnp.float32)


def layer_norm(inputs, norm_gain, norm_shift):
    center = inputs - jnp.mean(inputs, axis=-1, keepdims=True)
    inverse_std = lax.rsqrt(jnp.mean(center * center, axis=-1, keepdims=True) + epsilon)
    normed = center * inverse_std
    return (normed * norm_gain + norm_shift, normed, inverse_std)


def norm_back(upstream, normed, inverse_std, norm_gain):
    scaled = upstream * norm_gain
    inner_term = scaled - jnp.mean(scaled, axis=-1, keepdims=True)
    inner_term = inner_term - normed * jnp.mean(scaled * normed, axis=-1, keepdims=True)
    return (inverse_std * inner_term, jnp.sum(upstream * normed, axis=0), jnp.sum(upstream, axis=0))


def layer_forward(inputs, allowed, small, weights):
    ln1_gain, ln1_bias, qv_bias, out_bias, ln2_gain, ln2_bias, fc_bias, proj_bias = small
    qkv_weight, out_weight, fc_weight, proj_weight = weights
    row_count = inputs.shape[0]
    width_all = inputs.shape[1]
    first_norm, normed_one, inverse_one = layer_norm(inputs, ln1_gain, ln1_bias)
    first_low = first_norm.astype(jnp.bfloat16)
    offset = jnp.concatenate(
        [qv_bias[:width_all], jnp.zeros((width_all,), jnp.float32), qv_bias[width_all:]]
    )
    projected = (
        jnp.dot(first_low, qkv_weight, preferred_element_type=jnp.float32) + offset
    ).astype(jnp.bfloat16)
    queries = projected[:, :width_all].reshape(row_count, HEADS, HEAD)
    keys_all = projected[:, width_all : 2 * width_all].reshape(row_count, HEADS, HEAD)
    values_all = projected[:, 2 * width_all :].reshape(row_count, HEADS, HEAD)
    scores = jnp.einsum(
        "qhd,khd->hqk", queries, keys_all, preferred_element_type=jnp.float32
    ) * HEAD ** (-0.5)
    scores = jnp.where(allowed[None], scores, -1e30)
    row_max = jnp.max(scores, axis=-1, keepdims=True)
    log_total = row_max + jnp.log(jnp.sum(jnp.exp(scores - row_max), axis=-1, keepdims=True))
    attn_probs = jnp.exp(scores - log_total)
    probs_low = attn_probs.astype(jnp.bfloat16)
    attn_mixed = jnp.einsum(
        "hqk,khd->qhd", probs_low, values_all, preferred_element_type=jnp.float32
    )
    attn_mixed = attn_mixed.reshape(row_count, width_all).astype(jnp.bfloat16)
    after_attn = (
        inputs + jnp.dot(attn_mixed, out_weight, preferred_element_type=jnp.float32) + out_bias
    )
    second_norm, normed_two, inverse_two = layer_norm(after_attn, ln2_gain, ln2_bias)
    second_low = second_norm.astype(jnp.bfloat16)
    hidden_pre = jnp.dot(second_low, fc_weight, preferred_element_type=jnp.float32) + fc_bias
    hidden_low = jax.nn.gelu(hidden_pre, approximate=True).astype(jnp.bfloat16)
    return dict(
        normed_one=normed_one,
        inverse_one=inverse_one,
        first_low=first_low,
        queries=queries,
        keys_all=keys_all,
        values_all=values_all,
        attn_probs=attn_probs,
        probs_low=probs_low,
        attn_mixed=attn_mixed,
        normed_two=normed_two,
        inverse_two=inverse_two,
        second_low=second_low,
        hidden_pre=hidden_pre,
        hidden_low=hidden_low,
        after_attn=after_attn,
    )


def layer_backward(upstream, saved, small, weights):
    ln1_gain, ln1_bias, qv_bias, out_bias, ln2_gain, ln2_bias, fc_bias, proj_bias = small
    qkv_weight, out_weight, fc_weight, proj_weight = weights
    row_count = upstream.shape[0]
    width_all = upstream.shape[1]
    proj_in = upstream.astype(jnp.bfloat16)
    grad_proj_b = jnp.sum(to_float(proj_in), axis=0)
    hidden_grad = jnp.einsum("td,fd->tf", proj_in, proj_weight, preferred_element_type=jnp.float32)
    _, gelu_pull = jax.vjp(lambda value: jax.nn.gelu(value, approximate=True), saved["hidden_pre"])
    pre_grad = gelu_pull(hidden_grad)[0].astype(jnp.bfloat16)
    grad_fc_b = jnp.sum(to_float(pre_grad), axis=0)
    second_grad = jnp.einsum("tf,df->td", pre_grad, fc_weight, preferred_element_type=jnp.float32)
    norm_part, grad_ln2_g, grad_ln2_b = norm_back(
        second_grad, saved["normed_two"], saved["inverse_two"], ln2_gain
    )
    residual_grad = upstream + norm_part
    branch_in = residual_grad.astype(jnp.bfloat16)
    grad_out_b = jnp.sum(to_float(branch_in), axis=0)
    mixed_grad = jnp.einsum("td,cd->tc", branch_in, out_weight, preferred_element_type=jnp.float32)
    mixed_grad = mixed_grad.astype(jnp.bfloat16).reshape(row_count, HEADS, HEAD)
    prob_grad = jnp.einsum(
        "qhd,khd->hqk", mixed_grad, saved["values_all"], preferred_element_type=jnp.float32
    )
    attn_probs = saved["attn_probs"]
    row_delta = jnp.sum(attn_probs * prob_grad, axis=-1, keepdims=True)
    score_grad = (attn_probs * (prob_grad - row_delta)).astype(jnp.bfloat16)
    query_grad = jnp.einsum(
        "hqk,khd->hqd", score_grad, saved["keys_all"], preferred_element_type=jnp.float32
    ) * HEAD ** (-0.5)
    key_grad = jnp.einsum(
        "hqk,qhd->hkd", score_grad, saved["queries"], preferred_element_type=jnp.float32
    ) * HEAD ** (-0.5)
    value_grad = jnp.einsum(
        "hqk,qhd->hkd", saved["probs_low"], mixed_grad, preferred_element_type=jnp.float32
    )
    joined_grad = (
        jnp.stack([query_grad, key_grad, value_grad])
        .transpose(2, 0, 1, 3)
        .reshape(row_count, 3 * width_all)
        .astype(jnp.bfloat16)
    )
    column_sums = jnp.sum(to_float(joined_grad), axis=0)
    grad_qv_b = jnp.concatenate([column_sums[:width_all], column_sums[2 * width_all :]])
    first_grad = jnp.einsum(
        "te,ce->tc", joined_grad, qkv_weight, preferred_element_type=jnp.float32
    )
    norm_first, grad_ln1_g, grad_ln1_b = norm_back(
        first_grad, saved["normed_one"], saved["inverse_one"], ln1_gain
    )
    small_grads = (
        grad_ln1_g,
        grad_ln1_b,
        grad_qv_b,
        grad_out_b,
        grad_ln2_g,
        grad_ln2_b,
        grad_fc_b,
        grad_proj_b,
    )
    pairs = (
        (saved["first_low"], joined_grad),
        (saved["attn_mixed"], branch_in),
        (saved["second_low"], pre_grad),
        (saved["hidden_low"], proj_in),
    )
    return (residual_grad + norm_first, small_grads, pairs)


def ring_position(shard_index, n):
    if n != 8:
        return shard_index
    y = shard_index % 2
    z = shard_index // 2
    return z * (1 - 2 * y) + 7 * y


def ring_shard(position, n):
    position = position % n
    if n != 8:
        return position
    y = position // 4
    z = (position % 4) * (1 - 2 * y) + 3 * y
    return z * 2 + y


FIRST_CORE_HALF = (0, 3)


CHAIN_RANK = (0, 1, 2, 3, 4)
CHAIN_LAG = 0


def gather_kernel(n, count, parts, plane_only, first_core, *refs):
    local = refs[:count]
    full = refs[count : 2 * count]
    ring_send, ring_recv, pair_send, pair_recv, x_send, x_recv, relay_send, relay_recv = refs[2 * count :]
    count = len(parts)

    def lview(w):
        array, row, rows = parts[w]
        return local[array] if rows is None else local[array].at[pl.ds(row, rows)]

    def fview(w, pos):
        array, row, rows = parts[w]
        return full[array].at[pos] if rows is None else full[array].at[pos, pl.ds(row, rows)]
    rep = lax.axis_index("rep")
    shard = lax.axis_index("shard")
    core = rep % 2
    plane = rep // 2
    step_dir = 1 - 2 * core
    partner = (rep + step_dir, shard)
    x_partner = ((rep + 2) % 4, shard)
    here = ring_position(shard, n)
    target = (rep, ring_shard(here + step_dir, n))
    source = (rep, ring_shard(here - step_dir, n))
    steps = n // 2
    split_last = n % 2 == 0

    barrier = pltpu.get_barrier_semaphore()
    for peer in (target, source, partner, x_partner):
        pl.semaphore_signal(barrier, inc=1, device_id=peer, device_id_type=MESH)
    pl.semaphore_wait(barrier, 4)

    def both(a, b):
        if a is True:
            return b
        if b is True:
            return a
        return jnp.logical_and(a, b)

    def core_carries(k, w, which_core):
        if split_last and k == steps:
            return (which_core == 0) == (w in first_core)
        return True

    def plane_carries(w, which_plane):
        for only, sole in enumerate(plane_only):
            if w in sole:
                return which_plane == only
        return True

    def ring_in(k, w):
        return both(plane_carries(w, plane), core_carries(k, w, core))

    def x_out(k, w):
        if not any(w in sole for sole in plane_only):
            return False
        return both(plane_carries(w, plane), core_carries(k, w, core))

    def x_in(k, w):
        if not any(w in sole for sole in plane_only):
            return False
        return both(plane_carries(w, 1 - plane), core_carries(k, w, core))

    def partner_ring_in(k, w):
        return both(plane_carries(w, plane), core_carries(k, w, 1 - core))

    def partner_x_in(k, w):
        if not any(w in sole for sole in plane_only):
            return False
        return both(plane_carries(w, 1 - plane), core_carries(k, w, 1 - core))

    def guarded(cond, fn):
        if cond is False:
            return
        if cond is True:
            fn()
        else:
            pl.when(cond)(fn)

    def slot(position):
        return ring_shard(position, n)

    def remote(src, dst, ssem, rsem, device):
        return pltpu.make_async_remote_copy(
            src_ref=src, dst_ref=dst, send_sem=ssem, recv_sem=rsem, device_id=device, device_id_type=MESH
        )

    def ring_copy(k, w):
        src_pos = here - step_dir * (k - 1)
        src = lview(w) if k == 1 else fview(w, slot(src_pos))
        return remote(src, fview(w, slot(src_pos)), ring_send.at[k - 1, w], ring_recv.at[k - 1, w], target)

    def incoming_ring(k, w):
        pos = slot(here - step_dir * k)
        return remote(fview(w, pos), fview(w, pos), ring_send.at[k - 1, w], ring_recv.at[k - 1, w], source)

    def pair_copy(k, w, pos):
        src = lview(w) if k == 0 else fview(w, slot(pos))
        return remote(src, fview(w, slot(pos)), pair_send.at[k, w], pair_recv.at[k, w], partner)

    def x_copy(k, w):
        pos = slot(here - step_dir * k)
        return remote(fview(w, pos), fview(w, pos), x_send.at[k - 1, w], x_recv.at[k - 1, w], x_partner)

    def relay_copy(k, w, pos):
        pos = slot(pos)
        return remote(fview(w, pos), fview(w, pos), relay_send.at[k - 1, w], relay_recv.at[k - 1, w], partner)

    for w in range(count):
        pair_copy(0, w, here).start()
    for w in range(count):
        guarded(ring_in(1, w), lambda w=w: ring_copy(1, w).start())
    for k in range(1, steps + 1):
        for w in range(count):
            def arrived(k=k, w=w):
                incoming_ring(k, w).wait_recv()
                if k < steps:
                    guarded(ring_in(k + 1, w), lambda: ring_copy(k + 1, w).start())
                guarded(x_out(k, w), lambda: x_copy(k, w).start())
                pair_copy(k, w, here - step_dir * k).start()
            guarded(ring_in(k, w), arrived)
        for w in range(count):
            def crossed(k=k, w=w):
                x_copy(k, w).wait_recv()
                relay_copy(k, w, here - step_dir * k).start()
            guarded(x_in(k, w), crossed)
    for w in range(count):
        pair_copy(0, w, here).wait_recv()
    for k in range(1, steps + 1):
        for w in range(count):
            guarded(partner_ring_in(k, w), lambda k=k, w=w: pair_copy(k, w, here + step_dir * k).wait_recv())
            guarded(partner_x_in(k, w), lambda k=k, w=w: relay_copy(k, w, here + step_dir * k).wait_recv())
    for w in range(count):
        pair_copy(0, w, here).wait_send()
    for k in range(1, steps + 1):
        for w in range(count):
            def sent(k=k, w=w):
                ring_copy(k, w).wait_send()
                pair_copy(k, w, here - step_dir * k).wait_send()
            guarded(ring_in(k, w), sent)
            guarded(x_out(k, w), lambda k=k, w=w: x_copy(k, w).wait_send())
            guarded(x_in(k, w), lambda k=k, w=w: relay_copy(k, w, here - step_dir * k).wait_send())


def gather_weights(locals_, n):
    count = len(locals_)
    steps = n // 2
    rows = locals_[2].shape[0]
    if n == 8 and rows % 32 == 0:
        half = rows // 2
        parts = ((0, 0, None), (1, 0, None), (2, 0, half), (2, half, half), (3, 0, None), (4, 0, None))
        plane_only = ((0, 1), (2, 3))
        first_core = (0, 4)
    else:
        parts = tuple((a, 0, None) for a in range(count))
        plane_only = ((),)
        first_core = FIRST_CORE_HALF
    pieces = len(parts)
    dma = pltpu.SemaphoreType.DMA
    return pl.pallas_call(
        functools.partial(gather_kernel, n, count, parts, plane_only, first_core),
        out_shape=[jax.ShapeDtypeStruct((n,) + a.shape, a.dtype) for a in locals_],
        in_specs=[pl.BlockSpec(memory_space=pl.ANY)] * count,
        out_specs=[pl.BlockSpec(memory_space=pl.ANY)] * count,
        scratch_shapes=[
            dma((steps, pieces)),
            dma((steps, pieces)),
            dma((steps + 1, pieces)),
            dma((steps + 1, pieces)),
            dma((steps, pieces)),
            dma((steps, pieces)),
            dma((steps, pieces)),
            dma((steps, pieces)),
        ],
        compiler_params=pltpu.CompilerParams(collective_id=0, has_side_effects=True),
    )(*locals_)


def add_rows(dst, parts, rows, chunk):
    def body(i, carry):
        window = pl.ds(pl.multiple_of(i * chunk, chunk), chunk)
        total = parts[0][window, :].astype(jnp.float32)
        for part in parts[1:]:
            total = total + part[window, :].astype(jnp.float32)
        dst[window, :] = total.astype(dst.dtype)
        return carry

    lax.fori_loop(0, rows // chunk, body, 0)


def reduce_kernel(n, count, mm, *refs):
    xt = refs[:mm]
    dy = refs[mm : 2 * mm]
    xtp = refs[2 * mm : 3 * mm]
    dyp = refs[3 * mm : 4 * mm]
    contrib = (None,) * mm + refs[4 * mm : 3 * mm + count]
    refs = refs[3 * mm + count :]
    hidden, residual, bias, weight = refs[:4]
    refs = refs[4:]
    out = refs[:count]
    tokens = refs[count]
    refs = refs[count + 1 :]
    land, send, other, own, xland, stage, xsend = (refs[i * count : (i + 1) * count] for i in range(7))
    (load_sem, own_sem, ring_send, ring_recv, pair_send, pair_recv, x_send, x_recv, back_send, back_recv) = refs[
        7 * count : 7 * count + 10
    ]
    weight_vmem, weight_sem = refs[7 * count + 10 :]
    rep = lax.axis_index("rep")
    shard = lax.axis_index("shard")
    core = rep % 2
    plane = rep // 2
    step_dir = 1 - 2 * core
    partner = (rep + step_dir, shard)
    x_partner = ((rep + 2) % 4, shard)
    here = ring_position(shard, n)
    target = (rep, ring_shard(here + step_dir, n))
    source = (rep, ring_shard(here - step_dir, n))
    steps = n // 2
    split_first = n % 2 == 0

    def carried(k, w):
        if split_first and k == 1:
            return (core == 0) == (w in FIRST_CORE_HALF)
        return True

    def guarded(cond, fn):
        if cond is True:
            fn()
        else:
            pl.when(cond)(fn)

    def block_at(k):
        return here + step_dir * (steps - k + 1)

    def load(k, w):
        return pltpu.make_async_copy(contrib[w].at[ring_shard(block_at(k), n)], send[w].at[k - 1], load_sem.at[k - 1, w])

    def load_own(w):
        return pltpu.make_async_copy(contrib[w].at[shard], own[w], own_sem.at[w])

    def remote(src, dst, ssem, rsem, device):
        return pltpu.make_async_remote_copy(
            src_ref=src, dst_ref=dst, send_sem=ssem, recv_sem=rsem, device_id=device, device_id_type=MESH
        )

    def ring_copy(k, w, device):
        return remote(send[w].at[k - 1], land[w].at[k - 1], ring_send.at[k - 1, w], ring_recv.at[k - 1, w], device)

    def pair_copy(w):
        return remote(land[w].at[steps - 1], other[w], pair_send.at[w], pair_recv.at[w], partner)

    def x_copy(w):
        return remote(xsend[w], xland[w], x_send.at[w], x_recv.at[w], x_partner)

    def back_copy(w):
        return remote(out[w], out[w], back_send.at[w], back_recv.at[w], partner)

    def owner(w):
        return core == w % 2

    def contribute(dst, w, position):
        block = ring_shard(position, n)
        width = 256

        def body(i, carry):
            window = pl.ds(pl.multiple_of(i * width, width), width)
            dst[:, window] = jnp.dot(
                xt[w][block], dy[w][:, window], preferred_element_type=jnp.float32
            ) + jnp.dot(xtp[w][block], dyp[w][:, window], preferred_element_type=jnp.float32)
            return carry

        lax.fori_loop(0, dy[w].shape[1] // width, body, 0)

    weight_copy = pltpu.make_async_copy(weight, weight_vmem, weight_sem)
    weight_copy.start()
    for w in range(mm, count):
        load_own(w).start()
    for k in range(1, steps + 1):
        for w in range(mm, count):
            guarded(carried(k, w), lambda k=k, w=w: load(k, w).start())

    barrier = pltpu.get_barrier_semaphore()
    for peer in (target, source, partner, x_partner):
        pl.semaphore_signal(barrier, inc=1, device_id=peer, device_id_type=MESH)
    pl.semaphore_wait(barrier, 4)

    def add_into(dst, parts):
        rows = dst.shape[0]
        chunk = 16 if rows % 16 == 0 else rows
        add_rows(dst, parts, rows, chunk)

    def step(k, w):
        if w < mm:
            if k == 1:
                contribute(stage[w], w, block_at(k))
            if k > 1:
                def accumulate():
                    ring_copy(k - 1, w, source).wait_recv()
                    add_into(send[w].at[k - 1], [stage[w], land[w].at[k - 2]])

                def start_chain():
                    contribute(stage[w], w, block_at(k))
                    add_into(send[w].at[k - 1], [stage[w]])

                cond = carried(k - 1, w)
                if cond is True:
                    accumulate()
                else:
                    pl.when(cond)(accumulate)
                    pl.when(jnp.logical_not(cond))(start_chain)
            else:
                add_into(send[w].at[k - 1], [stage[w]])
            ring_copy(k, w, target).start()
            if k < steps:
                contribute(stage[w], w, block_at(k + 1))
            else:
                pl.when(owner(w))(lambda: contribute(own[w], w, here))
        else:
            load(k, w).wait()
            if k > 1:
                def accumulate():
                    ring_copy(k - 1, w, source).wait_recv()
                    add_into(send[w].at[k - 1], [send[w].at[k - 1], land[w].at[k - 2]])
                guarded(carried(k - 1, w), accumulate)
            ring_copy(k, w, target).start()

    def arrive(w):
        ring_copy(steps, w, source).wait_recv()
        pl.when(jnp.logical_not(owner(w)))(lambda: pair_copy(w).start())
        mine = land[w].at[steps - 1]

        def plane():
            if w >= mm:
                load_own(w).wait()
            pair_copy(w).wait_recv()

            @pl.when(core == 0)
            def _():
                add_into(xsend[w], [own[w], mine, other[w]])

            @pl.when(core == 1)
            def _():
                add_into(xsend[w], [own[w], other[w], mine])

            x_copy(w).start()

        pl.when(owner(w))(plane)

    def total(w):
        x_copy(w).wait_recv()

        @pl.when(plane == 0)
        def _():
            add_into(out[w], [xsend[w], xland[w]])

        @pl.when(plane == 1)
        def _():
            add_into(out[w], [xland[w], xsend[w]])
        back_copy(w).start()

    rank = [CHAIN_RANK[w] if w < len(CHAIN_RANK) else w for w in range(count)]
    slots = steps + CHAIN_LAG * (count - 1)
    by_rank = sorted(range(count), key=lambda w: rank[w])
    for t in range(slots + 1):
        for w in by_rank:
            k = t - CHAIN_LAG * rank[w] + 1
            if 1 <= k <= steps:
                guarded(carried(k, w), lambda k=k, w=w: step(k, w))
        for w in by_rank:
            if steps + CHAIN_LAG * rank[w] == t:
                arrive(w)
        if t == 0:
            weight_copy.wait()
            width = 256

            def project(i, carry):
                window = pl.ds(pl.multiple_of(i * width, width), width)
                product = jnp.dot(hidden[...], weight_vmem[:, window], preferred_element_type=jnp.float32)
                tokens[:, window] = (residual[:, window] + product + bias[:, window]).astype(tokens.dtype)
                return carry

            lax.fori_loop(0, weight_vmem.shape[1] // width, project, 0)
    for w in range(count):
        pl.when(owner(w))(lambda w=w: total(w))

    for w in range(count):
        def not_owner(w=w):
            if w >= mm:
                load_own(w).wait()
            back_copy(w).wait_recv()
            pair_copy(w).wait_send()

        def was_owner(w=w):
            x_copy(w).wait_send()
            back_copy(w).wait_send()

        pl.when(owner(w))(was_owner)
        pl.when(jnp.logical_not(owner(w)))(not_owner)
    for k in range(1, steps + 1):
        for w in range(count):
            guarded(carried(k, w), lambda k=k, w=w: ring_copy(k, w, target).wait_send())


def reduce_gradients(pairs_t, contribs, head, n):
    mm = len(pairs_t)
    count = mm + len(contribs)
    steps = n // 2
    blocks = [(xt.shape[1], dy.shape[1]) for xt, dy, _, _ in pairs_t] + [c.shape[1:] for c in contribs]
    ring_types = [jnp.bfloat16] * mm + [jnp.float32] * len(contribs)
    vmem = lambda shape, dtype=jnp.float32: pltpu.VMEM(shape, dtype)
    dma = pltpu.SemaphoreType.DMA
    return pl.pallas_call(
        functools.partial(reduce_kernel, n, count, mm),
        out_shape=[jax.ShapeDtypeStruct(b, jnp.float32) for b in blocks]
        + [jax.ShapeDtypeStruct(head[1].shape, jnp.bfloat16)],
        in_specs=[pl.BlockSpec(memory_space=pltpu.VMEM)] * (4 * mm)
        + [pl.BlockSpec(memory_space=pl.ANY)] * len(contribs)
        + [pl.BlockSpec(memory_space=pltpu.VMEM)] * 3
        + [pl.BlockSpec(memory_space=pl.ANY)],
        out_specs=[pl.BlockSpec(memory_space=pltpu.VMEM)] * (count + 1),
        scratch_shapes=[vmem((steps,) + b, t) for b, t in zip(blocks, ring_types)]
        + [vmem((steps,) + b, t) for b, t in zip(blocks, ring_types)]
        + [vmem(b, t) for b, t in zip(blocks, ring_types)]
        + [vmem(b) for b in blocks]
        + [vmem(b, t) for b, t in zip(blocks, ring_types)]
        + [vmem(b) for b in blocks]
        + [vmem(b, t) for b, t in zip(blocks, ring_types)]
        + [
            dma((steps, count)),
            dma((count,)),
            dma((steps, count)),
            dma((steps, count)),
            dma((count,)),
            dma((count,)),
            dma((count,)),
            dma((count,)),
            dma((count,)),
            dma((count,)),
            pltpu.VMEM(head[3].shape, head[3].dtype),
            dma(()),
        ],
        compiler_params=pltpu.CompilerParams(
            collective_id=1, has_side_effects=True, vmem_limit_bytes=62 * 1024 * 1024
        ),
    )(*[p[0] for p in pairs_t], *[p[1] for p in pairs_t], *[p[2] for p in pairs_t], *[p[3] for p in pairs_t], *contribs, *head)


def swap_core(value):
    rep = lax.axis_size("rep")
    return lax.ppermute(value, "rep", perm=[(i, i ^ 1) for i in range(rep)])


def swap_x(value):
    rep = lax.axis_size("rep")
    return lax.ppermute(value, "rep", perm=[(i, i ^ 2) for i in range(rep)])


def join_halves(mine, theirs, core, axis):
    first = jnp.where(core == 0, mine, theirs)
    second = jnp.where(core == 0, theirs, mine)
    return jnp.concatenate([first, second], axis=axis)


def take_half(value, core, axis):
    half = value.shape[axis] // 2
    return lax.dynamic_slice_in_dim(value, core * half, half, axis=axis)


def per_device(
    tokens,
    segment_ids,
    cotangent,
    ln1_gain,
    ln1_bias,
    qkv_weight,
    qv_bias,
    out_weight,
    out_bias,
    ln2_gain,
    ln2_bias,
    fc_weight,
    fc_bias,
    proj_weight,
    proj_bias,
):
    rep = lax.axis_size("rep")
    assert rep == 4
    core = lax.axis_index("rep") % 2
    row_count = tokens.shape[0]
    positions = jnp.arange(row_count)
    allowed = (segment_ids[:, None] == segment_ids[None, :]) & (
        positions[None, :] <= positions[:, None]
    )
    layer_index = 0
    shard = lax.axis_size("shard")
    small_local = (ln1_gain, ln1_bias, qv_bias, out_bias, ln2_gain, ln2_bias, fc_bias, proj_bias)
    widths = [v.shape[1] for v in small_local]
    local_weights = (
        qkv_weight[layer_index],
        out_weight[layer_index],
        fc_weight[layer_index],
        proj_weight[layer_index],
    )
    rows_local = local_weights[0].shape[0]
    small_row = jnp.concatenate(small_local, axis=1)
    fulls = gather_weights(list(local_weights) + [small_row], shard)
    weights = tuple(f.reshape(-1, f.shape[-1]) for f in fulls[:4])
    halves = [take_half(w, core, 1) for w in local_weights]
    half_widths = [h.size // rows_local for h in halves]
    packed_all = fulls[4].reshape(shard, -1)
    small = []
    start = 0
    for width in widths:
        small.append(to_float(packed_all[:, start : start + width].reshape(-1)))
        start += width
    small = tuple(small)

    residual = to_float(tokens)
    saved = layer_forward(residual, allowed, small, weights)
    upstream = to_float(cotangent)
    input_grad, small_grads, pairs = layer_backward(upstream, saved, small, weights)

    small_mine = jnp.concatenate([g.reshape(shard, -1) for g in small_grads], axis=1)
    small_theirs = swap_core(small_mine)
    small_chip = jnp.where(core == 0, small_mine + small_theirs, small_theirs + small_mine)
    pairs_t = []
    for x, dy in pairs:
        rows_t = x.T.reshape(shard, -1, x.shape[0])
        pairs_t.append((rows_t, dy, swap_core(rows_t), swap_core(dy)))
    head = (saved["hidden_low"], saved["after_attn"], small[7].reshape(1, -1), weights[3])
    *totals, out_tokens = reduce_gradients(pairs_t, [small_chip.reshape(shard, 1, -1)], head, shard)
    small_share = totals[4]
    owned = [t[None] for t in totals[:4]]
    small_owned = []
    start = 0
    for g in small_grads:
        width = g.shape[0] // shard
        small_owned.append(small_share[:, start : start + width])
        start += width

    (g_ln1_g, g_ln1_b, g_qv_b, g_out_b, g_ln2_g, g_ln2_b, g_fc_b, g_proj_b) = small_owned
    g_qkv, g_out, g_fc, g_proj = owned
    return (
        out_tokens,
        input_grad,
        g_ln1_g,
        g_ln1_b,
        g_qkv,
        g_qv_b,
        g_out,
        g_out_b,
        g_ln2_g,
        g_ln2_b,
        g_fc,
        g_fc_b,
        g_proj,
        g_proj_b,
    )


def solution(mesh):
    placed = (
        P(("rep", "shard"), None),
        P(("rep", "shard")),
        P(("rep", "shard"), None),
        P(None, "shard"),
        P(None, "shard"),
        P(None, "shard", None),
        P(None, "shard"),
        P(None, "shard", None),
        P(None, "shard"),
        P(None, "shard"),
        P(None, "shard"),
        P(None, "shard", None),
        P(None, "shard"),
        P(None, "shard", None),
        P(None, "shard"),
    )
    return jax.shard_map(
        per_device,
        mesh=mesh,
        in_specs=placed,
        out_specs=(
            P(("rep", "shard"), None),
            P(("rep", "shard"), None),
            P(None, "shard"),
            P(None, "shard"),
            P(None, "shard", None),
            P(None, "shard"),
            P(None, "shard", None),
            P(None, "shard"),
            P(None, "shard"),
            P(None, "shard"),
            P(None, "shard", None),
            P(None, "shard"),
            P(None, "shard", None),
            P(None, "shard"),
        ),
        check_vma=False,
    )
```

```python
import functools

import jax
import jax.numpy as jnp
from jax import lax
from jax.experimental import pallas as pl
from jax.experimental.pallas import tpu as pltpu
from jax.sharding import PartitionSpec as P

MESH = pl.DeviceIdType.MESH

HEADS = 12
HEAD = 64
LAYERS = 1

epsilon = 1e-05

def to_float(value):
    return value.astype(jnp.float32)


def layer_norm(inputs, norm_gain, norm_shift):
    center = inputs - jnp.mean(inputs, axis=-1, keepdims=True)
    inverse_std = lax.rsqrt(jnp.mean(center * center, axis=-1, keepdims=True) + epsilon)
    normed = center * inverse_std
    return (normed * norm_gain + norm_shift, normed, inverse_std)


def norm_back(upstream, normed, inverse_std, norm_gain):
    scaled = upstream * norm_gain
    inner_term = scaled - jnp.mean(scaled, axis=-1, keepdims=True)
    inner_term = inner_term - normed * jnp.mean(scaled * normed, axis=-1, keepdims=True)
    return (inverse_std * inner_term, jnp.sum(upstream * normed, axis=0), jnp.sum(upstream, axis=0))


def layer_forward(inputs, allowed, small, weights):
    ln1_gain, ln1_bias, qv_bias, out_bias, ln2_gain, ln2_bias, fc_bias, proj_bias = small
    qkv_weight, out_weight, fc_weight, proj_weight = weights
    row_count = inputs.shape[0]
    width_all = inputs.shape[1]
    first_norm, normed_one, inverse_one = layer_norm(inputs, ln1_gain, ln1_bias)
    first_low = first_norm.astype(jnp.bfloat16)
    offset = jnp.concatenate(
        [qv_bias[:width_all], jnp.zeros((width_all,), jnp.float32), qv_bias[width_all:]]
    )
    projected = (
        jnp.dot(first_low, qkv_weight, preferred_element_type=jnp.float32) + offset
    ).astype(jnp.bfloat16)
    queries = projected[:, :width_all].reshape(row_count, HEADS, HEAD)
    keys_all = projected[:, width_all : 2 * width_all].reshape(row_count, HEADS, HEAD)
    values_all = projected[:, 2 * width_all :].reshape(row_count, HEADS, HEAD)
    scores = jnp.einsum(
        "qhd,khd->hqk", queries, keys_all, preferred_element_type=jnp.float32
    ) * HEAD ** (-0.5)
    scores = jnp.where(allowed[None], scores, -1e30)
    row_max = jnp.max(scores, axis=-1, keepdims=True)
    log_total = row_max + jnp.log(jnp.sum(jnp.exp(scores - row_max), axis=-1, keepdims=True))
    attn_probs = jnp.exp(scores - log_total)
    probs_low = attn_probs.astype(jnp.bfloat16)
    attn_mixed = jnp.einsum(
        "hqk,khd->qhd", probs_low, values_all, preferred_element_type=jnp.float32
    )
    attn_mixed = attn_mixed.reshape(row_count, width_all).astype(jnp.bfloat16)
    after_attn = (
        inputs + jnp.dot(attn_mixed, out_weight, preferred_element_type=jnp.float32) + out_bias
    )
    second_norm, normed_two, inverse_two = layer_norm(after_attn, ln2_gain, ln2_bias)
    second_low = second_norm.astype(jnp.bfloat16)
    hidden_pre = jnp.dot(second_low, fc_weight, preferred_element_type=jnp.float32) + fc_bias
    hidden_low = jax.nn.gelu(hidden_pre, approximate=True).astype(jnp.bfloat16)
    return dict(
        normed_one=normed_one,
        inverse_one=inverse_one,
        first_low=first_low,
        queries=queries,
        keys_all=keys_all,
        values_all=values_all,
        attn_probs=attn_probs,
        probs_low=probs_low,
        attn_mixed=attn_mixed,
        normed_two=normed_two,
        inverse_two=inverse_two,
        second_low=second_low,
        hidden_pre=hidden_pre,
        hidden_low=hidden_low,
        after_attn=after_attn,
    )


def layer_backward(upstream, saved, small, weights):
    ln1_gain, ln1_bias, qv_bias, out_bias, ln2_gain, ln2_bias, fc_bias, proj_bias = small
    qkv_weight, out_weight, fc_weight, proj_weight = weights
    row_count = upstream.shape[0]
    width_all = upstream.shape[1]
    proj_in = upstream.astype(jnp.bfloat16)
    grad_proj_b = jnp.sum(to_float(proj_in), axis=0)
    hidden_grad = jnp.einsum("td,fd->tf", proj_in, proj_weight, preferred_element_type=jnp.float32)
    _, gelu_pull = jax.vjp(lambda value: jax.nn.gelu(value, approximate=True), saved["hidden_pre"])
    pre_grad = gelu_pull(hidden_grad)[0].astype(jnp.bfloat16)
    grad_fc_b = jnp.sum(to_float(pre_grad), axis=0)
    second_grad = jnp.einsum("tf,df->td", pre_grad, fc_weight, preferred_element_type=jnp.float32)
    norm_part, grad_ln2_g, grad_ln2_b = norm_back(
        second_grad, saved["normed_two"], saved["inverse_two"], ln2_gain
    )
    residual_grad = upstream + norm_part
    branch_in = residual_grad.astype(jnp.bfloat16)
    grad_out_b = jnp.sum(to_float(branch_in), axis=0)
    mixed_grad = jnp.einsum("td,cd->tc", branch_in, out_weight, preferred_element_type=jnp.float32)
    mixed_grad = mixed_grad.astype(jnp.bfloat16).reshape(row_count, HEADS, HEAD)
    prob_grad = jnp.einsum(
        "qhd,khd->hqk", mixed_grad, saved["values_all"], preferred_element_type=jnp.float32
    )
    attn_probs = saved["attn_probs"]
    row_delta = jnp.sum(attn_probs * prob_grad, axis=-1, keepdims=True)
    score_grad = (attn_probs * (prob_grad - row_delta)).astype(jnp.bfloat16)
    query_grad = jnp.einsum(
        "hqk,khd->hqd", score_grad, saved["keys_all"], preferred_element_type=jnp.float32
    ) * HEAD ** (-0.5)
    key_grad = jnp.einsum(
        "hqk,qhd->hkd", score_grad, saved["queries"], preferred_element_type=jnp.float32
    ) * HEAD ** (-0.5)
    value_grad = jnp.einsum(
        "hqk,qhd->hkd", saved["probs_low"], mixed_grad, preferred_element_type=jnp.float32
    )
    joined_grad = (
        jnp.stack([query_grad, key_grad, value_grad])
        .transpose(2, 0, 1, 3)
        .reshape(row_count, 3 * width_all)
        .astype(jnp.bfloat16)
    )
    column_sums = jnp.sum(to_float(joined_grad), axis=0)
    grad_qv_b = jnp.concatenate([column_sums[:width_all], column_sums[2 * width_all :]])
    first_grad = jnp.einsum(
        "te,ce->tc", joined_grad, qkv_weight, preferred_element_type=jnp.float32
    )
    norm_first, grad_ln1_g, grad_ln1_b = norm_back(
        first_grad, saved["normed_one"], saved["inverse_one"], ln1_gain
    )
    small_grads = (
        grad_ln1_g,
        grad_ln1_b,
        grad_qv_b,
        grad_out_b,
        grad_ln2_g,
        grad_ln2_b,
        grad_fc_b,
        grad_proj_b,
    )
    pairs = (
        (saved["first_low"], joined_grad),
        (saved["attn_mixed"], branch_in),
        (saved["second_low"], pre_grad),
        (saved["hidden_low"], proj_in),
    )
    return (residual_grad + norm_first, small_grads, pairs)


def ring_position(shard_index, n):
    if n != 8:
        return shard_index
    y = shard_index % 2
    z = shard_index // 2
    return z * (1 - 2 * y) + 7 * y


def ring_shard(position, n):
    position = position % n
    if n != 8:
        return position
    y = position // 4
    z = (position % 4) * (1 - 2 * y) + 3 * y
    return z * 2 + y


FIRST_CORE_HALF = (0, 3)


CHAIN_RANK = (2, 3, 0, 1, 4)
CHAIN_LAG = 0


def gather_kernel(n, count, parts, plane_only, first_core, *refs):
    local = refs[:count]
    full = refs[count : 2 * count]
    ring_send, ring_recv, pair_send, pair_recv, x_send, x_recv, relay_send, relay_recv = refs[2 * count :]
    count = len(parts)

    def lview(w):
        array, row, rows = parts[w]
        return local[array] if rows is None else local[array].at[pl.ds(row, rows)]

    def fview(w, pos):
        array, row, rows = parts[w]
        return full[array].at[pos] if rows is None else full[array].at[pos, pl.ds(row, rows)]
    rep = lax.axis_index("rep")
    shard = lax.axis_index("shard")
    core = rep % 2
    plane = rep // 2
    step_dir = 1 - 2 * core
    partner = (rep + step_dir, shard)
    x_partner = ((rep + 2) % 4, shard)
    here = ring_position(shard, n)
    target = (rep, ring_shard(here + step_dir, n))
    source = (rep, ring_shard(here - step_dir, n))
    steps = n // 2
    split_last = n % 2 == 0

    barrier = pltpu.get_barrier_semaphore()
    for peer in (target, source, partner, x_partner):
        pl.semaphore_signal(barrier, inc=1, device_id=peer, device_id_type=MESH)
    pl.semaphore_wait(barrier, 4)

    def both(a, b):
        if a is True:
            return b
        if b is True:
            return a
        return jnp.logical_and(a, b)

    def core_carries(k, w, which_core):
        if split_last and k == steps:
            return (which_core == 0) == (w in first_core)
        return True

    def plane_carries(w, which_plane):
        for only, sole in enumerate(plane_only):
            if w in sole:
                return which_plane == only
        return True

    def ring_in(k, w):
        return both(plane_carries(w, plane), core_carries(k, w, core))

    def x_out(k, w):
        if not any(w in sole for sole in plane_only):
            return False
        return both(plane_carries(w, plane), core_carries(k, w, core))

    def x_in(k, w):
        if not any(w in sole for sole in plane_only):
            return False
        return both(plane_carries(w, 1 - plane), core_carries(k, w, core))

    def partner_ring_in(k, w):
        return both(plane_carries(w, plane), core_carries(k, w, 1 - core))

    def partner_x_in(k, w):
        if not any(w in sole for sole in plane_only):
            return False
        return both(plane_carries(w, 1 - plane), core_carries(k, w, 1 - core))

    def guarded(cond, fn):
        if cond is False:
            return
        if cond is True:
            fn()
        else:
            pl.when(cond)(fn)

    def slot(position):
        return ring_shard(position, n)

    def remote(src, dst, ssem, rsem, device):
        return pltpu.make_async_remote_copy(
            src_ref=src, dst_ref=dst, send_sem=ssem, recv_sem=rsem, device_id=device, device_id_type=MESH
        )

    def ring_copy(k, w):
        src_pos = here - step_dir * (k - 1)
        src = lview(w) if k == 1 else fview(w, slot(src_pos))
        return remote(src, fview(w, slot(src_pos)), ring_send.at[k - 1, w], ring_recv.at[k - 1, w], target)

    def incoming_ring(k, w):
        pos = slot(here - step_dir * k)
        return remote(fview(w, pos), fview(w, pos), ring_send.at[k - 1, w], ring_recv.at[k - 1, w], source)

    def pair_copy(k, w, pos):
        src = lview(w) if k == 0 else fview(w, slot(pos))
        return remote(src, fview(w, slot(pos)), pair_send.at[k, w], pair_recv.at[k, w], partner)

    def x_copy(k, w):
        pos = slot(here - step_dir * k)
        return remote(fview(w, pos), fview(w, pos), x_send.at[k - 1, w], x_recv.at[k - 1, w], x_partner)

    def relay_copy(k, w, pos):
        pos = slot(pos)
        return remote(fview(w, pos), fview(w, pos), relay_send.at[k - 1, w], relay_recv.at[k - 1, w], partner)

    for w in range(count):
        pair_copy(0, w, here).start()
    for w in range(count):
        guarded(ring_in(1, w), lambda w=w: ring_copy(1, w).start())
    for k in range(1, steps + 1):
        for w in range(count):
            def arrived(k=k, w=w):
                incoming_ring(k, w).wait_recv()
                if k < steps:
                    guarded(ring_in(k + 1, w), lambda: ring_copy(k + 1, w).start())
                guarded(x_out(k, w), lambda: x_copy(k, w).start())
                pair_copy(k, w, here - step_dir * k).start()
            guarded(ring_in(k, w), arrived)
        for w in range(count):
            def crossed(k=k, w=w):
                x_copy(k, w).wait_recv()
                relay_copy(k, w, here - step_dir * k).start()
            guarded(x_in(k, w), crossed)
    for w in range(count):
        pair_copy(0, w, here).wait_recv()
    for k in range(1, steps + 1):
        for w in range(count):
            guarded(partner_ring_in(k, w), lambda k=k, w=w: pair_copy(k, w, here + step_dir * k).wait_recv())
            guarded(partner_x_in(k, w), lambda k=k, w=w: relay_copy(k, w, here + step_dir * k).wait_recv())
    for w in range(count):
        pair_copy(0, w, here).wait_send()
    for k in range(1, steps + 1):
        for w in range(count):
            def sent(k=k, w=w):
                ring_copy(k, w).wait_send()
                pair_copy(k, w, here - step_dir * k).wait_send()
            guarded(ring_in(k, w), sent)
            guarded(x_out(k, w), lambda k=k, w=w: x_copy(k, w).wait_send())
            guarded(x_in(k, w), lambda k=k, w=w: relay_copy(k, w, here - step_dir * k).wait_send())


def gather_weights(locals_, n):
    count = len(locals_)
    steps = n // 2
    rows = locals_[2].shape[0]
    if n == 8 and rows % 32 == 0:
        half = rows // 2
        parts = ((0, 0, None), (1, 0, None), (2, 0, half), (2, half, half), (3, 0, None), (4, 0, None))
        plane_only = ((0, 1), (2, 3))
        first_core = (0, 4)
    else:
        parts = tuple((a, 0, None) for a in range(count))
        plane_only = ((),)
        first_core = FIRST_CORE_HALF
    pieces = len(parts)
    dma = pltpu.SemaphoreType.DMA
    return pl.pallas_call(
        functools.partial(gather_kernel, n, count, parts, plane_only, first_core),
        out_shape=[jax.ShapeDtypeStruct((n,) + a.shape, a.dtype) for a in locals_],
        in_specs=[pl.BlockSpec(memory_space=pl.ANY)] * count,
        out_specs=[pl.BlockSpec(memory_space=pl.ANY)] * count,
        scratch_shapes=[
            dma((steps, pieces)),
            dma((steps, pieces)),
            dma((steps + 1, pieces)),
            dma((steps + 1, pieces)),
            dma((steps, pieces)),
            dma((steps, pieces)),
            dma((steps, pieces)),
            dma((steps, pieces)),
        ],
        compiler_params=pltpu.CompilerParams(collective_id=0, has_side_effects=True),
    )(*locals_)


def add_rows(dst, parts, rows, chunk):
    def body(i, carry):
        window = pl.ds(pl.multiple_of(i * chunk, chunk), chunk)
        total = parts[0][window, :].astype(jnp.float32)
        for part in parts[1:]:
            total = total + part[window, :].astype(jnp.float32)
        dst[window, :] = total.astype(dst.dtype)
        return carry

    lax.fori_loop(0, rows // chunk, body, 0)


def reduce_kernel(n, count, mm, *refs):
    xt = refs[:mm]
    dy = refs[mm : 2 * mm]
    xtp = refs[2 * mm : 3 * mm]
    dyp = refs[3 * mm : 4 * mm]
    contrib = (None,) * mm + refs[4 * mm : 3 * mm + count]
    refs = refs[3 * mm + count :]
    hidden, residual, bias, weight = refs[:4]
    refs = refs[4:]
    out = refs[:count]
    tokens = refs[count]
    refs = refs[count + 1 :]
    land, send, other, own, xland, stage, xsend = (refs[i * count : (i + 1) * count] for i in range(7))
    (load_sem, own_sem, ring_send, ring_recv, pair_send, pair_recv, x_send, x_recv, back_send, back_recv) = refs[
        7 * count : 7 * count + 10
    ]
    weight_vmem, weight_sem = refs[7 * count + 10 :]
    rep = lax.axis_index("rep")
    shard = lax.axis_index("shard")
    core = rep % 2
    plane = rep // 2
    step_dir = 1 - 2 * core
    partner = (rep + step_dir, shard)
    x_partner = ((rep + 2) % 4, shard)
    here = ring_position(shard, n)
    target = (rep, ring_shard(here + step_dir, n))
    source = (rep, ring_shard(here - step_dir, n))
    steps = n // 2
    split_first = n % 2 == 0

    def carried(k, w):
        if split_first and k == 1:
            return (core == 0) == (w in FIRST_CORE_HALF)
        return True

    def guarded(cond, fn):
        if cond is True:
            fn()
        else:
            pl.when(cond)(fn)

    def block_at(k):
        return here + step_dir * (steps - k + 1)

    def load(k, w):
        return pltpu.make_async_copy(contrib[w].at[ring_shard(block_at(k), n)], send[w].at[k - 1], load_sem.at[k - 1, w])

    def load_own(w):
        return pltpu.make_async_copy(contrib[w].at[shard], own[w], own_sem.at[w])

    def remote(src, dst, ssem, rsem, device):
        return pltpu.make_async_remote_copy(
            src_ref=src, dst_ref=dst, send_sem=ssem, recv_sem=rsem, device_id=device, device_id_type=MESH
        )

    def ring_copy(k, w, device):
        return remote(send[w].at[k - 1], land[w].at[k - 1], ring_send.at[k - 1, w], ring_recv.at[k - 1, w], device)

    def pair_copy(w):
        return remote(land[w].at[steps - 1], other[w], pair_send.at[w], pair_recv.at[w], partner)

    def x_copy(w):
        return remote(xsend[w], xland[w], x_send.at[w], x_recv.at[w], x_partner)

    def back_copy(w):
        return remote(out[w], out[w], back_send.at[w], back_recv.at[w], partner)

    def owner(w):
        return core == w % 2

    def contribute(dst, w, position):
        block = ring_shard(position, n)
        width = 256

        def body(i, carry):
            window = pl.ds(pl.multiple_of(i * width, width), width)
            dst[:, window] = jnp.dot(
                xt[w][block], dy[w][:, window], preferred_element_type=jnp.float32
            ) + jnp.dot(xtp[w][block], dyp[w][:, window], preferred_element_type=jnp.float32)
            return carry

        lax.fori_loop(0, dy[w].shape[1] // width, body, 0)

    weight_copy = pltpu.make_async_copy(weight, weight_vmem, weight_sem)
    weight_copy.start()
    for w in range(mm, count):
        load_own(w).start()
    for k in range(1, steps + 1):
        for w in range(mm, count):
            guarded(carried(k, w), lambda k=k, w=w: load(k, w).start())

    barrier = pltpu.get_barrier_semaphore()
    for peer in (target, source, partner, x_partner):
        pl.semaphore_signal(barrier, inc=1, device_id=peer, device_id_type=MESH)
    pl.semaphore_wait(barrier, 4)

    def add_into(dst, parts):
        rows = dst.shape[0]
        chunk = 16 if rows % 16 == 0 else rows
        add_rows(dst, parts, rows, chunk)

    def step(k, w):
        if w < mm:
            if k == 1:
                contribute(stage[w], w, block_at(k))
            if k > 1:
                def accumulate():
                    ring_copy(k - 1, w, source).wait_recv()
                    add_into(send[w].at[k - 1], [stage[w], land[w].at[k - 2]])

                def start_chain():
                    contribute(stage[w], w, block_at(k))
                    add_into(send[w].at[k - 1], [stage[w]])

                cond = carried(k - 1, w)
                if cond is True:
                    accumulate()
                else:
                    pl.when(cond)(accumulate)
                    pl.when(jnp.logical_not(cond))(start_chain)
            else:
                add_into(send[w].at[k - 1], [stage[w]])
            ring_copy(k, w, target).start()
            if k < steps:
                contribute(stage[w], w, block_at(k + 1))
            else:
                pl.when(owner(w))(lambda: contribute(own[w], w, here))
        else:
            load(k, w).wait()
            if k > 1:
                def accumulate():
                    ring_copy(k - 1, w, source).wait_recv()
                    add_into(send[w].at[k - 1], [send[w].at[k - 1], land[w].at[k - 2]])
                guarded(carried(k - 1, w), accumulate)
            ring_copy(k, w, target).start()

    def arrive(w):
        ring_copy(steps, w, source).wait_recv()
        pl.when(jnp.logical_not(owner(w)))(lambda: pair_copy(w).start())
        mine = land[w].at[steps - 1]

        def plane():
            if w >= mm:
                load_own(w).wait()
            pair_copy(w).wait_recv()

            @pl.when(core == 0)
            def _():
                add_into(xsend[w], [own[w], mine, other[w]])

            @pl.when(core == 1)
            def _():
                add_into(xsend[w], [own[w], other[w], mine])

            x_copy(w).start()

        pl.when(owner(w))(plane)

    def total(w):
        x_copy(w).wait_recv()

        @pl.when(plane == 0)
        def _():
            add_into(out[w], [xsend[w], xland[w]])

        @pl.when(plane == 1)
        def _():
            add_into(out[w], [xland[w], xsend[w]])
        back_copy(w).start()

    rank = [CHAIN_RANK[w] if w < len(CHAIN_RANK) else w for w in range(count)]
    slots = steps + CHAIN_LAG * (count - 1)
    by_rank = sorted(range(count), key=lambda w: rank[w])
    for t in range(slots + 1):
        for w in by_rank:
            k = t - CHAIN_LAG * rank[w] + 1
            if 1 <= k <= steps:
                guarded(carried(k, w), lambda k=k, w=w: step(k, w))
        for w in by_rank:
            if steps + CHAIN_LAG * rank[w] == t:
                arrive(w)
        if t == 0:
            weight_copy.wait()
            width = 256

            def project(i, carry):
                window = pl.ds(pl.multiple_of(i * width, width), width)
                product = jnp.dot(hidden[...], weight_vmem[:, window], preferred_element_type=jnp.float32)
                tokens[:, window] = (residual[:, window] + product + bias[:, window]).astype(tokens.dtype)
                return carry

            lax.fori_loop(0, weight_vmem.shape[1] // width, project, 0)
    for w in range(count):
        pl.when(owner(w))(lambda w=w: total(w))

    for w in range(count):
        def not_owner(w=w):
            if w >= mm:
                load_own(w).wait()
            back_copy(w).wait_recv()
            pair_copy(w).wait_send()

        def was_owner(w=w):
            x_copy(w).wait_send()
            back_copy(w).wait_send()

        pl.when(owner(w))(was_owner)
        pl.when(jnp.logical_not(owner(w)))(not_owner)
    for k in range(1, steps + 1):
        for w in range(count):
            guarded(carried(k, w), lambda k=k, w=w: ring_copy(k, w, target).wait_send())


def reduce_gradients(pairs_t, contribs, head, n):
    mm = len(pairs_t)
    count = mm + len(contribs)
    steps = n // 2
    blocks = [(xt.shape[1], dy.shape[1]) for xt, dy, _, _ in pairs_t] + [c.shape[1:] for c in contribs]
    ring_types = [jnp.bfloat16] * mm + [jnp.float32] * len(contribs)
    vmem = lambda shape, dtype=jnp.float32: pltpu.VMEM(shape, dtype)
    dma = pltpu.SemaphoreType.DMA
    return pl.pallas_call(
        functools.partial(reduce_kernel, n, count, mm),
        out_shape=[jax.ShapeDtypeStruct(b, jnp.float32) for b in blocks]
        + [jax.ShapeDtypeStruct(head[1].shape, jnp.bfloat16)],
        in_specs=[pl.BlockSpec(memory_space=pltpu.VMEM)] * (4 * mm)
        + [pl.BlockSpec(memory_space=pl.ANY)] * len(contribs)
        + [pl.BlockSpec(memory_space=pltpu.VMEM)] * 3
        + [pl.BlockSpec(memory_space=pl.ANY)],
        out_specs=[pl.BlockSpec(memory_space=pltpu.VMEM)] * (count + 1),
        scratch_shapes=[vmem((steps,) + b, t) for b, t in zip(blocks, ring_types)]
        + [vmem((steps,) + b, t) for b, t in zip(blocks, ring_types)]
        + [vmem(b, t) for b, t in zip(blocks, ring_types)]
        + [vmem(b) for b in blocks]
        + [vmem(b, t) for b, t in zip(blocks, ring_types)]
        + [vmem(b) for b in blocks]
        + [vmem(b, t) for b, t in zip(blocks, ring_types)]
        + [
            dma((steps, count)),
            dma((count,)),
            dma((steps, count)),
            dma((steps, count)),
            dma((count,)),
            dma((count,)),
            dma((count,)),
            dma((count,)),
            dma((count,)),
            dma((count,)),
            pltpu.VMEM(head[3].shape, head[3].dtype),
            dma(()),
        ],
        compiler_params=pltpu.CompilerParams(
            collective_id=1, has_side_effects=True, vmem_limit_bytes=62 * 1024 * 1024
        ),
    )(*[p[0] for p in pairs_t], *[p[1] for p in pairs_t], *[p[2] for p in pairs_t], *[p[3] for p in pairs_t], *contribs, *head)


def swap_core(value):
    rep = lax.axis_size("rep")
    return lax.ppermute(value, "rep", perm=[(i, i ^ 1) for i in range(rep)])


def swap_x(value):
    rep = lax.axis_size("rep")
    return lax.ppermute(value, "rep", perm=[(i, i ^ 2) for i in range(rep)])


def join_halves(mine, theirs, core, axis):
    first = jnp.where(core == 0, mine, theirs)
    second = jnp.where(core == 0, theirs, mine)
    return jnp.concatenate([first, second], axis=axis)


def take_half(value, core, axis):
    half = value.shape[axis] // 2
    return lax.dynamic_slice_in_dim(value, core * half, half, axis=axis)


def per_device(
    tokens,
    segment_ids,
    cotangent,
    ln1_gain,
    ln1_bias,
    qkv_weight,
    qv_bias,
    out_weight,
    out_bias,
    ln2_gain,
    ln2_bias,
    fc_weight,
    fc_bias,
    proj_weight,
    proj_bias,
):
    rep = lax.axis_size("rep")
    assert rep == 4
    core = lax.axis_index("rep") % 2
    row_count = tokens.shape[0]
    positions = jnp.arange(row_count)
    allowed = (segment_ids[:, None] == segment_ids[None, :]) & (
        positions[None, :] <= positions[:, None]
    )
    layer_index = 0
    shard = lax.axis_size("shard")
    small_local = (ln1_gain, ln1_bias, qv_bias, out_bias, ln2_gain, ln2_bias, fc_bias, proj_bias)
    widths = [v.shape[1] for v in small_local]
    local_weights = (
        qkv_weight[layer_index],
        out_weight[layer_index],
        fc_weight[layer_index],
        proj_weight[layer_index],
    )
    rows_local = local_weights[0].shape[0]
    small_row = jnp.concatenate(small_local, axis=1)
    fulls = gather_weights(list(local_weights) + [small_row], shard)
    weights = tuple(f.reshape(-1, f.shape[-1]) for f in fulls[:4])
    halves = [take_half(w, core, 1) for w in local_weights]
    half_widths = [h.size // rows_local for h in halves]
    packed_all = fulls[4].reshape(shard, -1)
    small = []
    start = 0
    for width in widths:
        small.append(to_float(packed_all[:, start : start + width].reshape(-1)))
        start += width
    small = tuple(small)

    residual = to_float(tokens)
    saved = layer_forward(residual, allowed, small, weights)
    upstream = to_float(cotangent)
    input_grad, small_grads, pairs = layer_backward(upstream, saved, small, weights)

    small_mine = jnp.concatenate([g.reshape(shard, -1) for g in small_grads], axis=1)
    small_theirs = swap_core(small_mine)
    small_chip = jnp.where(core == 0, small_mine + small_theirs, small_theirs + small_mine)
    pairs_t = []
    for x, dy in pairs:
        rows_t = x.T.reshape(shard, -1, x.shape[0])
        pairs_t.append((rows_t, dy, swap_core(rows_t), swap_core(dy)))
    head = (saved["hidden_low"], saved["after_attn"], small[7].reshape(1, -1), weights[3])
    *totals, out_tokens = reduce_gradients(pairs_t, [small_chip.reshape(shard, 1, -1)], head, shard)
    small_share = totals[4]
    owned = [t[None] for t in totals[:4]]
    small_owned = []
    start = 0
    for g in small_grads:
        width = g.shape[0] // shard
        small_owned.append(small_share[:, start : start + width])
        start += width

    (g_ln1_g, g_ln1_b, g_qv_b, g_out_b, g_ln2_g, g_ln2_b, g_fc_b, g_proj_b) = small_owned
    g_qkv, g_out, g_fc, g_proj = owned
    return (
        out_tokens,
        input_grad,
        g_ln1_g,
        g_ln1_b,
        g_qkv,
        g_qv_b,
        g_out,
        g_out_b,
        g_ln2_g,
        g_ln2_b,
        g_fc,
        g_fc_b,
        g_proj,
        g_proj_b,
    )


def solution(mesh):
    placed = (
        P(("rep", "shard"), None),
        P(("rep", "shard")),
        P(("rep", "shard"), None),
        P(None, "shard"),
        P(None, "shard"),
        P(None, "shard", None),
        P(None, "shard"),
        P(None, "shard", None),
        P(None, "shard"),
        P(None, "shard"),
        P(None, "shard"),
        P(None, "shard", None),
        P(None, "shard"),
        P(None, "shard", None),
        P(None, "shard"),
    )
    return jax.shard_map(
        per_device,
        mesh=mesh,
        in_specs=placed,
        out_specs=(
            P(("rep", "shard"), None),
            P(("rep", "shard"), None),
            P(None, "shard"),
            P(None, "shard"),
            P(None, "shard", None),
            P(None, "shard"),
            P(None, "shard", None),
            P(None, "shard"),
            P(None, "shard"),
            P(None, "shard"),
            P(None, "shard", None),
            P(None, "shard"),
            P(None, "shard", None),
            P(None, "shard"),
        ),
        check_vma=False,
    )
```

```python
import functools

import jax
import jax.numpy as jnp
from jax import lax
from jax.experimental import pallas as pl
from jax.experimental.pallas import tpu as pltpu
from jax.sharding import PartitionSpec as P

MESH = pl.DeviceIdType.MESH

HEADS = 12
HEAD = 64
LAYERS = 1

epsilon = 1e-05

def to_float(value):
    return value.astype(jnp.float32)


def layer_norm(inputs, norm_gain, norm_shift):
    center = inputs - jnp.mean(inputs, axis=-1, keepdims=True)
    inverse_std = lax.rsqrt(jnp.mean(center * center, axis=-1, keepdims=True) + epsilon)
    normed = center * inverse_std
    return (normed * norm_gain + norm_shift, normed, inverse_std)


def norm_back(upstream, normed, inverse_std, norm_gain):
    scaled = upstream * norm_gain
    inner_term = scaled - jnp.mean(scaled, axis=-1, keepdims=True)
    inner_term = inner_term - normed * jnp.mean(scaled * normed, axis=-1, keepdims=True)
    return (inverse_std * inner_term, jnp.sum(upstream * normed, axis=0), jnp.sum(upstream, axis=0))


def layer_forward(inputs, allowed, small, weights):
    ln1_gain, ln1_bias, qv_bias, out_bias, ln2_gain, ln2_bias, fc_bias, proj_bias = small
    qkv_weight, out_weight, fc_weight, proj_weight = weights
    row_count = inputs.shape[0]
    width_all = inputs.shape[1]
    first_norm, normed_one, inverse_one = layer_norm(inputs, ln1_gain, ln1_bias)
    first_low = first_norm.astype(jnp.bfloat16)
    offset = jnp.concatenate(
        [qv_bias[:width_all], jnp.zeros((width_all,), jnp.float32), qv_bias[width_all:]]
    )
    projected = (
        jnp.dot(first_low, qkv_weight, preferred_element_type=jnp.float32) + offset
    ).astype(jnp.bfloat16)
    queries = projected[:, :width_all].reshape(row_count, HEADS, HEAD)
    keys_all = projected[:, width_all : 2 * width_all].reshape(row_count, HEADS, HEAD)
    values_all = projected[:, 2 * width_all :].reshape(row_count, HEADS, HEAD)
    scores = jnp.einsum(
        "qhd,khd->hqk", queries, keys_all, preferred_element_type=jnp.float32
    ) * HEAD ** (-0.5)
    scores = jnp.where(allowed[None], scores, -1e30)
    row_max = jnp.max(scores, axis=-1, keepdims=True)
    log_total = row_max + jnp.log(jnp.sum(jnp.exp(scores - row_max), axis=-1, keepdims=True))
    attn_probs = jnp.exp(scores - log_total)
    probs_low = attn_probs.astype(jnp.bfloat16)
    attn_mixed = jnp.einsum(
        "hqk,khd->qhd", probs_low, values_all, preferred_element_type=jnp.float32
    )
    attn_mixed = attn_mixed.reshape(row_count, width_all).astype(jnp.bfloat16)
    after_attn = (
        inputs + jnp.dot(attn_mixed, out_weight, preferred_element_type=jnp.float32) + out_bias
    )
    second_norm, normed_two, inverse_two = layer_norm(after_attn, ln2_gain, ln2_bias)
    second_low = second_norm.astype(jnp.bfloat16)
    hidden_pre = jnp.dot(second_low, fc_weight, preferred_element_type=jnp.float32) + fc_bias
    hidden_low = jax.nn.gelu(hidden_pre, approximate=True).astype(jnp.bfloat16)
    return dict(
        normed_one=normed_one,
        inverse_one=inverse_one,
        first_low=first_low,
        queries=queries,
        keys_all=keys_all,
        values_all=values_all,
        attn_probs=attn_probs,
        probs_low=probs_low,
        attn_mixed=attn_mixed,
        normed_two=normed_two,
        inverse_two=inverse_two,
        second_low=second_low,
        hidden_pre=hidden_pre,
        hidden_low=hidden_low,
        after_attn=after_attn,
    )


def layer_backward(upstream, saved, small, weights):
    ln1_gain, ln1_bias, qv_bias, out_bias, ln2_gain, ln2_bias, fc_bias, proj_bias = small
    qkv_weight, out_weight, fc_weight, proj_weight = weights
    row_count = upstream.shape[0]
    width_all = upstream.shape[1]
    proj_in = upstream.astype(jnp.bfloat16)
    grad_proj_b = jnp.sum(to_float(proj_in), axis=0)
    hidden_grad = jnp.einsum("td,fd->tf", proj_in, proj_weight, preferred_element_type=jnp.float32)
    _, gelu_pull = jax.vjp(lambda value: jax.nn.gelu(value, approximate=True), saved["hidden_pre"])
    pre_grad = gelu_pull(hidden_grad)[0].astype(jnp.bfloat16)
    grad_fc_b = jnp.sum(to_float(pre_grad), axis=0)
    second_grad = jnp.einsum("tf,df->td", pre_grad, fc_weight, preferred_element_type=jnp.float32)
    norm_part, grad_ln2_g, grad_ln2_b = norm_back(
        second_grad, saved["normed_two"], saved["inverse_two"], ln2_gain
    )
    residual_grad = upstream + norm_part
    branch_in = residual_grad.astype(jnp.bfloat16)
    grad_out_b = jnp.sum(to_float(branch_in), axis=0)
    mixed_grad = jnp.einsum("td,cd->tc", branch_in, out_weight, preferred_element_type=jnp.float32)
    mixed_grad = mixed_grad.astype(jnp.bfloat16).reshape(row_count, HEADS, HEAD)
    prob_grad = jnp.einsum(
        "qhd,khd->hqk", mixed_grad, saved["values_all"], preferred_element_type=jnp.float32
    )
    attn_probs = saved["attn_probs"]
    row_delta = jnp.sum(attn_probs * prob_grad, axis=-1, keepdims=True)
    score_grad = (attn_probs * (prob_grad - row_delta)).astype(jnp.bfloat16)
    query_grad = jnp.einsum(
        "hqk,khd->hqd", score_grad, saved["keys_all"], preferred_element_type=jnp.float32
    ) * HEAD ** (-0.5)
    key_grad = jnp.einsum(
        "hqk,qhd->hkd", score_grad, saved["queries"], preferred_element_type=jnp.float32
    ) * HEAD ** (-0.5)
    value_grad = jnp.einsum(
        "hqk,qhd->hkd", saved["probs_low"], mixed_grad, preferred_element_type=jnp.float32
    )
    joined_grad = (
        jnp.stack([query_grad, key_grad, value_grad])
        .transpose(2, 0, 1, 3)
        .reshape(row_count, 3 * width_all)
        .astype(jnp.bfloat16)
    )
    column_sums = jnp.sum(to_float(joined_grad), axis=0)
    grad_qv_b = jnp.concatenate([column_sums[:width_all], column_sums[2 * width_all :]])
    first_grad = jnp.einsum(
        "te,ce->tc", joined_grad, qkv_weight, preferred_element_type=jnp.float32
    )
    norm_first, grad_ln1_g, grad_ln1_b = norm_back(
        first_grad, saved["normed_one"], saved["inverse_one"], ln1_gain
    )
    small_grads = (
        grad_ln1_g,
        grad_ln1_b,
        grad_qv_b,
        grad_out_b,
        grad_ln2_g,
        grad_ln2_b,
        grad_fc_b,
        grad_proj_b,
    )
    pairs = (
        (saved["first_low"], joined_grad),
        (saved["attn_mixed"], branch_in),
        (saved["second_low"], pre_grad),
        (saved["hidden_low"], proj_in),
    )
    return (residual_grad + norm_first, small_grads, pairs)


def ring_position(shard_index, n):
    if n != 8:
        return shard_index
    y = shard_index % 2
    z = shard_index // 2
    return z * (1 - 2 * y) + 7 * y


def ring_shard(position, n):
    position = position % n
    if n != 8:
        return position
    y = position // 4
    z = (position % 4) * (1 - 2 * y) + 3 * y
    return z * 2 + y


FIRST_CORE_HALF = (0, 3)


CHAIN_RANK = (0, 1, 2, 3, 4)
CHAIN_LAG = 0


def gather_kernel(n, count, parts, plane_only, first_core, *refs):
    local = refs[:count]
    full = refs[count : 2 * count]
    ring_send, ring_recv, pair_send, pair_recv, x_send, x_recv, relay_send, relay_recv = refs[2 * count :]
    count = len(parts)

    def lview(w):
        array, row, rows = parts[w]
        return local[array] if rows is None else local[array].at[pl.ds(row, rows)]

    def fview(w, pos):
        array, row, rows = parts[w]
        return full[array].at[pos] if rows is None else full[array].at[pos, pl.ds(row, rows)]
    rep = lax.axis_index("rep")
    shard = lax.axis_index("shard")
    core = rep % 2
    plane = rep // 2
    step_dir = 1 - 2 * core
    partner = (rep + step_dir, shard)
    x_partner = ((rep + 2) % 4, shard)
    here = ring_position(shard, n)
    target = (rep, ring_shard(here + step_dir, n))
    source = (rep, ring_shard(here - step_dir, n))
    steps = n // 2
    split_last = n % 2 == 0

    barrier = pltpu.get_barrier_semaphore()
    for peer in (target, source, partner, x_partner):
        pl.semaphore_signal(barrier, inc=1, device_id=peer, device_id_type=MESH)
    pl.semaphore_wait(barrier, 4)

    def both(a, b):
        if a is True:
            return b
        if b is True:
            return a
        return jnp.logical_and(a, b)

    def core_carries(k, w, which_core):
        if split_last and k == steps:
            return (which_core == 0) == (w in first_core)
        return True

    def plane_carries(w, which_plane):
        for only, sole in enumerate(plane_only):
            if w in sole:
                return which_plane == only
        return True

    def ring_in(k, w):
        return both(plane_carries(w, plane), core_carries(k, w, core))

    def x_out(k, w):
        if not any(w in sole for sole in plane_only):
            return False
        return both(plane_carries(w, plane), core_carries(k, w, core))

    def x_in(k, w):
        if not any(w in sole for sole in plane_only):
            return False
        return both(plane_carries(w, 1 - plane), core_carries(k, w, core))

    def partner_ring_in(k, w):
        return both(plane_carries(w, plane), core_carries(k, w, 1 - core))

    def partner_x_in(k, w):
        if not any(w in sole for sole in plane_only):
            return False
        return both(plane_carries(w, 1 - plane), core_carries(k, w, 1 - core))

    def guarded(cond, fn):
        if cond is False:
            return
        if cond is True:
            fn()
        else:
            pl.when(cond)(fn)

    def slot(position):
        return ring_shard(position, n)

    def remote(src, dst, ssem, rsem, device):
        return pltpu.make_async_remote_copy(
            src_ref=src, dst_ref=dst, send_sem=ssem, recv_sem=rsem, device_id=device, device_id_type=MESH
        )

    def ring_copy(k, w):
        src_pos = here - step_dir * (k - 1)
        src = lview(w) if k == 1 else fview(w, slot(src_pos))
        return remote(src, fview(w, slot(src_pos)), ring_send.at[k - 1, w], ring_recv.at[k - 1, w], target)

    def incoming_ring(k, w):
        pos = slot(here - step_dir * k)
        return remote(fview(w, pos), fview(w, pos), ring_send.at[k - 1, w], ring_recv.at[k - 1, w], source)

    def pair_copy(k, w, pos):
        src = lview(w) if k == 0 else fview(w, slot(pos))
        return remote(src, fview(w, slot(pos)), pair_send.at[k, w], pair_recv.at[k, w], partner)

    def x_copy(k, w):
        pos = slot(here - step_dir * k)
        return remote(fview(w, pos), fview(w, pos), x_send.at[k - 1, w], x_recv.at[k - 1, w], x_partner)

    def relay_copy(k, w, pos):
        pos = slot(pos)
        return remote(fview(w, pos), fview(w, pos), relay_send.at[k - 1, w], relay_recv.at[k - 1, w], partner)

    for w in range(count):
        pair_copy(0, w, here).start()
    for w in range(count):
        guarded(ring_in(1, w), lambda w=w: ring_copy(1, w).start())
    for k in range(1, steps + 1):
        for w in range(count):
            def arrived(k=k, w=w):
                incoming_ring(k, w).wait_recv()
                if k < steps:
                    guarded(ring_in(k + 1, w), lambda: ring_copy(k + 1, w).start())
                guarded(x_out(k, w), lambda: x_copy(k, w).start())
                pair_copy(k, w, here - step_dir * k).start()
            guarded(ring_in(k, w), arrived)
        for w in range(count):
            def crossed(k=k, w=w):
                x_copy(k, w).wait_recv()
                relay_copy(k, w, here - step_dir * k).start()
            guarded(x_in(k, w), crossed)
    for w in range(count):
        pair_copy(0, w, here).wait_recv()
    for k in range(1, steps + 1):
        for w in range(count):
            guarded(partner_ring_in(k, w), lambda k=k, w=w: pair_copy(k, w, here + step_dir * k).wait_recv())
            guarded(partner_x_in(k, w), lambda k=k, w=w: relay_copy(k, w, here + step_dir * k).wait_recv())
    for w in range(count):
        pair_copy(0, w, here).wait_send()
    for k in range(1, steps + 1):
        for w in range(count):
            def sent(k=k, w=w):
                ring_copy(k, w).wait_send()
                pair_copy(k, w, here - step_dir * k).wait_send()
            guarded(ring_in(k, w), sent)
            guarded(x_out(k, w), lambda k=k, w=w: x_copy(k, w).wait_send())
            guarded(x_in(k, w), lambda k=k, w=w: relay_copy(k, w, here - step_dir * k).wait_send())


def gather_weights(locals_, n):
    count = len(locals_)
    steps = n // 2
    rows = locals_[2].shape[0]
    if n == 8 and rows % 32 == 0:
        half = rows // 2
        parts = ((0, 0, None), (1, 0, None), (2, 0, half), (2, half, half), (3, 0, None))
        parts = parts + tuple((a, 0, None) for a in range(4, count))
        plane_only = ((0, 1), (2, 3))
        first_core = (0, 4)
    else:
        parts = tuple((a, 0, None) for a in range(count))
        plane_only = ((),)
        first_core = FIRST_CORE_HALF
    pieces = len(parts)
    dma = pltpu.SemaphoreType.DMA
    return pl.pallas_call(
        functools.partial(gather_kernel, n, count, parts, plane_only, first_core),
        out_shape=[jax.ShapeDtypeStruct((n,) + a.shape, a.dtype) for a in locals_],
        in_specs=[pl.BlockSpec(memory_space=pl.ANY)] * count,
        out_specs=[pl.BlockSpec(memory_space=pl.ANY)] * count,
        scratch_shapes=[
            dma((steps, pieces)),
            dma((steps, pieces)),
            dma((steps + 1, pieces)),
            dma((steps + 1, pieces)),
            dma((steps, pieces)),
            dma((steps, pieces)),
            dma((steps, pieces)),
            dma((steps, pieces)),
        ],
        compiler_params=pltpu.CompilerParams(collective_id=0, has_side_effects=True),
    )(*locals_)


def add_rows(dst, parts, rows, chunk):
    def body(i, carry):
        window = pl.ds(pl.multiple_of(i * chunk, chunk), chunk)
        total = parts[0][window, :].astype(jnp.float32)
        for part in parts[1:]:
            total = total + part[window, :].astype(jnp.float32)
        dst[window, :] = total.astype(dst.dtype)
        return carry

    lax.fori_loop(0, rows // chunk, body, 0)


def reduce_kernel(n, count, mm, *refs):
    xt = refs[:mm]
    dy = refs[mm : 2 * mm]
    xtp = refs[2 * mm : 3 * mm]
    dyp = refs[3 * mm : 4 * mm]
    contrib = (None,) * mm + refs[4 * mm : 3 * mm + count]
    refs = refs[3 * mm + count :]
    hidden, residual, bias, weight = refs[:4]
    refs = refs[4:]
    out = refs[:count]
    tokens = refs[count]
    refs = refs[count + 1 :]
    land, send, other, own, xland, stage, xsend = (refs[i * count : (i + 1) * count] for i in range(7))
    (load_sem, own_sem, ring_send, ring_recv, pair_send, pair_recv, x_send, x_recv, back_send, back_recv) = refs[
        7 * count : 7 * count + 10
    ]
    weight_vmem, weight_sem = refs[7 * count + 10 :]
    rep = lax.axis_index("rep")
    shard = lax.axis_index("shard")
    core = rep % 2
    plane = rep // 2
    step_dir = 1 - 2 * core
    partner = (rep + step_dir, shard)
    x_partner = ((rep + 2) % 4, shard)
    here = ring_position(shard, n)
    target = (rep, ring_shard(here + step_dir, n))
    source = (rep, ring_shard(here - step_dir, n))
    steps = n // 2
    split_first = n % 2 == 0

    def carried(k, w):
        if split_first and k == 1:
            return (core == 0) == (w in FIRST_CORE_HALF)
        return True

    def guarded(cond, fn):
        if cond is True:
            fn()
        else:
            pl.when(cond)(fn)

    def block_at(k):
        return here + step_dir * (steps - k + 1)

    def load(k, w):
        return pltpu.make_async_copy(contrib[w].at[ring_shard(block_at(k), n)], send[w].at[k - 1], load_sem.at[k - 1, w])

    def load_own(w):
        return pltpu.make_async_copy(contrib[w].at[shard], own[w], own_sem.at[w])

    def remote(src, dst, ssem, rsem, device):
        return pltpu.make_async_remote_copy(
            src_ref=src, dst_ref=dst, send_sem=ssem, recv_sem=rsem, device_id=device, device_id_type=MESH
        )

    def ring_copy(k, w, device):
        return remote(send[w].at[k - 1], land[w].at[k - 1], ring_send.at[k - 1, w], ring_recv.at[k - 1, w], device)

    def pair_copy(w):
        return remote(land[w].at[steps - 1], other[w], pair_send.at[w], pair_recv.at[w], partner)

    def x_copy(w):
        return remote(xsend[w], xland[w], x_send.at[w], x_recv.at[w], x_partner)

    def back_copy(w):
        return remote(out[w], out[w], back_send.at[w], back_recv.at[w], partner)

    def owner(w):
        return core == w % 2

    def contribute(dst, w, position):
        block = ring_shard(position, n)
        width = 256

        def body(i, carry):
            window = pl.ds(pl.multiple_of(i * width, width), width)
            dst[:, window] = jnp.dot(
                xt[w][block], dy[w][:, window], preferred_element_type=jnp.float32
            ) + jnp.dot(xtp[w][block], dyp[w][:, window], preferred_element_type=jnp.float32)
            return carry

        lax.fori_loop(0, dy[w].shape[1] // width, body, 0)

    weight_copy = pltpu.make_async_copy(weight, weight_vmem, weight_sem)
    weight_copy.start()
    for w in range(mm, count):
        load_own(w).start()
    for k in range(1, steps + 1):
        for w in range(mm, count):
            guarded(carried(k, w), lambda k=k, w=w: load(k, w).start())

    barrier = pltpu.get_barrier_semaphore()
    for peer in (target, source, partner, x_partner):
        pl.semaphore_signal(barrier, inc=1, device_id=peer, device_id_type=MESH)
    pl.semaphore_wait(barrier, 4)

    def add_into(dst, parts):
        rows = dst.shape[0]
        chunk = 16 if rows % 16 == 0 else rows
        add_rows(dst, parts, rows, chunk)

    def step(k, w):
        if w < mm:
            if k == 1:
                contribute(stage[w], w, block_at(k))
            if k > 1:
                def accumulate():
                    ring_copy(k - 1, w, source).wait_recv()
                    add_into(send[w].at[k - 1], [stage[w], land[w].at[k - 2]])

                def start_chain():
                    contribute(stage[w], w, block_at(k))
                    add_into(send[w].at[k - 1], [stage[w]])

                cond = carried(k - 1, w)
                if cond is True:
                    accumulate()
                else:
                    pl.when(cond)(accumulate)
                    pl.when(jnp.logical_not(cond))(start_chain)
            else:
                add_into(send[w].at[k - 1], [stage[w]])
            ring_copy(k, w, target).start()
            if k < steps:
                contribute(stage[w], w, block_at(k + 1))
            else:
                pl.when(owner(w))(lambda: contribute(own[w], w, here))
        else:
            load(k, w).wait()
            if k > 1:
                def accumulate():
                    ring_copy(k - 1, w, source).wait_recv()
                    add_into(send[w].at[k - 1], [send[w].at[k - 1], land[w].at[k - 2]])
                guarded(carried(k - 1, w), accumulate)
            ring_copy(k, w, target).start()

    def arrive(w):
        ring_copy(steps, w, source).wait_recv()
        pl.when(jnp.logical_not(owner(w)))(lambda: pair_copy(w).start())
        mine = land[w].at[steps - 1]

        def plane():
            if w >= mm:
                load_own(w).wait()
            pair_copy(w).wait_recv()

            @pl.when(core == 0)
            def _():
                add_into(xsend[w], [own[w], mine, other[w]])

            @pl.when(core == 1)
            def _():
                add_into(xsend[w], [own[w], other[w], mine])

            x_copy(w).start()

        pl.when(owner(w))(plane)

    def total(w):
        x_copy(w).wait_recv()

        @pl.when(plane == 0)
        def _():
            add_into(out[w], [xsend[w], xland[w]])

        @pl.when(plane == 1)
        def _():
            add_into(out[w], [xland[w], xsend[w]])
        back_copy(w).start()

    rank = [CHAIN_RANK[w] if w < len(CHAIN_RANK) else w for w in range(count)]
    slots = steps + CHAIN_LAG * (count - 1)
    by_rank = sorted(range(count), key=lambda w: rank[w])
    for t in range(slots + 1):
        for w in by_rank:
            k = t - CHAIN_LAG * rank[w] + 1
            if 1 <= k <= steps:
                guarded(carried(k, w), lambda k=k, w=w: step(k, w))
        for w in by_rank:
            if steps + CHAIN_LAG * rank[w] == t:
                arrive(w)
        if t == 0:
            weight_copy.wait()
            width = 256

            def project(i, carry):
                window = pl.ds(pl.multiple_of(i * width, width), width)
                product = jnp.dot(hidden[...], weight_vmem[:, window], preferred_element_type=jnp.float32)
                tokens[:, window] = (residual[:, window] + product + bias[:, window]).astype(tokens.dtype)
                return carry

            lax.fori_loop(0, weight_vmem.shape[1] // width, project, 0)
    for w in range(count):
        pl.when(owner(w))(lambda w=w: total(w))

    for w in range(count):
        def not_owner(w=w):
            if w >= mm:
                load_own(w).wait()
            back_copy(w).wait_recv()
            pair_copy(w).wait_send()

        def was_owner(w=w):
            x_copy(w).wait_send()
            back_copy(w).wait_send()

        pl.when(owner(w))(was_owner)
        pl.when(jnp.logical_not(owner(w)))(not_owner)
    for k in range(1, steps + 1):
        for w in range(count):
            guarded(carried(k, w), lambda k=k, w=w: ring_copy(k, w, target).wait_send())


def reduce_gradients(pairs_t, contribs, head, n):
    mm = len(pairs_t)
    count = mm + len(contribs)
    steps = n // 2
    blocks = [(xt.shape[1], dy.shape[1]) for xt, dy, _, _ in pairs_t] + [c.shape[1:] for c in contribs]
    ring_types = [jnp.bfloat16] * mm + [jnp.float32] * len(contribs)
    vmem = lambda shape, dtype=jnp.float32: pltpu.VMEM(shape, dtype)
    dma = pltpu.SemaphoreType.DMA
    return pl.pallas_call(
        functools.partial(reduce_kernel, n, count, mm),
        out_shape=[jax.ShapeDtypeStruct(b, jnp.float32) for b in blocks]
        + [jax.ShapeDtypeStruct(head[1].shape, jnp.bfloat16)],
        in_specs=[pl.BlockSpec(memory_space=pltpu.VMEM)] * (4 * mm)
        + [pl.BlockSpec(memory_space=pl.ANY)] * len(contribs)
        + [pl.BlockSpec(memory_space=pltpu.VMEM)] * 3
        + [pl.BlockSpec(memory_space=pl.ANY)],
        out_specs=[pl.BlockSpec(memory_space=pltpu.VMEM)] * (count + 1),
        scratch_shapes=[vmem((steps,) + b, t) for b, t in zip(blocks, ring_types)]
        + [vmem((steps,) + b, t) for b, t in zip(blocks, ring_types)]
        + [vmem(b, t) for b, t in zip(blocks, ring_types)]
        + [vmem(b) for b in blocks]
        + [vmem(b, t) for b, t in zip(blocks, ring_types)]
        + [vmem(b) for b in blocks]
        + [vmem(b, t) for b, t in zip(blocks, ring_types)]
        + [
            dma((steps, count)),
            dma((count,)),
            dma((steps, count)),
            dma((steps, count)),
            dma((count,)),
            dma((count,)),
            dma((count,)),
            dma((count,)),
            dma((count,)),
            dma((count,)),
            pltpu.VMEM(head[3].shape, head[3].dtype),
            dma(()),
        ],
        compiler_params=pltpu.CompilerParams(
            collective_id=1, has_side_effects=True, vmem_limit_bytes=62 * 1024 * 1024
        ),
    )(*[p[0] for p in pairs_t], *[p[1] for p in pairs_t], *[p[2] for p in pairs_t], *[p[3] for p in pairs_t], *contribs, *head)


def swap_core(value):
    rep = lax.axis_size("rep")
    return lax.ppermute(value, "rep", perm=[(i, i ^ 1) for i in range(rep)])


def swap_x(value):
    rep = lax.axis_size("rep")
    return lax.ppermute(value, "rep", perm=[(i, i ^ 2) for i in range(rep)])


def join_halves(mine, theirs, core, axis):
    first = jnp.where(core == 0, mine, theirs)
    second = jnp.where(core == 0, theirs, mine)
    return jnp.concatenate([first, second], axis=axis)


def take_half(value, core, axis):
    half = value.shape[axis] // 2
    return lax.dynamic_slice_in_dim(value, core * half, half, axis=axis)


def per_device(
    tokens,
    segment_ids,
    cotangent,
    ln1_gain,
    ln1_bias,
    qkv_weight,
    qv_bias,
    out_weight,
    out_bias,
    ln2_gain,
    ln2_bias,
    fc_weight,
    fc_bias,
    proj_weight,
    proj_bias,
):
    rep = lax.axis_size("rep")
    assert rep == 4
    core = lax.axis_index("rep") % 2
    row_count = tokens.shape[0]
    positions = jnp.arange(row_count)
    allowed = (segment_ids[:, None] == segment_ids[None, :]) & (
        positions[None, :] <= positions[:, None]
    )
    layer_index = 0
    shard = lax.axis_size("shard")
    small_local = (ln1_gain, ln1_bias, qv_bias, out_bias, ln2_gain, ln2_bias, fc_bias, proj_bias)
    widths = [v.shape[1] for v in small_local]
    local_weights = (
        qkv_weight[layer_index],
        out_weight[layer_index],
        fc_weight[layer_index],
        proj_weight[layer_index],
    )
    rows_local = local_weights[0].shape[0]
    fulls = gather_weights(list(local_weights) + list(small_local), shard)
    weights = tuple(f.reshape(-1, f.shape[-1]) for f in fulls[:4])
    small = tuple(to_float(f.reshape(-1)) for f in fulls[4:])

    residual = to_float(tokens)
    saved = layer_forward(residual, allowed, small, weights)
    upstream = to_float(cotangent)
    input_grad, small_grads, pairs = layer_backward(upstream, saved, small, weights)

    small_mine = jnp.concatenate([g.reshape(shard, -1) for g in small_grads], axis=1)
    small_theirs = swap_core(small_mine)
    small_chip = jnp.where(core == 0, small_mine + small_theirs, small_theirs + small_mine)
    pairs_t = []
    for x, dy in pairs:
        rows_t = x.T.reshape(shard, -1, x.shape[0])
        pairs_t.append((rows_t, dy, swap_core(rows_t), swap_core(dy)))
    head = (saved["hidden_low"], saved["after_attn"], small[7].reshape(1, -1), weights[3])
    *totals, out_tokens = reduce_gradients(pairs_t, [small_chip.reshape(shard, 1, -1)], head, shard)
    small_share = totals[4]
    owned = [t[None] for t in totals[:4]]
    small_owned = []
    start = 0
    for g in small_grads:
        width = g.shape[0] // shard
        small_owned.append(small_share[:, start : start + width])
        start += width

    (g_ln1_g, g_ln1_b, g_qv_b, g_out_b, g_ln2_g, g_ln2_b, g_fc_b, g_proj_b) = small_owned
    g_qkv, g_out, g_fc, g_proj = owned
    return (
        out_tokens,
        input_grad,
        g_ln1_g,
        g_ln1_b,
        g_qkv,
        g_qv_b,
        g_out,
        g_out_b,
        g_ln2_g,
        g_ln2_b,
        g_fc,
        g_fc_b,
        g_proj,
        g_proj_b,
    )


def solution(mesh):
    placed = (
        P(("rep", "shard"), None),
        P(("rep", "shard")),
        P(("rep", "shard"), None),
        P(None, "shard"),
        P(None, "shard"),
        P(None, "shard", None),
        P(None, "shard"),
        P(None, "shard", None),
        P(None, "shard"),
        P(None, "shard"),
        P(None, "shard"),
        P(None, "shard", None),
        P(None, "shard"),
        P(None, "shard", None),
        P(None, "shard"),
    )
    return jax.shard_map(
        per_device,
        mesh=mesh,
        in_specs=placed,
        out_specs=(
            P(("rep", "shard"), None),
            P(("rep", "shard"), None),
            P(None, "shard"),
            P(None, "shard"),
            P(None, "shard", None),
            P(None, "shard"),
            P(None, "shard", None),
            P(None, "shard"),
            P(None, "shard"),
            P(None, "shard"),
            P(None, "shard", None),
            P(None, "shard"),
            P(None, "shard", None),
            P(None, "shard"),
        ),
        check_vma=False,
    )
```

```python
import functools

import jax
import jax.numpy as jnp
from jax import lax
from jax.experimental import pallas as pl
from jax.experimental.pallas import tpu as pltpu
from jax.sharding import PartitionSpec as P

MESH = pl.DeviceIdType.MESH

HEADS = 12
HEAD = 64
LAYERS = 1

epsilon = 1e-05

def to_float(value):
    return value.astype(jnp.float32)


def layer_norm(inputs, norm_gain, norm_shift):
    center = inputs - jnp.mean(inputs, axis=-1, keepdims=True)
    inverse_std = lax.rsqrt(jnp.mean(center * center, axis=-1, keepdims=True) + epsilon)
    normed = center * inverse_std
    return (normed * norm_gain + norm_shift, normed, inverse_std)


def norm_back(upstream, normed, inverse_std, norm_gain):
    scaled = upstream * norm_gain
    inner_term = scaled - jnp.mean(scaled, axis=-1, keepdims=True)
    inner_term = inner_term - normed * jnp.mean(scaled * normed, axis=-1, keepdims=True)
    return (inverse_std * inner_term, jnp.sum(upstream * normed, axis=0), jnp.sum(upstream, axis=0))


def layer_forward(inputs, allowed, small, weights):
    ln1_gain, ln1_bias, qv_bias, out_bias, ln2_gain, ln2_bias, fc_bias, proj_bias = small
    qkv_weight, out_weight, fc_weight, proj_weight = weights
    row_count = inputs.shape[0]
    width_all = inputs.shape[1]
    first_norm, normed_one, inverse_one = layer_norm(inputs, ln1_gain, ln1_bias)
    first_low = first_norm.astype(jnp.bfloat16)
    offset = jnp.concatenate(
        [qv_bias[:width_all], jnp.zeros((width_all,), jnp.float32), qv_bias[width_all:]]
    )
    projected = (
        jnp.dot(first_low, qkv_weight, preferred_element_type=jnp.float32) + offset
    ).astype(jnp.bfloat16)
    queries = projected[:, :width_all].reshape(row_count, HEADS, HEAD)
    keys_all = projected[:, width_all : 2 * width_all].reshape(row_count, HEADS, HEAD)
    values_all = projected[:, 2 * width_all :].reshape(row_count, HEADS, HEAD)
    scores = jnp.einsum(
        "qhd,khd->hqk", queries, keys_all, preferred_element_type=jnp.float32
    ) * HEAD ** (-0.5)
    scores = jnp.where(allowed[None], scores, -1e30)
    row_max = jnp.max(scores, axis=-1, keepdims=True)
    log_total = row_max + jnp.log(jnp.sum(jnp.exp(scores - row_max), axis=-1, keepdims=True))
    attn_probs = jnp.exp(scores - log_total)
    probs_low = attn_probs.astype(jnp.bfloat16)
    attn_mixed = jnp.einsum(
        "hqk,khd->qhd", probs_low, values_all, preferred_element_type=jnp.float32
    )
    attn_mixed = attn_mixed.reshape(row_count, width_all).astype(jnp.bfloat16)
    after_attn = (
        inputs + jnp.dot(attn_mixed, out_weight, preferred_element_type=jnp.float32) + out_bias
    )
    second_norm, normed_two, inverse_two = layer_norm(after_attn, ln2_gain, ln2_bias)
    second_low = second_norm.astype(jnp.bfloat16)
    hidden_pre = jnp.dot(second_low, fc_weight, preferred_element_type=jnp.float32) + fc_bias
    hidden_low = jax.nn.gelu(hidden_pre, approximate=True).astype(jnp.bfloat16)
    return dict(
        normed_one=normed_one,
        inverse_one=inverse_one,
        first_low=first_low,
        queries=queries,
        keys_all=keys_all,
        values_all=values_all,
        attn_probs=attn_probs,
        probs_low=probs_low,
        attn_mixed=attn_mixed,
        normed_two=normed_two,
        inverse_two=inverse_two,
        second_low=second_low,
        hidden_pre=hidden_pre,
        hidden_low=hidden_low,
        after_attn=after_attn,
    )


def layer_backward(upstream, saved, small, weights):
    ln1_gain, ln1_bias, qv_bias, out_bias, ln2_gain, ln2_bias, fc_bias, proj_bias = small
    qkv_weight, out_weight, fc_weight, proj_weight = weights
    row_count = upstream.shape[0]
    width_all = upstream.shape[1]
    proj_in = upstream.astype(jnp.bfloat16)
    grad_proj_b = jnp.sum(to_float(proj_in), axis=0)
    hidden_grad = jnp.einsum("td,fd->tf", proj_in, proj_weight, preferred_element_type=jnp.float32)
    _, gelu_pull = jax.vjp(lambda value: jax.nn.gelu(value, approximate=True), saved["hidden_pre"])
    pre_grad = gelu_pull(hidden_grad)[0].astype(jnp.bfloat16)
    grad_fc_b = jnp.sum(to_float(pre_grad), axis=0)
    second_grad = jnp.einsum("tf,df->td", pre_grad, fc_weight, preferred_element_type=jnp.float32)
    norm_part, grad_ln2_g, grad_ln2_b = norm_back(
        second_grad, saved["normed_two"], saved["inverse_two"], ln2_gain
    )
    residual_grad = upstream + norm_part
    branch_in = residual_grad.astype(jnp.bfloat16)
    grad_out_b = jnp.sum(to_float(branch_in), axis=0)
    mixed_grad = jnp.einsum("td,cd->tc", branch_in, out_weight, preferred_element_type=jnp.float32)
    mixed_grad = mixed_grad.astype(jnp.bfloat16).reshape(row_count, HEADS, HEAD)
    prob_grad = jnp.einsum(
        "qhd,khd->hqk", mixed_grad, saved["values_all"], preferred_element_type=jnp.float32
    )
    attn_probs = saved["attn_probs"]
    row_delta = jnp.sum(attn_probs * prob_grad, axis=-1, keepdims=True)
    score_grad = (attn_probs * (prob_grad - row_delta)).astype(jnp.bfloat16)
    query_grad = jnp.einsum(
        "hqk,khd->hqd", score_grad, saved["keys_all"], preferred_element_type=jnp.float32
    ) * HEAD ** (-0.5)
    key_grad = jnp.einsum(
        "hqk,qhd->hkd", score_grad, saved["queries"], preferred_element_type=jnp.float32
    ) * HEAD ** (-0.5)
    value_grad = jnp.einsum(
        "hqk,qhd->hkd", saved["probs_low"], mixed_grad, preferred_element_type=jnp.float32
    )
    joined_grad = (
        jnp.stack([query_grad, key_grad, value_grad])
        .transpose(2, 0, 1, 3)
        .reshape(row_count, 3 * width_all)
        .astype(jnp.bfloat16)
    )
    column_sums = jnp.sum(to_float(joined_grad), axis=0)
    grad_qv_b = jnp.concatenate([column_sums[:width_all], column_sums[2 * width_all :]])
    first_grad = jnp.einsum(
        "te,ce->tc", joined_grad, qkv_weight, preferred_element_type=jnp.float32
    )
    norm_first, grad_ln1_g, grad_ln1_b = norm_back(
        first_grad, saved["normed_one"], saved["inverse_one"], ln1_gain
    )
    small_grads = (
        grad_ln1_g,
        grad_ln1_b,
        grad_qv_b,
        grad_out_b,
        grad_ln2_g,
        grad_ln2_b,
        grad_fc_b,
        grad_proj_b,
    )
    pairs = (
        (saved["first_low"], joined_grad),
        (saved["attn_mixed"], branch_in),
        (saved["second_low"], pre_grad),
        (saved["hidden_low"], proj_in),
    )
    return (residual_grad + norm_first, small_grads, pairs)


def ring_position(shard_index, n):
    if n != 8:
        return shard_index
    y = shard_index % 2
    z = shard_index // 2
    return z * (1 - 2 * y) + 7 * y


def ring_shard(position, n):
    position = position % n
    if n != 8:
        return position
    y = position // 4
    z = (position % 4) * (1 - 2 * y) + 3 * y
    return z * 2 + y


FIRST_CORE_HALF = (0, 3)


CHAIN_RANK = (0, 1, 2, 3, 4)
CHAIN_LAG = 0


def gather_kernel(n, count, parts, plane_only, first_core, *refs):
    local = refs[:count]
    full = refs[count : 2 * count]
    ring_send, ring_recv, pair_send, pair_recv, x_send, x_recv, relay_send, relay_recv = refs[2 * count :]
    count = len(parts)

    def lview(w):
        array, row, rows = parts[w]
        return local[array] if rows is None else local[array].at[pl.ds(row, rows)]

    def fview(w, pos):
        array, row, rows = parts[w]
        return full[array].at[pos] if rows is None else full[array].at[pos, pl.ds(row, rows)]
    rep = lax.axis_index("rep")
    shard = lax.axis_index("shard")
    core = rep % 2
    plane = rep // 2
    step_dir = 1 - 2 * core
    partner = (rep + step_dir, shard)
    x_partner = ((rep + 2) % 4, shard)
    here = ring_position(shard, n)
    target = (rep, ring_shard(here + step_dir, n))
    source = (rep, ring_shard(here - step_dir, n))
    steps = n // 2
    split_last = n % 2 == 0

    barrier = pltpu.get_barrier_semaphore()
    for peer in (target, source, partner, x_partner):
        pl.semaphore_signal(barrier, inc=1, device_id=peer, device_id_type=MESH)
    pl.semaphore_wait(barrier, 4)

    def both(a, b):
        if a is True:
            return b
        if b is True:
            return a
        return jnp.logical_and(a, b)

    def core_carries(k, w, which_core):
        if split_last and k == steps:
            return (which_core == 0) == (w in first_core)
        return True

    def plane_carries(w, which_plane):
        for only, sole in enumerate(plane_only):
            if w in sole:
                return which_plane == only
        return True

    def ring_in(k, w):
        return both(plane_carries(w, plane), core_carries(k, w, core))

    def x_out(k, w):
        if not any(w in sole for sole in plane_only):
            return False
        return both(plane_carries(w, plane), core_carries(k, w, core))

    def x_in(k, w):
        if not any(w in sole for sole in plane_only):
            return False
        return both(plane_carries(w, 1 - plane), core_carries(k, w, core))

    def partner_ring_in(k, w):
        return both(plane_carries(w, plane), core_carries(k, w, 1 - core))

    def partner_x_in(k, w):
        if not any(w in sole for sole in plane_only):
            return False
        return both(plane_carries(w, 1 - plane), core_carries(k, w, 1 - core))

    def guarded(cond, fn):
        if cond is False:
            return
        if cond is True:
            fn()
        else:
            pl.when(cond)(fn)

    def slot(position):
        return ring_shard(position, n)

    def remote(src, dst, ssem, rsem, device):
        return pltpu.make_async_remote_copy(
            src_ref=src, dst_ref=dst, send_sem=ssem, recv_sem=rsem, device_id=device, device_id_type=MESH
        )

    def ring_copy(k, w):
        src_pos = here - step_dir * (k - 1)
        src = lview(w) if k == 1 else fview(w, slot(src_pos))
        return remote(src, fview(w, slot(src_pos)), ring_send.at[k - 1, w], ring_recv.at[k - 1, w], target)

    def incoming_ring(k, w):
        pos = slot(here - step_dir * k)
        return remote(fview(w, pos), fview(w, pos), ring_send.at[k - 1, w], ring_recv.at[k - 1, w], source)

    def pair_copy(k, w, pos):
        src = lview(w) if k == 0 else fview(w, slot(pos))
        return remote(src, fview(w, slot(pos)), pair_send.at[k, w], pair_recv.at[k, w], partner)

    def x_copy(k, w):
        pos = slot(here - step_dir * k)
        return remote(fview(w, pos), fview(w, pos), x_send.at[k - 1, w], x_recv.at[k - 1, w], x_partner)

    def relay_copy(k, w, pos):
        pos = slot(pos)
        return remote(fview(w, pos), fview(w, pos), relay_send.at[k - 1, w], relay_recv.at[k - 1, w], partner)

    for w in range(count):
        pair_copy(0, w, here).start()
    for w in range(count):
        guarded(ring_in(1, w), lambda w=w: ring_copy(1, w).start())
    for k in range(1, steps + 1):
        for w in range(count):
            def arrived(k=k, w=w):
                incoming_ring(k, w).wait_recv()
                if k < steps:
                    guarded(ring_in(k + 1, w), lambda: ring_copy(k + 1, w).start())
                guarded(x_out(k, w), lambda: x_copy(k, w).start())
                pair_copy(k, w, here - step_dir * k).start()
            guarded(ring_in(k, w), arrived)
        for w in range(count):
            def crossed(k=k, w=w):
                x_copy(k, w).wait_recv()
                relay_copy(k, w, here - step_dir * k).start()
            guarded(x_in(k, w), crossed)
    for w in range(count):
        pair_copy(0, w, here).wait_recv()
    for k in range(1, steps + 1):
        for w in range(count):
            guarded(partner_ring_in(k, w), lambda k=k, w=w: pair_copy(k, w, here + step_dir * k).wait_recv())
            guarded(partner_x_in(k, w), lambda k=k, w=w: relay_copy(k, w, here + step_dir * k).wait_recv())
    for w in range(count):
        pair_copy(0, w, here).wait_send()
    for k in range(1, steps + 1):
        for w in range(count):
            def sent(k=k, w=w):
                ring_copy(k, w).wait_send()
                pair_copy(k, w, here - step_dir * k).wait_send()
            guarded(ring_in(k, w), sent)
            guarded(x_out(k, w), lambda k=k, w=w: x_copy(k, w).wait_send())
            guarded(x_in(k, w), lambda k=k, w=w: relay_copy(k, w, here - step_dir * k).wait_send())


def gather_weights(locals_, n):
    count = len(locals_)
    steps = n // 2
    rows = locals_[2].shape[0]
    if n == 8 and rows % 32 == 0:
        half = rows // 2
        parts = ((0, 0, None), (1, 0, None), (2, 0, half), (2, half, half), (3, 0, None), (4, 0, None))
        plane_only = ((0, 1), (2, 3))
        first_core = (0, 4)
    else:
        parts = tuple((a, 0, None) for a in range(count))
        plane_only = ((),)
        first_core = FIRST_CORE_HALF
    pieces = len(parts)
    dma = pltpu.SemaphoreType.DMA
    return pl.pallas_call(
        functools.partial(gather_kernel, n, count, parts, plane_only, first_core),
        out_shape=[jax.ShapeDtypeStruct((n,) + a.shape, a.dtype) for a in locals_],
        in_specs=[pl.BlockSpec(memory_space=pl.ANY)] * count,
        out_specs=[pl.BlockSpec(memory_space=pl.ANY)] * count,
        scratch_shapes=[
            dma((steps, pieces)),
            dma((steps, pieces)),
            dma((steps + 1, pieces)),
            dma((steps + 1, pieces)),
            dma((steps, pieces)),
            dma((steps, pieces)),
            dma((steps, pieces)),
            dma((steps, pieces)),
        ],
        compiler_params=pltpu.CompilerParams(collective_id=0, has_side_effects=True),
    )(*locals_)


def add_rows(dst, parts, rows, chunk):
    def body(i, carry):
        window = pl.ds(pl.multiple_of(i * chunk, chunk), chunk)
        total = parts[0][window, :].astype(jnp.float32)
        for part in parts[1:]:
            total = total + part[window, :].astype(jnp.float32)
        dst[window, :] = total.astype(dst.dtype)
        return carry

    lax.fori_loop(0, rows // chunk, body, 0)


def reduce_kernel(n, count, mm, *refs):
    xt = refs[:mm]
    dy = refs[mm : 2 * mm]
    xtp = refs[2 * mm : 3 * mm]
    dyp = refs[3 * mm : 4 * mm]
    contrib = (None,) * mm + refs[4 * mm : 3 * mm + count]
    refs = refs[3 * mm + count :]
    residual, bias, weight = refs[:3]
    refs = refs[3:]
    out = refs[:count]
    tokens = refs[count]
    refs = refs[count + 1 :]
    land, send, other, own, xland, stage, xsend = (refs[i * count : (i + 1) * count] for i in range(7))
    (load_sem, own_sem, ring_send, ring_recv, pair_send, pair_recv, x_send, x_recv, back_send, back_recv) = refs[
        7 * count : 7 * count + 10
    ]
    weight_vmem, weight_sem = refs[7 * count + 10 :]
    rep = lax.axis_index("rep")
    shard = lax.axis_index("shard")
    core = rep % 2
    plane = rep // 2
    step_dir = 1 - 2 * core
    partner = (rep + step_dir, shard)
    x_partner = ((rep + 2) % 4, shard)
    here = ring_position(shard, n)
    target = (rep, ring_shard(here + step_dir, n))
    source = (rep, ring_shard(here - step_dir, n))
    steps = n // 2
    split_first = n % 2 == 0

    def carried(k, w):
        if split_first and k == 1:
            return (core == 0) == (w in FIRST_CORE_HALF)
        return True

    def guarded(cond, fn):
        if cond is True:
            fn()
        else:
            pl.when(cond)(fn)

    def block_at(k):
        return here + step_dir * (steps - k + 1)

    def load(k, w):
        return pltpu.make_async_copy(contrib[w].at[ring_shard(block_at(k), n)], send[w].at[k - 1], load_sem.at[k - 1, w])

    def load_own(w):
        return pltpu.make_async_copy(contrib[w].at[shard], own[w], own_sem.at[w])

    def remote(src, dst, ssem, rsem, device):
        return pltpu.make_async_remote_copy(
            src_ref=src, dst_ref=dst, send_sem=ssem, recv_sem=rsem, device_id=device, device_id_type=MESH
        )

    def ring_copy(k, w, device):
        return remote(send[w].at[k - 1], land[w].at[k - 1], ring_send.at[k - 1, w], ring_recv.at[k - 1, w], device)

    def pair_copy(w):
        return remote(land[w].at[steps - 1], other[w], pair_send.at[w], pair_recv.at[w], partner)

    def x_copy(w):
        return remote(xsend[w], xland[w], x_send.at[w], x_recv.at[w], x_partner)

    def back_copy(w):
        return remote(out[w], out[w], back_send.at[w], back_recv.at[w], partner)

    def owner(w):
        return core == w % 2

    def contribute(dst, w, position):
        block = ring_shard(position, n)
        width = 256

        def body(i, carry):
            window = pl.ds(pl.multiple_of(i * width, width), width)
            dst[:, window] = jnp.dot(
                xt[w][block], dy[w][:, window], preferred_element_type=jnp.float32
            ) + jnp.dot(xtp[w][block], dyp[w][:, window], preferred_element_type=jnp.float32)
            return carry

        lax.fori_loop(0, dy[w].shape[1] // width, body, 0)

    weight_copy = pltpu.make_async_copy(weight, weight_vmem, weight_sem)
    weight_copy.start()
    for w in range(mm, count):
        load_own(w).start()
    for k in range(1, steps + 1):
        for w in range(mm, count):
            guarded(carried(k, w), lambda k=k, w=w: load(k, w).start())

    barrier = pltpu.get_barrier_semaphore()
    for peer in (target, source, partner, x_partner):
        pl.semaphore_signal(barrier, inc=1, device_id=peer, device_id_type=MESH)
    pl.semaphore_wait(barrier, 4)

    def add_into(dst, parts):
        rows = dst.shape[0]
        chunk = 16 if rows % 16 == 0 else rows
        add_rows(dst, parts, rows, chunk)

    def step(k, w):
        if w < mm:
            if k == 1:
                contribute(stage[w], w, block_at(k))
            if k > 1:
                def accumulate():
                    ring_copy(k - 1, w, source).wait_recv()
                    add_into(send[w].at[k - 1], [stage[w], land[w].at[k - 2]])

                def start_chain():
                    contribute(stage[w], w, block_at(k))
                    add_into(send[w].at[k - 1], [stage[w]])

                cond = carried(k - 1, w)
                if cond is True:
                    accumulate()
                else:
                    pl.when(cond)(accumulate)
                    pl.when(jnp.logical_not(cond))(start_chain)
            else:
                add_into(send[w].at[k - 1], [stage[w]])
            ring_copy(k, w, target).start()
            if k < steps:
                contribute(stage[w], w, block_at(k + 1))
            else:
                pl.when(owner(w))(lambda: contribute(own[w], w, here))
        else:
            load(k, w).wait()
            if k > 1:
                def accumulate():
                    ring_copy(k - 1, w, source).wait_recv()
                    add_into(send[w].at[k - 1], [send[w].at[k - 1], land[w].at[k - 2]])
                guarded(carried(k - 1, w), accumulate)
            ring_copy(k, w, target).start()

    def arrive(w):
        ring_copy(steps, w, source).wait_recv()
        pl.when(jnp.logical_not(owner(w)))(lambda: pair_copy(w).start())
        mine = land[w].at[steps - 1]

        def plane():
            if w >= mm:
                load_own(w).wait()
            pair_copy(w).wait_recv()

            @pl.when(core == 0)
            def _():
                add_into(xsend[w], [own[w], mine, other[w]])

            @pl.when(core == 1)
            def _():
                add_into(xsend[w], [own[w], other[w], mine])

            x_copy(w).start()

        pl.when(owner(w))(plane)

    def total(w):
        x_copy(w).wait_recv()

        @pl.when(plane == 0)
        def _():
            add_into(out[w], [xsend[w], xland[w]])

        @pl.when(plane == 1)
        def _():
            add_into(out[w], [xland[w], xsend[w]])
        back_copy(w).start()

    rank = [CHAIN_RANK[w] if w < len(CHAIN_RANK) else w for w in range(count)]
    slots = steps + CHAIN_LAG * (count - 1)
    by_rank = sorted(range(count), key=lambda w: rank[w])
    for t in range(slots + 1):
        for w in by_rank:
            k = t - CHAIN_LAG * rank[w] + 1
            if 1 <= k <= steps:
                guarded(carried(k, w), lambda k=k, w=w: step(k, w))
        for w in by_rank:
            if steps + CHAIN_LAG * rank[w] == t:
                arrive(w)
        if t == 0:
            weight_copy.wait()
            width = 256

            depth = xt[mm - 1].shape[1]

            def project(i, carry):
                window = pl.ds(pl.multiple_of(i * width, width), width)
                product = None
                for j in range(n):
                    part = lax.dot_general(
                        xt[mm - 1][j],
                        weight_vmem[j * depth : (j + 1) * depth, window],
                        (((0,), (0,)), ((), ())),
                        preferred_element_type=jnp.float32,
                    )
                    product = part if product is None else product + part
                tokens[:, window] = (residual[:, window] + product + bias[:, window]).astype(tokens.dtype)
                return carry

            lax.fori_loop(0, weight_vmem.shape[1] // width, project, 0)
    for w in range(count):
        pl.when(owner(w))(lambda w=w: total(w))

    for w in range(count):
        def not_owner(w=w):
            if w >= mm:
                load_own(w).wait()
            back_copy(w).wait_recv()
            pair_copy(w).wait_send()

        def was_owner(w=w):
            x_copy(w).wait_send()
            back_copy(w).wait_send()

        pl.when(owner(w))(was_owner)
        pl.when(jnp.logical_not(owner(w)))(not_owner)
    for k in range(1, steps + 1):
        for w in range(count):
            guarded(carried(k, w), lambda k=k, w=w: ring_copy(k, w, target).wait_send())


def reduce_gradients(pairs_t, contribs, head, n):
    mm = len(pairs_t)
    count = mm + len(contribs)
    steps = n // 2
    blocks = [(xt.shape[1], dy.shape[1]) for xt, dy, _, _ in pairs_t] + [c.shape[1:] for c in contribs]
    ring_types = [jnp.bfloat16] * mm + [jnp.float32] * len(contribs)
    vmem = lambda shape, dtype=jnp.float32: pltpu.VMEM(shape, dtype)
    dma = pltpu.SemaphoreType.DMA
    return pl.pallas_call(
        functools.partial(reduce_kernel, n, count, mm),
        out_shape=[jax.ShapeDtypeStruct(b, jnp.float32) for b in blocks]
        + [jax.ShapeDtypeStruct(head[0].shape, jnp.bfloat16)],
        in_specs=[pl.BlockSpec(memory_space=pltpu.VMEM)] * (4 * mm)
        + [pl.BlockSpec(memory_space=pl.ANY)] * len(contribs)
        + [pl.BlockSpec(memory_space=pltpu.VMEM)] * 2
        + [pl.BlockSpec(memory_space=pl.ANY)],
        out_specs=[pl.BlockSpec(memory_space=pltpu.VMEM)] * (count + 1),
        scratch_shapes=[vmem((steps,) + b, t) for b, t in zip(blocks, ring_types)]
        + [vmem((steps,) + b, t) for b, t in zip(blocks, ring_types)]
        + [vmem(b, t) for b, t in zip(blocks, ring_types)]
        + [vmem(b) for b in blocks]
        + [vmem(b, t) for b, t in zip(blocks, ring_types)]
        + [vmem(b) for b in blocks]
        + [vmem(b, t) for b, t in zip(blocks, ring_types)]
        + [
            dma((steps, count)),
            dma((count,)),
            dma((steps, count)),
            dma((steps, count)),
            dma((count,)),
            dma((count,)),
            dma((count,)),
            dma((count,)),
            dma((count,)),
            dma((count,)),
            pltpu.VMEM(head[2].shape, head[2].dtype),
            dma(()),
        ],
        compiler_params=pltpu.CompilerParams(
            collective_id=1, has_side_effects=True, vmem_limit_bytes=62 * 1024 * 1024
        ),
    )(*[p[0] for p in pairs_t], *[p[1] for p in pairs_t], *[p[2] for p in pairs_t], *[p[3] for p in pairs_t], *contribs, *head)


def swap_core(value):
    rep = lax.axis_size("rep")
    return lax.ppermute(value, "rep", perm=[(i, i ^ 1) for i in range(rep)])


def swap_x(value):
    rep = lax.axis_size("rep")
    return lax.ppermute(value, "rep", perm=[(i, i ^ 2) for i in range(rep)])


def join_halves(mine, theirs, core, axis):
    first = jnp.where(core == 0, mine, theirs)
    second = jnp.where(core == 0, theirs, mine)
    return jnp.concatenate([first, second], axis=axis)


def take_half(value, core, axis):
    half = value.shape[axis] // 2
    return lax.dynamic_slice_in_dim(value, core * half, half, axis=axis)


def per_device(
    tokens,
    segment_ids,
    cotangent,
    ln1_gain,
    ln1_bias,
    qkv_weight,
    qv_bias,
    out_weight,
    out_bias,
    ln2_gain,
    ln2_bias,
    fc_weight,
    fc_bias,
    proj_weight,
    proj_bias,
):
    rep = lax.axis_size("rep")
    assert rep == 4
    core = lax.axis_index("rep") % 2
    row_count = tokens.shape[0]
    positions = jnp.arange(row_count)
    allowed = (segment_ids[:, None] == segment_ids[None, :]) & (
        positions[None, :] <= positions[:, None]
    )
    layer_index = 0
    shard = lax.axis_size("shard")
    small_local = (ln1_gain, ln1_bias, qv_bias, out_bias, ln2_gain, ln2_bias, fc_bias, proj_bias)
    widths = [v.shape[1] for v in small_local]
    local_weights = (
        qkv_weight[layer_index],
        out_weight[layer_index],
        fc_weight[layer_index],
        proj_weight[layer_index],
    )
    rows_local = local_weights[0].shape[0]
    small_row = jnp.concatenate(small_local, axis=1)
    fulls = gather_weights(list(local_weights) + [small_row], shard)
    weights = tuple(f.reshape(-1, f.shape[-1]) for f in fulls[:4])
    halves = [take_half(w, core, 1) for w in local_weights]
    half_widths = [h.size // rows_local for h in halves]
    packed_all = fulls[4].reshape(shard, -1)
    small = []
    start = 0
    for width in widths:
        small.append(to_float(packed_all[:, start : start + width].reshape(-1)))
        start += width
    small = tuple(small)

    residual = to_float(tokens)
    saved = layer_forward(residual, allowed, small, weights)
    upstream = to_float(cotangent)
    input_grad, small_grads, pairs = layer_backward(upstream, saved, small, weights)

    small_mine = jnp.concatenate([g.reshape(shard, -1) for g in small_grads], axis=1)
    small_theirs = swap_core(small_mine)
    small_chip = jnp.where(core == 0, small_mine + small_theirs, small_theirs + small_mine)
    pairs_t = []
    for x, dy in pairs:
        rows_t = x.T.reshape(shard, -1, x.shape[0])
        pairs_t.append((rows_t, dy, swap_core(rows_t), swap_core(dy)))
    head = (saved["after_attn"], small[7].reshape(1, -1), weights[3])
    *totals, out_tokens = reduce_gradients(pairs_t, [small_chip.reshape(shard, 1, -1)], head, shard)
    small_share = totals[4]
    owned = [t[None] for t in totals[:4]]
    small_owned = []
    start = 0
    for g in small_grads:
        width = g.shape[0] // shard
        small_owned.append(small_share[:, start : start + width])
        start += width

    (g_ln1_g, g_ln1_b, g_qv_b, g_out_b, g_ln2_g, g_ln2_b, g_fc_b, g_proj_b) = small_owned
    g_qkv, g_out, g_fc, g_proj = owned
    return (
        out_tokens,
        input_grad,
        g_ln1_g,
        g_ln1_b,
        g_qkv,
        g_qv_b,
        g_out,
        g_out_b,
        g_ln2_g,
        g_ln2_b,
        g_fc,
        g_fc_b,
        g_proj,
        g_proj_b,
    )


def solution(mesh):
    placed = (
        P(("rep", "shard"), None),
        P(("rep", "shard")),
        P(("rep", "shard"), None),
        P(None, "shard"),
        P(None, "shard"),
        P(None, "shard", None),
        P(None, "shard"),
        P(None, "shard", None),
        P(None, "shard"),
        P(None, "shard"),
        P(None, "shard"),
        P(None, "shard", None),
        P(None, "shard"),
        P(None, "shard", None),
        P(None, "shard"),
    )
    return jax.shard_map(
        per_device,
        mesh=mesh,
        in_specs=placed,
        out_specs=(
            P(("rep", "shard"), None),
            P(("rep", "shard"), None),
            P(None, "shard"),
            P(None, "shard"),
            P(None, "shard", None),
            P(None, "shard"),
            P(None, "shard", None),
            P(None, "shard"),
            P(None, "shard"),
            P(None, "shard"),
            P(None, "shard", None),
            P(None, "shard"),
            P(None, "shard", None),
            P(None, "shard"),
        ),
        check_vma=False,
    )
```
